32 devices in a mesh: expert: 8 (over z, x), dp: 4 (over y, core).
Axes of the slice: x: 2, y: 2, z: 4, core: 2. Of those that a mesh axis runs over, the one named last changes fastest.
Arguments:
- layer_in: bfloat16 [4096, 1024], P(('expert', 'dp')), may hold values from -6 to 6
- routes: int32 [4096, 2], P(('expert', 'dp')), may hold values from 0 to 15, as said below
- queue_slots: int32 [4096, 2], P(('expert', 'dp')), may hold values from -1 to 4, as said below
- norm_attn: float32 [1024], replicated, may hold values from 0.5 to 1.5
- w_query: bfloat16 [1024, 1024], replicated, may hold values from -0.078125 to 0.078125
- w_key: bfloat16 [1024, 1024], replicated, may hold values from -0.078125 to 0.078125
- w_value: bfloat16 [1024, 1024], replicated, may hold values from -0.1875 to 0.1875
- w_out: bfloat16 [1024, 1024], replicated, may hold values from -0.75 to 0.75
- rel_table: float32 [32, 16], replicated, may hold values from -4 to 4
- norm_moe: float32 [1024], replicated, may hold values from 0.5 to 1.5
- router: float32 [1024, 16], replicated, may hold values from -0.375 to 0.375
- w_gate: bfloat16 [16, 1024, 2816], P('expert', None, 'dp'), may hold values from -0.1875 to 0.1875
- w_up: bfloat16 [16, 1024, 2816], P('expert', None, 'dp'), may hold values from -0.1875 to 0.1875
- w_down: bfloat16 [16, 2816, 1024], P('expert', 'dp'), may hold values from -0.109375 to 0.109375
- cotangent: bfloat16 [4096, 1024], P(('expert', 'dp')), may hold values from -6 to 6
Outputs:
- layer_out: bfloat16 [4096, 1024], P(('expert', 'dp'))
- grad_input: float32 [4096, 1024], P(('expert', 'dp'))
- grad_norm_attn: float32 [1024], replicated
- grad_w_query: float32 [1024, 1024], replicated
- grad_w_key: float32 [1024, 1024], replicated
- grad_w_value: float32 [1024, 1024], replicated
- grad_w_out: float32 [1024, 1024], replicated
- grad_rel_table: float32 [32, 16], replicated
- grad_norm_moe: float32 [1024], replicated
- grad_router: float32 [1024, 16], replicated
- grad_w_gate: float32 [16, 1024, 2816], P('expert', None, 'dp')
- grad_w_up: float32 [16, 1024, 2816], P('expert', None, 'dp')
- grad_w_down: float32 [16, 2816, 1024], P('expert', 'dp')
The draws below stay inside these ranges and needn't reach their ends.
Inputs may be any that keep to these rules, and one draw needn't show every extreme that they name: `routes`: each token names two different experts. `queue_slots`: A choice's place in its expert's queue within its routing group of 32 consecutive tokens, where all first choices queue before all second choices; -1 where 5 places are already taken. Within a group each place of an expert is held by at most one choice, and an expert's places are taken from 0 upward without gaps.
All inputs are finite; a program needn't handle non-finite values.
Results may differ from the reference program's by a relative error of at most 0.014.
The reference program's roundings to bfloat16 on the way count: a program that leaves them out, or rounds other values in their place, can miss the bound.
Values may be sent and summed in bfloat16 or wider, within the bound.
A program may use at most 192 MiB of HBM per device.

```python
import math
import jax
import jax.numpy as jnp
from jax import lax

D = 1024
HEADS = 16
DH = 64
FF = 2816
BUCKETS = 32
SEQ = 128
MICRO = 4
EXPERTS = 16
GROUP = 32
CAP = 5
TOKENS = 4096
DEVICES = 32


def route_draw(key):
    folded = jax.random.fold_in(key, 11)
    keys_all = jax.random.split(folded, 6)
    group_count = TOKENS // GROUP
    popular = jax.random.permutation(keys_all[0], EXPERTS).astype(jnp.int32)
    left_draw = jax.random.randint(keys_all[1], (TOKENS, 2), 0, EXPERTS)
    right_draw = jax.random.randint(keys_all[2], (TOKENS, 2), 0, EXPERTS)
    rank_ids = jnp.minimum(left_draw, right_draw)
    chosen = jnp.take(popular, rank_ids)
    first_pick = chosen[:, 0]
    second_pick = chosen[:, 1]
    order_keys = jax.random.split(keys_all[3], group_count)
    places = jax.vmap(lambda subkey: jax.random.permutation(subkey, GROUP))(order_keys).reshape(TOKENS)
    first_pick = jnp.where(places < GROUP // 4, popular[0], first_pick)
    shifted = (first_pick + 1 + jax.random.randint(keys_all[4], (TOKENS,), 0, EXPERTS - 1)) % EXPERTS
    second_pick = jnp.where(second_pick == first_pick, shifted, second_pick)
    routes = jnp.stack([first_pick, second_pick], axis=1).astype(jnp.int32)
    prio_keys = jax.random.split(keys_all[5], group_count)
    priority = jax.vmap(lambda subkey: jax.random.permutation(subkey, GROUP))(prio_keys).astype(jnp.int32)
    queue_key = jnp.stack([priority, priority + GROUP], axis=-1).reshape(group_count, 2 * GROUP)
    group_experts = routes.reshape(group_count, 2 * GROUP)

    def count_before(group_pair):
        chosen_group, ranked = group_pair
        earlier = (chosen_group[:, None] == chosen_group[None, :]) & (ranked[None, :] < ranked[:, None])
        return jnp.sum(earlier.astype(jnp.int32), axis=1)
    queue_pos = lax.map(count_before, (group_experts, queue_key))
    slot_pos = jnp.where(queue_pos < CAP, queue_pos, -1).reshape(TOKENS, 2).astype(jnp.int32)
    return (routes, slot_pos)


def draw_routes(key, part):
    routes, slot_pos = route_draw(key)
    return routes


def draw_queue_slots(key, part):
    routes, slot_pos = route_draw(key)
    return slot_pos


def steps_of(rng, extent, cuts, least, top_value):
    gain = 1.0
    for dim, blocks in cuts:
        steps = jax.random.uniform(jax.random.fold_in(jax.random.fold_in(rng, 6), dim), (blocks,), jnp.float32, least / len(cuts), top_value / len(cuts))
        gain = gain * jnp.repeat(jnp.exp(steps), extent[dim] // blocks).reshape((-1,) + (1,) * (len(extent) - 1 - dim))
    return gain


def centred(own_key, shape, spread, bound, cuts=(), kind=jnp.bfloat16):
    entries = spread * jax.random.normal(own_key, shape, jnp.float32)
    if cuts:
        entries = entries * steps_of(own_key, shape, cuts, -0.22, 0.18)
    return jnp.clip(entries, -bound, bound).astype(kind)


def setup_inputs(seed: int = 0) -> dict:
    key_of = jax.random.split(jax.random.key(seed), 16)
    layer_in = centred(key_of[0], (TOKENS, D), 1.0, 6.0, ((0, 32),))
    routes = draw_routes(jax.random.fold_in(key_of[15], 71), 0)
    queue_slots = draw_queue_slots(jax.random.fold_in(key_of[15], 71), 0)
    norm_attn = jnp.clip(1.0 + 0.1 * jax.random.normal(key_of[3], (D,), jnp.float32), 0.5, 1.5)
    w_query = centred(key_of[4], (D, HEADS * DH), (5 * D) ** -0.5, 0.078125)
    w_key = centred(key_of[5], (D, HEADS * DH), (5 * D) ** -0.5, 0.078125)
    w_value = centred(key_of[6], (D, HEADS * DH), D ** -0.5, 0.1875)
    w_out = centred(key_of[7], (HEADS * DH, D), (8 * D // SEQ) ** -0.5, 0.75)
    rel_table = centred(key_of[8], (BUCKETS, HEADS), 1.0, 4.0, (), jnp.float32)
    norm_moe = jnp.clip(1.0 + 0.1 * jax.random.normal(key_of[9], (D,), jnp.float32), 0.5, 1.5)
    router = centred(key_of[10], (D, EXPERTS), (D // 4) ** -0.5, 0.375, (), jnp.float32)
    w_gate = centred(key_of[11], (EXPERTS, D, FF), D ** -0.5, 0.1875, ((0, 8), (2, 4)))
    w_up = centred(key_of[12], (EXPERTS, D, FF), D ** -0.5, 0.1875, ((0, 8), (2, 4)))
    w_down = centred(key_of[13], (EXPERTS, FF, D), FF ** -0.5, 0.109375, ((0, 8), (1, 4)))
    cotangent = centred(key_of[14], (TOKENS, D), 1.0, 6.0, ((0, 32),))
    return {"layer_in": layer_in, "routes": routes, "queue_slots": queue_slots, "norm_attn": norm_attn, "w_query": w_query, "w_key": w_key, "w_value": w_value, "w_out": w_out, "rel_table": rel_table, "norm_moe": norm_moe, "router": router, "w_gate": w_gate, "w_up": w_up, "w_down": w_down, "cotangent": cotangent}


epsilon = 1e-06
bucket_edges = (12, 16, 23, 32, 46, 64, 91)
highest = lax.Precision.HIGHEST

@jax.custom_vjp
def low(v):
    return lax.optimization_barrier(v.astype(jnp.bfloat16)).astype(jnp.float32)

@jax.custom_vjp
def low_back(v):
    return v

def low_keep(v):
    return (low(v), None)

def low_pass(kept, grad):
    return (grad,)

def back_keep(v):
    return (v, None)

def back_low(kept, grad):
    return (low(grad),)
low.defvjp(low_keep, low_pass)
low_back.defvjp(back_keep, back_low)

def bucket_table(query_pos, key_pos):
    relative = key_pos[None, :] - query_pos[:, None]
    distance = jnp.abs(relative)
    far_bucket = jnp.full_like(distance, 8)
    for threshold in bucket_edges:
        far_bucket = far_bucket + (distance >= threshold).astype(jnp.int32)
    bucketed = jnp.where(distance < 8, distance, far_bucket)
    return bucketed + 16 * (relative > 0).astype(jnp.int32)

def block_forward(params, block_in):
    norm_attn, w_query, w_key, w_value, w_out, rel_table, norm_moe, router, w_gate, w_up, w_down = params
    layer_rows, routes, queue_slots = block_in
    seqs = layer_rows.shape[0]
    inv_attn = lax.rsqrt(lax.optimization_barrier(jnp.mean(layer_rows * layer_rows, axis=-1, keepdims=True)) + epsilon)
    attn_in = low(layer_rows * inv_attn * norm_attn)
    queries = low(low_back(jnp.einsum('bsd,de->bse', attn_in, w_query, precision=highest)))
    key_rows = low(low_back(jnp.einsum('bsd,de->bse', attn_in, w_key, precision=highest)))
    value_rows = low(low_back(jnp.einsum('bsd,de->bse', attn_in, w_value, precision=highest)))
    query_heads = queries.reshape(seqs, SEQ, HEADS, DH)
    key_heads = key_rows.reshape(seqs, SEQ, HEADS, DH)
    value_heads = value_rows.reshape(seqs, SEQ, HEADS, DH)
    positions = jnp.arange(SEQ, dtype=jnp.int32)
    buckets = bucket_table(positions, positions)
    bias = jnp.transpose(rel_table[buckets], (2, 0, 1))
    products = low_back(jnp.einsum('bihd,bjhd->bhij', query_heads, key_heads, precision=highest))
    attn_probs = low(jax.nn.softmax(products + bias[None], axis=-1))
    context = low(low_back(jnp.einsum('bhij,bjhd->bihd', attn_probs, value_heads, precision=highest)))
    context = context.reshape(seqs, SEQ, D)
    attn = low_back(jnp.einsum('bse,ed->bsd', context, w_out, precision=highest))
    residual = layer_rows + attn
    inv_moe = lax.rsqrt(lax.optimization_barrier(jnp.mean(residual * residual, axis=-1, keepdims=True)) + epsilon)
    moe_in = residual * inv_moe * norm_moe
    logits = jnp.einsum('bsd,de->bse', moe_in, router, precision=highest)
    gate_prob = jax.nn.softmax(logits, axis=-1)
    expert_ids = jnp.arange(EXPERTS, dtype=jnp.int32)
    first_hot = (routes[..., 0:1] == expert_ids).astype(jnp.float32)
    second_hot = (routes[..., 1:2] == expert_ids).astype(jnp.float32)
    prob_first = lax.optimization_barrier(jnp.sum(gate_prob * first_hot, axis=-1, keepdims=True))
    prob_second = lax.optimization_barrier(jnp.sum(gate_prob * second_hot, axis=-1, keepdims=True))
    weight_first = prob_first / (prob_first + prob_second)
    weight_second = prob_second / (prob_first + prob_second)
    groups = seqs * MICRO
    slot_ids = jnp.arange(CAP * EXPERTS, dtype=jnp.int32)
    place = queue_slots * EXPERTS + routes
    kept = queue_slots >= 0
    select_first = ((place[..., 0:1] == slot_ids) & kept[..., 0:1]).astype(jnp.float32).reshape(groups, GROUP, CAP * EXPERTS)
    select_second = ((place[..., 1:2] == slot_ids) & kept[..., 1:2]).astype(jnp.float32).reshape(groups, GROUP, CAP * EXPERTS)
    moe_low = low(moe_in).reshape(groups, GROUP, D)
    dispatched = low_back(jnp.einsum('gtp,gtd->gpd', select_first + select_second, moe_low, precision=highest))
    dispatched = dispatched.reshape(groups, CAP, EXPERTS, D)
    gate_pre = low_back(jnp.einsum('gced,edf->gcef', dispatched, w_gate, precision=highest))
    up_pre = low_back(jnp.einsum('gced,edf->gcef', dispatched, w_up, precision=highest))
    hidden = low(jax.nn.gelu(gate_pre, approximate=True) * up_pre)
    expert_out = low(low_back(jnp.einsum('gcef,efd->gced', hidden, w_down, precision=highest)))
    expert_out = expert_out.reshape(groups, CAP * EXPERTS, D)
    picked_first = jnp.einsum('gtp,gpd->gtd', select_first, expert_out, precision=highest).reshape(seqs, SEQ, D)
    picked_second = jnp.einsum('gtp,gpd->gtd', select_second, expert_out, precision=highest).reshape(seqs, SEQ, D)
    moe = weight_first * picked_first + weight_second * picked_second
    return residual + moe

def reference(layer_in, routes, queue_slots, norm_attn, w_query, w_key, w_value, w_out, rel_table, norm_moe, router, w_gate, w_up, w_down, cotangent):
    params = (norm_attn.astype(jnp.float32), w_query.astype(jnp.float32), w_key.astype(jnp.float32), w_value.astype(jnp.float32), w_out.astype(jnp.float32), rel_table.astype(jnp.float32), norm_moe.astype(jnp.float32), router.astype(jnp.float32), w_gate.astype(jnp.float32), w_up.astype(jnp.float32), w_down.astype(jnp.float32))
    seqs_block = math.gcd(DEVICES, max(1, 4096 // SEQ))
    blocks = DEVICES // seqs_block
    route_blocks = routes.reshape(blocks, seqs_block, SEQ, 2)
    slot_blocks = queue_slots.reshape(blocks, seqs_block, SEQ, 2)
    block_step = jax.checkpoint(block_forward)

    def forward(rows_in, params_in):
        shaped = rows_in.reshape(blocks, seqs_block, SEQ, D)
        outputs = lax.map(lambda block_in: block_step(params_in, block_in), (shaped, route_blocks, slot_blocks))
        return outputs.reshape(TOKENS, D)
    layer_out, pullback = jax.vjp(forward, layer_in.astype(jnp.float32), params)
    grad_input, grads = pullback(cotangent.astype(jnp.float32))
    return (layer_out.astype(jnp.bfloat16), grad_input, grads[0], grads[1], grads[2], grads[3], grads[4], grads[5], grads[6], grads[7], grads[8], grads[9], grads[10])
```

```python
import functools
import math

import jax
import jax.numpy as jnp
from jax import lax
from jax.experimental import pallas as pl
from jax.experimental.pallas import tpu as pltpu
from jax.sharding import PartitionSpec as P

MICRO = 4

epsilon = 1e-06
bucket_edges = (12, 16, 23, 32, 46, 64, 91)
highest = lax.Precision.HIGHEST

MESH = pl.DeviceIdType.MESH
VMEM = pl.BlockSpec(memory_space=pltpu.VMEM)
DMA = pltpu.SemaphoreType.DMA


class Place:
    def __init__(self, n_expert, n_dp):
        self.n_expert, self.n_dp = n_expert, n_dp
        self.nz = math.gcd(n_expert, 4)
        self.nx = n_expert // self.nz
        self.ny = n_dp // 2
        self.e = lax.axis_index("expert")
        self.d = lax.axis_index("dp")
        self.z, self.x = self.e // self.nx, self.e % self.nx
        self.y, self.c = self.d // 2, self.d % 2

    def at(self, z=None, x=None, y=None, c=None, e=None):
        z = self.z if z is None else z
        x = self.x if x is None else x
        y = self.y if y is None else y
        c = self.c if c is None else c
        e = z * self.nx + x if e is None else e
        return (e, y * 2 + c)


def remote(src, dst, send, recv, device):
    copy = pltpu.make_async_remote_copy(
        src_ref=src, dst_ref=dst, send_sem=send, recv_sem=recv, device_id=device, device_id_type=MESH
    )
    copy.start()
    return copy


def greet(devices):
    barrier = pltpu.get_barrier_semaphore()
    for device in devices:
        pl.semaphore_signal(barrier, inc=1, device_id=device, device_id_type=MESH)
    pl.semaphore_wait(barrier, len(devices))


def column_peers(me):
    out = [me.at(c=1 - me.c)]
    out += [me.at(y=(me.y + k) % me.ny) for k in range(1, me.ny)]
    out += [me.at(e=(me.e + k) % me.n_expert) for k in range(1, me.n_expert)]
    return out


def send_rows(me, rows, recv, send_sem, recv_sem):
    copies = []
    for k in range(1, me.n_expert):
        to = (me.e + k) % me.n_expert
        copies.append(
            remote(rows.at[to], recv.at[me.c, me.y, me.e], send_sem.at[k], recv_sem.at[k], me.at(e=to))
        )
    recv[me.c, me.y, me.e] = rows[me.e]
    return copies


def pass_on(me, recv, came, sy, ry, sc, rc):
    along_y = []
    for k in range(me.n_expert):
        src = (me.e - k + me.n_expert) % me.n_expert
        if k:
            came[k - 1].wait_recv()
        block = recv.at[me.c, me.y, src]
        for s in range(1, me.ny):
            along_y.append(
                remote(block, block, sy.at[s - 1, k], ry.at[s - 1, k], me.at(y=(me.y + s) % me.ny))
            )
    block = recv.at[me.c, me.y]
    across = [remote(block, block, sc.at[0], rc.at[0], me.at(c=1 - me.c))]
    return along_y, across


def pass_across(me, recv, along_y, across, sc, rc):
    for copy in along_y:
        copy.wait_recv()
    for s in range(1, me.ny):
        block = recv.at[me.c, (me.y - s + me.ny) % me.ny]
        across.append(remote(block, block, sc.at[s], rc.at[s], me.at(c=1 - me.c)))


def spread_kernel(
    sizes, rows_per, info_ref, cot_ref, moe_ref, w_ref, g_out, x_out, w_out,
    info_all, tok, wext, rows_g, rows_x, rows_w, sem_tok_s, sem_tok_r, se, re, sy, ry, sc, rc,
):
    me = Place(*sizes)
    micro, cap, per_core = rows_per
    seq = cot_ref.shape[0]
    greet(column_peers(me))
    mate = me.at(c=1 - me.c)
    c = me.c
    first = []
    info_all[c] = info_ref[...]
    tok[0, c] = cot_ref[...]
    tok[1, c] = moe_ref[...]
    lanes = lax.broadcasted_iota(jnp.int32, (seq, 128), 1)
    for k in range(2):
        w = w_ref[:, k : k + 1]
        hi = w.astype(jnp.bfloat16).astype(jnp.float32)
        mid = (w - hi).astype(jnp.bfloat16).astype(jnp.float32)
        low = w - hi - mid
        wext[c, k] = jnp.where(
            lanes == 0, hi, jnp.where(lanes == 1, mid, jnp.where(lanes == 2, low, 0.0))
        ).astype(jnp.bfloat16)
    first.append(remote(info_all.at[c], info_all.at[c], sem_tok_s.at[0], sem_tok_r.at[0], mate))
    first.append(remote(tok.at[0, c], tok.at[0, c], sem_tok_s.at[1], sem_tok_r.at[1], mate))
    first.append(remote(tok.at[1, c], tok.at[1, c], sem_tok_s.at[2], sem_tok_r.at[2], mate))
    first.append(remote(wext.at[c], wext.at[c], sem_tok_s.at[3], sem_tok_r.at[3], mate))
    first[0].wait_recv()
    n_rows = me.n_expert * 2 * per_core
    row_ids = lax.broadcasted_iota(jnp.int32, (n_rows, seq), 0)
    group = lax.broadcasted_iota(jnp.int32, (1, seq), 1) // (seq // micro)
    hots = [[], []]
    for cc in range(2):
        for k in range(2):
            route = info_all[cc, k : k + 1, :]
            slot = info_all[cc, 2 + k : 3 + k, :]
            target = (route // 2) * (2 * per_core) + cc * per_core + group * cap + slot
            target = jnp.where((slot >= 0) & (route % 2 == c), target, -1)
            hots[k].append(jnp.where(row_ids == target, 1.0, 0.0))
    hot1 = [h.astype(jnp.bfloat16) for h in hots[0]]
    hot2 = [h.astype(jnp.bfloat16) for h in hots[1]]
    both = [(p + q).astype(jnp.bfloat16) for p, q in zip(*hots)]

    def gather(left, right):
        total = None
        for p, q in zip(left, right):
            term = jnp.dot(p, q, preferred_element_type=jnp.float32)
            total = term if total is None else total + term
        return total.astype(jnp.bfloat16).reshape(me.n_expert, 2 * per_core, -1)

    first[1].wait_recv()
    rows_g[...] = gather(both, [tok[0, 0], tok[0, 1]])
    came_g = send_rows(me, rows_g, g_out, se.at[0], re.at[0])
    first[2].wait_recv()
    first[3].wait_recv()
    rows_x[...] = gather(both, [tok[1, 0], tok[1, 1]])
    came_x = send_rows(me, rows_x, x_out, se.at[1], re.at[1])
    rows_w[...] = gather(hot1 + hot2, [wext[0, 0], wext[1, 0], wext[0, 1], wext[1, 1]])
    came_w = send_rows(me, rows_w, w_out, se.at[2], re.at[2])
    state = []
    for i, (ref, came) in enumerate(((g_out, came_g), (x_out, came_x), (w_out, came_w))):
        state.append(pass_on(me, ref, came, sy.at[i], ry.at[i], sc.at[i], rc.at[i]))
    for i, ref in enumerate((g_out, x_out, w_out)):
        pass_across(me, ref, state[i][0], state[i][1], sc.at[i], rc.at[i])
    for along_y, across in state:
        for copy in across:
            copy.wait()
        for copy in along_y:
            copy.wait_send()
    for copy in first + came_g + came_x + came_w:
        copy.wait_send()


def spread(sizes, micro, cap, info, cot, moe, weights):
    n_expert, n_dp = sizes
    ny, per_core = n_dp // 2, micro * cap
    seq, width = cot.shape
    block = (2, ny, n_expert, 2 * per_core)
    bf = jnp.bfloat16
    return pl.pallas_call(
        functools.partial(spread_kernel, sizes, (micro, cap, per_core)),
        out_shape=(
            jax.ShapeDtypeStruct(block + (width,), bf),
            jax.ShapeDtypeStruct(block + (width,), bf),
            jax.ShapeDtypeStruct(block + (128,), bf),
        ),
        in_specs=[VMEM] * 4,
        out_specs=(VMEM,) * 3,
        scratch_shapes=[
            pltpu.VMEM((2,) + info.shape, jnp.int32),
            pltpu.VMEM((2, 2, seq, width), bf),
            pltpu.VMEM((2, 2, seq, 128), bf),
            pltpu.VMEM(block[2:] + (width,), bf),
            pltpu.VMEM(block[2:] + (width,), bf),
            pltpu.VMEM(block[2:] + (128,), bf),
            DMA((4,)),
            DMA((4,)),
            DMA((3, n_expert)),
            DMA((3, n_expert)),
            DMA((3, ny, n_expert)),
            DMA((3, ny, n_expert)),
            DMA((3, ny)),
            DMA((3, ny)),
        ],
        name="spread",
        compiler_params=pltpu.CompilerParams(
            collective_id=1, has_side_effects=True, vmem_limit_bytes=48 << 20
        ),
    )(info, cot, moe, weights)


def gather_back_kernel(sizes, p0_ref, p1_ref, q_out, r1, stage, r2, final, s1, t1, s2, t2, s3, t3, s4, t4):
    me = Place(*sizes)
    greet(column_peers(me))
    c, mate = me.c, me.at(c=1 - me.c)
    p_refs = (p0_ref, p1_ref)
    count = 2
    ys = [(me.y + k) % me.ny for k in range(me.ny)]
    order = list(range(1, me.n_expert)) + [0]
    first = {}
    for i in range(count):
        for k in list(range(1, me.ny)) + [0]:
            y = ys[k]
            first[i, k] = remote(
                p_refs[i].at[1 - c, y], r1.at[i, y], s1.at[i, k], t1.at[i, k], mate
            )
    second, third, fourth = {}, {}, []
    for i in range(count):
        for k in range(1, me.ny):
            first[i, k].wait_recv()
            for j in order:
                e = (me.e + j) % me.n_expert
                total = p_refs[i][c, ys[k], e].astype(jnp.float32) + r1[i, ys[k], e].astype(jnp.float32)
                stage[i, k - 1, e] = total.astype(jnp.bfloat16)
                second[i, k, j] = remote(
                    stage.at[i, k - 1, e], r2.at[i, k - 1, e], s2.at[i, k - 1, j], t2.at[i, k - 1, j],
                    me.at(y=ys[k]),
                )
    for i in range(count):
        first[i, 0].wait_recv()
        for j in order:
            e = (me.e + j) % me.n_expert
            total = p_refs[i][c, me.y, e].astype(jnp.float32) + r1[i, me.y, e].astype(jnp.float32)
            for k in range(1, me.ny):
                second[i, k, j].wait_recv()
                total = total + r2[i, k - 1, e].astype(jnp.float32)
            if j:
                final[i, e] = total.astype(jnp.bfloat16)
                third[i, j] = remote(
                    final.at[i, e], q_out.at[i, c, me.e], s3.at[i, j], t3.at[i, j], me.at(e=e)
                )
            else:
                q_out[i, c, me.e] = total.astype(jnp.bfloat16)
    for i in range(count):
        for j in order[:-1]:
            third[i, j].wait_recv()
        block = q_out.at[i, c]
        fourth.append(remote(block, block, s4.at[i], t4.at[i], mate))
    for copy in fourth:
        copy.wait()
    for copies in (first, second, third):
        for copy in copies.values():
            copy.wait_send()


def gather_back(sizes, first, second):
    n_expert, n_dp = sizes
    count = 2
    _, ny, _, rows, width = first.shape
    bf = jnp.bfloat16
    most = max(ny - 1, 1)
    return pl.pallas_call(
        functools.partial(gather_back_kernel, sizes),
        out_shape=jax.ShapeDtypeStruct((count, 2, n_expert, rows, width), bf),
        in_specs=[VMEM] * 2,
        out_specs=VMEM,
        scratch_shapes=[
            pltpu.VMEM((count, ny, n_expert, rows, width), bf),
            pltpu.VMEM((count, most, n_expert, rows, width), bf),
            pltpu.VMEM((count, most, n_expert, rows, width), bf),
            pltpu.VMEM((count, n_expert, rows, width), bf),
            DMA((count, ny)),
            DMA((count, ny)),
            DMA((count, most, n_expert)),
            DMA((count, most, n_expert)),
            DMA((count, n_expert)),
            DMA((count, n_expert)),
            DMA((count,)),
            DMA((count,)),
        ],
        name="gather_back",
        compiler_params=pltpu.CompilerParams(
            collective_id=2, has_side_effects=True, vmem_limit_bytes=48 << 20
        ),
    )(first, second)


def reduce_kernel(
    sizes, pieces, left_ref, right_ref, small_ref, out, small_out,
    buf_a, buf_b, acc, part0, part1, part2, got0, got1, got2, half, small_half, small_got,
    fs, fr, os, ps, pr, gs, gr, ms, mr, cs, cr, ss, sr,
):
    me = Place(*sizes)
    c, mate = me.c, me.at(c=1 - me.c)
    n = me.nx
    seq = right_ref.shape[1]
    total_rows = out.shape[1]
    is0 = c == 0
    pair = jnp.where(is0, me.x, me.y)
    other = jnp.where(is0, me.y, me.x)
    lo, hi, nh = pair % 2, pair // 2, n // 2

    def along(pair_at, other_at, z=None):
        return me.at(x=jnp.where(is0, pair_at, other_at), y=jnp.where(is0, other_at, pair_at), z=z)

    flip_x, flip_y = me.x + 1 - 2 * (me.x % 2), me.y + 1 - 2 * (me.y % 2)
    dims = [
        (n, other, lambda q: along(pair, q)),
        (nh, hi, lambda q: along(q * 2 + lo, other)),
        (me.nz, me.z, lambda q: me.at(z=q)),
    ]
    parts, gots = [part0, part1, part2], [got0, got1, got2]
    levels = [i for i, d in enumerate(dims) if d[0] > 1]
    x_peers = [me.at(x=(me.x + k) % n) for k in range(1, n)]
    y_peers = [me.at(y=(me.y + k) % n) for k in range(1, n)]
    z_peers = [me.at(z=(me.z + k) % me.nz) for k in range(1, me.nz)]
    greet(
        [mate, me.at(x=flip_x, c=1 - c), me.at(y=flip_y, c=1 - c)] + x_peers + y_peers + z_peers
    )

    def slot_a(slot):
        return buf_a.at[:, pl.ds(pl.multiple_of(slot * seq, seq), seq)]

    def slot_b(slot):
        return buf_b.at[pl.ds(pl.multiple_of(slot * seq, seq), seq), :]

    targets = [
        (mate, 1 - c, other % 2, c),
        (me.at(x=flip_x, c=0), 0, flip_x % 2, 2 + c),
        (me.at(y=flip_y, c=1), 1, flip_y % 2, 2 + c),
    ]
    factor = []
    for i, (device, role, parity, slot) in enumerate(targets):
        a, b = jnp.where(role == 0, 0, parity), role * 2 + parity
        factor.append(remote(left_ref.at[a], slot_a(slot), fs.at[i, 0], fr.at[slot, 0], device))
        factor.append(remote(right_ref.at[b], slot_b(slot), fs.at[i, 1], fr.at[slot, 1], device))
    own = [
        pltpu.make_async_copy(left_ref.at[jnp.where(is0, 0, lo)], slot_a(c), os.at[0]),
        pltpu.make_async_copy(right_ref.at[c * 2 + lo], slot_b(c), os.at[1]),
    ]
    for copy in own:
        copy.start()
    rows_s = half.shape[0]
    small = [remote(small_ref.at[pl.ds((1 - c) * rows_s, rows_s)], half, ss.at[0], sr.at[0], mate)]
    small[0].wait_recv()
    small_half[0] = small_ref[pl.ds(c * rows_s, rows_s)] + half[...]
    slot = 1
    for level, (count, index, peer) in enumerate(
        ((n, me.x, lambda q: me.at(x=q)), (n, me.y, lambda q: me.at(y=q)), (me.nz, me.z, lambda q: me.at(z=q)))
    ):
        if count > 1:
            copies = []
            for k in range(1, count):
                copies.append(
                    remote(
                        small_half.at[level], small_got.at[level, index], ss.at[slot], sr.at[slot],
                        peer((index + k) % count),
                    )
                )
                slot += 1
            small_got[level, index] = small_half[level]
            for copy in copies:
                copy.wait_recv()
            small += copies
            total = small_got[level, 0]
            for k in range(1, count):
                total = total + small_got[level, k]
        else:
            total = small_half[level]
        if level < 2:
            small_half[level + 1] = total
        else:
            small_out[pl.ds(c * rows_s, rows_s)] = total
    block = small_out.at[pl.ds(c * rows_s, rows_s)]
    small.append(remote(block, block, ss.at[slot], sr.at[slot], mate))
    for where in (1 - c, 2, 3):
        for i, (src, dst) in enumerate(((left_ref, slot_a(where)), (right_ref, slot_b(where)))):
            pltpu.make_async_remote_copy(
                src_ref=src.at[0], dst_ref=dst, send_sem=fs.at[0, i], recv_sem=fr.at[where, i],
                device_id=mate, device_id_type=MESH,
            ).wait_recv()
    for copy in own:
        copy.wait()

    rows_k = total_rows // pieces
    matrix = c * 2 + lo
    pending = {}

    def multiply(k):
        acc[k] = jnp.dot(
            buf_a[k * rows_k : (k + 1) * rows_k, :], buf_b[...], preferred_element_type=jnp.float32
        )
        push(k, 0, rows_k)

    def push(k, at, rows):
        level = levels[at]
        count, index, peer = dims[level]
        size = rows // count
        copies = []
        for s in range(1, count):
            to = (index + s) % count
            parts[level][k, s - 1] = acc[k, pl.ds(pl.multiple_of(to * size, 8), size), :].astype(jnp.bfloat16)
            copies.append(
                remote(
                    parts[level].at[k, s - 1], gots[level].at[k, s - 1],
                    ps.at[level, k, s - 1], pr.at[level, k, s - 1], peer(to),
                )
            )
        pending["push", at, k] = copies

    def rows_at(at):
        rows = rows_k
        for i in range(at):
            rows //= dims[levels[i]][0]
        return rows

    def add(k, at):
        level = levels[at]
        count, index, _ = dims[level]
        size = rows_at(at) // count
        for copy in pending["push", at, k]:
            copy.wait_recv()
        total = acc[k, pl.ds(pl.multiple_of(index * size, 8), size), :]
        for s in range(1, count):
            total = total + gots[level][k, s - 1].astype(jnp.float32)
        if at + 1 < len(levels):
            acc[k, :size, :] = total
            push(k, at + 1, size)
        else:
            out[matrix, pl.ds(offset(k, at), size), :] = total.astype(jnp.bfloat16)
            share(k, at)

    def offset(k, at):
        start, rows = k * rows_k, rows_k
        for i in range(at + 1):
            count, index, _ = dims[levels[i]]
            rows //= count
            start = start + index * rows
        return pl.multiple_of(start, 8)

    def share(k, at):
        level = levels[at]
        count, index, peer = dims[level]
        size = rows_at(at) // count
        block = out.at[matrix, pl.ds(offset(k, at), size), :]
        pending["share", at, k] = [
            remote(block, block, gs.at[level, k, s - 1], gr.at[level, k, s - 1], peer((index + s) % count))
            for s in range(1, count)
        ]

    def shared(k, at):
        for copy in pending["share", at, k]:
            copy.wait_recv()
        if at:
            share(k, at - 1)
        else:
            block = out.at[matrix, pl.ds(k * rows_k, rows_k), :]
            pending["mate", k] = remote(
                block, block, ms.at[k], mr.at[k], along(pair + 1 - 2 * lo, other)
            )

    def across(k):
        pending["mate", k].wait_recv()
        block = out.at[pl.ds(2 * c, 2), pl.ds(k * rows_k, rows_k), :]
        pending["core", k] = remote(block, block, cs.at[k], cr.at[k], mate)

    steps = [multiply]
    steps += [functools.partial(add, at=i) for i in range(len(levels))]
    steps += [functools.partial(shared, at=i) for i in reversed(range(len(levels)))]
    steps += [across, lambda k: pending["core", k].wait_recv()]
    for t in range(pieces + len(steps) - 1):
        for p in reversed(range(len(steps))):
            if 0 <= t - p < pieces:
                steps[p](t - p)
    small[-1].wait_recv()
    for copy in factor + small:
        copy.wait_send()
    for copies in pending.values():
        for copy in copies if isinstance(copies, list) else [copies]:
            copy.wait_send()


def reduce_all(sizes, left, right, small):
    n_expert, n_dp = sizes
    nz = math.gcd(n_expert, 4)
    n = n_expert // nz
    nh = n // 2
    assert n == n_dp // 2
    width, seq = left.shape[1:]
    pieces = 4
    rows_k = width // pieces
    bf, f32 = jnp.bfloat16, jnp.float32
    rows_s = small.shape[0] // 2
    sizes_at = [rows_k // n, rows_k // (n * nh), rows_k // (n * nh * nz)]
    counts = [max(n - 1, 1), max(nh - 1, 1), max(nz - 1, 1)]
    most = max(counts)
    boxes = [pltpu.VMEM((pieces, q, s, width), bf) for q, s in zip(counts, sizes_at)]
    smalls = 2 * n + nz
    return pl.pallas_call(
        functools.partial(reduce_kernel, sizes, pieces),
        out_shape=(
            jax.ShapeDtypeStruct((4, width, width), bf),
            jax.ShapeDtypeStruct(small.shape, f32),
        ),
        in_specs=[VMEM] * 3,
        out_specs=(VMEM, VMEM),
        scratch_shapes=[
            pltpu.VMEM((width, 4 * seq), bf),
            pltpu.VMEM((4 * seq, width), bf),
            pltpu.VMEM((pieces, rows_k, width), f32),
            *boxes,
            *boxes,
            pltpu.VMEM((rows_s, width), f32),
            pltpu.VMEM((3, rows_s, width), f32),
            pltpu.VMEM((3, max(n, nz), rows_s, width), f32),
            DMA((3, 2)),
            DMA((4, 2)),
            DMA((2,)),
            DMA((3, pieces, most)),
            DMA((3, pieces, most)),
            DMA((3, pieces, most)),
            DMA((3, pieces, most)),
            DMA((pieces,)),
            DMA((pieces,)),
            DMA((pieces,)),
            DMA((pieces,)),
            DMA((smalls,)),
            DMA((smalls,)),
        ],
        name="reduce_all",
        compiler_params=pltpu.CompilerParams(
            collective_id=3, has_side_effects=True, vmem_limit_bytes=56 << 20
        ),
    )(left, right, small)


def rms_scale(values):
    return lax.rsqrt(jnp.mean(values * values, axis=-1, keepdims=True) + epsilon)


def bucket_hot(seq_len, buckets):
    position = jnp.arange(seq_len, dtype=jnp.int32)
    relative = position[None, :] - position[:, None]
    distance = jnp.abs(relative)
    far_bucket = jnp.full_like(distance, 8)
    for threshold in bucket_edges:
        far_bucket = far_bucket + (distance >= threshold).astype(jnp.int32)
    bucketed = jnp.where(distance < 8, distance, far_bucket) + 16 * (relative > 0).astype(jnp.int32)
    bucket_ids = jnp.arange(buckets, dtype=jnp.int32)
    return (bucketed[None, :, :] == bucket_ids[:, None, None]).astype(jnp.float32)


def gated_product(gate_pre, up_pre):
    return jax.nn.gelu(gate_pre, approximate=True) * up_pre


def dot32(pattern, left, right):
    return jnp.einsum(pattern, left, right, preferred_element_type=jnp.float32)


def shards(
    layer_in, routes, queue_slots, norm_attn, w_query, w_key, w_value, w_out, rel_table,
    norm_moe, router, w_gate, w_up, w_down, cotangent,
):
    bf, f32 = jnp.bfloat16, jnp.float32
    seq_len, width = layer_in.shape
    buckets, heads = rel_table.shape
    expert_count = router.shape[1]
    sizes = (lax.axis_size("expert"), lax.axis_size("dp"))
    n_expert, n_dp = sizes
    assert w_gate.shape[0] == 2 and expert_count == 2 * n_expert
    group_len = seq_len // MICRO
    capacity = (5 * group_len + 2 * expert_count - 1) // (2 * expert_count)
    split_heads = (seq_len, heads, width // heads)
    layer_rows = layer_in.astype(f32)
    inv_attn = rms_scale(layer_rows)
    normed_attn = layer_rows * inv_attn
    attn_in = (normed_attn * norm_attn).astype(bf)
    query_heads = dot32("sd,de->se", attn_in, w_query).astype(bf).reshape(split_heads)
    key_heads = dot32("sd,de->se", attn_in, w_key).astype(bf).reshape(split_heads)
    value_heads = dot32("sd,de->se", attn_in, w_value).astype(bf).reshape(split_heads)
    one_hot = bucket_hot(seq_len, buckets)
    bias = jnp.einsum("bij,bh->hij", one_hot, rel_table, precision=highest)
    scores = dot32("ihd,jhd->hij", query_heads, key_heads) + bias
    exponent = jnp.exp(scores - jnp.max(scores, axis=-1, keepdims=True))
    probs = exponent / jnp.sum(exponent, axis=-1, keepdims=True)
    probs_low = probs.astype(bf)
    context = dot32("hij,jhd->ihd", probs_low, value_heads).astype(bf).reshape(seq_len, width)
    residual = layer_rows + dot32("se,ed->sd", context, w_out)
    inv_moe = rms_scale(residual)
    normed_moe = residual * inv_moe
    moe_in = normed_moe * norm_moe
    logits = jnp.dot(moe_in, router, precision=highest)
    gate_prob = jax.nn.softmax(logits, axis=-1)
    expert_ids = jnp.arange(expert_count, dtype=jnp.int32)
    first_hot = (routes[:, 0:1] == expert_ids).astype(f32)
    second_hot = (routes[:, 1:2] == expert_ids).astype(f32)
    prob_first = jnp.sum(gate_prob * first_hot, axis=-1, keepdims=True)
    prob_second = jnp.sum(gate_prob * second_hot, axis=-1, keepdims=True)
    weight_first = prob_first / (prob_first + prob_second)
    weight_second = prob_second / (prob_first + prob_second)
    weights = jnp.concatenate([weight_first, weight_second], axis=1)

    info = jnp.concatenate([routes.T, queue_slots.T, jnp.zeros((4, seq_len), jnp.int32)])
    grad_in, rows_in, weight_in = spread(
        sizes, MICRO, capacity, info, cotangent, moe_in.astype(bf), weights
    )
    block = grad_in.shape[:-1]
    expert_rows = rows_in.reshape(2, -1, width)
    slot_weight = jnp.sum(weight_in[..., :3].astype(f32), axis=-1).reshape(2, -1, 1)
    grad_rows = (slot_weight * grad_in.reshape(2, -1, width).astype(f32)).astype(bf)
    gate_pre = dot32("jrd,jdf->jrf", expert_rows, w_gate)
    up_pre = dot32("jrd,jdf->jrf", expert_rows, w_up)
    product, pullback = jax.vjp(gated_product, gate_pre, up_pre)
    hidden = product.astype(bf)
    partial_out = dot32("jrf,jfd->jrd", hidden, w_down).astype(bf)
    hidden_grad = dot32("jrd,jfd->jrf", grad_rows, w_down)
    gate_grad, up_grad = [g.astype(bf) for g in pullback(hidden_grad)]
    rows_grad = dot32("jrf,jdf->jrd", gate_grad, w_gate) + dot32("jrf,jdf->jrd", up_grad, w_up)
    grad_w_gate = dot32("jrd,jrf->jdf", expert_rows, gate_grad)
    grad_w_up = dot32("jrd,jrf->jdf", expert_rows, up_grad)
    grad_w_down = dot32("jrf,jrd->jfd", hidden, grad_rows)
    back = gather_back(
        sizes, partial_out.reshape(block + (width,)), rows_grad.astype(bf).reshape(block + (width,))
    )
    back = back.reshape(2, -1, width)

    core = lax.axis_index("dp") % 2
    per_core = MICRO * capacity
    token = jnp.arange(seq_len, dtype=jnp.int32)[:, None]
    place = (routes % 2) * (n_expert * 2 * per_core) + (routes // 2) * (2 * per_core)
    place = place + core * per_core + (token // group_len) * capacity + queue_slots
    place = jnp.where(queue_slots >= 0, place, -1)
    slot_ids = jnp.arange(2 * n_expert * 2 * per_core, dtype=jnp.int32)
    select_first = (place[:, 0:1] == slot_ids).astype(bf)
    select_second = (place[:, 1:2] == slot_ids).astype(bf)
    picked_first = dot32("tp,pd->td", select_first, back[0])
    picked_second = dot32("tp,pd->td", select_second, back[0])
    moe = weight_first * picked_first + weight_second * picked_second
    layer_out = (residual + moe).astype(bf)
    cot_rows = cotangent.astype(f32)
    grad_weight_first = jnp.sum(cot_rows * picked_first, axis=-1, keepdims=True)
    grad_weight_second = jnp.sum(cot_rows * picked_second, axis=-1, keepdims=True)
    grad_from_slots = dot32("tp,pd->td", select_first + select_second, back[1])
    mean_grad = weight_first * grad_weight_first + weight_second * grad_weight_second
    logit_first = weight_first * (grad_weight_first - mean_grad)
    logit_second = weight_second * (grad_weight_second - mean_grad)
    grad_logits = logit_first * first_hot + logit_second * second_hot
    grad_router = jnp.einsum("sd,se->ed", moe_in, grad_logits, precision=highest)
    grad_moe_in = grad_from_slots + jnp.einsum("se,de->sd", grad_logits, router, precision=highest)
    grad_norm_moe = jnp.sum(grad_moe_in * normed_moe, axis=0)
    grad_normed = grad_moe_in * norm_moe
    grad_residual = cot_rows + inv_moe * (
        grad_normed - normed_moe * jnp.mean(grad_normed * normed_moe, axis=-1, keepdims=True)
    )
    grad_attn_low = grad_residual.astype(bf)
    grad_context = dot32("sd,ed->se", grad_attn_low, w_out).astype(bf).reshape(split_heads)
    grad_values = dot32("hij,ihd->jhd", probs_low, grad_context).astype(bf).reshape(seq_len, width)
    grad_probs = dot32("ihd,jhd->hij", grad_context, value_heads)
    grad_scores = probs * (grad_probs - jnp.sum(probs * grad_probs, axis=-1, keepdims=True))
    grad_rel_table = jnp.einsum("bij,hij->bh", one_hot, grad_scores, precision=highest)
    scores_low = grad_scores.astype(bf)
    grad_queries = dot32("hij,jhd->ihd", scores_low, key_heads).astype(bf).reshape(seq_len, width)
    grad_keys = dot32("hij,ihd->jhd", scores_low, query_heads).astype(bf).reshape(seq_len, width)
    grad_attn_in = dot32("se,de->sd", grad_queries, w_query)
    grad_attn_in = grad_attn_in + dot32("se,de->sd", grad_keys, w_key)
    grad_attn_in = grad_attn_in + dot32("se,de->sd", grad_values, w_value)
    grad_norm_attn = jnp.sum(grad_attn_in * normed_attn, axis=0)
    grad_normed_attn = grad_attn_in * norm_attn
    grad_input = grad_residual + inv_attn * (
        grad_normed_attn
        - normed_attn * jnp.mean(grad_normed_attn * normed_attn, axis=-1, keepdims=True)
    )
    table = grad_rel_table.reshape(-1)
    small = jnp.concatenate(
        [
            grad_router,
            grad_norm_attn[None],
            grad_norm_moe[None],
            jnp.pad(table, (0, width - table.size))[None],
        ]
    )
    small = jnp.pad(small, ((0, -small.shape[0] % 16), (0, 0)))
    sums, small = reduce_all(
        sizes,
        jnp.stack([attn_in.T, context.T]),
        jnp.stack([grad_queries, grad_keys, grad_values, grad_attn_low]),
        small,
    )
    matrices = [sums[i].astype(f32) for i in range(4)]
    return (
        layer_out, grad_input, small[expert_count], *matrices,
        small[expert_count + 2, : table.size].reshape(buckets, heads),
        small[expert_count + 1], small[:expert_count].T, grad_w_gate, grad_w_up, grad_w_down,
    )


def solution(mesh):
    in_specs = (
        P(("expert", "dp"), None),
        P(("expert", "dp"), None),
        P(("expert", "dp"), None),
        P(),
        P(),
        P(),
        P(),
        P(),
        P(),
        P(),
        P(),
        P("expert", None, "dp"),
        P("expert", None, "dp"),
        P("expert", "dp", None),
        P(("expert", "dp"), None),
    )
    out_specs = (
        P(("expert", "dp"), None),
        P(("expert", "dp"), None),
        P(),
        P(),
        P(),
        P(),
        P(),
        P(),
        P(),
        P(),
        P("expert", None, "dp"),
        P("expert", None, "dp"),
        P("expert", "dp", None),
    )
    return jax.shard_map(shards, mesh=mesh, in_specs=in_specs, out_specs=out_specs, check_vma=False)
```

```python
import functools
import math

import jax
import jax.numpy as jnp
from jax import lax
from jax.experimental import pallas as pl
from jax.experimental.pallas import tpu as pltpu
from jax.sharding import PartitionSpec as P

MICRO = 4

epsilon = 1e-06
bucket_edges = (12, 16, 23, 32, 46, 64, 91)
highest = lax.Precision.HIGHEST

MESH = pl.DeviceIdType.MESH
VMEM = pl.BlockSpec(memory_space=pltpu.VMEM)
DMA = pltpu.SemaphoreType.DMA


class Place:
    def __init__(self, n_expert, n_dp):
        self.n_expert, self.n_dp = n_expert, n_dp
        self.nz = math.gcd(n_expert, 4)
        self.nx = n_expert // self.nz
        self.ny = n_dp // 2
        self.e = lax.axis_index("expert")
        self.d = lax.axis_index("dp")
        self.z, self.x = self.e // self.nx, self.e % self.nx
        self.y, self.c = self.d // 2, self.d % 2

    def at(self, z=None, x=None, y=None, c=None, e=None):
        z = self.z if z is None else z
        x = self.x if x is None else x
        y = self.y if y is None else y
        c = self.c if c is None else c
        e = z * self.nx + x if e is None else e
        return (e, y * 2 + c)


def remote(src, dst, send, recv, device):
    copy = pltpu.make_async_remote_copy(
        src_ref=src, dst_ref=dst, send_sem=send, recv_sem=recv, device_id=device, device_id_type=MESH
    )
    copy.start()
    return copy


def greet(devices):
    barrier = pltpu.get_barrier_semaphore()
    for device in devices:
        pl.semaphore_signal(barrier, inc=1, device_id=device, device_id_type=MESH)
    pl.semaphore_wait(barrier, len(devices))


def column_peers(me):
    out = [me.at(c=1 - me.c)]
    out += [me.at(y=(me.y + k) % me.ny) for k in range(1, me.ny)]
    out += [me.at(e=(me.e + k) % me.n_expert) for k in range(1, me.n_expert)]
    return out


def send_rows(me, rows, recv, send_sem, recv_sem):
    copies = []
    for k in range(1, me.n_expert):
        to = (me.e + k) % me.n_expert
        copies.append(
            remote(
                rows.at[to], recv.at[me.c, me.y * me.n_expert + me.e],
                send_sem.at[k], recv_sem.at[k], me.at(e=to),
            )
        )
    recv[me.c, me.y * me.n_expert + me.e] = rows[me.e]
    return copies


def pass_on(me, recv, came, sy, ry, sc, rc):
    along_y = []
    for k in range(me.n_expert):
        src = (me.e - k + me.n_expert) % me.n_expert
        if k:
            came[k - 1].wait_recv()
        block = recv.at[me.c, me.y * me.n_expert + src]
        for s in range(1, me.ny):
            along_y.append(
                remote(block, block, sy.at[s - 1, k], ry.at[s - 1, k], me.at(y=(me.y + s) % me.ny))
            )
    block = recv.at[me.c, pl.ds(me.y * me.n_expert, me.n_expert)]
    across = [remote(block, block, sc.at[0], rc.at[0], me.at(c=1 - me.c))]
    return along_y, across


def pass_across(me, recv, along_y, across, sc, rc):
    for copy in along_y:
        copy.wait_recv()
    for s in range(1, me.ny):
        column = (me.y - s + me.ny) % me.ny * me.n_expert
        block = recv.at[me.c, pl.ds(column, me.n_expert)]
        across.append(remote(block, block, sc.at[s], rc.at[s], me.at(c=1 - me.c)))


def spread_kernel(
    sizes, rows_per, info_ref, cot_ref, moe_ref, w_ref, g_out, x_out, w_out,
    info_all, tok, wext, rows_g, rows_x, rows_w, sem_tok_s, sem_tok_r, se, re, sy, ry, sc, rc,
):
    me = Place(*sizes)
    micro, cap, per_core = rows_per
    seq = cot_ref.shape[0]
    greet(column_peers(me))
    mate = me.at(c=1 - me.c)
    c = me.c
    first = []
    info_all[c] = info_ref[...]
    tok[0, c] = cot_ref[...]
    tok[1, c] = moe_ref[...]
    lanes = lax.broadcasted_iota(jnp.int32, (seq, 128), 1)
    for k in range(2):
        w = w_ref[:, k : k + 1]
        hi = w.astype(jnp.bfloat16).astype(jnp.float32)
        mid = (w - hi).astype(jnp.bfloat16).astype(jnp.float32)
        low = w - hi - mid
        wext[c, k] = jnp.where(
            lanes == 0, hi, jnp.where(lanes == 1, mid, jnp.where(lanes == 2, low, 0.0))
        ).astype(jnp.bfloat16)
    first.append(remote(info_all.at[c], info_all.at[c], sem_tok_s.at[0], sem_tok_r.at[0], mate))
    first.append(remote(tok.at[0, c], tok.at[0, c], sem_tok_s.at[1], sem_tok_r.at[1], mate))
    first.append(remote(tok.at[1, c], tok.at[1, c], sem_tok_s.at[2], sem_tok_r.at[2], mate))
    first.append(remote(wext.at[c], wext.at[c], sem_tok_s.at[3], sem_tok_r.at[3], mate))
    first[0].wait_recv()
    n_rows = me.n_expert * 2 * per_core
    row_ids = lax.broadcasted_iota(jnp.int32, (n_rows, seq), 0)
    group = lax.broadcasted_iota(jnp.int32, (1, seq), 1) // (seq // micro)
    hots = [[], []]
    for cc in range(2):
        for k in range(2):
            route = info_all[cc, k : k + 1, :]
            slot = info_all[cc, 2 + k : 3 + k, :]
            target = (route // 2) * (2 * per_core) + cc * per_core + group * cap + slot
            target = jnp.where((slot >= 0) & (route % 2 == c), target, -1)
            hots[k].append(jnp.where(row_ids == target, 1.0, 0.0))
    hot1 = [h.astype(jnp.bfloat16) for h in hots[0]]
    hot2 = [h.astype(jnp.bfloat16) for h in hots[1]]
    both = [(p + q).astype(jnp.bfloat16) for p, q in zip(*hots)]

    def gather(left, right):
        total = None
        for p, q in zip(left, right):
            term = jnp.dot(p, q, preferred_element_type=jnp.float32)
            total = term if total is None else total + term
        return total.astype(jnp.bfloat16).reshape(me.n_expert, 2 * per_core, -1)

    first[1].wait_recv()
    rows_g[...] = gather(both, [tok[0, 0], tok[0, 1]])
    came_g = send_rows(me, rows_g, g_out, se.at[0], re.at[0])
    first[2].wait_recv()
    first[3].wait_recv()
    rows_x[...] = gather(both, [tok[1, 0], tok[1, 1]])
    came_x = send_rows(me, rows_x, x_out, se.at[1], re.at[1])
    rows_w[...] = gather(hot1 + hot2, [wext[0, 0], wext[1, 0], wext[0, 1], wext[1, 1]])
    came_w = send_rows(me, rows_w, w_out, se.at[2], re.at[2])
    state = []
    for i, (ref, came) in enumerate(((g_out, came_g), (x_out, came_x), (w_out, came_w))):
        state.append(pass_on(me, ref, came, sy.at[i], ry.at[i], sc.at[i], rc.at[i]))
    for i, ref in enumerate((g_out, x_out, w_out)):
        pass_across(me, ref, state[i][0], state[i][1], sc.at[i], rc.at[i])
    for along_y, across in state:
        for copy in across:
            copy.wait()
        for copy in along_y:
            copy.wait_send()
    for copy in first + came_g + came_x + came_w:
        copy.wait_send()


def spread(sizes, micro, cap, info, cot, moe, weights):
    n_expert, n_dp = sizes
    ny, per_core = n_dp // 2, micro * cap
    seq, width = cot.shape
    block = (2, ny * n_expert, 2 * per_core)
    mine = (n_expert, 2 * per_core)
    bf = jnp.bfloat16
    return pl.pallas_call(
        functools.partial(spread_kernel, sizes, (micro, cap, per_core)),
        out_shape=(
            jax.ShapeDtypeStruct(block + (width,), bf),
            jax.ShapeDtypeStruct(block + (width,), bf),
            jax.ShapeDtypeStruct(block + (128,), bf),
        ),
        in_specs=[VMEM] * 4,
        out_specs=(VMEM,) * 3,
        scratch_shapes=[
            pltpu.VMEM((2,) + info.shape, jnp.int32),
            pltpu.VMEM((2, 2, seq, width), bf),
            pltpu.VMEM((2, 2, seq, 128), bf),
            pltpu.VMEM(mine + (width,), bf),
            pltpu.VMEM(mine + (width,), bf),
            pltpu.VMEM(mine + (128,), bf),
            DMA((4,)),
            DMA((4,)),
            DMA((3, n_expert)),
            DMA((3, n_expert)),
            DMA((3, ny, n_expert)),
            DMA((3, ny, n_expert)),
            DMA((3, ny)),
            DMA((3, ny)),
        ],
        name="spread",
        compiler_params=pltpu.CompilerParams(
            collective_id=1, has_side_effects=True, vmem_limit_bytes=48 << 20
        ),
    )(info, cot, moe, weights)


class Back:
    def __init__(self, me, away, own, q_out, r1, stage, r2, final, sems):
        self.me, self.away, self.own = me, away, own
        self.q_out, self.r1, self.stage, self.r2, self.final = q_out, r1, stage, r2, final
        self.sems = sems
        self.ys = [(me.y + k) % me.ny for k in range(me.ny)]
        self.order = list(range(1, me.n_expert)) + [0]
        self.first, self.second, self.third, self.fourth = {}, {}, {}, {}

    def to_mate(self, i):
        s, r = self.sems[0].at[i], self.sems[1].at[i]
        self.first[i] = remote(self.away(i), self.r1.at[i], s, r, self.me.at(c=1 - self.me.c))

    def partial(self, i, y, e):
        block = y * self.me.n_expert + e
        return self.own(i, block) + self.r1[i, block].astype(jnp.float32)

    def along_y(self, i):
        me = self.me
        self.first[i].wait_recv()
        for k in range(1, me.ny):
            for j in self.order:
                e = (me.e + j) % me.n_expert
                self.stage[i, k - 1, e] = self.partial(i, self.ys[k], e).astype(jnp.bfloat16)
                self.second[i, k, j] = remote(
                    self.stage.at[i, k - 1, e], self.r2.at[i, k - 1, e],
                    self.sems[2].at[i, k - 1, j], self.sems[3].at[i, k - 1, j], me.at(y=self.ys[k]),
                )

    def finish(self, i, order):
        me = self.me
        for j in order:
            e = (me.e + j) % me.n_expert
            total = self.partial(i, me.y, e)
            for k in range(1, me.ny):
                self.second[i, k, j].wait_recv()
                total = total + self.r2[i, k - 1, e].astype(jnp.float32)
            if j:
                self.final[i, e] = total.astype(jnp.bfloat16)
                self.third[i, j] = remote(
                    self.final.at[i, e], self.q_out.at[i, me.c, me.e],
                    self.sems[4].at[i, j], self.sems[5].at[i, j], me.at(e=e),
                )
            else:
                self.q_out[i, me.c, me.e] = total.astype(jnp.bfloat16)

    def across(self, i):
        for j in self.order[:-1]:
            self.third[i, j].wait_recv()
        block = self.q_out.at[i, self.me.c]
        s, r = self.sems[6].at[i], self.sems[7].at[i]
        self.fourth[i] = remote(block, block, s, r, self.me.at(c=1 - self.me.c))

    def close(self):
        for copy in self.fourth.values():
            copy.wait()
        for copies in (self.first, self.second, self.third):
            for copy in copies.values():
                copy.wait_send()


def back_scratch(sizes, size, width):
    n_expert, ny = sizes[0], sizes[1] // 2
    most = max(ny - 1, 1)
    bf = jnp.bfloat16
    return [
        pltpu.VMEM((2, ny * n_expert, size, width), bf),
        pltpu.VMEM((2, most, n_expert, size, width), bf),
        pltpu.VMEM((2, most, n_expert, size, width), bf),
        pltpu.VMEM((2, n_expert, size, width), bf),
        DMA((2,)),
        DMA((2,)),
        DMA((2, most, n_expert)),
        DMA((2, most, n_expert)),
        DMA((2, n_expert)),
        DMA((2, n_expert)),
        DMA((2,)),
        DMA((2,)),
    ]


def gather_back_kernel(sizes, p0_ref, p1_ref, q_out, *scratch):
    me = Place(*sizes)
    greet(column_peers(me))
    p_refs = (p0_ref, p1_ref)
    back = Back(
        me, lambda i: p_refs[i].at[1 - me.c],
        lambda i, block: p_refs[i][me.c, block].astype(jnp.float32), q_out, *scratch[:4], scratch[4:],
    )
    for i in range(2):
        back.to_mate(i)
    for i in range(2):
        back.along_y(i)
    for i in range(2):
        back.finish(i, back.order)
        back.across(i)
    back.close()


def gather_back(sizes, first, second):
    n_expert = sizes[0]
    _, _, size, width = first.shape
    return pl.pallas_call(
        functools.partial(gather_back_kernel, sizes),
        out_shape=jax.ShapeDtypeStruct((2, 2, n_expert, size, width), jnp.bfloat16),
        in_specs=[VMEM] * 2,
        out_specs=VMEM,
        scratch_shapes=back_scratch(sizes, size, width),
        name="gather_back",
        compiler_params=pltpu.CompilerParams(
            collective_id=2, has_side_effects=True, vmem_limit_bytes=48 << 20
        ),
    )(first, second)


def gated_terms(gate_pre, up_pre):
    root = math.sqrt(2.0 / math.pi)
    square = gate_pre * gate_pre
    bend = jnp.tanh(root * (gate_pre + 0.044715 * square * gate_pre))
    half = 0.5 * (1.0 + bend)
    active = gate_pre * half
    slope = half + 0.5 * gate_pre * (1.0 - bend * bend) * root * (1.0 + 3 * 0.044715 * square)
    return active * up_pre, active, up_pre * slope


def expert_kernel(
    sizes, x_ref, g_ref, w_ref, wg_hbm, wu_hbm, wd_hbm,
    q_out, hid_out, dg_out, du_out, gr_out,
    wg, wu, wd, act, slope, away, own, sem_w, *scratch,
):
    me = Place(*sizes)
    c = me.c
    fetch = {}
    for n, j in enumerate((1 - c, c)):
        for i, (src, dst) in enumerate(((wg_hbm, wg), (wu_hbm, wu), (wd_hbm, wd))):
            fetch[n, i] = pltpu.make_async_copy(src.at[j], dst.at[j], sem_w.at[n, i])
            fetch[n, i].start()
    greet(column_peers(me))
    bf, f32 = jnp.bfloat16, jnp.float32
    size = x_ref.shape[2]
    column = me.n_expert
    half = column // 2
    step = math.gcd(column, 4)
    chunk = step * size
    back = Back(
        me, lambda i: away.at[i],
        lambda i, block: own[i, pl.ds(pl.multiple_of(block * size, 8), size), :],
        q_out, *scratch[:4], scratch[4:],
    )

    def dot(left, right, contract):
        return lax.dot_general(left, right, (contract, ((), ())), preferred_element_type=f32)

    def flat(value):
        return value.reshape(chunk, value.shape[-1])

    def blocks(value):
        return value.reshape(step, size, value.shape[-1])

    def store(i, first, some, rows, value):
        if first:
            away[i, some] = blocks(value.astype(bf))
        else:
            own[i, rows, :] = value

    def each(start, count, body):
        @pl.loop(0, count // step)
        def _(n):
            at = start + n * step
            body(pl.ds(at, step), pl.ds(pl.multiple_of(at * size, 8), chunk))

    def forward(first, j, start, count):
        def body(some, rows):
            x = flat(x_ref[j, some])
            gate_pre = dot(x, wg[j], ((1,), (0,)))
            up_pre = dot(x, wu[j], ((1,), (0,)))
            hidden, active, lean = gated_terms(gate_pre, up_pre)
            act[j, rows, :] = active
            slope[j, rows, :] = lean
            hidden = hidden.astype(bf)
            hid_out[j, some] = blocks(hidden)
            store(0, first, some, rows, dot(hidden, wd[j], ((1,), (0,))))

        each(start, count, body)

    def backward(first, j, start, count):
        def body(some, rows):
            pieces = flat(w_ref[j, some].astype(f32))
            weight = pieces[:, 0:1] + pieces[:, 1:2] + pieces[:, 2:3]
            grad = (weight * flat(g_ref[j, some].astype(f32))).astype(bf)
            gr_out[j, some] = blocks(grad)
            grad_hidden = dot(grad, wd[j], ((1,), (1,)))
            dg = (grad_hidden * slope[j, rows, :]).astype(bf)
            du = (grad_hidden * act[j, rows, :]).astype(bf)
            dg_out[j, some] = blocks(dg)
            du_out[j, some] = blocks(du)
            store(1, first, some, rows, dot(dg, wg[j], ((1,), (1,))) + dot(du, wu[j], ((1,), (1,))))

        each(start, count, body)

    for i in range(3):
        fetch[0, i].wait()
    forward(True, 1 - c, 0, me.ny * column)
    back.to_mate(0)
    for i in range(3):
        fetch[1, i].wait()
    for k in range(1, me.ny):
        forward(False, c, back.ys[k] * column, column)
    back.along_y(0)
    forward(False, c, me.y * column, column)
    backward(True, 1 - c, 0, me.ny * column)
    back.to_mate(1)
    back.finish(0, back.order[:half])
    for k in range(1, me.ny):
        backward(False, c, back.ys[k] * column, column)
    back.along_y(1)
    backward(False, c, me.y * column, column)
    back.finish(0, back.order[half:])
    back.across(0)
    back.finish(1, back.order)
    back.across(1)
    back.close()


def experts(sizes, x, g, w, w_gate, w_up, w_down):
    n_expert = sizes[0]
    _, count, size, width = x.shape
    units = w_gate.shape[2]
    bf, f32 = jnp.bfloat16, jnp.float32
    any_space = pl.BlockSpec(memory_space=pl.ANY)
    inner = jax.ShapeDtypeStruct((2, count, size, units), bf)
    return pl.pallas_call(
        functools.partial(expert_kernel, sizes),
        out_shape=(
            jax.ShapeDtypeStruct((2, 2, n_expert, size, width), bf),
            inner, inner, inner,
            jax.ShapeDtypeStruct(x.shape, bf),
        ),
        in_specs=[VMEM] * 3 + [any_space] * 3,
        out_specs=(VMEM,) * 5,
        scratch_shapes=[
            pltpu.VMEM(w_gate.shape, bf),
            pltpu.VMEM(w_up.shape, bf),
            pltpu.VMEM(w_down.shape, bf),
            pltpu.VMEM((2, count * size, units), f32),
            pltpu.VMEM((2, count * size, units), f32),
            pltpu.VMEM((2, count, size, width), bf),
            pltpu.VMEM((2, count * size, width), f32),
            DMA((2, 3)),
        ]
        + back_scratch(sizes, size, width),
        name="experts",
        compiler_params=pltpu.CompilerParams(
            collective_id=4, has_side_effects=True, vmem_limit_bytes=60 << 20
        ),
    )(x, g, w, w_gate, w_up, w_down)


def reduce_kernel(
    sizes, pieces, left_ref, right_ref, small_ref, out, small_out,
    buf_a, buf_b, acc, *boxes,
):
    me = Place(*sizes)
    c, mate = me.c, me.at(c=1 - me.c)
    n = me.nx
    seq = right_ref.shape[1]
    total_rows = out.shape[1]
    is0 = c == 0
    pair = jnp.where(is0, me.x, me.y)
    other = jnp.where(is0, me.y, me.x)
    lo, hi, nh = pair % 2, pair // 2, n // 2

    def along(pair_at, other_at, z=None):
        return me.at(x=jnp.where(is0, pair_at, other_at), y=jnp.where(is0, other_at, pair_at), z=z)

    flip_x, flip_y = me.x + 1 - 2 * (me.x % 2), me.y + 1 - 2 * (me.y % 2)
    dims = [
        (n, other, lambda q: along(pair, q)),
        (nh, hi, lambda q: along(q * 2 + lo, other)),
        (2, me.z % 2, lambda q: me.at(z=me.z // 2 * 2 + q)),
        (me.nz // 2, me.z // 2, lambda q: me.at(z=q * 2 + me.z % 2)),
    ]
    parts, gots = boxes[:4], boxes[4:8]
    half, small_half, small_got, fs, fr, os, ps, pr, gs, gr, ms, mr, cs, cr, ss, sr = boxes[8:]
    levels = [i for i, d in enumerate(dims) if d[0] > 1]
    x_peers = [me.at(x=(me.x + k) % n) for k in range(1, n)]
    y_peers = [me.at(y=(me.y + k) % n) for k in range(1, n)]
    z_peers = [me.at(z=(me.z + k) % me.nz) for k in range(1, me.nz)]
    greet(
        [mate, me.at(x=flip_x, c=1 - c), me.at(y=flip_y, c=1 - c)] + x_peers + y_peers + z_peers
    )

    def slot_a(slot):
        return buf_a.at[pl.ds(pl.multiple_of(slot * seq, seq), seq), :]

    def slot_b(slot):
        return buf_b.at[pl.ds(pl.multiple_of(slot * seq, seq), seq), :]

    targets = [
        (mate, 1 - c, other % 2, c),
        (me.at(x=flip_x, c=0), 0, flip_x % 2, 2 + c),
        (me.at(y=flip_y, c=1), 1, flip_y % 2, 2 + c),
    ]
    factor = []
    for i, (device, role, parity, slot) in enumerate(targets):
        a, b = jnp.where(role == 0, 0, parity), role * 2 + parity
        factor.append(remote(left_ref.at[a], slot_a(slot), fs.at[i, 0], fr.at[slot, 0], device))
        factor.append(remote(right_ref.at[b], slot_b(slot), fs.at[i, 1], fr.at[slot, 1], device))
    own = [
        pltpu.make_async_copy(left_ref.at[jnp.where(is0, 0, lo)], slot_a(c), os.at[0]),
        pltpu.make_async_copy(right_ref.at[c * 2 + lo], slot_b(c), os.at[1]),
    ]
    for copy in own:
        copy.start()
    rows_s = half.shape[0]
    small = [remote(small_ref.at[pl.ds((1 - c) * rows_s, rows_s)], half, ss.at[0], sr.at[0], mate)]
    small_dims = [
        (n, me.x, lambda q: me.at(x=q)),
        (n, me.y, lambda q: me.at(y=q)),
        (me.nz, me.z, lambda q: me.at(z=q)),
    ]
    small_wait = [small[0]]
    small_slot = [1]

    def small_step(step):
        for copy in small_wait:
            copy.wait_recv()
        small_wait.clear()
        if step == 0:
            total = small_ref[pl.ds(c * rows_s, rows_s)] + half[...]
        elif step <= 3:
            total = small_got[step - 1, 0]
            for k in range(1, small_dims[step - 1][0]):
                total = total + small_got[step - 1, k]
        if step < 3:
            count, index, peer = small_dims[step]
            small_half[step] = total
            small_got[step, index] = total
            for k in range(1, count):
                small_wait.append(
                    remote(
                        small_half.at[step], small_got.at[step, index], ss.at[small_slot[0]],
                        sr.at[small_slot[0]], peer((index + k) % count),
                    )
                )
                small_slot[0] += 1
        elif step == 3:
            small_out[pl.ds(c * rows_s, rows_s)] = total
            block = small_out.at[pl.ds(c * rows_s, rows_s)]
            small_wait.append(
                remote(block, block, ss.at[small_slot[0]], sr.at[small_slot[0]], mate)
            )
        small.extend(small_wait)

    for where in (1 - c, 2, 3):
        for i, (src, dst) in enumerate(((left_ref, slot_a(where)), (right_ref, slot_b(where)))):
            pltpu.make_async_remote_copy(
                src_ref=src.at[0], dst_ref=dst, send_sem=fs.at[0, i], recv_sem=fr.at[where, i],
                device_id=mate, device_id_type=MESH,
            ).wait_recv()
    for copy in own:
        copy.wait()

    rows_k = total_rows // pieces
    matrix = c * 2 + lo
    pending = {}

    def multiply(k):
        acc[k] = lax.dot_general(
            buf_a[:, k * rows_k : (k + 1) * rows_k], buf_b[...], (((0,), (0,)), ((), ())),
            preferred_element_type=jnp.float32,
        )
        push(k, 0, rows_k)

    def push(k, at, rows):
        level = levels[at]
        count, index, peer = dims[level]
        size = rows // count
        copies = []
        for s in range(1, count):
            to = (index + s) % count
            parts[level][k, s - 1] = acc[k, pl.ds(pl.multiple_of(to * size, 8), size), :].astype(jnp.bfloat16)
            copies.append(
                remote(
                    parts[level].at[k, s - 1], gots[level].at[k, s - 1],
                    ps.at[level, k, s - 1], pr.at[level, k, s - 1], peer(to),
                )
            )
        pending["push", at, k] = copies

    def rows_at(at):
        rows = rows_k
        for i in range(at):
            rows //= dims[levels[i]][0]
        return rows

    def add(k, at):
        level = levels[at]
        count, index, _ = dims[level]
        size = rows_at(at) // count
        for copy in pending["push", at, k]:
            copy.wait_recv()
        total = acc[k, pl.ds(pl.multiple_of(index * size, 8), size), :]
        for s in range(1, count):
            total = total + gots[level][k, s - 1].astype(jnp.float32)
        if at + 1 < len(levels):
            acc[k, :size, :] = total
            push(k, at + 1, size)
        else:
            out[matrix, pl.ds(offset(k, at), size), :] = total.astype(jnp.bfloat16)
            share(k, at)

    def offset(k, at):
        start, rows = k * rows_k, rows_k
        for i in range(at + 1):
            count, index, _ = dims[levels[i]]
            rows //= count
            start = start + index * rows
        return pl.multiple_of(start, 8)

    def share(k, at):
        level = levels[at]
        count, index, peer = dims[level]
        size = rows_at(at) // count
        block = out.at[matrix, pl.ds(offset(k, at), size), :]
        pending["share", at, k] = [
            remote(block, block, gs.at[level, k, s - 1], gr.at[level, k, s - 1], peer((index + s) % count))
            for s in range(1, count)
        ]

    def shared(k, at):
        for copy in pending["share", at, k]:
            copy.wait_recv()
        if at:
            share(k, at - 1)
        else:
            block = out.at[matrix, pl.ds(k * rows_k, rows_k), :]
            pending["mate", k] = remote(
                block, block, ms.at[k], mr.at[k], along(pair + 1 - 2 * lo, other)
            )

    def across(k):
        pending["mate", k].wait_recv()
        block = out.at[pl.ds(2 * c, 2), pl.ds(k * rows_k, rows_k), :]
        pending["core", k] = remote(block, block, cs.at[k], cr.at[k], mate)

    steps = [multiply]
    steps += [functools.partial(add, at=i) for i in range(len(levels))]
    steps += [functools.partial(shared, at=i) for i in reversed(range(len(levels)))]
    events = sorted((0 if p == 0 else p + k, -p, k) for p in range(len(steps)) for k in range(pieces))
    before = 0
    for t, p, k in events:
        if before < t <= 5:
            small_step(t - 1)
        before = t
        steps[-p](k)
    for k in range(pieces):
        across(k)
    for k in range(pieces):
        pending["core", k].wait_recv()
    for copy in factor + small:
        copy.wait_send()
    for copies in pending.values():
        for copy in copies if isinstance(copies, list) else [copies]:
            copy.wait_send()


def reduce_all(sizes, left, right, small, pieces=8):
    n_expert, n_dp = sizes
    nz = math.gcd(n_expert, 4)
    n = n_expert // nz
    nh = n // 2
    assert n == n_dp // 2
    seq, width = left.shape[1:]
    rows_k = width // pieces
    bf, f32 = jnp.bfloat16, jnp.float32
    rows_s = small.shape[0] // 2
    splits = [n, nh, 2, nz // 2]
    sizes_at = [rows_k // math.prod(splits[: i + 1]) for i in range(4)]
    counts = [max(q - 1, 1) for q in splits]
    most = max(counts)
    boxes = [pltpu.VMEM((pieces, q, s, width), bf) for q, s in zip(counts, sizes_at)]
    smalls = 2 * n + nz
    return pl.pallas_call(
        functools.partial(reduce_kernel, sizes, pieces),
        out_shape=(
            jax.ShapeDtypeStruct((4, width, width), bf),
            jax.ShapeDtypeStruct(small.shape, f32),
        ),
        in_specs=[VMEM] * 3,
        out_specs=(VMEM, VMEM),
        scratch_shapes=[
            pltpu.VMEM((4 * seq, width), bf),
            pltpu.VMEM((4 * seq, width), bf),
            pltpu.VMEM((pieces, rows_k, width), f32),
            *boxes,
            *boxes,
            pltpu.VMEM((rows_s, width), f32),
            pltpu.VMEM((3, rows_s, width), f32),
            pltpu.VMEM((3, max(n, nz), rows_s, width), f32),
            DMA((3, 2)),
            DMA((4, 2)),
            DMA((2,)),
            DMA((4, pieces, most)),
            DMA((4, pieces, most)),
            DMA((4, pieces, most)),
            DMA((4, pieces, most)),
            DMA((pieces,)),
            DMA((pieces,)),
            DMA((pieces,)),
            DMA((pieces,)),
            DMA((smalls,)),
            DMA((smalls,)),
        ],
        name="reduce_all",
        compiler_params=pltpu.CompilerParams(
            collective_id=3, has_side_effects=True, vmem_limit_bytes=24 << 20
        ),
    )(left, right, small)


def rms_scale(values):
    return lax.rsqrt(jnp.mean(values * values, axis=-1, keepdims=True) + epsilon)


def bucket_hot(seq_len, buckets):
    position = jnp.arange(seq_len, dtype=jnp.int32)
    relative = position[None, :] - position[:, None]
    distance = jnp.abs(relative)
    far_bucket = jnp.full_like(distance, 8)
    for threshold in bucket_edges:
        far_bucket = far_bucket + (distance >= threshold).astype(jnp.int32)
    bucketed = jnp.where(distance < 8, distance, far_bucket) + 16 * (relative > 0).astype(jnp.int32)
    bucket_ids = jnp.arange(buckets, dtype=jnp.int32)
    return (bucketed[None, :, :] == bucket_ids[:, None, None]).astype(jnp.float32)


def dot32(pattern, left, right):
    return jnp.einsum(pattern, left, right, preferred_element_type=jnp.float32)


def shards(
    layer_in, routes, queue_slots, norm_attn, w_query, w_key, w_value, w_out, rel_table,
    norm_moe, router, w_gate, w_up, w_down, cotangent,
):
    bf, f32 = jnp.bfloat16, jnp.float32
    seq_len, width = layer_in.shape
    buckets, heads = rel_table.shape
    expert_count = router.shape[1]
    sizes = (lax.axis_size("expert"), lax.axis_size("dp"))
    n_expert, n_dp = sizes
    assert w_gate.shape[0] == 2 and expert_count == 2 * n_expert
    group_len = seq_len // MICRO
    capacity = (5 * group_len + 2 * expert_count - 1) // (2 * expert_count)
    split_heads = (seq_len, heads, width // heads)
    layer_rows = layer_in.astype(f32)
    inv_attn = rms_scale(layer_rows)
    normed_attn = layer_rows * inv_attn
    attn_in = (normed_attn * norm_attn).astype(bf)
    query_heads = dot32("sd,de->se", attn_in, w_query).astype(bf).reshape(split_heads)
    key_heads = dot32("sd,de->se", attn_in, w_key).astype(bf).reshape(split_heads)
    value_heads = dot32("sd,de->se", attn_in, w_value).astype(bf).reshape(split_heads)
    one_hot = bucket_hot(seq_len, buckets)
    bias = jnp.einsum("bij,bh->hij", one_hot, rel_table, precision=highest)
    scores = dot32("ihd,jhd->hij", query_heads, key_heads) + bias
    exponent = jnp.exp(scores - jnp.max(scores, axis=-1, keepdims=True))
    probs = exponent / jnp.sum(exponent, axis=-1, keepdims=True)
    probs_low = probs.astype(bf)
    context = dot32("hij,jhd->ihd", probs_low, value_heads).astype(bf).reshape(seq_len, width)
    residual = layer_rows + dot32("se,ed->sd", context, w_out)
    inv_moe = rms_scale(residual)
    normed_moe = residual * inv_moe
    moe_in = normed_moe * norm_moe
    logits = jnp.dot(moe_in, router, precision=highest)
    gate_prob = jax.nn.softmax(logits, axis=-1)
    expert_ids = jnp.arange(expert_count, dtype=jnp.int32)
    first_hot = (routes[:, 0:1] == expert_ids).astype(f32)
    second_hot = (routes[:, 1:2] == expert_ids).astype(f32)
    prob_first = jnp.sum(gate_prob * first_hot, axis=-1, keepdims=True)
    prob_second = jnp.sum(gate_prob * second_hot, axis=-1, keepdims=True)
    weight_first = prob_first / (prob_first + prob_second)
    weight_second = prob_second / (prob_first + prob_second)
    weights = jnp.concatenate([weight_first, weight_second], axis=1)

    info = jnp.concatenate([routes.T, queue_slots.T, jnp.zeros((4, seq_len), jnp.int32)])
    grad_in, rows_in, weight_in = spread(
        sizes, MICRO, capacity, info, cotangent, moe_in.astype(bf), weights
    )
    if 23 * rows_in.size + 6 * w_gate.size < 52 << 20:
        back, hidden, gate_grad, up_grad, grad_rows = experts(
            sizes, rows_in, grad_in, weight_in, w_gate, w_up, w_down
        )
    else:
        blocks = rows_in.shape[:-1] + (-1,)
        rows_in, grad_in, weight_in = [
            a.reshape(2, -1, a.shape[-1]) for a in (rows_in, grad_in, weight_in)
        ]
        slot_weight = jnp.sum(weight_in[..., :3].astype(f32), axis=-1, keepdims=True)
        grad_rows = (slot_weight * grad_in.astype(f32)).astype(bf)
        gate_pre = dot32("jrd,jdf->jrf", rows_in, w_gate)
        up_pre = dot32("jrd,jdf->jrf", rows_in, w_up)
        hidden, active, lean = gated_terms(gate_pre, up_pre)
        hidden = hidden.astype(bf)
        partial_out = dot32("jrf,jfd->jrd", hidden, w_down).astype(bf)
        hidden_grad = dot32("jrd,jfd->jrf", grad_rows, w_down)
        gate_grad, up_grad = (hidden_grad * lean).astype(bf), (hidden_grad * active).astype(bf)
        rows_grad = dot32("jrf,jdf->jrd", gate_grad, w_gate) + dot32("jrf,jdf->jrd", up_grad, w_up)
        back = gather_back(sizes, partial_out.reshape(blocks), rows_grad.astype(bf).reshape(blocks))
    rows_in, hidden, gate_grad, up_grad, grad_rows = [
        a.reshape(2, -1, a.shape[-1]) for a in (rows_in, hidden, gate_grad, up_grad, grad_rows)
    ]
    grad_w_gate = dot32("jrd,jrf->jdf", rows_in, gate_grad)
    grad_w_up = dot32("jrd,jrf->jdf", rows_in, up_grad)
    grad_w_down = dot32("jrf,jrd->jfd", hidden, grad_rows)
    back = back.reshape(2, -1, width)

    core = lax.axis_index("dp") % 2
    per_core = MICRO * capacity
    token = jnp.arange(seq_len, dtype=jnp.int32)[:, None]
    place = (routes % 2) * (n_expert * 2 * per_core) + (routes // 2) * (2 * per_core)
    place = place + core * per_core + (token // group_len) * capacity + queue_slots
    place = jnp.where(queue_slots >= 0, place, -1)
    slot_ids = jnp.arange(2 * n_expert * 2 * per_core, dtype=jnp.int32)
    select_first = (place[:, 0:1] == slot_ids).astype(bf)
    select_second = (place[:, 1:2] == slot_ids).astype(bf)
    picked_first = dot32("tp,pd->td", select_first, back[0])
    picked_second = dot32("tp,pd->td", select_second, back[0])
    moe = weight_first * picked_first + weight_second * picked_second
    layer_out = (residual + moe).astype(bf)
    cot_rows = cotangent.astype(f32)
    grad_weight_first = jnp.sum(cot_rows * picked_first, axis=-1, keepdims=True)
    grad_weight_second = jnp.sum(cot_rows * picked_second, axis=-1, keepdims=True)
    grad_from_slots = dot32("tp,pd->td", select_first + select_second, back[1])
    mean_grad = weight_first * grad_weight_first + weight_second * grad_weight_second
    logit_first = weight_first * (grad_weight_first - mean_grad)
    logit_second = weight_second * (grad_weight_second - mean_grad)
    grad_logits = logit_first * first_hot + logit_second * second_hot
    grad_router = jnp.einsum("sd,se->ed", moe_in, grad_logits, precision=highest)
    grad_moe_in = grad_from_slots + jnp.einsum("se,de->sd", grad_logits, router, precision=highest)
    grad_norm_moe = jnp.sum(grad_moe_in * normed_moe, axis=0)
    grad_normed = grad_moe_in * norm_moe
    grad_residual = cot_rows + inv_moe * (
        grad_normed - normed_moe * jnp.mean(grad_normed * normed_moe, axis=-1, keepdims=True)
    )
    grad_attn_low = grad_residual.astype(bf)
    grad_context = dot32("sd,ed->se", grad_attn_low, w_out).astype(bf).reshape(split_heads)
    grad_values = dot32("hij,ihd->jhd", probs_low, grad_context).astype(bf).reshape(seq_len, width)
    grad_probs = dot32("ihd,jhd->hij", grad_context, value_heads)
    grad_scores = probs * (grad_probs - jnp.sum(probs * grad_probs, axis=-1, keepdims=True))
    grad_rel_table = jnp.einsum("bij,hij->bh", one_hot, grad_scores, precision=highest)
    scores_low = grad_scores.astype(bf)
    grad_queries = dot32("hij,jhd->ihd", scores_low, key_heads).astype(bf).reshape(seq_len, width)
    grad_keys = dot32("hij,ihd->jhd", scores_low, query_heads).astype(bf).reshape(seq_len, width)
    grad_attn_in = dot32("se,de->sd", grad_queries, w_query)
    grad_attn_in = grad_attn_in + dot32("se,de->sd", grad_keys, w_key)
    grad_attn_in = grad_attn_in + dot32("se,de->sd", grad_values, w_value)
    grad_norm_attn = jnp.sum(grad_attn_in * normed_attn, axis=0)
    grad_normed_attn = grad_attn_in * norm_attn
    grad_input = grad_residual + inv_attn * (
        grad_normed_attn
        - normed_attn * jnp.mean(grad_normed_attn * normed_attn, axis=-1, keepdims=True)
    )
    table = grad_rel_table.reshape(-1)
    small = jnp.concatenate(
        [
            grad_router,
            grad_norm_attn[None],
            grad_norm_moe[None],
            jnp.pad(table, (0, width - table.size))[None],
        ]
    )
    small = jnp.pad(small, ((0, -small.shape[0] % 16), (0, 0)))
    sums, small = reduce_all(
        sizes,
        jnp.stack([attn_in, context]),
        jnp.stack([grad_queries, grad_keys, grad_values, grad_attn_low]),
        small,
    )
    matrices = [sums[i].astype(f32) for i in range(4)]
    return (
        layer_out, grad_input, small[expert_count], *matrices,
        small[expert_count + 2, : table.size].reshape(buckets, heads),
        small[expert_count + 1], small[:expert_count].T, grad_w_gate, grad_w_up, grad_w_down,
    )


def solution(mesh):
    in_specs = (
        P(("expert", "dp"), None),
        P(("expert", "dp"), None),
        P(("expert", "dp"), None),
        P(),
        P(),
        P(),
        P(),
        P(),
        P(),
        P(),
        P(),
        P("expert", None, "dp"),
        P("expert", None, "dp"),
        P("expert", "dp", None),
        P(("expert", "dp"), None),
    )
    out_specs = (
        P(("expert", "dp"), None),
        P(("expert", "dp"), None),
        P(),
        P(),
        P(),
        P(),
        P(),
        P(),
        P(),
        P(),
        P("expert", None, "dp"),
        P("expert", None, "dp"),
        P("expert", "dp", None),
    )
    return jax.shard_map(shards, mesh=mesh, in_specs=in_specs, out_specs=out_specs, check_vma=False)
```

```python
import functools
import math

import jax
import jax.numpy as jnp
from jax import lax
from jax.experimental import pallas as pl
from jax.experimental.pallas import tpu as pltpu
from jax.sharding import PartitionSpec as P

MICRO = 4

epsilon = 1e-06
bucket_edges = (12, 16, 23, 32, 46, 64, 91)
highest = lax.Precision.HIGHEST

MESH = pl.DeviceIdType.MESH
VMEM = pl.BlockSpec(memory_space=pltpu.VMEM)
DMA = pltpu.SemaphoreType.DMA


class Place:
    def __init__(self, n_expert, n_dp):
        self.n_expert, self.n_dp = n_expert, n_dp
        self.nz = math.gcd(n_expert, 4)
        self.nx = n_expert // self.nz
        self.ny = n_dp // 2
        self.e = lax.axis_index("expert")
        self.d = lax.axis_index("dp")
        self.z, self.x = self.e // self.nx, self.e % self.nx
        self.y, self.c = self.d // 2, self.d % 2

    def at(self, z=None, x=None, y=None, c=None, e=None):
        z = self.z if z is None else z
        x = self.x if x is None else x
        y = self.y if y is None else y
        c = self.c if c is None else c
        e = z * self.nx + x if e is None else e
        return (e, y * 2 + c)


def remote(src, dst, send, recv, device):
    copy = pltpu.make_async_remote_copy(
        src_ref=src, dst_ref=dst, send_sem=send, recv_sem=recv, device_id=device, device_id_type=MESH
    )
    copy.start()
    return copy


def greet(devices):
    barrier = pltpu.get_barrier_semaphore()
    for device in devices:
        pl.semaphore_signal(barrier, inc=1, device_id=device, device_id_type=MESH)
    pl.semaphore_wait(barrier, len(devices))


def column_peers(me):
    out = [me.at(c=1 - me.c)]
    out += [me.at(y=(me.y + k) % me.ny) for k in range(1, me.ny)]
    out += [me.at(e=(me.e + k) % me.n_expert) for k in range(1, me.n_expert)]
    return out


class Spread:
    def __init__(self, me, rows, recv, sems):
        self.me, self.rows, self.recv = me, rows, recv
        self.se, self.re, self.sy, self.ry, self.sc, self.rc = sems
        self.came, self.along, self.crossed = {}, {}, {}

    def send(self):
        me = self.me
        for k in range(1, me.n_expert):
            to = (me.e + k) % me.n_expert
            self.came[k] = remote(
                self.rows.at[to], self.recv.at[me.c, me.y * me.n_expert + me.e],
                self.se.at[k], self.re.at[k], me.at(e=to),
            )
        self.recv[me.c, me.y * me.n_expert + me.e] = self.rows[me.e]

    def pass_on(self, blocks):
        me = self.me
        for k in blocks:
            if k:
                self.came[k].wait_recv()
            src = (me.e - k + me.n_expert) % me.n_expert
            block = self.recv.at[me.c, me.y * me.n_expert + src]
            for s in range(1, me.ny):
                self.along[s, k] = remote(
                    block, block, self.sy.at[s - 1, k], self.ry.at[s - 1, k], me.at(y=(me.y + s) % me.ny)
                )

    def cross(self, s):
        me = self.me
        if s:
            for k in range(me.n_expert):
                self.along[s, k].wait_recv()
        block = self.recv.at[me.c, pl.ds((me.y - s + me.ny) % me.ny * me.n_expert, me.n_expert)]
        self.crossed[s] = remote(block, block, self.sc.at[s], self.rc.at[s], me.at(c=1 - me.c))

    def arrive(self):
        for copy in self.crossed.values():
            copy.wait_recv()

    def close(self):
        for copies in (self.came, self.along, self.crossed):
            for copy in copies.values():
                copy.wait_send()


def spread_sems(sizes):
    n_expert, ny = sizes[0], sizes[1] // 2
    most = max(ny - 1, 1)
    return [
        DMA((3, n_expert)), DMA((3, n_expert)), DMA((3, most, n_expert)), DMA((3, most, n_expert)),
        DMA((3, ny)), DMA((3, ny)),
    ]


class Rows:
    def __init__(self, me, rows_per, info_ref, moe_ref, cot_ref, w_ref, info_all, tok, wext, send, recv):
        self.me, self.rows_per, self.info_all, self.tok, self.wext = me, rows_per, info_all, tok, wext
        seq = cot_ref.shape[0]
        self.seq = seq
        c, mate = me.c, me.at(c=1 - me.c)
        info_all[c] = info_ref[...]
        tok[0, c] = moe_ref[...]
        lanes = lax.broadcasted_iota(jnp.int32, (seq, 128), 1)
        for k in range(2):
            w = w_ref[:, k : k + 1]
            hi = w.astype(jnp.bfloat16).astype(jnp.float32)
            mid = (w - hi).astype(jnp.bfloat16).astype(jnp.float32)
            low = w - hi - mid
            wext[c, k] = jnp.where(
                lanes == 0, hi, jnp.where(lanes == 1, mid, jnp.where(lanes == 2, low, 0.0))
            ).astype(jnp.bfloat16)
        self.copies = [
            remote(ref, ref, send.at[i], recv.at[i], mate)
            for i, ref in enumerate((info_all.at[c], tok.at[0, c], wext.at[c]))
        ]
        tok[1, c] = cot_ref[...]
        self.copies.append(remote(tok.at[1, c], tok.at[1, c], send.at[3], recv.at[3], mate))

    def hots(self):
        me, seq = self.me, self.seq
        micro, cap, per_core = self.rows_per
        self.copies[0].wait_recv()
        row_ids = lax.broadcasted_iota(jnp.int32, (me.n_expert * 2 * per_core, seq), 0)
        group = lax.broadcasted_iota(jnp.int32, (1, seq), 1) // (seq // micro)
        hots = [[], []]
        for cc in range(2):
            for k in range(2):
                route = self.info_all[cc, k : k + 1, :]
                slot = self.info_all[cc, 2 + k : 3 + k, :]
                target = (route // 2) * (2 * per_core) + cc * per_core + group * cap + slot
                target = jnp.where((slot >= 0) & (route % 2 == me.c), target, -1)
                hots[k].append(jnp.where(row_ids == target, 1.0, 0.0))
        self.each = [[h.astype(jnp.bfloat16) for h in hots[k]] for k in range(2)]
        self.both = [(p + q).astype(jnp.bfloat16) for p, q in zip(*hots)]

    def gather(self, left, right):
        total = None
        for p, q in zip(left, right):
            term = jnp.dot(p, q, preferred_element_type=jnp.float32)
            total = term if total is None else total + term
        per_core = self.rows_per[2]
        return total.astype(jnp.bfloat16).reshape(self.me.n_expert, 2 * per_core, -1)

    def moe(self):
        self.copies[1].wait_recv()
        return self.gather(self.both, [self.tok[0, 0], self.tok[0, 1]])

    def weights(self):
        self.copies[2].wait_recv()
        wext = self.wext
        return self.gather(self.each[0] + self.each[1], [wext[0, 0], wext[1, 0], wext[0, 1], wext[1, 1]])

    def cot(self):
        self.copies[3].wait_recv()
        return self.gather(self.both, [self.tok[1, 0], self.tok[1, 1]])

    def close(self):
        for copy in self.copies:
            copy.wait_send()


def rows_scratch(sizes, per_core, seq, width):
    mine = (sizes[0], 2 * per_core)
    bf = jnp.bfloat16
    return [
        pltpu.VMEM((2, 8, seq), jnp.int32),
        pltpu.VMEM((2, 2, seq, width), bf),
        pltpu.VMEM((2, 2, seq, 128), bf),
        DMA((4,)),
        DMA((4,)),
        pltpu.VMEM(mine + (width,), bf),
        pltpu.VMEM(mine + (128,), bf),
        pltpu.VMEM(mine + (width,), bf),
    ]


def send_out(me, rows_per, refs, recvs, scratch, sems):
    rows = Rows(me, rows_per, *refs, *scratch[:5])
    rows.hots()
    out = []
    for i, (make, buf) in enumerate(zip((rows.moe, rows.weights, rows.cot), scratch[5:])):
        buf[...] = make()
        payload = Spread(me, buf, recvs[i], [s.at[i] for s in sems])
        payload.send()
        out.append(payload)
    return rows, out


def spread_kernel(sizes, rows_per, info_ref, moe_ref, cot_ref, w_ref, x_out, w_out, g_out, *scratch):
    me = Place(*sizes)
    greet(column_peers(me))
    rows, payloads = send_out(
        me, rows_per, (info_ref, moe_ref, cot_ref, w_ref), (x_out, w_out, g_out), scratch[:8], scratch[8:]
    )
    for payload in payloads:
        payload.pass_on(range(me.n_expert))
        payload.cross(0)
    for payload in payloads:
        for s in range(1, me.ny):
            payload.cross(s)
    for payload in payloads:
        payload.arrive()
        payload.close()
    rows.close()


def spread(sizes, micro, cap, info, moe, cot, weights):
    n_expert, ny, per_core = sizes[0], sizes[1] // 2, micro * cap
    seq, width = cot.shape
    block = (2, ny * n_expert, 2 * per_core)
    bf = jnp.bfloat16
    return pl.pallas_call(
        functools.partial(spread_kernel, sizes, (micro, cap, per_core)),
        out_shape=tuple(jax.ShapeDtypeStruct(block + (n,), bf) for n in (width, 128, width)),
        in_specs=[VMEM] * 4,
        out_specs=(VMEM,) * 3,
        scratch_shapes=rows_scratch(sizes, per_core, seq, width) + spread_sems(sizes),
        name="spread",
        compiler_params=pltpu.CompilerParams(
            collective_id=1, has_side_effects=True, vmem_limit_bytes=48 << 20
        ),
    )(info, moe, cot, weights)


class Back:
    def __init__(self, me, away, own, q_out, r1, stage, r2, final, sems):
        self.me, self.away, self.own = me, away, own
        self.q_out, self.r1, self.stage, self.r2, self.final = q_out, r1, stage, r2, final
        self.sems = sems
        self.ys = [(me.y + k) % me.ny for k in range(me.ny)]
        self.order = list(range(1, me.n_expert)) + [0]
        self.first, self.second, self.third, self.fourth = {}, {}, {}, {}

    def to_mate(self, i):
        s, r = self.sems[0].at[i], self.sems[1].at[i]
        self.first[i] = remote(self.away(i), self.r1.at[i], s, r, self.me.at(c=1 - self.me.c))

    def partial(self, i, y, e):
        block = y * self.me.n_expert + e
        return self.own(i, block) + self.r1[i, block].astype(jnp.float32)

    def along_y(self, i):
        me = self.me
        self.first[i].wait_recv()
        for k in range(1, me.ny):
            for j in self.order:
                e = (me.e + j) % me.n_expert
                self.stage[i, k - 1, e] = self.partial(i, self.ys[k], e).astype(jnp.bfloat16)
                self.second[i, k, j] = remote(
                    self.stage.at[i, k - 1, e], self.r2.at[i, k - 1, e],
                    self.sems[2].at[i, k - 1, j], self.sems[3].at[i, k - 1, j], me.at(y=self.ys[k]),
                )

    def finish(self, i, order):
        me = self.me
        for j in order:
            e = (me.e + j) % me.n_expert
            total = self.partial(i, me.y, e)
            for k in range(1, me.ny):
                self.second[i, k, j].wait_recv()
                total = total + self.r2[i, k - 1, e].astype(jnp.float32)
            if j:
                self.final[i, e] = total.astype(jnp.bfloat16)
                self.third[i, j] = remote(
                    self.final.at[i, e], self.q_out.at[i, me.c, me.e],
                    self.sems[4].at[i, j], self.sems[5].at[i, j], me.at(e=e),
                )
            else:
                self.q_out[i, me.c, me.e] = total.astype(jnp.bfloat16)

    def across(self, i):
        for j in self.order[:-1]:
            self.third[i, j].wait_recv()
        block = self.q_out.at[i, self.me.c]
        s, r = self.sems[6].at[i], self.sems[7].at[i]
        self.fourth[i] = remote(block, block, s, r, self.me.at(c=1 - self.me.c))

    def close(self):
        for copy in self.fourth.values():
            copy.wait()
        for copies in (self.first, self.second, self.third):
            for copy in copies.values():
                copy.wait_send()


def back_scratch(sizes, size, width):
    n_expert, ny = sizes[0], sizes[1] // 2
    most = max(ny - 1, 1)
    bf = jnp.bfloat16
    return [
        pltpu.VMEM((2, ny * n_expert, size, width), bf),
        pltpu.VMEM((2, most, n_expert, size, width), bf),
        pltpu.VMEM((2, most, n_expert, size, width), bf),
        pltpu.VMEM((2, n_expert, size, width), bf),
        DMA((2,)),
        DMA((2,)),
        DMA((2, most, n_expert)),
        DMA((2, most, n_expert)),
        DMA((2, n_expert)),
        DMA((2, n_expert)),
        DMA((2,)),
        DMA((2,)),
    ]


def gather_back_kernel(sizes, p0_ref, p1_ref, q_out, *scratch):
    me = Place(*sizes)
    greet(column_peers(me))
    p_refs = (p0_ref, p1_ref)
    back = Back(
        me, lambda i: p_refs[i].at[1 - me.c],
        lambda i, block: p_refs[i][me.c, block].astype(jnp.float32), q_out, *scratch[:4], scratch[4:],
    )
    for i in range(2):
        back.to_mate(i)
    for i in range(2):
        back.along_y(i)
    for i in range(2):
        back.finish(i, back.order)
        back.across(i)
    back.close()


def gather_back(sizes, first, second):
    n_expert = sizes[0]
    _, _, size, width = first.shape
    return pl.pallas_call(
        functools.partial(gather_back_kernel, sizes),
        out_shape=jax.ShapeDtypeStruct((2, 2, n_expert, size, width), jnp.bfloat16),
        in_specs=[VMEM] * 2,
        out_specs=VMEM,
        scratch_shapes=back_scratch(sizes, size, width),
        name="gather_back",
        compiler_params=pltpu.CompilerParams(
            collective_id=2, has_side_effects=True, vmem_limit_bytes=48 << 20
        ),
    )(first, second)


def gated_terms(gate_pre, up_pre):
    root = math.sqrt(2.0 / math.pi)
    square = gate_pre * gate_pre
    bend = jnp.tanh(root * (gate_pre + 0.044715 * square * gate_pre))
    half = 0.5 * (1.0 + bend)
    active = gate_pre * half
    slope = half + 0.5 * gate_pre * (1.0 - bend * bend) * root * (1.0 + 3 * 0.044715 * square)
    return active * up_pre, active, up_pre * slope


def expert_kernel(
    sizes, rows_per, info_ref, moe_ref, cot_ref, w_in, wg_hbm, wu_hbm, wd_hbm,
    q_out, x_ref, hid_out, dg_out, du_out, gr_out,
    g_ref, w_ref, wg, wu, wd, act, slope, away, own, sem_w, *scratch,
):
    me = Place(*sizes)
    c = me.c
    fetch = {}
    for n, j in enumerate((1 - c, c)):
        for i, (src, dst) in enumerate(((wg_hbm, wg), (wu_hbm, wu), (wd_hbm, wd))):
            fetch[n, i] = pltpu.make_async_copy(src.at[j], dst.at[j], sem_w.at[n, i])
            fetch[n, i].start()
    greet(column_peers(me))
    rows_of, (out_x, out_w, out_g) = send_out(
        me, rows_per, (info_ref, moe_ref, cot_ref, w_in), (x_ref, w_ref, g_ref), scratch[:8], scratch[8:14]
    )
    scratch = scratch[14:]
    bf, f32 = jnp.bfloat16, jnp.float32
    size = x_ref.shape[2]
    column = me.n_expert
    half = column // 2
    step = math.gcd(column, 4)
    chunk = step * size
    back = Back(
        me, lambda i: away.at[i],
        lambda i, block: own[i, pl.ds(pl.multiple_of(block * size, 8), size), :],
        q_out, *scratch[:4], scratch[4:],
    )

    def dot(left, right, contract):
        return lax.dot_general(left, right, (contract, ((), ())), preferred_element_type=f32)

    def flat(value):
        return value.reshape(chunk, value.shape[-1])

    def blocks(value):
        return value.reshape(step, size, value.shape[-1])

    def store(i, first, some, rows, value):
        if first:
            away[i, some] = blocks(value.astype(bf))
        else:
            own[i, rows, :] = value

    def each(start, count, body):
        @pl.loop(0, count // step)
        def _(n):
            at = start + n * step
            body(pl.ds(at, step), pl.ds(pl.multiple_of(at * size, 8), chunk))

    def forward(first, j, start, count):
        def body(some, rows):
            x = flat(x_ref[j, some])
            gate_pre = dot(x, wg[j], ((1,), (1,)))
            up_pre = dot(x, wu[j], ((1,), (1,)))
            hidden, active, lean = gated_terms(gate_pre, up_pre)
            act[j, rows, :] = active
            slope[j, rows, :] = lean
            hidden = hidden.astype(bf)
            hid_out[j, some] = blocks(hidden)
            store(0, first, some, rows, dot(hidden, wd[j], ((1,), (0,))))

        each(start, count, body)

    def backward(first, j, start, count):
        def body(some, rows):
            pieces = flat(w_ref[j, some].astype(f32))
            weight = pieces[:, 0:1] + pieces[:, 1:2] + pieces[:, 2:3]
            grad = (weight * flat(g_ref[j, some].astype(f32))).astype(bf)
            gr_out[j, some] = blocks(grad)
            grad_hidden = dot(grad, wd[j], ((1,), (1,)))
            dg = (grad_hidden * slope[j, rows, :]).astype(bf)
            du = (grad_hidden * act[j, rows, :]).astype(bf)
            dg_out[j, some] = blocks(dg)
            du_out[j, some] = blocks(du)
            store(1, first, some, rows, dot(dg, wg[j], ((1,), (0,))) + dot(du, wu[j], ((1,), (0,))))

        each(start, count, body)

    for payload in (out_x, out_w):
        payload.pass_on(range(column))
        payload.cross(0)
    for payload in (out_x, out_w):
        for s in range(1, me.ny):
            payload.cross(s)
    for i in range(3):
        fetch[0, i].wait()
    out_x.arrive()
    forward(True, 1 - c, 0, me.ny * column)
    back.to_mate(0)
    out_g.pass_on(range(half))
    for i in range(3):
        fetch[1, i].wait()
    for k in range(1, me.ny):
        forward(False, c, back.ys[k] * column, column)
    back.along_y(0)
    out_g.pass_on(range(half, column))
    out_g.cross(0)
    forward(False, c, me.y * column, column)
    for s in range(1, me.ny):
        out_g.cross(s)
    out_g.arrive()
    out_w.arrive()
    backward(True, 1 - c, 0, me.ny * column)
    back.to_mate(1)
    back.finish(0, back.order[:half])
    for k in range(1, me.ny):
        backward(False, c, back.ys[k] * column, column)
    back.along_y(1)
    backward(False, c, me.y * column, column)
    back.finish(0, back.order[half:])
    back.across(0)
    back.finish(1, back.order)
    back.across(1)
    back.close()
    for payload in (out_x, out_w, out_g):
        payload.close()
    rows_of.close()


def experts(sizes, micro, cap, info, moe, cot, weights, w_gate, w_up, w_down):
    n_expert, ny, per_core = sizes[0], sizes[1] // 2, micro * cap
    seq, width = cot.shape
    units = w_down.shape[1]
    count, size = ny * n_expert, 2 * per_core
    bf, f32 = jnp.bfloat16, jnp.float32
    any_space = pl.BlockSpec(memory_space=pl.ANY)
    inner = jax.ShapeDtypeStruct((2, count, size, units), bf)
    outer = jax.ShapeDtypeStruct((2, count, size, width), bf)
    return pl.pallas_call(
        functools.partial(expert_kernel, sizes, (micro, cap, per_core)),
        out_shape=(
            jax.ShapeDtypeStruct((2, 2, n_expert, size, width), bf), outer, inner, inner, inner, outer,
        ),
        in_specs=[VMEM] * 4 + [any_space] * 3,
        out_specs=(VMEM,) * 6,
        scratch_shapes=[
            pltpu.VMEM((2, count, size, width), bf),
            pltpu.VMEM((2, count, size, 128), bf),
            pltpu.VMEM(w_gate.shape, bf),
            pltpu.VMEM(w_up.shape, bf),
            pltpu.VMEM(w_down.shape, bf),
            pltpu.VMEM((2, count * size, units), f32),
            pltpu.VMEM((2, count * size, units), f32),
            pltpu.VMEM((2, count, size, width), bf),
            pltpu.VMEM((2, count * size, width), f32),
            DMA((2, 3)),
        ]
        + rows_scratch(sizes, per_core, seq, width)
        + spread_sems(sizes)
        + back_scratch(sizes, size, width),
        name="experts",
        compiler_params=pltpu.CompilerParams(
            collective_id=4, has_side_effects=True, vmem_limit_bytes=60 << 20
        ),
    )(info, moe, cot, weights, w_gate, w_up, w_down)


def finish_kernel(sums_ref, x_hbm, h_hbm, dg_hbm, du_hbm, gr_hbm, *refs):
    outs, (x, h, dg, du, gr, stage, sem_in, sem_out) = refs[:7], refs[7:]
    loads = []
    for i, (src, dst) in enumerate(((x_hbm, x), (h_hbm, h), (dg_hbm, dg), (du_hbm, du), (gr_hbm, gr))):
        loads.append(pltpu.make_async_copy(src, dst, sem_in.at[i]))
        loads[-1].start()
    slots, rows = stage.shape[:2]
    width = sums_ref.shape[1]
    units = h.shape[2]
    jobs = []
    products = [
        (left, right, out, j, f)
        for left, right, out in ((dg, x, outs[4]), (du, x, outs[5]), (h, gr, outs[6]))
        for j in range(2)
        for f in range(0, units, rows)
    ]
    casts = [(m, r) for m in range(4) for r in range(0, width, rows)]
    while casts or products:
        if casts:
            jobs.append(casts.pop(0))
        if products and (len(jobs) > 3 or not casts):
            jobs.append(products.pop(0))
    flying = [None] * slots
    loaded = False
    for n, job in enumerate(jobs):
        slot = n % slots
        if flying[slot] is not None:
            flying[slot].wait()
        if len(job) == 2:
            m, r = job
            stage[slot] = sums_ref[m, r : r + rows, :].astype(jnp.float32)
            src, dst = stage.at[slot], outs[m].at[pl.ds(r, rows)]
        else:
            if not loaded:
                for load in loads:
                    load.wait()
                loaded = True
            left, right, out, j, f = job
            size = min(rows, units - f)
            stage[slot, :size] = lax.dot_general(
                left[j, :, f : f + size], right[j], (((0,), (0,)), ((), ())),
                preferred_element_type=jnp.float32,
            )
            src, dst = stage.at[slot, pl.ds(0, size)], out.at[j, pl.ds(f, size)]
        flying[slot] = pltpu.make_async_copy(src, dst, sem_out.at[slot])
        flying[slot].start()
    for copy in flying:
        if copy is not None:
            copy.wait()


def finish(sums, x, h, dg, du, gr):
    f32 = jnp.float32
    width = sums.shape[1]
    units = h.shape[2]
    any_space = pl.BlockSpec(memory_space=pl.ANY)
    return pl.pallas_call(
        finish_kernel,
        out_shape=(jax.ShapeDtypeStruct((width, width), f32),) * 4
        + (jax.ShapeDtypeStruct((2, units, width), f32),) * 3,
        in_specs=[VMEM] + [any_space] * 5,
        out_specs=(any_space,) * 7,
        scratch_shapes=[pltpu.VMEM(a.shape, a.dtype) for a in (x, h, dg, du, gr)]
        + [pltpu.VMEM((4, 256, width), f32), DMA((5,)), DMA((4,))],
        name="finish",
        compiler_params=pltpu.CompilerParams(vmem_limit_bytes=32 << 20),
    )(sums, x, h, dg, du, gr)


def reduce_kernel(
    sizes, pieces, left_ref, right_ref, small_ref, out, small_out,
    buf_a, buf_b, acc, *boxes,
):
    me = Place(*sizes)
    c, mate = me.c, me.at(c=1 - me.c)
    n = me.nx
    seq = right_ref.shape[1]
    total_rows = out.shape[1]
    is0 = c == 0
    pair = jnp.where(is0, me.x, me.y)
    other = jnp.where(is0, me.y, me.x)
    lo, hi, nh = pair % 2, pair // 2, n // 2

    def along(pair_at, other_at, z=None):
        return me.at(x=jnp.where(is0, pair_at, other_at), y=jnp.where(is0, other_at, pair_at), z=z)

    flip_x, flip_y = me.x + 1 - 2 * (me.x % 2), me.y + 1 - 2 * (me.y % 2)
    dims = [
        (n, other, lambda q: along(pair, q)),
        (nh, hi, lambda q: along(q * 2 + lo, other)),
        (2, me.z % 2, lambda q: me.at(z=me.z // 2 * 2 + q)),
        (me.nz // 2, me.z // 2, lambda q: me.at(z=q * 2 + me.z % 2)),
    ]
    parts, gots = boxes[:4], boxes[4:8]
    half, small_half, small_got, fs, fr, os, ps, pr, gs, gr, ms, mr, cs, cr, ss, sr = boxes[8:]
    levels = [i for i, d in enumerate(dims) if d[0] > 1]
    x_peers = [me.at(x=(me.x + k) % n) for k in range(1, n)]
    y_peers = [me.at(y=(me.y + k) % n) for k in range(1, n)]
    z_peers = [me.at(z=(me.z + k) % me.nz) for k in range(1, me.nz)]
    greet(
        [mate, me.at(x=flip_x, c=1 - c), me.at(y=flip_y, c=1 - c)] + x_peers + y_peers + z_peers
    )

    def slot_a(slot):
        return buf_a.at[pl.ds(pl.multiple_of(slot * seq, seq), seq), :]

    def slot_b(slot):
        return buf_b.at[pl.ds(pl.multiple_of(slot * seq, seq), seq), :]

    targets = [
        (mate, 1 - c, other % 2, c),
        (me.at(x=flip_x, c=0), 0, flip_x % 2, 2 + c),
        (me.at(y=flip_y, c=1), 1, flip_y % 2, 2 + c),
    ]
    factor = []
    for i, (device, role, parity, slot) in enumerate(targets):
        a, b = jnp.where(role == 0, 0, parity), role * 2 + parity
        factor.append(remote(left_ref.at[a], slot_a(slot), fs.at[i, 0], fr.at[slot, 0], device))
        factor.append(remote(right_ref.at[b], slot_b(slot), fs.at[i, 1], fr.at[slot, 1], device))
    own = [
        pltpu.make_async_copy(left_ref.at[jnp.where(is0, 0, lo)], slot_a(c), os.at[0]),
        pltpu.make_async_copy(right_ref.at[c * 2 + lo], slot_b(c), os.at[1]),
    ]
    for copy in own:
        copy.start()
    rows_s = half.shape[0]
    small = [remote(small_ref.at[pl.ds((1 - c) * rows_s, rows_s)], half, ss.at[0], sr.at[0], mate)]
    small_dims = [
        (n, me.x, lambda q: me.at(x=q)),
        (n, me.y, lambda q: me.at(y=q)),
        (me.nz, me.z, lambda q: me.at(z=q)),
    ]
    small_wait = [small[0]]
    small_slot = [1]

    def small_step(step):
        for copy in small_wait:
            copy.wait_recv()
        small_wait.clear()
        if step == 0:
            total = small_ref[pl.ds(c * rows_s, rows_s)] + half[...]
        elif step <= 3:
            total = small_got[step - 1, 0]
            for k in range(1, small_dims[step - 1][0]):
                total = total + small_got[step - 1, k]
        if step < 3:
            count, index, peer = small_dims[step]
            small_half[step] = total
            small_got[step, index] = total
            for k in range(1, count):
                small_wait.append(
                    remote(
                        small_half.at[step], small_got.at[step, index], ss.at[small_slot[0]],
                        sr.at[small_slot[0]], peer((index + k) % count),
                    )
                )
                small_slot[0] += 1
        elif step == 3:
            small_out[pl.ds(c * rows_s, rows_s)] = total
            block = small_out.at[pl.ds(c * rows_s, rows_s)]
            small_wait.append(
                remote(block, block, ss.at[small_slot[0]], sr.at[small_slot[0]], mate)
            )
        small.extend(small_wait)

    for where in (1 - c, 2, 3):
        for i, (src, dst) in enumerate(((left_ref, slot_a(where)), (right_ref, slot_b(where)))):
            pltpu.make_async_remote_copy(
                src_ref=src.at[0], dst_ref=dst, send_sem=fs.at[0, i], recv_sem=fr.at[where, i],
                device_id=mate, device_id_type=MESH,
            ).wait_recv()
    for copy in own:
        copy.wait()

    rows_k = total_rows // pieces
    matrix = c * 2 + lo
    pending = {}

    def multiply(k):
        acc[k] = lax.dot_general(
            buf_a[:, k * rows_k : (k + 1) * rows_k], buf_b[...], (((0,), (0,)), ((), ())),
            preferred_element_type=jnp.float32,
        )
        push(k, 0, rows_k)

    def push(k, at, rows):
        level = levels[at]
        count, index, peer = dims[level]
        size = rows // count
        copies = []
        for s in range(1, count):
            to = (index + s) % count
            parts[level][k, s - 1] = acc[k, pl.ds(pl.multiple_of(to * size, 8), size), :].astype(jnp.bfloat16)
            copies.append(
                remote(
                    parts[level].at[k, s - 1], gots[level].at[k, s - 1],
                    ps.at[level, k, s - 1], pr.at[level, k, s - 1], peer(to),
                )
            )
        pending["push", at, k] = copies

    def rows_at(at):
        rows = rows_k
        for i in range(at):
            rows //= dims[levels[i]][0]
        return rows

    def add(k, at):
        level = levels[at]
        count, index, _ = dims[level]
        size = rows_at(at) // count
        for copy in pending["push", at, k]:
            copy.wait_recv()
        total = acc[k, pl.ds(pl.multiple_of(index * size, 8), size), :]
        for s in range(1, count):
            total = total + gots[level][k, s - 1].astype(jnp.float32)
        if at + 1 < len(levels):
            acc[k, :size, :] = total
            push(k, at + 1, size)
        else:
            out[matrix, pl.ds(offset(k, at), size), :] = total.astype(jnp.bfloat16)
            share(k, at)

    def offset(k, at):
        start, rows = k * rows_k, rows_k
        for i in range(at + 1):
            count, index, _ = dims[levels[i]]
            rows //= count
            start = start + index * rows
        return pl.multiple_of(start, 8)

    def share(k, at):
        level = levels[at]
        count, index, peer = dims[level]
        size = rows_at(at) // count
        block = out.at[matrix, pl.ds(offset(k, at), size), :]
        pending["share", at, k] = [
            remote(block, block, gs.at[level, k, s - 1], gr.at[level, k, s - 1], peer((index + s) % count))
            for s in range(1, count)
        ]

    def shared(k, at):
        for copy in pending["share", at, k]:
            copy.wait_recv()
        if at:
            share(k, at - 1)
        else:
            block = out.at[matrix, pl.ds(k * rows_k, rows_k), :]
            pending["mate", k] = remote(
                block, block, ms.at[k], mr.at[k], along(pair + 1 - 2 * lo, other)
            )

    def across(k):
        pending["mate", k].wait_recv()
        block = out.at[pl.ds(2 * c, 2), pl.ds(k * rows_k, rows_k), :]
        pending["core", k] = remote(block, block, cs.at[k], cr.at[k], mate)

    steps = [multiply]
    steps += [functools.partial(add, at=i) for i in range(len(levels))]
    steps += [functools.partial(shared, at=i) for i in reversed(range(len(levels)))]
    events = sorted((0 if p == 0 else p + k, -p, k) for p in range(len(steps)) for k in range(pieces))
    before = 0
    for t, p, k in events:
        if before < t <= 5:
            small_step(t - 1)
        before = t
        steps[-p](k)
    for k in range(pieces):
        across(k)
    for k in range(pieces):
        pending["core", k].wait_recv()
    for copy in factor + small:
        copy.wait_send()
    for copies in pending.values():
        for copy in copies if isinstance(copies, list) else [copies]:
            copy.wait_send()


def reduce_all(sizes, left, right, small, pieces=8):
    n_expert, n_dp = sizes
    nz = math.gcd(n_expert, 4)
    n = n_expert // nz
    nh = n // 2
    assert n == n_dp // 2
    seq, width = left.shape[1:]
    rows_k = width // pieces
    bf, f32 = jnp.bfloat16, jnp.float32
    rows_s = small.shape[0] // 2
    splits = [n, nh, 2, nz // 2]
    sizes_at = [rows_k // math.prod(splits[: i + 1]) for i in range(4)]
    counts = [max(q - 1, 1) for q in splits]
    most = max(counts)
    boxes = [pltpu.VMEM((pieces, q, s, width), bf) for q, s in zip(counts, sizes_at)]
    smalls = 2 * n + nz
    return pl.pallas_call(
        functools.partial(reduce_kernel, sizes, pieces),
        out_shape=(
            jax.ShapeDtypeStruct((4, width, width), bf),
            jax.ShapeDtypeStruct(small.shape, f32),
        ),
        in_specs=[VMEM] * 3,
        out_specs=(VMEM, VMEM),
        scratch_shapes=[
            pltpu.VMEM((4 * seq, width), bf),
            pltpu.VMEM((4 * seq, width), bf),
            pltpu.VMEM((pieces, rows_k, width), f32),
            *boxes,
            *boxes,
            pltpu.VMEM((rows_s, width), f32),
            pltpu.VMEM((3, rows_s, width), f32),
            pltpu.VMEM((3, max(n, nz), rows_s, width), f32),
            DMA((3, 2)),
            DMA((4, 2)),
            DMA((2,)),
            DMA((4, pieces, most)),
            DMA((4, pieces, most)),
            DMA((4, pieces, most)),
            DMA((4, pieces, most)),
            DMA((pieces,)),
            DMA((pieces,)),
            DMA((pieces,)),
            DMA((pieces,)),
            DMA((smalls,)),
            DMA((smalls,)),
        ],
        name="reduce_all",
        compiler_params=pltpu.CompilerParams(
            collective_id=3, has_side_effects=True, vmem_limit_bytes=24 << 20
        ),
    )(left, right, small)


def rms_scale(values):
    return lax.rsqrt(jnp.mean(values * values, axis=-1, keepdims=True) + epsilon)


def bucket_hot(seq_len, buckets):
    position = jnp.arange(seq_len, dtype=jnp.int32)
    relative = position[None, :] - position[:, None]
    distance = jnp.abs(relative)
    far_bucket = jnp.full_like(distance, 8)
    for threshold in bucket_edges:
        far_bucket = far_bucket + (distance >= threshold).astype(jnp.int32)
    bucketed = jnp.where(distance < 8, distance, far_bucket) + 16 * (relative > 0).astype(jnp.int32)
    bucket_ids = jnp.arange(buckets, dtype=jnp.int32)
    return (bucketed[None, :, :] == bucket_ids[:, None, None]).astype(jnp.float32)


def dot32(pattern, left, right):
    return jnp.einsum(pattern, left, right, preferred_element_type=jnp.float32)


def shards(
    layer_in, routes, queue_slots, norm_attn, w_query, w_key, w_value, w_out, rel_table,
    norm_moe, router, w_gate, w_up, w_down, cotangent,
):
    bf, f32 = jnp.bfloat16, jnp.float32
    seq_len, width = layer_in.shape
    buckets, heads = rel_table.shape
    expert_count = router.shape[1]
    sizes = (lax.axis_size("expert"), lax.axis_size("dp"))
    n_expert, n_dp = sizes
    assert w_gate.shape[0] == 2 and expert_count == 2 * n_expert
    group_len = seq_len // MICRO
    capacity = (5 * group_len + 2 * expert_count - 1) // (2 * expert_count)
    split_heads = (seq_len, heads, width // heads)
    layer_rows = layer_in.astype(f32)
    inv_attn = rms_scale(layer_rows)
    normed_attn = layer_rows * inv_attn
    attn_in = (normed_attn * norm_attn).astype(bf)
    query_heads = dot32("sd,de->se", attn_in, w_query).astype(bf).reshape(split_heads)
    key_heads = dot32("sd,de->se", attn_in, w_key).astype(bf).reshape(split_heads)
    value_heads = dot32("sd,de->se", attn_in, w_value).astype(bf).reshape(split_heads)
    one_hot = bucket_hot(seq_len, buckets)
    bias = jnp.einsum("bij,bh->hij", one_hot, rel_table, precision=highest)
    scores = dot32("ihd,jhd->hij", query_heads, key_heads) + bias
    exponent = jnp.exp(scores - jnp.max(scores, axis=-1, keepdims=True))
    probs = exponent / jnp.sum(exponent, axis=-1, keepdims=True)
    probs_low = probs.astype(bf)
    context = dot32("hij,jhd->ihd", probs_low, value_heads).astype(bf).reshape(seq_len, width)
    residual = layer_rows + dot32("se,ed->sd", context, w_out)
    inv_moe = rms_scale(residual)
    normed_moe = residual * inv_moe
    moe_in = normed_moe * norm_moe
    logits = jnp.dot(moe_in, router, precision=highest)
    gate_prob = jax.nn.softmax(logits, axis=-1)
    expert_ids = jnp.arange(expert_count, dtype=jnp.int32)
    first_hot = (routes[:, 0:1] == expert_ids).astype(f32)
    second_hot = (routes[:, 1:2] == expert_ids).astype(f32)
    prob_first = jnp.sum(gate_prob * first_hot, axis=-1, keepdims=True)
    prob_second = jnp.sum(gate_prob * second_hot, axis=-1, keepdims=True)
    weight_first = prob_first / (prob_first + prob_second)
    weight_second = prob_second / (prob_first + prob_second)
    weights = jnp.concatenate([weight_first, weight_second], axis=1)

    info = jnp.concatenate([routes.T, queue_slots.T, jnp.zeros((4, seq_len), jnp.int32)])
    gate_t, up_t = jnp.swapaxes(w_gate, 1, 2), jnp.swapaxes(w_up, 1, 2)
    slots = n_dp // 2 * n_expert * 2 * MICRO * capacity
    if 2 * slots * width * 20 + 6 * w_gate.size < 52 << 20:
        back, rows_in, hidden, gate_grad, up_grad, grad_rows = experts(
            sizes, MICRO, capacity, info, moe_in.astype(bf), cotangent, weights, gate_t, up_t, w_down
        )
    else:
        rows_in, weight_in, grad_in = spread(
            sizes, MICRO, capacity, info, moe_in.astype(bf), cotangent, weights
        )
        blocks = rows_in.shape[:-1] + (-1,)
        rows_in, grad_in, weight_in = [
            a.reshape(2, -1, a.shape[-1]) for a in (rows_in, grad_in, weight_in)
        ]
        slot_weight = jnp.sum(weight_in[..., :3].astype(f32), axis=-1, keepdims=True)
        grad_rows = (slot_weight * grad_in.astype(f32)).astype(bf)
        gate_pre = dot32("jrd,jdf->jrf", rows_in, w_gate)
        up_pre = dot32("jrd,jdf->jrf", rows_in, w_up)
        hidden, active, lean = gated_terms(gate_pre, up_pre)
        hidden = hidden.astype(bf)
        partial_out = dot32("jrf,jfd->jrd", hidden, w_down).astype(bf)
        hidden_grad = dot32("jrd,jfd->jrf", grad_rows, w_down)
        gate_grad, up_grad = (hidden_grad * lean).astype(bf), (hidden_grad * active).astype(bf)
        rows_grad = dot32("jrf,jdf->jrd", gate_grad, w_gate) + dot32("jrf,jdf->jrd", up_grad, w_up)
        back = gather_back(sizes, partial_out.reshape(blocks), rows_grad.astype(bf).reshape(blocks))
    rows_in, hidden, gate_grad, up_grad, grad_rows = [
        a.reshape(2, -1, a.shape[-1]) for a in (rows_in, hidden, gate_grad, up_grad, grad_rows)
    ]
    back = back.reshape(2, -1, width)

    core = lax.axis_index("dp") % 2
    per_core = MICRO * capacity
    token = jnp.arange(seq_len, dtype=jnp.int32)[:, None]
    place = (routes % 2) * (n_expert * 2 * per_core) + (routes // 2) * (2 * per_core)
    place = place + core * per_core + (token // group_len) * capacity + queue_slots
    place = jnp.where(queue_slots >= 0, place, -1)
    slot_ids = jnp.arange(2 * n_expert * 2 * per_core, dtype=jnp.int32)
    select_first = (place[:, 0:1] == slot_ids).astype(bf)
    select_second = (place[:, 1:2] == slot_ids).astype(bf)
    picked_first = dot32("tp,pd->td", select_first, back[0])
    picked_second = dot32("tp,pd->td", select_second, back[0])
    moe = weight_first * picked_first + weight_second * picked_second
    layer_out = (residual + moe).astype(bf)
    cot_rows = cotangent.astype(f32)
    grad_weight_first = jnp.sum(cot_rows * picked_first, axis=-1, keepdims=True)
    grad_weight_second = jnp.sum(cot_rows * picked_second, axis=-1, keepdims=True)
    grad_from_slots = dot32("tp,pd->td", select_first + select_second, back[1])
    mean_grad = weight_first * grad_weight_first + weight_second * grad_weight_second
    logit_first = weight_first * (grad_weight_first - mean_grad)
    logit_second = weight_second * (grad_weight_second - mean_grad)
    grad_logits = logit_first * first_hot + logit_second * second_hot
    grad_router = jnp.einsum("sd,se->ed", moe_in, grad_logits, precision=highest)
    grad_moe_in = grad_from_slots + jnp.einsum("se,de->sd", grad_logits, router, precision=highest)
    grad_norm_moe = jnp.sum(grad_moe_in * normed_moe, axis=0)
    grad_normed = grad_moe_in * norm_moe
    grad_residual = cot_rows + inv_moe * (
        grad_normed - normed_moe * jnp.mean(grad_normed * normed_moe, axis=-1, keepdims=True)
    )
    grad_attn_low = grad_residual.astype(bf)
    grad_context = dot32("sd,ed->se", grad_attn_low, w_out).astype(bf).reshape(split_heads)
    grad_values = dot32("hij,ihd->jhd", probs_low, grad_context).astype(bf).reshape(seq_len, width)
    grad_probs = dot32("ihd,jhd->hij", grad_context, value_heads)
    grad_scores = probs * (grad_probs - jnp.sum(probs * grad_probs, axis=-1, keepdims=True))
    grad_rel_table = jnp.einsum("bij,hij->bh", one_hot, grad_scores, precision=highest)
    scores_low = grad_scores.astype(bf)
    grad_queries = dot32("hij,jhd->ihd", scores_low, key_heads).astype(bf).reshape(seq_len, width)
    grad_keys = dot32("hij,ihd->jhd", scores_low, query_heads).astype(bf).reshape(seq_len, width)
    grad_attn_in = dot32("se,de->sd", grad_queries, w_query)
    grad_attn_in = grad_attn_in + dot32("se,de->sd", grad_keys, w_key)
    grad_attn_in = grad_attn_in + dot32("se,de->sd", grad_values, w_value)
    grad_norm_attn = jnp.sum(grad_attn_in * normed_attn, axis=0)
    grad_normed_attn = grad_attn_in * norm_attn
    grad_input = grad_residual + inv_attn * (
        grad_normed_attn
        - normed_attn * jnp.mean(grad_normed_attn * normed_attn, axis=-1, keepdims=True)
    )
    table = grad_rel_table.reshape(-1)
    small = jnp.concatenate(
        [
            grad_router,
            grad_norm_attn[None],
            grad_norm_moe[None],
            jnp.pad(table, (0, width - table.size))[None],
        ]
    )
    small = jnp.pad(small, ((0, -small.shape[0] % 16), (0, 0)))
    sums, small = reduce_all(
        sizes,
        jnp.stack([attn_in, context]),
        jnp.stack([grad_queries, grad_keys, grad_values, grad_attn_low]),
        small,
    )
    *matrices, grad_w_gate, grad_w_up, grad_w_down = finish(
        sums, rows_in, hidden, gate_grad, up_grad, grad_rows
    )
    grad_w_gate, grad_w_up = jnp.swapaxes(grad_w_gate, 1, 2), jnp.swapaxes(grad_w_up, 1, 2)
    return (
        layer_out, grad_input, small[expert_count], *matrices,
        small[expert_count + 2, : table.size].reshape(buckets, heads),
        small[expert_count + 1], small[:expert_count].T, grad_w_gate, grad_w_up, grad_w_down,
    )


def solution(mesh):
    in_specs = (
        P(("expert", "dp"), None),
        P(("expert", "dp"), None),
        P(("expert", "dp"), None),
        P(),
        P(),
        P(),
        P(),
        P(),
        P(),
        P(),
        P(),
        P("expert", None, "dp"),
        P("expert", None, "dp"),
        P("expert", "dp", None),
        P(("expert", "dp"), None),
    )
    out_specs = (
        P(("expert", "dp"), None),
        P(("expert", "dp"), None),
        P(),
        P(),
        P(),
        P(),
        P(),
        P(),
        P(),
        P(),
        P("expert", None, "dp"),
        P("expert", None, "dp"),
        P("expert", "dp", None),
    )
    return jax.shard_map(shards, mesh=mesh, in_specs=in_specs, out_specs=out_specs, check_vma=False)
```

```python
import functools
import math

import jax
import jax.numpy as jnp
from jax import lax
from jax.experimental import pallas as pl
from jax.experimental.pallas import tpu as pltpu
from jax.sharding import PartitionSpec as P

MICRO = 4

epsilon = 1e-06
bucket_edges = (12, 16, 23, 32, 46, 64, 91)
highest = lax.Precision.HIGHEST

MESH = pl.DeviceIdType.MESH
VMEM = pl.BlockSpec(memory_space=pltpu.VMEM)
DMA = pltpu.SemaphoreType.DMA


class Place:
    def __init__(self, n_expert, n_dp):
        self.n_expert, self.n_dp = n_expert, n_dp
        self.nz = math.gcd(n_expert, 4)
        self.nx = n_expert // self.nz
        self.ny = n_dp // 2
        self.e = lax.axis_index("expert")
        self.d = lax.axis_index("dp")
        self.z, self.x = self.e // self.nx, self.e % self.nx
        self.y, self.c = self.d // 2, self.d % 2

    def at(self, z=None, x=None, y=None, c=None, e=None):
        z = self.z if z is None else z
        x = self.x if x is None else x
        y = self.y if y is None else y
        c = self.c if c is None else c
        e = z * self.nx + x if e is None else e
        return (e, y * 2 + c)


def remote(src, dst, send, recv, device):
    copy = pltpu.make_async_remote_copy(
        src_ref=src, dst_ref=dst, send_sem=send, recv_sem=recv, device_id=device, device_id_type=MESH
    )
    copy.start()
    return copy


def greet(devices):
    barrier = pltpu.get_barrier_semaphore()
    for device in devices:
        pl.semaphore_signal(barrier, inc=1, device_id=device, device_id_type=MESH)
    pl.semaphore_wait(barrier, len(devices))


def column_peers(me):
    out = [me.at(c=1 - me.c)]
    out += [me.at(y=(me.y + k) % me.ny) for k in range(1, me.ny)]
    out += [me.at(e=(me.e + k) % me.n_expert) for k in range(1, me.n_expert)]
    return out


class Spread:
    def __init__(self, me, rows, recv, sems):
        self.me, self.rows, self.recv = me, rows, recv
        self.se, self.re, self.sy, self.ry, self.sc, self.rc = sems
        self.came, self.along, self.crossed = {}, {}, {}

    def send(self):
        me = self.me
        for k in range(1, me.n_expert):
            to = (me.e + k) % me.n_expert
            self.came[k] = remote(
                self.rows.at[to], self.recv.at[me.c, me.y * me.n_expert + me.e],
                self.se.at[k], self.re.at[k], me.at(e=to),
            )
        self.recv[me.c, me.y * me.n_expert + me.e] = self.rows[me.e]

    def pass_on(self, blocks):
        me = self.me
        for k in blocks:
            if k:
                self.came[k].wait_recv()
            src = (me.e - k + me.n_expert) % me.n_expert
            block = self.recv.at[me.c, me.y * me.n_expert + src]
            for s in range(1, me.ny):
                self.along[s, k] = remote(
                    block, block, self.sy.at[s - 1, k], self.ry.at[s - 1, k], me.at(y=(me.y + s) % me.ny)
                )

    def cross(self, s):
        me = self.me
        if s:
            for k in range(me.n_expert):
                self.along[s, k].wait_recv()
        block = self.recv.at[me.c, pl.ds((me.y - s + me.ny) % me.ny * me.n_expert, me.n_expert)]
        self.crossed[s] = remote(block, block, self.sc.at[s], self.rc.at[s], me.at(c=1 - me.c))

    def arrive(self):
        for copy in self.crossed.values():
            copy.wait_recv()

    def close(self):
        for copies in (self.came, self.along, self.crossed):
            for copy in copies.values():
                copy.wait_send()


def spread_sems(sizes):
    n_expert, ny = sizes[0], sizes[1] // 2
    most = max(ny - 1, 1)
    return [
        DMA((3, n_expert)), DMA((3, n_expert)), DMA((3, most, n_expert)), DMA((3, most, n_expert)),
        DMA((3, ny)), DMA((3, ny)),
    ]


class Rows:
    def __init__(self, me, rows_per, info_ref, moe_ref, cot_ref, w_ref, info_all, tok, wext, send, recv):
        self.me, self.rows_per, self.info_all, self.tok, self.wext = me, rows_per, info_all, tok, wext
        seq = cot_ref.shape[0]
        self.seq = seq
        c, mate = me.c, me.at(c=1 - me.c)
        info_all[c] = info_ref[...]
        tok[0, c] = moe_ref[...]
        lanes = lax.broadcasted_iota(jnp.int32, (seq, 128), 1)
        for k in range(2):
            w = w_ref[:, k : k + 1]
            hi = w.astype(jnp.bfloat16).astype(jnp.float32)
            mid = (w - hi).astype(jnp.bfloat16).astype(jnp.float32)
            low = w - hi - mid
            wext[c, k] = jnp.where(
                lanes == 0, hi, jnp.where(lanes == 1, mid, jnp.where(lanes == 2, low, 0.0))
            ).astype(jnp.bfloat16)
        self.copies = [
            remote(ref, ref, send.at[i], recv.at[i], mate)
            for i, ref in enumerate((info_all.at[c], tok.at[0, c], wext.at[c]))
        ]
        tok[1, c] = cot_ref[...]
        self.copies.append(remote(tok.at[1, c], tok.at[1, c], send.at[3], recv.at[3], mate))

    def hots(self):
        me, seq = self.me, self.seq
        micro, cap, per_core = self.rows_per
        self.copies[0].wait_recv()
        row_ids = lax.broadcasted_iota(jnp.int32, (me.n_expert * 2 * per_core, seq), 0)
        group = lax.broadcasted_iota(jnp.int32, (1, seq), 1) // (seq // micro)
        hots = [[], []]
        for cc in range(2):
            for k in range(2):
                route = self.info_all[cc, k : k + 1, :]
                slot = self.info_all[cc, 2 + k : 3 + k, :]
                target = (route // 2) * (2 * per_core) + cc * per_core + group * cap + slot
                target = jnp.where((slot >= 0) & (route % 2 == me.c), target, -1)
                hots[k].append(jnp.where(row_ids == target, 1.0, 0.0))
        self.each = [[h.astype(jnp.bfloat16) for h in hots[k]] for k in range(2)]
        self.both = [(p + q).astype(jnp.bfloat16) for p, q in zip(*hots)]

    def gather(self, left, right):
        total = None
        for p, q in zip(left, right):
            term = jnp.dot(p, q, preferred_element_type=jnp.float32)
            total = term if total is None else total + term
        per_core = self.rows_per[2]
        return total.astype(jnp.bfloat16).reshape(self.me.n_expert, 2 * per_core, -1)

    def moe(self):
        self.copies[1].wait_recv()
        return self.gather(self.both, [self.tok[0, 0], self.tok[0, 1]])

    def weights(self):
        self.copies[2].wait_recv()
        wext = self.wext
        return self.gather(self.each[0] + self.each[1], [wext[0, 0], wext[1, 0], wext[0, 1], wext[1, 1]])

    def cot(self):
        self.copies[3].wait_recv()
        return self.gather(self.both, [self.tok[1, 0], self.tok[1, 1]])

    def close(self):
        for copy in self.copies:
            copy.wait_send()


def rows_scratch(sizes, per_core, seq, width):
    mine = (sizes[0], 2 * per_core)
    bf = jnp.bfloat16
    return [
        pltpu.VMEM((2, 8, seq), jnp.int32),
        pltpu.VMEM((2, 2, seq, width), bf),
        pltpu.VMEM((2, 2, seq, 128), bf),
        DMA((4,)),
        DMA((4,)),
        pltpu.VMEM(mine + (width,), bf),
        pltpu.VMEM(mine + (128,), bf),
        pltpu.VMEM(mine + (width,), bf),
    ]


def send_out(me, rows_per, refs, recvs, scratch, sems):
    rows = Rows(me, rows_per, *refs, *scratch[:5])
    rows.hots()
    out = []
    for i, (make, buf) in enumerate(zip((rows.moe, rows.weights, rows.cot), scratch[5:])):
        buf[...] = make()
        payload = Spread(me, buf, recvs[i], [s.at[i] for s in sems])
        payload.send()
        out.append(payload)
    return rows, out


def spread_kernel(sizes, rows_per, info_ref, moe_ref, cot_ref, w_ref, x_out, w_out, g_out, *scratch):
    me = Place(*sizes)
    greet(column_peers(me))
    rows, payloads = send_out(
        me, rows_per, (info_ref, moe_ref, cot_ref, w_ref), (x_out, w_out, g_out), scratch[:8], scratch[8:]
    )
    for payload in payloads:
        payload.pass_on(range(me.n_expert))
        payload.cross(0)
    for payload in payloads:
        for s in range(1, me.ny):
            payload.cross(s)
    for payload in payloads:
        payload.arrive()
        payload.close()
    rows.close()


def spread(sizes, micro, cap, info, moe, cot, weights):
    n_expert, ny, per_core = sizes[0], sizes[1] // 2, micro * cap
    seq, width = cot.shape
    block = (2, ny * n_expert, 2 * per_core)
    bf = jnp.bfloat16
    return pl.pallas_call(
        functools.partial(spread_kernel, sizes, (micro, cap, per_core)),
        out_shape=tuple(jax.ShapeDtypeStruct(block + (n,), bf) for n in (width, 128, width)),
        in_specs=[VMEM] * 4,
        out_specs=(VMEM,) * 3,
        scratch_shapes=rows_scratch(sizes, per_core, seq, width) + spread_sems(sizes),
        name="spread",
        compiler_params=pltpu.CompilerParams(
            collective_id=1, has_side_effects=True, vmem_limit_bytes=48 << 20
        ),
    )(info, moe, cot, weights)


class Back:
    def __init__(self, me, away, own, q_out, r1, stage, r2, final, sems):
        self.me, self.away, self.own = me, away, own
        self.q_out, self.r1, self.stage, self.r2, self.final = q_out, r1, stage, r2, final
        self.sems = sems
        self.ys = [(me.y + k) % me.ny for k in range(me.ny)]
        self.order = list(range(1, me.n_expert)) + [0]
        self.first, self.second, self.third, self.fourth = {}, {}, {}, {}
        self.arrived = set()

    def to_mate(self, i, k):
        me = self.me
        column = pl.ds(self.ys[k] * me.n_expert, me.n_expert)
        self.first[i, k] = remote(
            self.away(i).at[column], self.r1.at[i, column], self.sems[0].at[i, k], self.sems[1].at[i, k],
            me.at(c=1 - me.c),
        )

    def partial(self, i, y, e):
        block = y * self.me.n_expert + e
        return self.own(i, block) + self.r1[i, block].astype(jnp.float32)

    def along_y(self, i):
        me = self.me
        for k in range(1, me.ny):
            self.first[i, k].wait_recv()
            for j in self.order:
                e = (me.e + j) % me.n_expert
                self.stage[i, k - 1, e] = self.partial(i, self.ys[k], e).astype(jnp.bfloat16)
                self.second[i, k, j] = remote(
                    self.stage.at[i, k - 1, e], self.r2.at[i, k - 1, e],
                    self.sems[2].at[i, k - 1, j], self.sems[3].at[i, k - 1, j], me.at(y=self.ys[k]),
                )

    def finish(self, i, order):
        me = self.me
        if (i, 0) not in self.arrived:
            self.arrived.add((i, 0))
            self.first[i, 0].wait_recv()
        for j in order:
            e = (me.e + j) % me.n_expert
            total = self.partial(i, me.y, e)
            for k in range(1, me.ny):
                self.second[i, k, j].wait_recv()
                total = total + self.r2[i, k - 1, e].astype(jnp.float32)
            if j:
                self.final[i, e] = total.astype(jnp.bfloat16)
                self.third[i, j] = remote(
                    self.final.at[i, e], self.q_out.at[i, me.c, me.e],
                    self.sems[4].at[i, j], self.sems[5].at[i, j], me.at(e=e),
                )
            else:
                self.q_out[i, me.c, me.e] = total.astype(jnp.bfloat16)

    def across(self, i):
        for j in self.order[:-1]:
            self.third[i, j].wait_recv()
        block = self.q_out.at[i, self.me.c]
        s, r = self.sems[6].at[i], self.sems[7].at[i]
        self.fourth[i] = remote(block, block, s, r, self.me.at(c=1 - self.me.c))

    def close(self):
        for copy in self.fourth.values():
            copy.wait()
        for copies in (self.first, self.second, self.third):
            for copy in copies.values():
                copy.wait_send()


def back_scratch(sizes, size, width):
    n_expert, ny = sizes[0], sizes[1] // 2
    most = max(ny - 1, 1)
    bf = jnp.bfloat16
    return [
        pltpu.VMEM((2, ny * n_expert, size, width), bf),
        pltpu.VMEM((2, most, n_expert, size, width), bf),
        pltpu.VMEM((2, most, n_expert, size, width), bf),
        pltpu.VMEM((2, n_expert, size, width), bf),
        DMA((2, ny)),
        DMA((2, ny)),
        DMA((2, most, n_expert)),
        DMA((2, most, n_expert)),
        DMA((2, n_expert)),
        DMA((2, n_expert)),
        DMA((2,)),
        DMA((2,)),
    ]


def gather_back_kernel(sizes, p0_ref, p1_ref, q_out, *scratch):
    me = Place(*sizes)
    greet(column_peers(me))
    p_refs = (p0_ref, p1_ref)
    back = Back(
        me, lambda i: p_refs[i].at[1 - me.c],
        lambda i, block: p_refs[i][me.c, block].astype(jnp.float32), q_out, *scratch[:4], scratch[4:],
    )
    for i in range(2):
        for k in reversed(range(me.ny)):
            back.to_mate(i, k)
    for i in range(2):
        back.along_y(i)
    for i in range(2):
        back.finish(i, back.order)
        back.across(i)
    back.close()


def gather_back(sizes, first, second):
    n_expert = sizes[0]
    _, _, size, width = first.shape
    return pl.pallas_call(
        functools.partial(gather_back_kernel, sizes),
        out_shape=jax.ShapeDtypeStruct((2, 2, n_expert, size, width), jnp.bfloat16),
        in_specs=[VMEM] * 2,
        out_specs=VMEM,
        scratch_shapes=back_scratch(sizes, size, width),
        name="gather_back",
        compiler_params=pltpu.CompilerParams(
            collective_id=2, has_side_effects=True, vmem_limit_bytes=48 << 20
        ),
    )(first, second)


def gated_terms(gate_pre, up_pre):
    root = math.sqrt(2.0 / math.pi)
    square = gate_pre * gate_pre
    bend = jnp.tanh(root * (gate_pre + 0.044715 * square * gate_pre))
    half = 0.5 * (1.0 + bend)
    active = gate_pre * half
    slope = half + 0.5 * gate_pre * (1.0 - bend * bend) * root * (1.0 + 3 * 0.044715 * square)
    return active * up_pre, active, up_pre * slope


def expert_kernel(
    sizes, rows_per, info_ref, moe_ref, cot_ref, w_in, wg_hbm, wu_hbm, wd_hbm,
    q_out, x_ref, hid_out, dg_out, du_out, gr_out,
    g_ref, w_ref, wg, wu, wd, act, slope, away, own, sem_w, *scratch,
):
    me = Place(*sizes)
    c = me.c
    fetch = {}
    for n, j in enumerate((c, 1 - c)):
        for i, (src, dst) in enumerate(((wg_hbm, wg), (wu_hbm, wu), (wd_hbm, wd))):
            fetch[n, i] = pltpu.make_async_copy(src.at[j], dst.at[j], sem_w.at[n, i])
            fetch[n, i].start()
    greet(column_peers(me))
    rows_of, (out_x, out_w, out_g) = send_out(
        me, rows_per, (info_ref, moe_ref, cot_ref, w_in), (x_ref, w_ref, g_ref), scratch[:8], scratch[8:14]
    )
    scratch = scratch[14:]
    bf, f32 = jnp.bfloat16, jnp.float32
    size = x_ref.shape[2]
    column = me.n_expert
    step = math.gcd(column, 4)
    chunk = step * size
    back = Back(
        me, lambda i: away.at[i],
        lambda i, block: own[i, pl.ds(pl.multiple_of(block * size, 8), size), :],
        q_out, *scratch[:4], scratch[4:],
    )

    def dot(left, right, contract):
        return lax.dot_general(left, right, (contract, ((), ())), preferred_element_type=f32)

    def flat(value):
        return value.reshape(chunk, value.shape[-1])

    def blocks(value):
        return value.reshape(step, size, value.shape[-1])

    def store(i, first, some, rows, value):
        if first:
            away[i, some] = blocks(value.astype(bf))
        else:
            own[i, rows, :] = value

    def each(start, count, body):
        @pl.loop(0, count // step)
        def _(n):
            at = start + n * step
            body(pl.ds(at, step), pl.ds(pl.multiple_of(at * size, 8), chunk))

    def forward(first, j, start, count):
        def body(some, rows):
            x = flat(x_ref[j, some])
            gate_pre = dot(x, wg[j], ((1,), (1,)))
            up_pre = dot(x, wu[j], ((1,), (1,)))
            hidden, active, lean = gated_terms(gate_pre, up_pre)
            act[j, rows, :] = active
            slope[j, rows, :] = lean
            hidden = hidden.astype(bf)
            hid_out[j, some] = blocks(hidden)
            store(0, first, some, rows, dot(hidden, wd[j], ((1,), (0,))))

        each(start, count, body)

    def backward(first, j, start, count):
        def body(some, rows):
            pieces = flat(w_ref[j, some].astype(f32))
            weight = pieces[:, 0:1] + pieces[:, 1:2] + pieces[:, 2:3]
            grad = (weight * flat(g_ref[j, some].astype(f32))).astype(bf)
            gr_out[j, some] = blocks(grad)
            grad_hidden = dot(grad, wd[j], ((1,), (1,)))
            dg = (grad_hidden * slope[j, rows, :]).astype(bf)
            du = (grad_hidden * act[j, rows, :]).astype(bf)
            dg_out[j, some] = blocks(dg)
            du_out[j, some] = blocks(du)
            store(1, first, some, rows, dot(dg, wg[j], ((1,), (0,))) + dot(du, wu[j], ((1,), (0,))))

        each(start, count, body)

    here = me.y * column
    away_ys = [back.ys[k] * column for k in range(1, me.ny)]
    shares = [back.order[i * column // 4 : (i + 1) * column // 4] for i in range(4)]
    out_x.pass_on(range(column))
    out_x.cross(0)
    out_g.pass_on(range(column // 4))
    for i in range(3):
        fetch[0, i].wait()
    forward(False, c, here, column)
    out_g.pass_on(range(column // 4, 3 * column // 4))
    for i in range(3):
        fetch[1, i].wait()
    out_x.crossed[0].wait_recv()
    forward(True, 1 - c, here, column)
    back.to_mate(0, 0)
    out_w.pass_on(range(column))
    out_w.cross(0)
    for s in range(1, me.ny):
        out_x.cross(s)
    out_g.pass_on(range(3 * column // 4, column))
    out_g.cross(0)
    for k in range(1, me.ny):
        out_x.crossed[k].wait_recv()
        forward(True, 1 - c, away_ys[k - 1], column)
        back.to_mate(0, k)
    for s in range(1, me.ny):
        out_w.cross(s)
    for k in range(1, me.ny):
        forward(False, c, away_ys[k - 1], column)
    back.along_y(0)
    for s in range(1, me.ny):
        out_g.cross(s)
    out_g.arrive()
    out_w.arrive()
    for k in range(1, me.ny):
        backward(True, 1 - c, away_ys[k - 1], column)
        back.to_mate(1, k)
    back.finish(0, shares[0])
    for k in range(1, me.ny):
        backward(False, c, away_ys[k - 1], column)
    back.along_y(1)
    back.finish(0, shares[1])
    backward(True, 1 - c, here, column)
    back.to_mate(1, 0)
    back.finish(0, shares[2])
    backward(False, c, here, column)
    back.finish(0, shares[3])
    back.across(0)
    back.finish(1, back.order)
    back.across(1)
    back.close()
    for payload in (out_x, out_w, out_g):
        payload.close()
    rows_of.close()


def experts(sizes, micro, cap, info, moe, cot, weights, w_gate, w_up, w_down):
    n_expert, ny, per_core = sizes[0], sizes[1] // 2, micro * cap
    seq, width = cot.shape
    units = w_down.shape[1]
    count, size = ny * n_expert, 2 * per_core
    bf, f32 = jnp.bfloat16, jnp.float32
    any_space = pl.BlockSpec(memory_space=pl.ANY)
    inner = jax.ShapeDtypeStruct((2, count, size, units), bf)
    outer = jax.ShapeDtypeStruct((2, count, size, width), bf)
    return pl.pallas_call(
        functools.partial(expert_kernel, sizes, (micro, cap, per_core)),
        out_shape=(
            jax.ShapeDtypeStruct((2, 2, n_expert, size, width), bf), outer, inner, inner, inner, outer,
        ),
        in_specs=[VMEM] * 4 + [any_space] * 3,
        out_specs=(VMEM,) * 6,
        scratch_shapes=[
            pltpu.VMEM((2, count, size, width), bf),
            pltpu.VMEM((2, count, size, 128), bf),
            pltpu.VMEM(w_gate.shape, bf),
            pltpu.VMEM(w_up.shape, bf),
            pltpu.VMEM(w_down.shape, bf),
            pltpu.VMEM((2, count * size, units), f32),
            pltpu.VMEM((2, count * size, units), f32),
            pltpu.VMEM((2, count, size, width), bf),
            pltpu.VMEM((2, count * size, width), f32),
            DMA((2, 3)),
        ]
        + rows_scratch(sizes, per_core, seq, width)
        + spread_sems(sizes)
        + back_scratch(sizes, size, width),
        name="experts",
        compiler_params=pltpu.CompilerParams(
            collective_id=4, has_side_effects=True, vmem_limit_bytes=42 << 20
        ),
    )(info, moe, cot, weights, w_gate, w_up, w_down)


def finish_kernel(sums_hbm, x_hbm, h_hbm, dg_hbm, du_hbm, gr_hbm, *refs):
    outs, (sums, x, h, dg, du, gr, stage, sem_sum, sem_in, sem_out) = refs[:7], refs[7:]
    slots, rows = stage.shape[:2]
    width = sums.shape[1]
    units = h.shape[2]
    loads = {}

    def load(key, src, dst, sem):
        loads[key] = pltpu.make_async_copy(src, dst, sem)
        loads[key].start()

    def load_sums(keys):
        for n in keys:
            part = n * rows // width, pl.ds(n * rows % width, rows)
            load(("sums", n), sums_hbm.at[part], sums.at[part], sem_sum.at[n])

    casts = range(4 * width // rows)
    load_sums(casts[:4])
    for i, (key, src, dst) in enumerate(
        (("dg", dg_hbm, dg), ("x", x_hbm, x), ("du", du_hbm, du), ("h", h_hbm, h), ("gr", gr_hbm, gr))
    ):
        for j in range(2):
            load((key, j), src.at[j], dst.at[j], sem_in.at[i, j])
    load_sums(casts[4:])

    def need(key):
        if key in loads:
            loads.pop(key).wait()

    jobs = []
    products = [
        (left, right, out, j, f)
        for left, right, out in ((("dg", dg), ("x", x), 4), (("du", du), ("x", x), 5), (("h", h), ("gr", gr), 6))
        for j in range(2)
        for f in range(0, units, rows)
    ]
    casts = list(casts)
    while casts or products:
        if casts:
            jobs.append(casts.pop(0))
        if products and (len(jobs) > 3 or not casts):
            jobs.append(products.pop(0))
    flying = [None] * slots
    for n, job in enumerate(jobs):
        slot = n % slots
        if flying[slot] is not None:
            flying[slot].wait()
        if isinstance(job, int):
            need(("sums", job))
            m, r = job * rows // width, job * rows % width
            stage[slot] = sums[m, r : r + rows, :].astype(jnp.float32)
            src, dst = stage.at[slot], outs[m].at[pl.ds(r, rows)]
        else:
            (left_key, left), (right_key, right), out, j, f = job
            need((left_key, j))
            need((right_key, j))
            size = min(rows, units - f)
            stage[slot, :size] = lax.dot_general(
                left[j, :, f : f + size], right[j], (((0,), (0,)), ((), ())),
                preferred_element_type=jnp.float32,
            )
            src, dst = stage.at[slot, pl.ds(0, size)], outs[out].at[j, pl.ds(f, size)]
        flying[slot] = pltpu.make_async_copy(src, dst, sem_out.at[slot])
        flying[slot].start()
    for copy in flying:
        if copy is not None:
            copy.wait()


def finish(sums, x, h, dg, du, gr):
    f32 = jnp.float32
    width = sums.shape[1]
    units = h.shape[2]
    any_space = pl.BlockSpec(memory_space=pl.ANY)
    return pl.pallas_call(
        finish_kernel,
        out_shape=(jax.ShapeDtypeStruct((width, width), f32),) * 4
        + (jax.ShapeDtypeStruct((2, units, width), f32),) * 3,
        in_specs=[any_space] * 6,
        out_specs=(any_space,) * 7,
        scratch_shapes=[pltpu.VMEM(a.shape, a.dtype) for a in (sums, x, h, dg, du, gr)]
        + [pltpu.VMEM((6, 256, width), f32), DMA((4 * width // 256,)), DMA((5, 2)), DMA((6,))],
        name="finish",
        compiler_params=pltpu.CompilerParams(vmem_limit_bytes=60 << 20),
    )(sums, x, h, dg, du, gr)


def reduce_kernel(
    sizes, pieces, left_ref, right_ref, small_ref, out_hbm, small_out,
    out, sem_out, buf_a, buf_b, acc, *boxes,
):
    me = Place(*sizes)
    c, mate = me.c, me.at(c=1 - me.c)
    n = me.nx
    seq = right_ref.shape[1]
    total_rows = out.shape[1]
    is0 = c == 0
    pair = jnp.where(is0, me.x, me.y)
    other = jnp.where(is0, me.y, me.x)
    lo, hi, nh = pair % 2, pair // 2, n // 2

    def along(pair_at, other_at, z=None):
        return me.at(x=jnp.where(is0, pair_at, other_at), y=jnp.where(is0, other_at, pair_at), z=z)

    flip_x, flip_y = me.x + 1 - 2 * (me.x % 2), me.y + 1 - 2 * (me.y % 2)
    dims = [
        (n, other, lambda q: along(pair, q)),
        (nh, hi, lambda q: along(q * 2 + lo, other)),
        (2, me.z % 2, lambda q: me.at(z=me.z // 2 * 2 + q)),
        (me.nz // 2, me.z // 2, lambda q: me.at(z=q * 2 + me.z % 2)),
    ]
    parts, gots = boxes[:4], boxes[4:8]
    half, small_half, small_got, fs, fr, os, ps, pr, gs, gr, ms, mr, cs, cr, ss, sr = boxes[8:]
    levels = [i for i, d in enumerate(dims) if d[0] > 1]
    x_peers = [me.at(x=(me.x + k) % n) for k in range(1, n)]
    y_peers = [me.at(y=(me.y + k) % n) for k in range(1, n)]
    z_peers = [me.at(z=(me.z + k) % me.nz) for k in range(1, me.nz)]
    greet(
        [mate, me.at(x=flip_x, c=1 - c), me.at(y=flip_y, c=1 - c)] + x_peers + y_peers + z_peers
    )

    def slot_a(slot):
        return buf_a.at[pl.ds(pl.multiple_of(slot * seq, seq), seq), :]

    def slot_b(slot):
        return buf_b.at[pl.ds(pl.multiple_of(slot * seq, seq), seq), :]

    targets = [
        (mate, 1 - c, other % 2, c),
        (me.at(x=flip_x, c=0), 0, flip_x % 2, 2 + c),
        (me.at(y=flip_y, c=1), 1, flip_y % 2, 2 + c),
    ]
    factor = []
    for i, (device, role, parity, slot) in enumerate(targets):
        a, b = jnp.where(role == 0, 0, parity), role * 2 + parity
        factor.append(remote(left_ref.at[a], slot_a(slot), fs.at[i, 0], fr.at[slot, 0], device))
        factor.append(remote(right_ref.at[b], slot_b(slot), fs.at[i, 1], fr.at[slot, 1], device))
    own = [
        pltpu.make_async_copy(left_ref.at[jnp.where(is0, 0, lo)], slot_a(c), os.at[0]),
        pltpu.make_async_copy(right_ref.at[c * 2 + lo], slot_b(c), os.at[1]),
    ]
    for copy in own:
        copy.start()
    rows_s = half.shape[0]
    small = [remote(small_ref.at[pl.ds((1 - c) * rows_s, rows_s)], half, ss.at[0], sr.at[0], mate)]
    small_dims = [
        (n, me.x, lambda q: me.at(x=q)),
        (n, me.y, lambda q: me.at(y=q)),
        (me.nz, me.z, lambda q: me.at(z=q)),
    ]
    small_wait = [small[0]]
    small_slot = [1]

    def small_step(step):
        for copy in small_wait:
            copy.wait_recv()
        small_wait.clear()
        if step == 0:
            total = small_ref[pl.ds(c * rows_s, rows_s)] + half[...]
        elif step <= 3:
            total = small_got[step - 1, 0]
            for k in range(1, small_dims[step - 1][0]):
                total = total + small_got[step - 1, k]
        if step < 3:
            count, index, peer = small_dims[step]
            small_half[step] = total
            small_got[step, index] = total
            for k in range(1, count):
                small_wait.append(
                    remote(
                        small_half.at[step], small_got.at[step, index], ss.at[small_slot[0]],
                        sr.at[small_slot[0]], peer((index + k) % count),
                    )
                )
                small_slot[0] += 1
        elif step == 3:
            small_out[pl.ds(c * rows_s, rows_s)] = total
            block = small_out.at[pl.ds(c * rows_s, rows_s)]
            small_wait.append(
                remote(block, block, ss.at[small_slot[0]], sr.at[small_slot[0]], mate)
            )
        small.extend(small_wait)

    for where in (1 - c, 2, 3):
        for i, (src, dst) in enumerate(((left_ref, slot_a(where)), (right_ref, slot_b(where)))):
            pltpu.make_async_remote_copy(
                src_ref=src.at[0], dst_ref=dst, send_sem=fs.at[0, i], recv_sem=fr.at[where, i],
                device_id=mate, device_id_type=MESH,
            ).wait_recv()
    for copy in own:
        copy.wait()

    rows_k = total_rows // pieces
    matrix = c * 2 + lo
    pending, written = {}, []

    def multiply(k):
        acc[k] = lax.dot_general(
            buf_a[:, k * rows_k : (k + 1) * rows_k], buf_b[...], (((0,), (0,)), ((), ())),
            preferred_element_type=jnp.float32,
        )
        push(k, 0, rows_k)

    def push(k, at, rows):
        level = levels[at]
        count, index, peer = dims[level]
        size = rows // count
        copies = []
        for s in range(1, count):
            to = (index + s) % count
            parts[level][k, s - 1] = acc[k, pl.ds(pl.multiple_of(to * size, 8), size), :].astype(jnp.bfloat16)
            copies.append(
                remote(
                    parts[level].at[k, s - 1], gots[level].at[k, s - 1],
                    ps.at[level, k, s - 1], pr.at[level, k, s - 1], peer(to),
                )
            )
        pending["push", at, k] = copies

    def rows_at(at):
        rows = rows_k
        for i in range(at):
            rows //= dims[levels[i]][0]
        return rows

    def add(k, at):
        level = levels[at]
        count, index, _ = dims[level]
        size = rows_at(at) // count
        for copy in pending["push", at, k]:
            copy.wait_recv()
        total = acc[k, pl.ds(pl.multiple_of(index * size, 8), size), :]
        for s in range(1, count):
            total = total + gots[level][k, s - 1].astype(jnp.float32)
        if at + 1 < len(levels):
            acc[k, :size, :] = total
            push(k, at + 1, size)
        else:
            out[matrix, pl.ds(offset(k, at), size), :] = total.astype(jnp.bfloat16)
            share(k, at)

    def offset(k, at):
        start, rows = k * rows_k, rows_k
        for i in range(at + 1):
            count, index, _ = dims[levels[i]]
            rows //= count
            start = start + index * rows
        return pl.multiple_of(start, 8)

    def share(k, at):
        level = levels[at]
        count, index, peer = dims[level]
        size = rows_at(at) // count
        block = out.at[matrix, pl.ds(offset(k, at), size), :]
        pending["share", at, k] = [
            remote(block, block, gs.at[level, k, s - 1], gr.at[level, k, s - 1], peer((index + s) % count))
            for s in range(1, count)
        ]

    def shared(k, at):
        for copy in pending["share", at, k]:
            copy.wait_recv()
        if at:
            share(k, at - 1)
        else:
            block = out.at[matrix, pl.ds(k * rows_k, rows_k), :]
            pending["mate", k] = remote(
                block, block, ms.at[k], mr.at[k], along(pair + 1 - 2 * lo, other)
            )

    def across(k):
        pending["mate", k].wait_recv()
        block = out.at[pl.ds(2 * c, 2), pl.ds(k * rows_k, rows_k), :]
        pending["core", k] = remote(block, block, cs.at[k], cr.at[k], mate)
        write(k, c)

    def write(k, core):
        part = pl.ds(2 * core, 2), pl.ds(k * rows_k, rows_k), slice(None)
        written.append(pltpu.make_async_copy(out.at[part], out_hbm.at[part], sem_out.at[core, k]))
        written[-1].start()

    def close(k):
        pending["core", k].wait_recv()
        write(k, 1 - c)

    steps = [multiply]
    steps += [functools.partial(add, at=i) for i in range(len(levels))]
    steps += [functools.partial(shared, at=i) for i in reversed(range(len(levels)))]
    events = sorted((0 if p == 0 else p + k, p, k) for p in range(len(steps)) for k in range(pieces))
    before = 0
    for t, p, k in events:
        if before < t <= 5:
            small_step(t - 1)
        before = t
        steps[p](k)
    for k in range(pieces):
        across(k)
    for k in range(pieces):
        close(k)
    for copy in factor + small:
        copy.wait_send()
    for copies in pending.values():
        for copy in copies if isinstance(copies, list) else [copies]:
            copy.wait_send()
    for copy in written:
        copy.wait()


def reduce_all(sizes, left, right, small, pieces=8):
    n_expert, n_dp = sizes
    nz = math.gcd(n_expert, 4)
    n = n_expert // nz
    nh = n // 2
    assert n == n_dp // 2
    seq, width = left.shape[1:]
    rows_k = width // pieces
    bf, f32 = jnp.bfloat16, jnp.float32
    rows_s = small.shape[0] // 2
    splits = [n, nh, 2, nz // 2]
    sizes_at = [rows_k // math.prod(splits[: i + 1]) for i in range(4)]
    counts = [max(q - 1, 1) for q in splits]
    most = max(counts)
    boxes = [pltpu.VMEM((pieces, q, s, width), bf) for q, s in zip(counts, sizes_at)]
    smalls = 2 * n + nz
    return pl.pallas_call(
        functools.partial(reduce_kernel, sizes, pieces),
        out_shape=(
            jax.ShapeDtypeStruct((4, width, width), bf),
            jax.ShapeDtypeStruct(small.shape, f32),
        ),
        in_specs=[VMEM] * 3,
        out_specs=(pl.BlockSpec(memory_space=pl.ANY), VMEM),
        scratch_shapes=[
            pltpu.VMEM((4, width, width), bf),
            DMA((2, pieces)),
            pltpu.VMEM((4 * seq, width), bf),
            pltpu.VMEM((4 * seq, width), bf),
            pltpu.VMEM((pieces, rows_k, width), f32),
            *boxes,
            *boxes,
            pltpu.VMEM((rows_s, width), f32),
            pltpu.VMEM((3, rows_s, width), f32),
            pltpu.VMEM((3, max(n, nz), rows_s, width), f32),
            DMA((3, 2)),
            DMA((4, 2)),
            DMA((2,)),
            DMA((4, pieces, most)),
            DMA((4, pieces, most)),
            DMA((4, pieces, most)),
            DMA((4, pieces, most)),
            DMA((pieces,)),
            DMA((pieces,)),
            DMA((pieces,)),
            DMA((pieces,)),
            DMA((smalls,)),
            DMA((smalls,)),
        ],
        name="reduce_all",
        compiler_params=pltpu.CompilerParams(
            collective_id=3, has_side_effects=True, vmem_limit_bytes=56 << 20
        ),
    )(left, right, small)


def rms_scale(values):
    return lax.rsqrt(jnp.mean(values * values, axis=-1, keepdims=True) + epsilon)


def bucket_hot(seq_len, buckets):
    position = jnp.arange(seq_len, dtype=jnp.int32)
    relative = position[None, :] - position[:, None]
    distance = jnp.abs(relative)
    far_bucket = jnp.full_like(distance, 8)
    for threshold in bucket_edges:
        far_bucket = far_bucket + (distance >= threshold).astype(jnp.int32)
    bucketed = jnp.where(distance < 8, distance, far_bucket) + 16 * (relative > 0).astype(jnp.int32)
    bucket_ids = jnp.arange(buckets, dtype=jnp.int32)
    return (bucketed[None, :, :] == bucket_ids[:, None, None]).astype(jnp.float32)


def dot32(pattern, left, right):
    return jnp.einsum(pattern, left, right, preferred_element_type=jnp.float32)


def shards(
    layer_in, routes, queue_slots, norm_attn, w_query, w_key, w_value, w_out, rel_table,
    norm_moe, router, w_gate, w_up, w_down, cotangent,
):
    bf, f32 = jnp.bfloat16, jnp.float32
    seq_len, width = layer_in.shape
    buckets, heads = rel_table.shape
    expert_count = router.shape[1]
    sizes = (lax.axis_size("expert"), lax.axis_size("dp"))
    n_expert, n_dp = sizes
    assert w_gate.shape[0] == 2 and expert_count == 2 * n_expert
    group_len = seq_len // MICRO
    capacity = (5 * group_len + 2 * expert_count - 1) // (2 * expert_count)
    split_heads = (seq_len, heads, width // heads)
    layer_rows = layer_in.astype(f32)
    inv_attn = rms_scale(layer_rows)
    normed_attn = layer_rows * inv_attn
    attn_in = (normed_attn * norm_attn).astype(bf)
    query_heads = dot32("sd,de->se", attn_in, w_query).astype(bf).reshape(split_heads)
    key_heads = dot32("sd,de->se", attn_in, w_key).astype(bf).reshape(split_heads)
    value_heads = dot32("sd,de->se", attn_in, w_value).astype(bf).reshape(split_heads)
    one_hot = bucket_hot(seq_len, buckets)
    bias = jnp.einsum("bij,bh->hij", one_hot, rel_table, precision=highest)
    scores = dot32("ihd,jhd->hij", query_heads, key_heads) + bias
    exponent = jnp.exp(scores - jnp.max(scores, axis=-1, keepdims=True))
    probs = exponent / jnp.sum(exponent, axis=-1, keepdims=True)
    probs_low = probs.astype(bf)
    context = dot32("hij,jhd->ihd", probs_low, value_heads).astype(bf).reshape(seq_len, width)
    residual = layer_rows + dot32("se,ed->sd", context, w_out)
    inv_moe = rms_scale(residual)
    normed_moe = residual * inv_moe
    moe_in = normed_moe * norm_moe
    logits = jnp.dot(moe_in, router, precision=highest)
    gate_prob = jax.nn.softmax(logits, axis=-1)
    expert_ids = jnp.arange(expert_count, dtype=jnp.int32)
    first_hot = (routes[:, 0:1] == expert_ids).astype(f32)
    second_hot = (routes[:, 1:2] == expert_ids).astype(f32)
    prob_first = jnp.sum(gate_prob * first_hot, axis=-1, keepdims=True)
    prob_second = jnp.sum(gate_prob * second_hot, axis=-1, keepdims=True)
    weight_first = prob_first / (prob_first + prob_second)
    weight_second = prob_second / (prob_first + prob_second)
    weights = jnp.concatenate([weight_first, weight_second], axis=1)

    info = jnp.concatenate([routes.T, queue_slots.T, jnp.zeros((4, seq_len), jnp.int32)])
    gate_t, up_t = jnp.swapaxes(w_gate, 1, 2), jnp.swapaxes(w_up, 1, 2)
    slots = n_dp // 2 * n_expert * 2 * MICRO * capacity
    if 2 * slots * width * 20 + 6 * w_gate.size < 52 << 20:
        back, rows_in, hidden, gate_grad, up_grad, grad_rows = experts(
            sizes, MICRO, capacity, info, moe_in.astype(bf), cotangent, weights, gate_t, up_t, w_down
        )
    else:
        rows_in, weight_in, grad_in = spread(
            sizes, MICRO, capacity, info, moe_in.astype(bf), cotangent, weights
        )
        blocks = rows_in.shape[:-1] + (-1,)
        rows_in, grad_in, weight_in = [
            a.reshape(2, -1, a.shape[-1]) for a in (rows_in, grad_in, weight_in)
        ]
        slot_weight = jnp.sum(weight_in[..., :3].astype(f32), axis=-1, keepdims=True)
        grad_rows = (slot_weight * grad_in.astype(f32)).astype(bf)
        gate_pre = dot32("jrd,jdf->jrf", rows_in, w_gate)
        up_pre = dot32("jrd,jdf->jrf", rows_in, w_up)
        hidden, active, lean = gated_terms(gate_pre, up_pre)
        hidden = hidden.astype(bf)
        partial_out = dot32("jrf,jfd->jrd", hidden, w_down).astype(bf)
        hidden_grad = dot32("jrd,jfd->jrf", grad_rows, w_down)
        gate_grad, up_grad = (hidden_grad * lean).astype(bf), (hidden_grad * active).astype(bf)
        rows_grad = dot32("jrf,jdf->jrd", gate_grad, w_gate) + dot32("jrf,jdf->jrd", up_grad, w_up)
        back = gather_back(sizes, partial_out.reshape(blocks), rows_grad.astype(bf).reshape(blocks))
    rows_in, hidden, gate_grad, up_grad, grad_rows = [
        a.reshape(2, -1, a.shape[-1]) for a in (rows_in, hidden, gate_grad, up_grad, grad_rows)
    ]
    back = back.reshape(2, -1, width)

    core = lax.axis_index("dp") % 2
    per_core = MICRO * capacity
    token = jnp.arange(seq_len, dtype=jnp.int32)[:, None]
    place = (routes % 2) * (n_expert * 2 * per_core) + (routes // 2) * (2 * per_core)
    place = place + core * per_core + (token // group_len) * capacity + queue_slots
    place = jnp.where(queue_slots >= 0, place, -1)
    slot_ids = jnp.arange(2 * n_expert * 2 * per_core, dtype=jnp.int32)
    select_first = (place[:, 0:1] == slot_ids).astype(bf)
    select_second = (place[:, 1:2] == slot_ids).astype(bf)
    picked_first = dot32("tp,pd->td", select_first, back[0])
    picked_second = dot32("tp,pd->td", select_second, back[0])
    moe = weight_first * picked_first + weight_second * picked_second
    layer_out = (residual + moe).astype(bf)
    cot_rows = cotangent.astype(f32)
    grad_weight_first = jnp.sum(cot_rows * picked_first, axis=-1, keepdims=True)
    grad_weight_second = jnp.sum(cot_rows * picked_second, axis=-1, keepdims=True)
    grad_from_slots = dot32("tp,pd->td", select_first + select_second, back[1])
    mean_grad = weight_first * grad_weight_first + weight_second * grad_weight_second
    logit_first = weight_first * (grad_weight_first - mean_grad)
    logit_second = weight_second * (grad_weight_second - mean_grad)
    grad_logits = logit_first * first_hot + logit_second * second_hot
    grad_router = jnp.einsum("sd,se->ed", moe_in, grad_logits, precision=highest)
    grad_moe_in = grad_from_slots + jnp.einsum("se,de->sd", grad_logits, router, precision=highest)
    grad_norm_moe = jnp.sum(grad_moe_in * normed_moe, axis=0)
    grad_normed = grad_moe_in * norm_moe
    grad_residual = cot_rows + inv_moe * (
        grad_normed - normed_moe * jnp.mean(grad_normed * normed_moe, axis=-1, keepdims=True)
    )
    grad_attn_low = grad_residual.astype(bf)
    grad_context = dot32("sd,ed->se", grad_attn_low, w_out).astype(bf).reshape(split_heads)
    grad_values = dot32("hij,ihd->jhd", probs_low, grad_context).astype(bf).reshape(seq_len, width)
    grad_probs = dot32("ihd,jhd->hij", grad_context, value_heads)
    grad_scores = probs * (grad_probs - jnp.sum(probs * grad_probs, axis=-1, keepdims=True))
    grad_rel_table = jnp.einsum("bij,hij->bh", one_hot, grad_scores, precision=highest)
    scores_low = grad_scores.astype(bf)
    grad_queries = dot32("hij,jhd->ihd", scores_low, key_heads).astype(bf).reshape(seq_len, width)
    grad_keys = dot32("hij,ihd->jhd", scores_low, query_heads).astype(bf).reshape(seq_len, width)
    grad_attn_in = dot32("se,de->sd", grad_queries, w_query)
    grad_attn_in = grad_attn_in + dot32("se,de->sd", grad_keys, w_key)
    grad_attn_in = grad_attn_in + dot32("se,de->sd", grad_values, w_value)
    grad_norm_attn = jnp.sum(grad_attn_in * normed_attn, axis=0)
    grad_normed_attn = grad_attn_in * norm_attn
    grad_input = grad_residual + inv_attn * (
        grad_normed_attn
        - normed_attn * jnp.mean(grad_normed_attn * normed_attn, axis=-1, keepdims=True)
    )
    table = grad_rel_table.reshape(-1)
    small = jnp.concatenate(
        [
            grad_router,
            grad_norm_attn[None],
            grad_norm_moe[None],
            jnp.pad(table, (0, width - table.size))[None],
        ]
    )
    small = jnp.pad(small, ((0, -small.shape[0] % 16), (0, 0)))
    sums, small = reduce_all(
        sizes,
        jnp.stack([attn_in, context]),
        jnp.stack([grad_queries, grad_keys, grad_values, grad_attn_low]),
        small,
    )
    *matrices, grad_w_gate, grad_w_up, grad_w_down = finish(
        sums, rows_in, hidden, gate_grad, up_grad, grad_rows
    )
    grad_w_gate, grad_w_up = jnp.swapaxes(grad_w_gate, 1, 2), jnp.swapaxes(grad_w_up, 1, 2)
    return (
        layer_out, grad_input, small[expert_count], *matrices,
        small[expert_count + 2, : table.size].reshape(buckets, heads),
        small[expert_count + 1], small[:expert_count].T, grad_w_gate, grad_w_up, grad_w_down,
    )


def solution(mesh):
    in_specs = (
        P(("expert", "dp"), None),
        P(("expert", "dp"), None),
        P(("expert", "dp"), None),
        P(),
        P(),
        P(),
        P(),
        P(),
        P(),
        P(),
        P(),
        P("expert", None, "dp"),
        P("expert", None, "dp"),
        P("expert", "dp", None),
        P(("expert", "dp"), None),
    )
    out_specs = (
        P(("expert", "dp"), None),
        P(("expert", "dp"), None),
        P(),
        P(),
        P(),
        P(),
        P(),
        P(),
        P(),
        P(),
        P("expert", None, "dp"),
        P("expert", None, "dp"),
        P("expert", "dp", None),
    )
    return jax.shard_map(shards, mesh=mesh, in_specs=in_specs, out_specs=out_specs, check_vma=False)
```

```python
import functools
import math

import jax
import jax.numpy as jnp
from jax import lax
from jax.experimental import pallas as pl
from jax.experimental.pallas import tpu as pltpu
from jax.sharding import PartitionSpec as P

MICRO = 4

epsilon = 1e-06
bucket_edges = (12, 16, 23, 32, 46, 64, 91)
highest = lax.Precision.HIGHEST

MESH = pl.DeviceIdType.MESH
VMEM = pl.BlockSpec(memory_space=pltpu.VMEM)
DMA = pltpu.SemaphoreType.DMA


class Place:
    def __init__(self, n_expert, n_dp):
        self.n_expert, self.n_dp = n_expert, n_dp
        self.nz = math.gcd(n_expert, 4)
        self.nx = n_expert // self.nz
        self.ny = n_dp // 2
        self.e = lax.axis_index("expert")
        self.d = lax.axis_index("dp")
        self.z, self.x = self.e // self.nx, self.e % self.nx
        self.y, self.c = self.d // 2, self.d % 2

    def at(self, z=None, x=None, y=None, c=None, e=None):
        z = self.z if z is None else z
        x = self.x if x is None else x
        y = self.y if y is None else y
        c = self.c if c is None else c
        e = z * self.nx + x if e is None else e
        return (e, y * 2 + c)


def remote(src, dst, send, recv, device):
    copy = pltpu.make_async_remote_copy(
        src_ref=src, dst_ref=dst, send_sem=send, recv_sem=recv, device_id=device, device_id_type=MESH
    )
    copy.start()
    return copy


def greet(devices):
    barrier = pltpu.get_barrier_semaphore()
    for device in devices:
        pl.semaphore_signal(barrier, inc=1, device_id=device, device_id_type=MESH)
    pl.semaphore_wait(barrier, len(devices))


def column_peers(me):
    out = [me.at(c=1 - me.c)]
    out += [me.at(y=(me.y + k) % me.ny) for k in range(1, me.ny)]
    out += [me.at(e=(me.e + k) % me.n_expert) for k in range(1, me.n_expert)]
    return out


class Spread:
    def __init__(self, me, rows, recv, sems):
        self.me, self.rows, self.recv = me, rows, recv
        self.se, self.re, self.sy, self.ry, self.sc, self.rc = sems
        self.came, self.along, self.crossed = {}, {}, {}

    def send(self):
        me = self.me
        for k in range(1, me.n_expert):
            to = (me.e + k) % me.n_expert
            self.came[k] = remote(
                self.rows.at[to], self.recv.at[me.c, me.y * me.n_expert + me.e],
                self.se.at[k], self.re.at[k], me.at(e=to),
            )
        self.recv[me.c, me.y * me.n_expert + me.e] = self.rows[me.e]

    def pass_on(self, blocks):
        me = self.me
        for k in blocks:
            if k:
                self.came[k].wait_recv()
            src = (me.e - k + me.n_expert) % me.n_expert
            block = self.recv.at[me.c, me.y * me.n_expert + src]
            for s in range(1, me.ny):
                self.along[s, k] = remote(
                    block, block, self.sy.at[s - 1, k], self.ry.at[s - 1, k], me.at(y=(me.y + s) % me.ny)
                )

    def pass_column(self):
        me = self.me
        for k in range(1, me.n_expert):
            self.came[k].wait_recv()
        block = self.recv.at[me.c, pl.ds(me.y * me.n_expert, me.n_expert)]
        for s in range(1, me.ny):
            self.along[s, 0] = remote(
                block, block, self.sy.at[s - 1, 0], self.ry.at[s - 1, 0], me.at(y=(me.y + s) % me.ny)
            )

    def cross(self, s):
        me = self.me
        if s:
            for key, copy in self.along.items():
                if key[0] == s:
                    copy.wait_recv()
        block = self.recv.at[me.c, pl.ds((me.y - s + me.ny) % me.ny * me.n_expert, me.n_expert)]
        self.crossed[s] = remote(block, block, self.sc.at[s], self.rc.at[s], me.at(c=1 - me.c))

    def arrive(self):
        for copy in self.crossed.values():
            copy.wait_recv()

    def close(self):
        for copies in (self.came, self.along, self.crossed):
            for copy in copies.values():
                copy.wait_send()


def spread_sems(sizes):
    n_expert, ny = sizes[0], sizes[1] // 2
    most = max(ny - 1, 1)
    return [
        DMA((3, n_expert)), DMA((3, n_expert)), DMA((3, most, n_expert)), DMA((3, most, n_expert)),
        DMA((3, ny)), DMA((3, ny)),
    ]


class Rows:
    def __init__(self, me, rows_per, info_all, gates, tok, send, recv):
        self.me, self.rows_per, self.info_all, self.gates, self.tok = me, rows_per, info_all, gates, tok
        self.send, self.recv, self.copies = send, recv, {}
        self.seq = tok.shape[2]

    def share(self, i, ref):
        block = ref.at[self.me.c]
        mate = self.me.at(c=1 - self.me.c)
        self.copies[i] = remote(block, block, self.send.at[i], self.recv.at[i], mate)

    def hots(self):
        me, seq = self.me, self.seq
        micro, cap, per_core = self.rows_per
        self.copies["info"].wait_recv()
        row_ids = lax.broadcasted_iota(jnp.int32, (me.n_expert * 2 * per_core, seq), 0)
        group = lax.broadcasted_iota(jnp.int32, (1, seq), 1) // (seq // micro)
        self.each = []
        for cc in range(2):
            for k in range(2):
                route = self.info_all[cc, k : k + 1, :]
                slot = self.info_all[cc, 2 + k : 3 + k, :]
                target = (route // 2) * (2 * per_core) + cc * per_core + group * cap + slot
                target = jnp.where((slot >= 0) & (route % 2 == me.c), target, -1)
                self.each.append(jnp.where(row_ids == target, 1.0, 0.0))
        self.both = [(self.each[2 * cc] + self.each[2 * cc + 1]).astype(jnp.bfloat16) for cc in range(2)]

    def gather(self, i):
        self.copies[i].wait_recv()
        total = None
        for cc in range(2):
            term = jnp.dot(self.both[cc], self.tok[i, cc], preferred_element_type=jnp.float32)
            total = term if total is None else total + term
        return total.astype(jnp.bfloat16).reshape(self.me.n_expert, 2 * self.rows_per[2], -1)

    def weights(self):
        self.copies["gates"].wait_recv()
        size = 2 * self.rows_per[2]
        column = None
        for n, hot in enumerate(self.each):
            term = jnp.sum(hot * self.gates[n // 2, n % 2 : n % 2 + 1, :], axis=1, keepdims=True)
            column = term if column is None else column + term
        lane = lax.broadcasted_iota(jnp.int32, (size, 128), 1)
        row = lax.broadcasted_iota(jnp.int32, (size, 128), 0)
        tiles = []
        for e in range(self.me.n_expert):
            block = jnp.where(lane == row, column[e * size : (e + 1) * size, :], 0.0)
            tiles.append(jnp.broadcast_to(jnp.sum(block, axis=0, keepdims=True), (8, 128)))
        return tiles

    def close(self):
        for copy in self.copies.values():
            copy.wait_send()


NAMED = ("info", "gates", 0, 1)


class Named:
    def __init__(self, sems):
        self.at = {name: sems.at[i] for i, name in enumerate(NAMED)}


def rows_scratch(sizes, per_core, seq, width):
    mine = (sizes[0], 2 * per_core, width)
    bf = jnp.bfloat16
    return [
        pltpu.VMEM((2, 8, seq), jnp.int32),
        pltpu.VMEM((2, 8, seq), jnp.float32),
        pltpu.VMEM((2, 2, seq, width), bf),
        DMA((4,)),
        DMA((4,)),
        pltpu.VMEM(mine, bf),
        pltpu.VMEM((sizes[0], 8, 128), jnp.float32),
        pltpu.VMEM(mine, bf),
    ]


def rows_of(me, rows_per, scratch):
    info_all, gates, tok, send, recv = scratch[:5]
    return Rows(me, rows_per, info_all, gates, tok, Named(send), Named(recv))


def spread_kernel(sizes, rows_per, info_ref, moe_ref, cot_ref, w_ref, x_out, w_out, g_out, *scratch):
    me = Place(*sizes)
    c = me.c
    greet(column_peers(me))
    scratch, sems = scratch[:8], scratch[8:]
    rows = rows_of(me, rows_per, scratch)
    info_all, gates, tok = scratch[:3]
    info_all[c] = info_ref[...]
    rows.share("info", info_all)
    gates[c] = w_ref[...]
    rows.share("gates", gates)
    for i, ref in enumerate((moe_ref, cot_ref)):
        tok[i, c] = ref[...]
        rows.share(i, tok.at[i])
    rows.hots()
    buf_x, buf_w, buf_g = scratch[5:]
    out_x, out_w, out_g = [
        Spread(me, buf, recv, [s.at[i] for s in sems])
        for i, (buf, recv) in enumerate(((buf_x, x_out), (buf_w, w_out), (buf_g, g_out)))
    ]
    for i, payload in enumerate((out_x, out_g)):
        payload.rows[...] = rows.gather(i)
        payload.send()
    for e, tile in enumerate(rows.weights()):
        buf_w[e] = tile
    out_w.send()
    for payload in (out_x, out_g):
        payload.pass_on(range(me.n_expert))
        payload.cross(0)
    out_w.pass_column()
    out_w.cross(0)
    for payload in (out_x, out_g, out_w):
        for s in range(1, me.ny):
            payload.cross(s)
    for payload in (out_x, out_g, out_w):
        payload.arrive()
        payload.close()
    rows.close()


def spread(sizes, micro, cap, info, moe, cot, weights):
    n_expert, ny, per_core = sizes[0], sizes[1] // 2, micro * cap
    seq, width = cot.shape
    block = (2, ny * n_expert, 2 * per_core)
    bf = jnp.bfloat16
    return pl.pallas_call(
        functools.partial(spread_kernel, sizes, (micro, cap, per_core)),
        out_shape=(
            jax.ShapeDtypeStruct(block + (width,), bf),
            jax.ShapeDtypeStruct(block[:2] + (8, 128), jnp.float32),
            jax.ShapeDtypeStruct(block + (width,), bf),
        ),
        in_specs=[VMEM] * 4,
        out_specs=(VMEM,) * 3,
        scratch_shapes=rows_scratch(sizes, per_core, seq, width) + spread_sems(sizes),
        name="spread",
        compiler_params=pltpu.CompilerParams(
            collective_id=1, has_side_effects=True, vmem_limit_bytes=48 << 20
        ),
    )(info, moe, cot, weights)


class Back:
    def __init__(self, me, away, own, q_out, r1, stage, r2, final, sems):
        self.me, self.away, self.own = me, away, own
        self.q_out, self.r1, self.stage, self.r2, self.final = q_out, r1, stage, r2, final
        self.sems = sems
        self.ys = [(me.y + k) % me.ny for k in range(me.ny)]
        self.order = list(range(1, me.n_expert)) + [0]
        self.first, self.second, self.third, self.fourth = {}, {}, {}, {}
        self.arrived = set()

    def to_mate(self, i, k):
        me = self.me
        column = pl.ds(self.ys[k] * me.n_expert, me.n_expert)
        self.first[i, k] = remote(
            self.away(i).at[column], self.r1.at[i, column], self.sems[0].at[i, k], self.sems[1].at[i, k],
            me.at(c=1 - me.c),
        )

    def partial(self, i, y, e):
        block = y * self.me.n_expert + e
        return self.own(i, block) + self.r1[i, block].astype(jnp.float32)

    def along_y(self, i):
        me = self.me
        for k in range(1, me.ny):
            self.first[i, k].wait_recv()
            for j in self.order:
                e = (me.e + j) % me.n_expert
                self.stage[i, k - 1, e] = self.partial(i, self.ys[k], e).astype(jnp.bfloat16)
                self.second[i, k, j] = remote(
                    self.stage.at[i, k - 1, e], self.r2.at[i, k - 1, e],
                    self.sems[2].at[i, k - 1, j], self.sems[3].at[i, k - 1, j], me.at(y=self.ys[k]),
                )

    def finish(self, i, order):
        me = self.me
        if (i, 0) not in self.arrived:
            self.arrived.add((i, 0))
            self.first[i, 0].wait_recv()
        for j in order:
            e = (me.e + j) % me.n_expert
            total = self.partial(i, me.y, e)
            for k in range(1, me.ny):
                self.second[i, k, j].wait_recv()
                total = total + self.r2[i, k - 1, e].astype(jnp.float32)
            if j:
                self.final[i, e] = total.astype(jnp.bfloat16)
                self.third[i, j] = remote(
                    self.final.at[i, e], self.q_out.at[i, me.c, me.e],
                    self.sems[4].at[i, j], self.sems[5].at[i, j], me.at(e=e),
                )
            else:
                self.q_out[i, me.c, me.e] = total.astype(jnp.bfloat16)

    def across(self, i):
        for j in self.order[:-1]:
            self.third[i, j].wait_recv()
        block = self.q_out.at[i, self.me.c]
        s, r = self.sems[6].at[i], self.sems[7].at[i]
        self.fourth[i] = remote(block, block, s, r, self.me.at(c=1 - self.me.c))

    def close(self):
        for copy in self.fourth.values():
            copy.wait()
        for copies in (self.first, self.second, self.third):
            for copy in copies.values():
                copy.wait_send()


def back_scratch(sizes, size, width):
    n_expert, ny = sizes[0], sizes[1] // 2
    most = max(ny - 1, 1)
    bf = jnp.bfloat16
    return [
        pltpu.VMEM((2, ny * n_expert, size, width), bf),
        pltpu.VMEM((2, most, n_expert, size, width), bf),
        pltpu.VMEM((2, most, n_expert, size, width), bf),
        pltpu.VMEM((2, n_expert, size, width), bf),
        DMA((2, ny)),
        DMA((2, ny)),
        DMA((2, most, n_expert)),
        DMA((2, most, n_expert)),
        DMA((2, n_expert)),
        DMA((2, n_expert)),
        DMA((2,)),
        DMA((2,)),
    ]


def gather_back_kernel(sizes, p0_ref, p1_ref, q_out, *scratch):
    me = Place(*sizes)
    greet(column_peers(me))
    p_refs = (p0_ref, p1_ref)
    back = Back(
        me, lambda i: p_refs[i].at[1 - me.c],
        lambda i, block: p_refs[i][me.c, block].astype(jnp.float32), q_out, *scratch[:4], scratch[4:],
    )
    for i in range(2):
        for k in reversed(range(me.ny)):
            back.to_mate(i, k)
    for i in range(2):
        back.along_y(i)
    for i in range(2):
        back.finish(i, back.order)
        back.across(i)
    back.close()


def gather_back(sizes, first, second):
    n_expert = sizes[0]
    _, _, size, width = first.shape
    return pl.pallas_call(
        functools.partial(gather_back_kernel, sizes),
        out_shape=jax.ShapeDtypeStruct((2, 2, n_expert, size, width), jnp.bfloat16),
        in_specs=[VMEM] * 2,
        out_specs=VMEM,
        scratch_shapes=back_scratch(sizes, size, width),
        name="gather_back",
        compiler_params=pltpu.CompilerParams(
            collective_id=2, has_side_effects=True, vmem_limit_bytes=48 << 20
        ),
    )(first, second)


def gated_terms(gate_pre, up_pre):
    root = math.sqrt(2.0 / math.pi)
    square = gate_pre * gate_pre
    bend = jnp.tanh(root * (gate_pre + 0.044715 * square * gate_pre))
    half = 0.5 * (1.0 + bend)
    active = gate_pre * half
    slope = half + 0.5 * gate_pre * (1.0 - bend * bend) * root * (1.0 + 3 * 0.044715 * square)
    return active * up_pre, active, up_pre * slope


def bucket_of(relative):
    distance = jnp.abs(relative)
    far_bucket = jnp.full_like(distance, 8)
    for threshold in bucket_edges:
        far_bucket = far_bucket + (distance >= threshold).astype(jnp.int32)
    return jnp.where(distance < 8, distance, far_bucket) + 16 * (relative > 0).astype(jnp.int32)


def row_scale(values):
    return lax.rsqrt(jnp.mean(values * values, axis=-1, keepdims=True) + epsilon)


def dot_as(left, right, contract):
    return lax.dot_general(left, right, (contract, ((), ())), preferred_element_type=jnp.float32)


NN, NT, TN = ((1,), (0,)), ((1,), (1,)), ((0,), (0,))


def layer_kernel(
    sizes, rows_per, layer_in, norm_attn, norm_moe, table_t, router_t, info_ref, cot_ref,
    wq_hbm, wk_hbm, wv_hbm, wo_hbm, wg_hbm, wu_hbm, wd_hbm,
    q_out, x_ref, hid_out, dg_out, du_out, gr_out, query, key, value, probs, context, residual, attn_in, gate_out,
    g_ref, w_ref, weights, act, slope, away, own, sem_a, sem_w, *scratch,
):
    me = Place(*sizes)
    c = me.c
    seq, width = layer_in.shape
    heads, buckets = table_t.shape
    units = wg_hbm.shape[1]
    bf, f32 = jnp.bfloat16, jnp.float32

    attn_w = []
    for i, src in enumerate((wq_hbm, wk_hbm, wv_hbm, wo_hbm)):
        dst = weights.at[pl.ds(i * width, width)]
        attn_w.append(pltpu.make_async_copy(src, dst, sem_a.at[i]))
        attn_w[-1].start()
    greet(column_peers(me))
    rows_in = rows_of(me, rows_per, scratch[:8])
    info_all, gates, tok = scratch[:3]
    buf_x, buf_w, buf_g = scratch[5:8]
    out_x, out_w, out_g = [
        Spread(me, buf, recv, [s.at[i] for s in scratch[8:14]])
        for i, (buf, recv) in enumerate(((buf_x, x_ref), (buf_w, w_ref), (buf_g, g_ref)))
    ]
    scratch = scratch[14:]
    column = me.n_expert
    quarter = [range(i * column // 4, (i + 1) * column // 4) for i in range(4)]
    info_all[c] = info_ref[...]
    rows_in.share("info", info_all)
    tok[1, c] = cot_ref[...]
    rows_in.share(1, tok.at[1])
    rows = layer_in[...].astype(f32)
    attn_in[...] = (rows * row_scale(rows) * norm_attn[...]).astype(bf)
    rows_in.hots()
    buf_g[...] = rows_in.gather(1)
    out_g.send()
    for i, ref in enumerate((query, key, value)):
        attn_w[i].wait()
        ref[...] = dot_as(attn_in[...], weights[i * width : (i + 1) * width, :], NN).astype(bf)
    relative = lax.broadcasted_iota(jnp.int32, (heads, 2 * seq), 1) - seq
    bucket = bucket_of(relative)
    bias_of = jnp.zeros((heads, 2 * seq), f32)
    for n in range(buckets):
        bias_of = jnp.where(bucket == n, table_t[:, n : n + 1], bias_of)
    pair = 2 * width // heads
    low_half = lax.broadcasted_iota(jnp.int32, (seq, pair), 1) < pair // 2
    for n in range(heads // 2):
        lanes = slice(n * pair, (n + 1) * pair)
        k2, v2 = key[:, lanes], value[:, lanes]
        total = None
        for h in range(2):
            mine = low_half if h == 0 else ~low_half
            head = 2 * n + h
            line = jnp.broadcast_to(bias_of[head : head + 1, :], (seq, 2 * seq))
            bias = pltpu.roll(line, seq, 1, stride=1, stride_axis=0)[:, :seq]
            scores = dot_as(query[:, lanes], jnp.where(mine, k2, jnp.zeros_like(k2)), NT) + bias
            exponent = jnp.exp(scores - jnp.max(scores, axis=-1, keepdims=True))
            prob = exponent / jnp.sum(exponent, axis=-1, keepdims=True)
            probs[head] = prob
            term = dot_as(prob.astype(bf), jnp.where(mine, v2, jnp.zeros_like(v2)), NN)
            total = term if total is None else total + term
        context[:, lanes] = total.astype(bf)
        if n % 4 == 3:
            out_g.pass_on(quarter[n // 4])
    attn_w[3].wait()
    resid = rows + dot_as(context[...], weights[3 * width : 4 * width, :], NN)
    residual[...] = resid
    fetch = {}
    for n, j in enumerate((c, 1 - c)):
        for i, src in enumerate((wg_hbm, wu_hbm, wd_hbm)):
            dst = weights.at[pl.ds(pl.multiple_of((2 * i + j) * units, 16), units)]
            fetch[n, i] = pltpu.make_async_copy(src.at[j], dst, sem_w.at[n, i])
            fetch[n, i].start()
    moe_in = resid * row_scale(resid) * norm_moe[...]
    tok[0, c] = moe_in.astype(bf)
    rows_in.share(0, tok.at[0])
    logits = lax.dot_general(
        router_t[...], moe_in, (NT, ((), ())), preferred_element_type=f32, precision=highest
    )
    logits = jnp.exp(logits - jnp.max(logits, axis=0, keepdims=True))
    gate_prob = logits / jnp.sum(logits, axis=0, keepdims=True)
    expert_ids = lax.broadcasted_iota(jnp.int32, gate_prob.shape, 0)
    picked = [
        jnp.sum(jnp.where(info_ref[k : k + 1, :] == expert_ids, gate_prob, 0.0), axis=0, keepdims=True)
        for k in range(2)
    ]
    both = picked[0] + picked[1]
    for k in range(2):
        gates[c, k : k + 1, :] = picked[k] / both
    gates[c, 2:, :] = jnp.zeros((6, seq), f32)
    gate_out[...] = gates[c]
    rows_in.share("gates", gates)
    buf_x[...] = rows_in.gather(0)
    out_x.send()
    out_g.pass_on(quarter[2])
    for e, tile in enumerate(rows_in.weights()):
        buf_w[e] = tile
    out_w.send()
    out_g.pass_on(quarter[3])
    out_g.cross(0)

    size = x_ref.shape[2]
    step = math.gcd(column, 4)
    chunk = step * size
    back = Back(
        me, lambda i: away.at[i],
        lambda i, block: own[i, pl.ds(pl.multiple_of(block * size, 8), size), :],
        q_out, *scratch[:4], scratch[4:],
    )

    def part(i, j):
        return weights[pl.ds(pl.multiple_of((2 * i + j) * units, 16), units), :]

    def flat(value):
        return value.reshape(chunk, value.shape[-1])

    def blocks(value):
        return value.reshape(step, size, value.shape[-1])

    def store(i, first, some, rows, value):
        if first:
            away[i, some] = blocks(value.astype(bf))
        else:
            own[i, rows, :] = value

    def each(start, count, body):
        @pl.loop(0, count // step)
        def _(n):
            at = start + n * step
            body(pl.ds(at, step), pl.ds(pl.multiple_of(at * size, 8), chunk))

    def forward(first, j, start, count):
        def body(some, rows):
            x = flat(x_ref[j, some])
            gate_pre = dot_as(x, part(0, j), NT)
            up_pre = dot_as(x, part(1, j), NT)
            hidden, active, lean = gated_terms(gate_pre, up_pre)
            act[j, rows, :] = active
            slope[j, rows, :] = lean
            hidden = hidden.astype(bf)
            hid_out[j, some] = blocks(hidden)
            store(0, first, some, rows, dot_as(hidden, part(2, j), NN))

        each(start, count, body)

    lane = lax.broadcasted_iota(jnp.int32, (size, 128), 1)
    row = lax.broadcasted_iota(jnp.int32, (size, 128), 0)

    def backward(first, j, start, count):
        def body(some, rows):
            tiles = w_ref[j, some]
            grad = []
            for n in range(step):
                line = jnp.broadcast_to(tiles[n, 0:1, :], (size, 128))
                weight = jnp.sum(jnp.where(lane == row, line, 0.0), axis=1, keepdims=True)
                grad.append(weight * g_ref[j, some.start + n].astype(f32))
            grad = jnp.concatenate(grad, axis=0).astype(bf)
            gr_out[j, some] = blocks(grad)
            grad_hidden = dot_as(grad, part(2, j), NT)
            dg = (grad_hidden * slope[j, rows, :]).astype(bf)
            du = (grad_hidden * act[j, rows, :]).astype(bf)
            dg_out[j, some] = blocks(dg)
            du_out[j, some] = blocks(du)
            store(1, first, some, rows, dot_as(dg, part(0, j), NN) + dot_as(du, part(1, j), NN))

        each(start, count, body)

    here = me.y * column
    away_ys = [back.ys[k] * column for k in range(1, me.ny)]
    shares = [back.order[i * column // 4 : (i + 1) * column // 4] for i in range(4)]
    out_x.pass_on(range(column))
    out_x.cross(0)
    for s in range(1, me.ny):
        out_g.cross(s)
    for i in range(3):
        fetch[0, i].wait()
    forward(False, c, here, column)
    for i in range(3):
        fetch[1, i].wait()
    out_x.crossed[0].wait_recv()
    forward(True, 1 - c, here, column)
    back.to_mate(0, 0)
    out_w.pass_column()
    out_w.cross(0)
    for s in range(1, me.ny):
        out_x.cross(s)
    for k in range(1, me.ny):
        out_x.crossed[k].wait_recv()
        forward(True, 1 - c, away_ys[k - 1], column)
        back.to_mate(0, k)
    for s in range(1, me.ny):
        out_w.cross(s)
    for k in range(1, me.ny):
        forward(False, c, away_ys[k - 1], column)
    back.along_y(0)
    out_g.arrive()
    out_w.arrive()
    for k in range(1, me.ny):
        backward(True, 1 - c, away_ys[k - 1], column)
        back.to_mate(1, k)
    back.finish(0, shares[0])
    for k in range(1, me.ny):
        backward(False, c, away_ys[k - 1], column)
    back.along_y(1)
    back.finish(0, shares[1])
    backward(True, 1 - c, here, column)
    back.to_mate(1, 0)
    back.finish(0, shares[2])
    backward(False, c, here, column)
    back.finish(0, shares[3])
    back.across(0)
    back.finish(1, back.order)
    back.across(1)
    back.close()
    for payload in (out_x, out_w, out_g):
        payload.close()
    rows_in.close()


def layer(sizes, micro, cap, layer_in, norms, table_t, router_t, info, cot, attn_w, expert_w):
    n_expert, ny, per_core = sizes[0], sizes[1] // 2, micro * cap
    seq, width = cot.shape
    units = expert_w[0].shape[1]
    heads = table_t.shape[0]
    count, size = ny * n_expert, 2 * per_core
    bf, f32 = jnp.bfloat16, jnp.float32
    any_space = pl.BlockSpec(memory_space=pl.ANY)
    inner = jax.ShapeDtypeStruct((2, count, size, units), bf)
    outer = jax.ShapeDtypeStruct((2, count, size, width), bf)
    low, full = jax.ShapeDtypeStruct((seq, width), bf), jax.ShapeDtypeStruct((seq, width), f32)
    return pl.pallas_call(
        functools.partial(layer_kernel, sizes, (micro, cap, per_core)),
        out_shape=(
            jax.ShapeDtypeStruct((2, 2, n_expert, size, width), bf), outer, inner, inner, inner, outer,
            low, low, low, jax.ShapeDtypeStruct((heads, seq, seq), f32), low, full, low,
            jax.ShapeDtypeStruct((8, seq), f32),
        ),
        in_specs=[VMEM] * 7 + [any_space] * 7,
        out_specs=(VMEM,) * 14,
        scratch_shapes=[
            pltpu.VMEM((2, count, size, width), bf),
            pltpu.VMEM((2, count, 8, 128), f32),
            pltpu.VMEM((max(4 * width, 6 * units), width), bf),
            pltpu.VMEM((2, count * size, units), f32),
            pltpu.VMEM((2, count * size, units), f32),
            pltpu.VMEM((2, count, size, width), bf),
            pltpu.VMEM((2, count * size, width), f32),
            DMA((4,)),
            DMA((2, 3)),
        ]
        + rows_scratch(sizes, per_core, seq, width)
        + spread_sems(sizes)
        + back_scratch(sizes, size, width),
        name="layer",
        compiler_params=pltpu.CompilerParams(
            collective_id=4, has_side_effects=True, vmem_limit_bytes=54 << 20
        ),
    )(layer_in, *norms, table_t, router_t, info, cot, *attn_w, *expert_w)


def finish_kernel(sums_hbm, x_hbm, h_hbm, dg_hbm, du_hbm, gr_hbm, *refs):
    outs, (sums, x, h, dg, du, gr, stage, sem_sum, sem_in, sem_out) = refs[:7], refs[7:]
    slots, rows = stage.shape[:2]
    width = sums.shape[1]
    units = h.shape[2]
    loads = {}

    def load(key, src, dst, sem):
        loads[key] = pltpu.make_async_copy(src, dst, sem)
        loads[key].start()

    def load_sums(keys):
        for n in keys:
            part = n * rows // width, pl.ds(n * rows % width, rows)
            load(("sums", n), sums_hbm.at[part], sums.at[part], sem_sum.at[n])

    casts = range(4 * width // rows)
    load_sums(casts[:4])
    for i, (key, src, dst) in enumerate(
        (("dg", dg_hbm, dg), ("x", x_hbm, x), ("du", du_hbm, du), ("h", h_hbm, h), ("gr", gr_hbm, gr))
    ):
        for j in range(2):
            load((key, j), src.at[j], dst.at[j], sem_in.at[i, j])
    load_sums(casts[4:])

    def need(key):
        if key in loads:
            loads.pop(key).wait()

    jobs = []
    products = [
        (left, right, out, j, f)
        for left, right, out in ((("dg", dg), ("x", x), 4), (("du", du), ("x", x), 5), (("h", h), ("gr", gr), 6))
        for j in range(2)
        for f in range(0, units, rows)
    ]
    casts = list(casts)
    while casts or products:
        if casts:
            jobs.append(casts.pop(0))
        if products and (len(jobs) > 3 or not casts):
            jobs.append(products.pop(0))
    flying = [None] * slots
    for n, job in enumerate(jobs):
        slot = n % slots
        if flying[slot] is not None:
            flying[slot].wait()
        if isinstance(job, int):
            need(("sums", job))
            m, r = job * rows // width, job * rows % width
            stage[slot] = sums[m, r : r + rows, :].astype(jnp.float32)
            src, dst = stage.at[slot], outs[m].at[pl.ds(r, rows)]
        else:
            (left_key, left), (right_key, right), out, j, f = job
            need((left_key, j))
            need((right_key, j))
            size = min(rows, units - f)
            stage[slot, :size] = lax.dot_general(
                left[j, :, f : f + size], right[j], (((0,), (0,)), ((), ())),
                preferred_element_type=jnp.float32,
            )
            src, dst = stage.at[slot, pl.ds(0, size)], outs[out].at[j, pl.ds(f, size)]
        flying[slot] = pltpu.make_async_copy(src, dst, sem_out.at[slot])
        flying[slot].start()
    for copy in flying:
        if copy is not None:
            copy.wait()


def finish(sums, x, h, dg, du, gr):
    f32 = jnp.float32
    width = sums.shape[1]
    units = h.shape[2]
    any_space = pl.BlockSpec(memory_space=pl.ANY)
    return pl.pallas_call(
        finish_kernel,
        out_shape=(jax.ShapeDtypeStruct((width, width), f32),) * 4
        + (jax.ShapeDtypeStruct((2, units, width), f32),) * 3,
        in_specs=[any_space] * 6,
        out_specs=(any_space,) * 7,
        scratch_shapes=[pltpu.VMEM(a.shape, a.dtype) for a in (sums, x, h, dg, du, gr)]
        + [pltpu.VMEM((6, 256, width), f32), DMA((4 * width // 256,)), DMA((5, 2)), DMA((6,))],
        name="finish",
        compiler_params=pltpu.CompilerParams(vmem_limit_bytes=60 << 20),
    )(sums, x, h, dg, du, gr)


def reduce_kernel(
    sizes, pieces, left_ref, right_ref, small_ref, out_hbm, small_out,
    out, sem_out, buf_a, buf_b, acc, *boxes,
):
    me = Place(*sizes)
    c, mate = me.c, me.at(c=1 - me.c)
    n = me.nx
    seq = right_ref.shape[1]
    total_rows = out.shape[1]
    is0 = c == 0
    pair = jnp.where(is0, me.x, me.y)
    other = jnp.where(is0, me.y, me.x)
    lo, hi, nh = pair % 2, pair // 2, n // 2

    def along(pair_at, other_at, z=None):
        return me.at(x=jnp.where(is0, pair_at, other_at), y=jnp.where(is0, other_at, pair_at), z=z)

    flip_x, flip_y = me.x + 1 - 2 * (me.x % 2), me.y + 1 - 2 * (me.y % 2)
    dims = [
        (n, other, lambda q: along(pair, q)),
        (nh, hi, lambda q: along(q * 2 + lo, other)),
        (2, me.z % 2, lambda q: me.at(z=me.z // 2 * 2 + q)),
        (me.nz // 2, me.z // 2, lambda q: me.at(z=q * 2 + me.z % 2)),
    ]
    parts, gots = boxes[:4], boxes[4:8]
    half, small_half, small_got, fs, fr, os, ps, pr, gs, gr, ms, mr, cs, cr, ss, sr = boxes[8:]
    levels = [i for i, d in enumerate(dims) if d[0] > 1]
    x_peers = [me.at(x=(me.x + k) % n) for k in range(1, n)]
    y_peers = [me.at(y=(me.y + k) % n) for k in range(1, n)]
    z_peers = [me.at(z=(me.z + k) % me.nz) for k in range(1, me.nz)]
    greet(
        [mate, me.at(x=flip_x, c=1 - c), me.at(y=flip_y, c=1 - c)] + x_peers + y_peers + z_peers
    )

    def slot_a(slot):
        return buf_a.at[pl.ds(pl.multiple_of(slot * seq, seq), seq), :]

    def slot_b(slot):
        return buf_b.at[pl.ds(pl.multiple_of(slot * seq, seq), seq), :]

    targets = [
        (mate, 1 - c, other % 2, c),
        (me.at(x=flip_x, c=0), 0, flip_x % 2, 2 + c),
        (me.at(y=flip_y, c=1), 1, flip_y % 2, 2 + c),
    ]
    factor = []
    for i, (device, role, parity, slot) in enumerate(targets):
        a, b = jnp.where(role == 0, 0, parity), role * 2 + parity
        factor.append(remote(left_ref.at[a], slot_a(slot), fs.at[i, 0], fr.at[slot, 0], device))
        factor.append(remote(right_ref.at[b], slot_b(slot), fs.at[i, 1], fr.at[slot, 1], device))
    own = [
        pltpu.make_async_copy(left_ref.at[jnp.where(is0, 0, lo)], slot_a(c), os.at[0]),
        pltpu.make_async_copy(right_ref.at[c * 2 + lo], slot_b(c), os.at[1]),
    ]
    for copy in own:
        copy.start()
    rows_s = half.shape[0]
    small = [remote(small_ref.at[pl.ds((1 - c) * rows_s, rows_s)], half, ss.at[0], sr.at[0], mate)]
    small_dims = [
        (n, me.x, lambda q: me.at(x=q)),
        (n, me.y, lambda q: me.at(y=q)),
        (me.nz, me.z, lambda q: me.at(z=q)),
    ]
    small_wait = [small[0]]
    small_slot = [1]

    def small_step(step):
        for copy in small_wait:
            copy.wait_recv()
        small_wait.clear()
        if step == 0:
            total = small_ref[pl.ds(c * rows_s, rows_s)] + half[...]
        elif step <= 3:
            total = small_got[step - 1, 0]
            for k in range(1, small_dims[step - 1][0]):
                total = total + small_got[step - 1, k]
        if step < 3:
            count, index, peer = small_dims[step]
            small_half[step] = total
            small_got[step, index] = total
            for k in range(1, count):
                small_wait.append(
                    remote(
                        small_half.at[step], small_got.at[step, index], ss.at[small_slot[0]],
                        sr.at[small_slot[0]], peer((index + k) % count),
                    )
                )
                small_slot[0] += 1
        elif step == 3:
            small_out[pl.ds(c * rows_s, rows_s)] = total
            block = small_out.at[pl.ds(c * rows_s, rows_s)]
            small_wait.append(
                remote(block, block, ss.at[small_slot[0]], sr.at[small_slot[0]], mate)
            )
        small.extend(small_wait)

    for where in (1 - c, 2, 3):
        for i, (src, dst) in enumerate(((left_ref, slot_a(where)), (right_ref, slot_b(where)))):
            pltpu.make_async_remote_copy(
                src_ref=src.at[0], dst_ref=dst, send_sem=fs.at[0, i], recv_sem=fr.at[where, i],
                device_id=mate, device_id_type=MESH,
            ).wait_recv()
    for copy in own:
        copy.wait()

    rows_k = total_rows // pieces
    matrix = c * 2 + lo
    pending, written = {}, []

    def multiply(k):
        acc[k] = lax.dot_general(
            buf_a[:, k * rows_k : (k + 1) * rows_k], buf_b[...], (((0,), (0,)), ((), ())),
            preferred_element_type=jnp.float32,
        )
        push(k, 0, rows_k)

    def push(k, at, rows):
        level = levels[at]
        count, index, peer = dims[level]
        size = rows // count
        copies = []
        for s in range(1, count):
            to = (index + s) % count
            parts[level][k, s - 1] = acc[k, pl.ds(pl.multiple_of(to * size, 8), size), :].astype(jnp.bfloat16)
            copies.append(
                remote(
                    parts[level].at[k, s - 1], gots[level].at[k, s - 1],
                    ps.at[level, k, s - 1], pr.at[level, k, s - 1], peer(to),
                )
            )
        pending["push", at, k] = copies

    def rows_at(at):
        rows = rows_k
        for i in range(at):
            rows //= dims[levels[i]][0]
        return rows

    def add(k, at):
        level = levels[at]
        count, index, _ = dims[level]
        size = rows_at(at) // count
        for copy in pending["push", at, k]:
            copy.wait_recv()
        total = acc[k, pl.ds(pl.multiple_of(index * size, 8), size), :]
        for s in range(1, count):
            total = total + gots[level][k, s - 1].astype(jnp.float32)
        if at + 1 < len(levels):
            acc[k, :size, :] = total
            push(k, at + 1, size)
        else:
            out[matrix, pl.ds(offset(k, at), size), :] = total.astype(jnp.bfloat16)
            share(k, at)

    def offset(k, at):
        start, rows = k * rows_k, rows_k
        for i in range(at + 1):
            count, index, _ = dims[levels[i]]
            rows //= count
            start = start + index * rows
        return pl.multiple_of(start, 8)

    def share(k, at):
        level = levels[at]
        count, index, peer = dims[level]
        size = rows_at(at) // count
        block = out.at[matrix, pl.ds(offset(k, at), size), :]
        pending["share", at, k] = [
            remote(block, block, gs.at[level, k, s - 1], gr.at[level, k, s - 1], peer((index + s) % count))
            for s in range(1, count)
        ]

    def shared(k, at):
        for copy in pending["share", at, k]:
            copy.wait_recv()
        if at:
            share(k, at - 1)
        else:
            block = out.at[matrix, pl.ds(k * rows_k, rows_k), :]
            pending["mate", k] = remote(
                block, block, ms.at[k], mr.at[k], along(pair + 1 - 2 * lo, other)
            )

    def across(k):
        pending["mate", k].wait_recv()
        block = out.at[pl.ds(2 * c, 2), pl.ds(k * rows_k, rows_k), :]
        pending["core", k] = remote(block, block, cs.at[k], cr.at[k], mate)
        write(k, c)

    def write(k, core):
        part = pl.ds(2 * core, 2), pl.ds(k * rows_k, rows_k), slice(None)
        written.append(pltpu.make_async_copy(out.at[part], out_hbm.at[part], sem_out.at[core, k]))
        written[-1].start()

    def close(k):
        pending["core", k].wait_recv()
        write(k, 1 - c)

    steps = [multiply]
    steps += [functools.partial(add, at=i) for i in range(len(levels))]
    steps += [functools.partial(shared, at=i) for i in reversed(range(len(levels)))]
    events = sorted((0 if p == 0 else p + k, p, k) for p in range(len(steps)) for k in range(pieces))
    before = 0
    for t, p, k in events:
        if before < t <= 5:
            small_step(t - 1)
        before = t
        steps[p](k)
    for k in range(pieces):
        across(k)
    for k in range(pieces):
        close(k)
    for copy in factor + small:
        copy.wait_send()
    for copies in pending.values():
        for copy in copies if isinstance(copies, list) else [copies]:
            copy.wait_send()
    for copy in written:
        copy.wait()


def reduce_all(sizes, left, right, small, pieces=8):
    n_expert, n_dp = sizes
    nz = math.gcd(n_expert, 4)
    n = n_expert // nz
    nh = n // 2
    assert n == n_dp // 2
    seq, width = left.shape[1:]
    rows_k = width // pieces
    bf, f32 = jnp.bfloat16, jnp.float32
    rows_s = small.shape[0] // 2
    splits = [n, nh, 2, nz // 2]
    sizes_at = [rows_k // math.prod(splits[: i + 1]) for i in range(4)]
    counts = [max(q - 1, 1) for q in splits]
    most = max(counts)
    boxes = [pltpu.VMEM((pieces, q, s, width), bf) for q, s in zip(counts, sizes_at)]
    smalls = 2 * n + nz
    return pl.pallas_call(
        functools.partial(reduce_kernel, sizes, pieces),
        out_shape=(
            jax.ShapeDtypeStruct((4, width, width), bf),
            jax.ShapeDtypeStruct(small.shape, f32),
        ),
        in_specs=[VMEM] * 3,
        out_specs=(pl.BlockSpec(memory_space=pl.ANY), VMEM),
        scratch_shapes=[
            pltpu.VMEM((4, width, width), bf),
            DMA((2, pieces)),
            pltpu.VMEM((4 * seq, width), bf),
            pltpu.VMEM((4 * seq, width), bf),
            pltpu.VMEM((pieces, rows_k, width), f32),
            *boxes,
            *boxes,
            pltpu.VMEM((rows_s, width), f32),
            pltpu.VMEM((3, rows_s, width), f32),
            pltpu.VMEM((3, max(n, nz), rows_s, width), f32),
            DMA((3, 2)),
            DMA((4, 2)),
            DMA((2,)),
            DMA((4, pieces, most)),
            DMA((4, pieces, most)),
            DMA((4, pieces, most)),
            DMA((4, pieces, most)),
            DMA((pieces,)),
            DMA((pieces,)),
            DMA((pieces,)),
            DMA((pieces,)),
            DMA((smalls,)),
            DMA((smalls,)),
        ],
        name="reduce_all",
        compiler_params=pltpu.CompilerParams(
            collective_id=3, has_side_effects=True, vmem_limit_bytes=56 << 20
        ),
    )(left, right, small)


def rms_scale(values):
    return lax.rsqrt(jnp.mean(values * values, axis=-1, keepdims=True) + epsilon)


def bucket_hot(seq_len, buckets):
    position = jnp.arange(seq_len, dtype=jnp.int32)
    relative = position[None, :] - position[:, None]
    distance = jnp.abs(relative)
    far_bucket = jnp.full_like(distance, 8)
    for threshold in bucket_edges:
        far_bucket = far_bucket + (distance >= threshold).astype(jnp.int32)
    bucketed = jnp.where(distance < 8, distance, far_bucket) + 16 * (relative > 0).astype(jnp.int32)
    bucket_ids = jnp.arange(buckets, dtype=jnp.int32)
    return (bucketed[None, :, :] == bucket_ids[:, None, None]).astype(jnp.float32)


def dot32(pattern, left, right):
    return jnp.einsum(pattern, left, right, preferred_element_type=jnp.float32)


def shards(
    layer_in, routes, queue_slots, norm_attn, w_query, w_key, w_value, w_out, rel_table,
    norm_moe, router, w_gate, w_up, w_down, cotangent,
):
    bf, f32 = jnp.bfloat16, jnp.float32
    seq_len, width = layer_in.shape
    buckets, heads = rel_table.shape
    expert_count = router.shape[1]
    sizes = (lax.axis_size("expert"), lax.axis_size("dp"))
    n_expert, n_dp = sizes
    assert w_gate.shape[0] == 2 and expert_count == 2 * n_expert
    group_len = seq_len // MICRO
    capacity = (5 * group_len + 2 * expert_count - 1) // (2 * expert_count)
    split_heads = (seq_len, heads, width // heads)
    layer_rows = layer_in.astype(f32)
    inv_attn = rms_scale(layer_rows)
    normed_attn = layer_rows * inv_attn
    one_hot = bucket_hot(seq_len, buckets)
    info = jnp.concatenate([routes.T, queue_slots.T, jnp.zeros((4, seq_len), jnp.int32)])
    expert_w = [jnp.swapaxes(w_gate, 1, 2), jnp.swapaxes(w_up, 1, 2), w_down]
    slots = n_dp // 2 * n_expert * 2 * MICRO * capacity
    fused = 2 * slots * width * 20 + 6 * w_gate.size < 52 << 20
    if fused:
        (
            back, rows_in, hidden, gate_grad, up_grad, grad_rows,
            query, key, value, probs, context, residual, attn_in, gates,
        ) = layer(
            sizes, MICRO, capacity, layer_in, (norm_attn[None], norm_moe[None]), rel_table.T, router.T,
            info, cotangent, (w_query, w_key, w_value, w_out), expert_w,
        )
    else:
        attn_in = (normed_attn * norm_attn).astype(bf)
        query = dot32("sd,de->se", attn_in, w_query).astype(bf)
        key = dot32("sd,de->se", attn_in, w_key).astype(bf)
        value = dot32("sd,de->se", attn_in, w_value).astype(bf)
        bias = jnp.einsum("bij,bh->hij", one_hot, rel_table, precision=highest)
        scores = dot32("ihd,jhd->hij", query.reshape(split_heads), key.reshape(split_heads)) + bias
        exponent = jnp.exp(scores - jnp.max(scores, axis=-1, keepdims=True))
        probs = exponent / jnp.sum(exponent, axis=-1, keepdims=True)
        context = dot32("hij,jhd->ihd", probs.astype(bf), value.reshape(split_heads))
        context = context.astype(bf).reshape(seq_len, width)
        residual = layer_rows + dot32("se,ed->sd", context, w_out)
    inv_moe = rms_scale(residual)
    normed_moe = residual * inv_moe
    moe_in = normed_moe * norm_moe
    expert_ids = jnp.arange(expert_count, dtype=jnp.int32)
    first_hot = (routes[:, 0:1] == expert_ids).astype(f32)
    second_hot = (routes[:, 1:2] == expert_ids).astype(f32)
    if not fused:
        gate_prob = jax.nn.softmax(jnp.dot(moe_in, router, precision=highest), axis=-1)
        prob_first, prob_second = jnp.sum(gate_prob * first_hot, axis=-1), jnp.sum(gate_prob * second_hot, axis=-1)
        gates = jnp.stack([prob_first, prob_second]) / (prob_first + prob_second)
        gates = jnp.pad(gates, ((0, 6), (0, 0)))
        rows_in, weight_in, grad_in = spread(
            sizes, MICRO, capacity, info, moe_in.astype(bf), cotangent, gates
        )
        blocks = rows_in.shape[:-1] + (-1,)
        rows_in, grad_in = [a.reshape(2, -1, width) for a in (rows_in, grad_in)]
        slot_weight = weight_in[:, :, 0, : 2 * MICRO * capacity].reshape(2, -1, 1)
        grad_rows = (slot_weight * grad_in.astype(f32)).astype(bf)
        gate_pre = dot32("jrd,jdf->jrf", rows_in, w_gate)
        up_pre = dot32("jrd,jdf->jrf", rows_in, w_up)
        hidden, active, lean = gated_terms(gate_pre, up_pre)
        hidden = hidden.astype(bf)
        partial_out = dot32("jrf,jfd->jrd", hidden, w_down).astype(bf)
        hidden_grad = dot32("jrd,jfd->jrf", grad_rows, w_down)
        gate_grad, up_grad = (hidden_grad * lean).astype(bf), (hidden_grad * active).astype(bf)
        rows_grad = dot32("jrf,jdf->jrd", gate_grad, w_gate) + dot32("jrf,jdf->jrd", up_grad, w_up)
        back = gather_back(sizes, partial_out.reshape(blocks), rows_grad.astype(bf).reshape(blocks))
    weight_first, weight_second = gates[0][:, None], gates[1][:, None]
    query_heads, key_heads, value_heads = [a.reshape(split_heads) for a in (query, key, value)]
    probs_low = probs.astype(bf)
    rows_in, hidden, gate_grad, up_grad, grad_rows = [
        a.reshape(2, -1, a.shape[-1]) for a in (rows_in, hidden, gate_grad, up_grad, grad_rows)
    ]
    back = back.reshape(2, -1, width)

    core = lax.axis_index("dp") % 2
    per_core = MICRO * capacity
    token = jnp.arange(seq_len, dtype=jnp.int32)[:, None]
    place = (routes % 2) * (n_expert * 2 * per_core) + (routes // 2) * (2 * per_core)
    place = place + core * per_core + (token // group_len) * capacity + queue_slots
    place = jnp.where(queue_slots >= 0, place, -1)
    slot_ids = jnp.arange(2 * n_expert * 2 * per_core, dtype=jnp.int32)
    select_first = (place[:, 0:1] == slot_ids).astype(bf)
    select_second = (place[:, 1:2] == slot_ids).astype(bf)
    picked_first = dot32("tp,pd->td", select_first, back[0])
    picked_second = dot32("tp,pd->td", select_second, back[0])
    moe = weight_first * picked_first + weight_second * picked_second
    layer_out = (residual + moe).astype(bf)
    cot_rows = cotangent.astype(f32)
    grad_weight_first = jnp.sum(cot_rows * picked_first, axis=-1, keepdims=True)
    grad_weight_second = jnp.sum(cot_rows * picked_second, axis=-1, keepdims=True)
    grad_from_slots = dot32("tp,pd->td", select_first + select_second, back[1])
    mean_grad = weight_first * grad_weight_first + weight_second * grad_weight_second
    logit_first = weight_first * (grad_weight_first - mean_grad)
    logit_second = weight_second * (grad_weight_second - mean_grad)
    grad_logits = logit_first * first_hot + logit_second * second_hot
    grad_router = jnp.einsum("sd,se->ed", moe_in, grad_logits, precision=highest)
    grad_moe_in = grad_from_slots + jnp.einsum("se,de->sd", grad_logits, router, precision=highest)
    grad_norm_moe = jnp.sum(grad_moe_in * normed_moe, axis=0)
    grad_normed = grad_moe_in * norm_moe
    grad_residual = cot_rows + inv_moe * (
        grad_normed - normed_moe * jnp.mean(grad_normed * normed_moe, axis=-1, keepdims=True)
    )
    grad_attn_low = grad_residual.astype(bf)
    grad_context = dot32("sd,ed->se", grad_attn_low, w_out).astype(bf).reshape(split_heads)
    grad_values = dot32("hij,ihd->jhd", probs_low, grad_context).astype(bf).reshape(seq_len, width)
    grad_probs = dot32("ihd,jhd->hij", grad_context, value_heads)
    grad_scores = probs * (grad_probs - jnp.sum(probs * grad_probs, axis=-1, keepdims=True))
    grad_rel_table = jnp.einsum("bij,hij->bh", one_hot, grad_scores, precision=highest)
    scores_low = grad_scores.astype(bf)
    grad_queries = dot32("hij,jhd->ihd", scores_low, key_heads).astype(bf).reshape(seq_len, width)
    grad_keys = dot32("hij,ihd->jhd", scores_low, query_heads).astype(bf).reshape(seq_len, width)
    grad_attn_in = dot32("se,de->sd", grad_queries, w_query)
    grad_attn_in = grad_attn_in + dot32("se,de->sd", grad_keys, w_key)
    grad_attn_in = grad_attn_in + dot32("se,de->sd", grad_values, w_value)
    grad_norm_attn = jnp.sum(grad_attn_in * normed_attn, axis=0)
    grad_normed_attn = grad_attn_in * norm_attn
    grad_input = grad_residual + inv_attn * (
        grad_normed_attn
        - normed_attn * jnp.mean(grad_normed_attn * normed_attn, axis=-1, keepdims=True)
    )
    table = grad_rel_table.reshape(-1)
    small = jnp.concatenate(
        [
            grad_router,
            grad_norm_attn[None],
            grad_norm_moe[None],
            jnp.pad(table, (0, width - table.size))[None],
        ]
    )
    small = jnp.pad(small, ((0, -small.shape[0] % 16), (0, 0)))
    sums, small = reduce_all(
        sizes,
        jnp.stack([attn_in, context]),
        jnp.stack([grad_queries, grad_keys, grad_values, grad_attn_low]),
        small,
    )
    *matrices, grad_w_gate, grad_w_up, grad_w_down = finish(
        sums, rows_in, hidden, gate_grad, up_grad, grad_rows
    )
    grad_w_gate, grad_w_up = jnp.swapaxes(grad_w_gate, 1, 2), jnp.swapaxes(grad_w_up, 1, 2)
    return (
        layer_out, grad_input, small[expert_count], *matrices,
        small[expert_count + 2, : table.size].reshape(buckets, heads),
        small[expert_count + 1], small[:expert_count].T, grad_w_gate, grad_w_up, grad_w_down,
    )


def solution(mesh):
    in_specs = (
        P(("expert", "dp"), None),
        P(("expert", "dp"), None),
        P(("expert", "dp"), None),
        P(),
        P(),
        P(),
        P(),
        P(),
        P(),
        P(),
        P(),
        P("expert", None, "dp"),
        P("expert", None, "dp"),
        P("expert", "dp", None),
        P(("expert", "dp"), None),
    )
    out_specs = (
        P(("expert", "dp"), None),
        P(("expert", "dp"), None),
        P(),
        P(),
        P(),
        P(),
        P(),
        P(),
        P(),
        P(),
        P("expert", None, "dp"),
        P("expert", None, "dp"),
        P("expert", "dp", None),
    )
    return jax.shard_map(shards, mesh=mesh, in_specs=in_specs, out_specs=out_specs, check_vma=False)
```

```python
import functools
import math

import jax
import jax.numpy as jnp
from jax import lax
from jax.experimental import pallas as pl
from jax.experimental.pallas import tpu as pltpu
from jax.sharding import PartitionSpec as P

MICRO = 4

epsilon = 1e-06
bucket_edges = (12, 16, 23, 32, 46, 64, 91)
highest = lax.Precision.HIGHEST

MESH = pl.DeviceIdType.MESH
VMEM = pl.BlockSpec(memory_space=pltpu.VMEM)
DMA = pltpu.SemaphoreType.DMA


class Place:
    def __init__(self, n_expert, n_dp):
        self.n_expert, self.n_dp = n_expert, n_dp
        self.nz = math.gcd(n_expert, 4)
        self.nx = n_expert // self.nz
        self.ny = n_dp // 2
        self.e = lax.axis_index("expert")
        self.d = lax.axis_index("dp")
        self.z, self.x = self.e // self.nx, self.e % self.nx
        self.y, self.c = self.d // 2, self.d % 2

    def at(self, z=None, x=None, y=None, c=None, e=None):
        z = self.z if z is None else z
        x = self.x if x is None else x
        y = self.y if y is None else y
        c = self.c if c is None else c
        e = z * self.nx + x if e is None else e
        return (e, y * 2 + c)


def remote(src, dst, send, recv, device):
    copy = pltpu.make_async_remote_copy(
        src_ref=src, dst_ref=dst, send_sem=send, recv_sem=recv, device_id=device, device_id_type=MESH
    )
    copy.start()
    return copy


def greet(devices):
    barrier = pltpu.get_barrier_semaphore()
    for device in devices:
        pl.semaphore_signal(barrier, inc=1, device_id=device, device_id_type=MESH)
    pl.semaphore_wait(barrier, len(devices))


def column_peers(me):
    out = [me.at(c=1 - me.c)]
    out += [me.at(y=(me.y + k) % me.ny) for k in range(1, me.ny)]
    out += [me.at(e=(me.e + k) % me.n_expert) for k in range(1, me.n_expert)]
    return out


class Spread:
    def __init__(self, me, rows, recv, sems):
        self.me, self.rows, self.recv = me, rows, recv
        self.se, self.re, self.sy, self.ry, self.sc, self.rc = sems
        self.came, self.along, self.crossed = {}, {}, {}

    def send(self):
        me = self.me
        for k in range(1, me.n_expert):
            to = (me.e + k) % me.n_expert
            self.came[k] = remote(
                self.rows.at[to], self.recv.at[me.c, me.y * me.n_expert + me.e],
                self.se.at[k], self.re.at[k], me.at(e=to),
            )
        self.recv[me.c, me.y * me.n_expert + me.e] = self.rows[me.e]

    def pass_on(self, blocks):
        me = self.me
        for k in blocks:
            if k:
                self.came[k].wait_recv()
            src = (me.e - k + me.n_expert) % me.n_expert
            block = self.recv.at[me.c, me.y * me.n_expert + src]
            for s in range(1, me.ny):
                self.along[s, k] = remote(
                    block, block, self.sy.at[s - 1, k], self.ry.at[s - 1, k], me.at(y=(me.y + s) % me.ny)
                )

    def pass_column(self):
        me = self.me
        for k in range(1, me.n_expert):
            self.came[k].wait_recv()
        block = self.recv.at[me.c, pl.ds(me.y * me.n_expert, me.n_expert)]
        for s in range(1, me.ny):
            self.along[s, 0] = remote(
                block, block, self.sy.at[s - 1, 0], self.ry.at[s - 1, 0], me.at(y=(me.y + s) % me.ny)
            )

    def cross(self, s):
        me = self.me
        if s:
            for key, copy in self.along.items():
                if key[0] == s:
                    copy.wait_recv()
        block = self.recv.at[me.c, pl.ds((me.y - s + me.ny) % me.ny * me.n_expert, me.n_expert)]
        self.crossed[s] = remote(block, block, self.sc.at[s], self.rc.at[s], me.at(c=1 - me.c))

    def arrive(self):
        for copy in self.crossed.values():
            copy.wait_recv()

    def close(self):
        for copies in (self.came, self.along, self.crossed):
            for copy in copies.values():
                copy.wait_send()


def spread_sems(sizes):
    n_expert, ny = sizes[0], sizes[1] // 2
    most = max(ny - 1, 1)
    return [
        DMA((3, n_expert)), DMA((3, n_expert)), DMA((3, most, n_expert)), DMA((3, most, n_expert)),
        DMA((3, ny)), DMA((3, ny)),
    ]


class Rows:
    def __init__(self, me, rows_per, info_all, gates, tok, send, recv):
        self.me, self.rows_per, self.info_all, self.gates, self.tok = me, rows_per, info_all, gates, tok
        self.send, self.recv, self.copies = send, recv, {}
        self.seq = tok.shape[2]

    def share(self, i, ref):
        block = ref.at[self.me.c]
        mate = self.me.at(c=1 - self.me.c)
        self.copies[i] = remote(block, block, self.send.at[i], self.recv.at[i], mate)

    def hots(self):
        me, seq = self.me, self.seq
        micro, cap, per_core = self.rows_per
        self.copies["info"].wait_recv()
        row_ids = lax.broadcasted_iota(jnp.int32, (me.n_expert * 2 * per_core, seq), 0)
        group = lax.broadcasted_iota(jnp.int32, (1, seq), 1) // (seq // micro)
        self.each = []
        for cc in range(2):
            for k in range(2):
                route = self.info_all[cc, k : k + 1, :]
                slot = self.info_all[cc, 2 + k : 3 + k, :]
                target = (route // 2) * (2 * per_core) + cc * per_core + group * cap + slot
                target = jnp.where((slot >= 0) & (route % 2 == me.c), target, -1)
                self.each.append(jnp.where(row_ids == target, 1.0, 0.0))
        self.both = [(self.each[2 * cc] + self.each[2 * cc + 1]).astype(jnp.bfloat16) for cc in range(2)]

    def gather(self, i):
        self.copies[i].wait_recv()
        total = None
        for cc in range(2):
            term = jnp.dot(self.both[cc], self.tok[i, cc], preferred_element_type=jnp.float32)
            total = term if total is None else total + term
        return total.astype(jnp.bfloat16).reshape(self.me.n_expert, 2 * self.rows_per[2], -1)

    def weights(self):
        self.copies["gates"].wait_recv()
        size = 2 * self.rows_per[2]
        column = None
        for n, hot in enumerate(self.each):
            term = jnp.sum(hot * self.gates[n // 2, n % 2 : n % 2 + 1, :], axis=1, keepdims=True)
            column = term if column is None else column + term
        lane = lax.broadcasted_iota(jnp.int32, (size, 128), 1)
        row = lax.broadcasted_iota(jnp.int32, (size, 128), 0)
        tiles = []
        for e in range(self.me.n_expert):
            block = jnp.where(lane == row, column[e * size : (e + 1) * size, :], 0.0)
            tiles.append(jnp.broadcast_to(jnp.sum(block, axis=0, keepdims=True), (8, 128)))
        return tiles

    def close(self):
        for copy in self.copies.values():
            copy.wait_send()


NAMED = ("info", "gates", 0, 1)


class Named:
    def __init__(self, sems):
        self.at = {name: sems.at[i] for i, name in enumerate(NAMED)}


def rows_scratch(sizes, per_core, seq, width):
    mine = (sizes[0], 2 * per_core, width)
    bf = jnp.bfloat16
    return [
        pltpu.VMEM((2, 8, seq), jnp.int32),
        pltpu.VMEM((2, 8, seq), jnp.float32),
        pltpu.VMEM((2, 2, seq, width), bf),
        DMA((4,)),
        DMA((4,)),
        pltpu.VMEM(mine, bf),
        pltpu.VMEM((sizes[0], 8, 128), jnp.float32),
        pltpu.VMEM(mine, bf),
    ]


def rows_of(me, rows_per, scratch):
    info_all, gates, tok, send, recv = scratch[:5]
    return Rows(me, rows_per, info_all, gates, tok, Named(send), Named(recv))


def spread_kernel(sizes, rows_per, info_ref, moe_ref, cot_ref, w_ref, x_out, w_out, g_out, *scratch):
    me = Place(*sizes)
    c = me.c
    greet(column_peers(me))
    scratch, sems = scratch[:8], scratch[8:]
    rows = rows_of(me, rows_per, scratch)
    info_all, gates, tok = scratch[:3]
    info_all[c] = info_ref[...]
    rows.share("info", info_all)
    gates[c] = w_ref[...]
    rows.share("gates", gates)
    for i, ref in enumerate((moe_ref, cot_ref)):
        tok[i, c] = ref[...]
        rows.share(i, tok.at[i])
    rows.hots()
    buf_x, buf_w, buf_g = scratch[5:]
    out_x, out_w, out_g = [
        Spread(me, buf, recv, [s.at[i] for s in sems])
        for i, (buf, recv) in enumerate(((buf_x, x_out), (buf_w, w_out), (buf_g, g_out)))
    ]
    for i, payload in enumerate((out_x, out_g)):
        payload.rows[...] = rows.gather(i)
        payload.send()
    for e, tile in enumerate(rows.weights()):
        buf_w[e] = tile
    out_w.send()
    for payload in (out_x, out_g):
        payload.pass_on(range(me.n_expert))
        payload.cross(0)
    out_w.pass_column()
    out_w.cross(0)
    for payload in (out_x, out_g, out_w):
        for s in range(1, me.ny):
            payload.cross(s)
    for payload in (out_x, out_g, out_w):
        payload.arrive()
        payload.close()
    rows.close()


def spread(sizes, micro, cap, info, moe, cot, weights):
    n_expert, ny, per_core = sizes[0], sizes[1] // 2, micro * cap
    seq, width = cot.shape
    block = (2, ny * n_expert, 2 * per_core)
    bf = jnp.bfloat16
    return pl.pallas_call(
        functools.partial(spread_kernel, sizes, (micro, cap, per_core)),
        out_shape=(
            jax.ShapeDtypeStruct(block + (width,), bf),
            jax.ShapeDtypeStruct(block[:2] + (8, 128), jnp.float32),
            jax.ShapeDtypeStruct(block + (width,), bf),
        ),
        in_specs=[VMEM] * 4,
        out_specs=(VMEM,) * 3,
        scratch_shapes=rows_scratch(sizes, per_core, seq, width) + spread_sems(sizes),
        name="spread",
        compiler_params=pltpu.CompilerParams(
            collective_id=1, has_side_effects=True, vmem_limit_bytes=48 << 20
        ),
    )(info, moe, cot, weights)


class Back:
    def __init__(self, me, away, own, q_out, r1, stage, r2, final, sems):
        self.me, self.away, self.own = me, away, own
        self.q_out, self.r1, self.stage, self.r2, self.final = q_out, r1, stage, r2, final
        self.sems = sems
        self.ys = [(me.y + k) % me.ny for k in range(me.ny)]
        self.order = list(range(1, me.n_expert)) + [0]
        self.first, self.second, self.third, self.fourth = {}, {}, {}, {}
        self.arrived = set()

    def to_mate(self, i, k):
        me = self.me
        column = pl.ds(self.ys[k] * me.n_expert, me.n_expert)
        self.first[i, k] = remote(
            self.away(i).at[column], self.r1.at[i, column], self.sems[0].at[i, k], self.sems[1].at[i, k],
            me.at(c=1 - me.c),
        )

    def partial(self, i, y, e):
        block = y * self.me.n_expert + e
        return self.own(i, block) + self.r1[i, block].astype(jnp.float32)

    def along_y(self, i):
        me = self.me
        for k in range(1, me.ny):
            self.first[i, k].wait_recv()
            for j in self.order:
                e = (me.e + j) % me.n_expert
                self.stage[i, k - 1, e] = self.partial(i, self.ys[k], e).astype(jnp.bfloat16)
                self.second[i, k, j] = remote(
                    self.stage.at[i, k - 1, e], self.r2.at[i, k - 1, e],
                    self.sems[2].at[i, k - 1, j], self.sems[3].at[i, k - 1, j], me.at(y=self.ys[k]),
                )

    def finish(self, i, order):
        me = self.me
        if (i, 0) not in self.arrived:
            self.arrived.add((i, 0))
            self.first[i, 0].wait_recv()
        for j in order:
            e = (me.e + j) % me.n_expert
            total = self.partial(i, me.y, e)
            for k in range(1, me.ny):
                self.second[i, k, j].wait_recv()
                total = total + self.r2[i, k - 1, e].astype(jnp.float32)
            if j:
                self.final[i, e] = total.astype(jnp.bfloat16)
                self.third[i, j] = remote(
                    self.final.at[i, e], self.q_out.at[i, me.c, me.e],
                    self.sems[4].at[i, j], self.sems[5].at[i, j], me.at(e=e),
                )
            else:
                self.q_out[i, me.c, me.e] = total.astype(jnp.bfloat16)

    def across(self, i):
        for j in self.order[:-1]:
            self.third[i, j].wait_recv()
        block = self.q_out.at[i, self.me.c]
        s, r = self.sems[6].at[i], self.sems[7].at[i]
        self.fourth[i] = remote(block, block, s, r, self.me.at(c=1 - self.me.c))

    def close(self):
        for copy in self.fourth.values():
            copy.wait()
        for copies in (self.first, self.second, self.third):
            for copy in copies.values():
                copy.wait_send()


def back_scratch(sizes, size, width):
    n_expert, ny = sizes[0], sizes[1] // 2
    most = max(ny - 1, 1)
    bf = jnp.bfloat16
    return [
        pltpu.VMEM((2, ny * n_expert, size, width), bf),
        pltpu.VMEM((2, most, n_expert, size, width), bf),
        pltpu.VMEM((2, most, n_expert, size, width), bf),
        pltpu.VMEM((2, n_expert, size, width), bf),
        DMA((2, ny)),
        DMA((2, ny)),
        DMA((2, most, n_expert)),
        DMA((2, most, n_expert)),
        DMA((2, n_expert)),
        DMA((2, n_expert)),
        DMA((2,)),
        DMA((2,)),
    ]


def gather_back_kernel(sizes, p0_ref, p1_ref, q_out, *scratch):
    me = Place(*sizes)
    greet(column_peers(me))
    p_refs = (p0_ref, p1_ref)
    back = Back(
        me, lambda i: p_refs[i].at[1 - me.c],
        lambda i, block: p_refs[i][me.c, block].astype(jnp.float32), q_out, *scratch[:4], scratch[4:],
    )
    for i in range(2):
        for k in reversed(range(me.ny)):
            back.to_mate(i, k)
    for i in range(2):
        back.along_y(i)
    for i in range(2):
        back.finish(i, back.order)
        back.across(i)
    back.close()


def gather_back(sizes, first, second):
    n_expert = sizes[0]
    _, _, size, width = first.shape
    return pl.pallas_call(
        functools.partial(gather_back_kernel, sizes),
        out_shape=jax.ShapeDtypeStruct((2, 2, n_expert, size, width), jnp.bfloat16),
        in_specs=[VMEM] * 2,
        out_specs=VMEM,
        scratch_shapes=back_scratch(sizes, size, width),
        name="gather_back",
        compiler_params=pltpu.CompilerParams(
            collective_id=2, has_side_effects=True, vmem_limit_bytes=48 << 20
        ),
    )(first, second)


def gated_terms(gate_pre, up_pre):
    root = math.sqrt(2.0 / math.pi)
    square = gate_pre * gate_pre
    bend = jnp.tanh(root * (gate_pre + 0.044715 * square * gate_pre))
    half = 0.5 * (1.0 + bend)
    active = gate_pre * half
    slope = half + 0.5 * gate_pre * (1.0 - bend * bend) * root * (1.0 + 3 * 0.044715 * square)
    return active * up_pre, active, up_pre * slope


def bucket_of(relative):
    distance = jnp.abs(relative)
    far_bucket = jnp.full_like(distance, 8)
    for threshold in bucket_edges:
        far_bucket = far_bucket + (distance >= threshold).astype(jnp.int32)
    return jnp.where(distance < 8, distance, far_bucket) + 16 * (relative > 0).astype(jnp.int32)


def row_scale(values):
    return lax.rsqrt(jnp.mean(values * values, axis=-1, keepdims=True) + epsilon)


def dot_as(left, right, contract):
    return lax.dot_general(left, right, (contract, ((), ())), preferred_element_type=jnp.float32)


NN, NT, TN = ((1,), (0,)), ((1,), (1,)), ((0,), (0,))


def layer_kernel(
    sizes, rows_per, layer_in, norm_attn, norm_moe, table_t, router_t, info_ref, cot_ref,
    wq_hbm, wk_hbm, wv_hbm, wo_hbm, wg_hbm, wu_hbm, wd_hbm,
    q_out, x_ref, hid_out, dg_out, du_out, gr_out, query, key, value, probs, context, residual, attn_in, gate_out,
    g_ref, w_ref, weights, act, slope, away, own, sem_a, sem_w, *scratch,
):
    me = Place(*sizes)
    c = me.c
    seq, width = layer_in.shape
    heads, buckets = table_t.shape
    units = wg_hbm.shape[1]
    bf, f32 = jnp.bfloat16, jnp.float32

    attn_w = []
    for i, src in enumerate((wq_hbm, wk_hbm, wv_hbm, wo_hbm)):
        dst = weights.at[pl.ds(i * width, width)]
        attn_w.append(pltpu.make_async_copy(src, dst, sem_a.at[i]))
        attn_w[-1].start()
    greet(column_peers(me))
    rows_in = rows_of(me, rows_per, scratch[:8])
    info_all, gates, tok = scratch[:3]
    buf_x, buf_w, buf_g = scratch[5:8]
    out_x, out_w, out_g = [
        Spread(me, buf, recv, [s.at[i] for s in scratch[8:14]])
        for i, (buf, recv) in enumerate(((buf_x, x_ref), (buf_w, w_ref), (buf_g, g_ref)))
    ]
    scratch = scratch[14:]
    column = me.n_expert
    quarter = [range(i * column // 4, (i + 1) * column // 4) for i in range(4)]
    info_all[c] = info_ref[...]
    rows_in.share("info", info_all)
    tok[1, c] = cot_ref[...]
    rows_in.share(1, tok.at[1])
    rows = layer_in[...].astype(f32)
    attn_in[...] = (rows * row_scale(rows) * norm_attn[...]).astype(bf)
    rows_in.hots()
    buf_g[...] = rows_in.gather(1)
    out_g.send()
    for i, ref in enumerate((query, key, value)):
        attn_w[i].wait()
        ref[...] = dot_as(attn_in[...], weights[i * width : (i + 1) * width, :], NN).astype(bf)
    relative = lax.broadcasted_iota(jnp.int32, (heads, 2 * seq), 1) - seq
    bucket = bucket_of(relative)
    bias_of = jnp.zeros((heads, 2 * seq), f32)
    for n in range(buckets):
        bias_of = jnp.where(bucket == n, table_t[:, n : n + 1], bias_of)
    pair = 2 * width // heads
    low_half = lax.broadcasted_iota(jnp.int32, (seq, pair), 1) < pair // 2
    for n in range(heads // 2):
        lanes = slice(n * pair, (n + 1) * pair)
        k2, v2 = key[:, lanes], value[:, lanes]
        total = None
        for h in range(2):
            mine = low_half if h == 0 else ~low_half
            head = 2 * n + h
            line = jnp.broadcast_to(bias_of[head : head + 1, :], (seq, 2 * seq))
            bias = pltpu.roll(line, seq, 1, stride=1, stride_axis=0)[:, :seq]
            scores = dot_as(query[:, lanes], jnp.where(mine, k2, jnp.zeros_like(k2)), NT) + bias
            exponent = jnp.exp(scores - jnp.max(scores, axis=-1, keepdims=True))
            prob = exponent / jnp.sum(exponent, axis=-1, keepdims=True)
            probs[head] = prob
            term = dot_as(prob.astype(bf), jnp.where(mine, v2, jnp.zeros_like(v2)), NN)
            total = term if total is None else total + term
        context[:, lanes] = total.astype(bf)
        if n % 4 == 3:
            out_g.pass_on(quarter[n // 4])
    attn_w[3].wait()
    resid = rows + dot_as(context[...], weights[3 * width : 4 * width, :], NN)
    residual[...] = resid
    fetch = {}
    for n, j in enumerate((c, 1 - c)):
        for i, src in enumerate((wg_hbm, wu_hbm, wd_hbm)):
            dst = weights.at[pl.ds(pl.multiple_of((2 * i + j) * units, 16), units)]
            fetch[n, i] = pltpu.make_async_copy(src.at[j], dst, sem_w.at[n, i])
            fetch[n, i].start()
    moe_in = resid * row_scale(resid) * norm_moe[...]
    tok[0, c] = moe_in.astype(bf)
    rows_in.share(0, tok.at[0])
    logits = lax.dot_general(
        router_t[...], moe_in, (NT, ((), ())), preferred_element_type=f32, precision=highest
    )
    logits = jnp.exp(logits - jnp.max(logits, axis=0, keepdims=True))
    gate_prob = logits / jnp.sum(logits, axis=0, keepdims=True)
    expert_ids = lax.broadcasted_iota(jnp.int32, gate_prob.shape, 0)
    picked = [
        jnp.sum(jnp.where(info_ref[k : k + 1, :] == expert_ids, gate_prob, 0.0), axis=0, keepdims=True)
        for k in range(2)
    ]
    both = picked[0] + picked[1]
    for k in range(2):
        gates[c, k : k + 1, :] = picked[k] / both
    gates[c, 2:, :] = jnp.zeros((6, seq), f32)
    gate_out[...] = gates[c]
    rows_in.share("gates", gates)
    buf_x[...] = rows_in.gather(0)
    out_x.send()
    out_g.pass_on(quarter[2])
    for e, tile in enumerate(rows_in.weights()):
        buf_w[e] = tile
    out_w.send()
    out_g.pass_on(quarter[3])
    out_g.cross(0)

    size = x_ref.shape[2]
    step = math.gcd(column, 4)
    chunk = step * size
    back = Back(
        me, lambda i: away.at[i],
        lambda i, block: own[i, pl.ds(pl.multiple_of(block * size, 8), size), :],
        q_out, *scratch[:4], scratch[4:],
    )

    def part(i, j):
        return weights[pl.ds(pl.multiple_of((2 * i + j) * units, 16), units), :]

    def flat(value):
        return value.reshape(chunk, value.shape[-1])

    def blocks(value):
        return value.reshape(step, size, value.shape[-1])

    def store(i, first, some, rows, value):
        if first:
            away[i, some] = blocks(value.astype(bf))
        else:
            own[i, rows, :] = value

    def each(start, count, body):
        @pl.loop(0, count // step)
        def _(n):
            at = start + n * step
            body(pl.ds(at, step), pl.ds(pl.multiple_of(at * size, 8), chunk))

    def forward(first, j, start, count):
        def body(some, rows):
            x = flat(x_ref[j, some])
            gate_pre = dot_as(x, part(0, j), NT)
            up_pre = dot_as(x, part(1, j), NT)
            hidden, active, lean = gated_terms(gate_pre, up_pre)
            act[j, rows, :] = active
            slope[j, rows, :] = lean
            hidden = hidden.astype(bf)
            hid_out[j, some] = blocks(hidden)
            store(0, first, some, rows, dot_as(hidden, part(2, j), NN))

        each(start, count, body)

    lane = lax.broadcasted_iota(jnp.int32, (size, 128), 1)
    row = lax.broadcasted_iota(jnp.int32, (size, 128), 0)

    def backward(first, j, start, count):
        def body(some, rows):
            tiles = w_ref[j, some]
            grad = []
            for n in range(step):
                line = jnp.broadcast_to(tiles[n, 0:1, :], (size, 128))
                weight = jnp.sum(jnp.where(lane == row, line, 0.0), axis=1, keepdims=True)
                grad.append(weight * g_ref[j, some.start + n].astype(f32))
            grad = jnp.concatenate(grad, axis=0).astype(bf)
            gr_out[j, some] = blocks(grad)
            grad_hidden = dot_as(grad, part(2, j), NT)
            dg = (grad_hidden * slope[j, rows, :]).astype(bf)
            du = (grad_hidden * act[j, rows, :]).astype(bf)
            dg_out[j, some] = blocks(dg)
            du_out[j, some] = blocks(du)
            store(1, first, some, rows, dot_as(dg, part(0, j), NN) + dot_as(du, part(1, j), NN))

        each(start, count, body)

    here = me.y * column
    away_ys = [back.ys[k] * column for k in range(1, me.ny)]
    shares = [back.order[i * column // 4 : (i + 1) * column // 4] for i in range(4)]
    out_x.pass_on(range(column))
    out_x.cross(0)
    for s in range(1, me.ny):
        out_g.cross(s)
    for i in range(3):
        fetch[0, i].wait()
    forward(False, c, here, column)
    for i in range(3):
        fetch[1, i].wait()
    out_x.crossed[0].wait_recv()
    forward(True, 1 - c, here, column)
    back.to_mate(0, 0)
    out_w.pass_column()
    out_w.cross(0)
    for s in range(1, me.ny):
        out_x.cross(s)
    for k in range(1, me.ny):
        out_x.crossed[k].wait_recv()
        forward(True, 1 - c, away_ys[k - 1], column)
        back.to_mate(0, k)
    for s in range(1, me.ny):
        out_w.cross(s)
    for k in range(1, me.ny):
        forward(False, c, away_ys[k - 1], column)
    back.along_y(0)
    out_g.arrive()
    out_w.arrive()
    for k in range(1, me.ny):
        backward(True, 1 - c, away_ys[k - 1], column)
        back.to_mate(1, k)
    back.finish(0, shares[0])
    for k in range(1, me.ny):
        backward(False, c, away_ys[k - 1], column)
    back.along_y(1)
    back.finish(0, shares[1])
    backward(True, 1 - c, here, column)
    back.to_mate(1, 0)
    back.finish(0, shares[2])
    backward(False, c, here, column)
    back.finish(0, shares[3])
    back.across(0)
    back.finish(1, back.order)
    back.across(1)
    back.close()
    for payload in (out_x, out_w, out_g):
        payload.close()
    rows_in.close()


def layer(sizes, micro, cap, layer_in, norms, table_t, router_t, info, cot, attn_w, expert_w):
    n_expert, ny, per_core = sizes[0], sizes[1] // 2, micro * cap
    seq, width = cot.shape
    units = expert_w[0].shape[1]
    heads = table_t.shape[0]
    count, size = ny * n_expert, 2 * per_core
    bf, f32 = jnp.bfloat16, jnp.float32
    any_space = pl.BlockSpec(memory_space=pl.ANY)
    inner = jax.ShapeDtypeStruct((2, count, size, units), bf)
    outer = jax.ShapeDtypeStruct((2, count, size, width), bf)
    low, full = jax.ShapeDtypeStruct((seq, width), bf), jax.ShapeDtypeStruct((seq, width), f32)
    return pl.pallas_call(
        functools.partial(layer_kernel, sizes, (micro, cap, per_core)),
        out_shape=(
            jax.ShapeDtypeStruct((2, 2, n_expert, size, width), bf), outer, inner, inner, inner, outer,
            low, low, low, jax.ShapeDtypeStruct((heads, seq, seq), f32), low, full, low,
            jax.ShapeDtypeStruct((8, seq), f32),
        ),
        in_specs=[VMEM] * 7 + [any_space] * 7,
        out_specs=(VMEM,) * 14,
        scratch_shapes=[
            pltpu.VMEM((2, count, size, width), bf),
            pltpu.VMEM((2, count, 8, 128), f32),
            pltpu.VMEM((max(4 * width, 6 * units), width), bf),
            pltpu.VMEM((2, count * size, units), f32),
            pltpu.VMEM((2, count * size, units), f32),
            pltpu.VMEM((2, count, size, width), bf),
            pltpu.VMEM((2, count * size, width), f32),
            DMA((4,)),
            DMA((2, 3)),
        ]
        + rows_scratch(sizes, per_core, seq, width)
        + spread_sems(sizes)
        + back_scratch(sizes, size, width),
        name="layer",
        compiler_params=pltpu.CompilerParams(
            collective_id=4, has_side_effects=True, vmem_limit_bytes=54 << 20
        ),
    )(layer_in, *norms, table_t, router_t, info, cot, *attn_w, *expert_w)


def finish_kernel(sums_hbm, x_hbm, h_hbm, dg_hbm, du_hbm, gr_hbm, *refs):
    outs, (sums, x, h, dg, du, gr, stage, sem_sum, sem_in, sem_out) = refs[:7], refs[7:]
    slots, rows = stage.shape[:2]
    width = sums.shape[1]
    units = h.shape[2]
    loads = {}

    def load(key, src, dst, sem):
        loads[key] = pltpu.make_async_copy(src, dst, sem)
        loads[key].start()

    def load_sums(keys):
        for n in keys:
            part = n * rows // width, pl.ds(n * rows % width, rows)
            load(("sums", n), sums_hbm.at[part], sums.at[part], sem_sum.at[n])

    casts = range(4 * width // rows)
    load_sums(casts[:4])
    for i, (key, src, dst) in enumerate(
        (("dg", dg_hbm, dg), ("x", x_hbm, x), ("du", du_hbm, du), ("h", h_hbm, h), ("gr", gr_hbm, gr))
    ):
        for j in range(2):
            load((key, j), src.at[j], dst.at[j], sem_in.at[i, j])
    load_sums(casts[4:])

    def need(key):
        if key in loads:
            loads.pop(key).wait()

    jobs = []
    products = [
        (left, right, out, j, f)
        for left, right, out in ((("dg", dg), ("x", x), 4), (("du", du), ("x", x), 5), (("h", h), ("gr", gr), 6))
        for j in range(2)
        for f in range(0, units, rows)
    ]
    casts = list(casts)
    while casts or products:
        if casts:
            jobs.append(casts.pop(0))
        if products and (len(jobs) > 3 or not casts):
            jobs.append(products.pop(0))
    flying = [None] * slots
    for n, job in enumerate(jobs):
        slot = n % slots
        if flying[slot] is not None:
            flying[slot].wait()
        if isinstance(job, int):
            need(("sums", job))
            m, r = job * rows // width, job * rows % width
            stage[slot] = sums[m, r : r + rows, :].astype(jnp.float32)
            src, dst = stage.at[slot], outs[m].at[pl.ds(r, rows)]
        else:
            (left_key, left), (right_key, right), out, j, f = job
            need((left_key, j))
            need((right_key, j))
            size = min(rows, units - f)
            stage[slot, :size] = lax.dot_general(
                left[j, :, f : f + size], right[j], (((0,), (0,)), ((), ())),
                preferred_element_type=jnp.float32,
            )
            src, dst = stage.at[slot, pl.ds(0, size)], outs[out].at[j, pl.ds(f, size)]
        flying[slot] = pltpu.make_async_copy(src, dst, sem_out.at[slot])
        flying[slot].start()
    for copy in flying:
        if copy is not None:
            copy.wait()


def finish(sums, x, h, dg, du, gr):
    f32 = jnp.float32
    width = sums.shape[1]
    units = h.shape[2]
    any_space = pl.BlockSpec(memory_space=pl.ANY)
    return pl.pallas_call(
        finish_kernel,
        out_shape=(jax.ShapeDtypeStruct((width, width), f32),) * 4
        + (jax.ShapeDtypeStruct((2, units, width), f32),) * 3,
        in_specs=[any_space] * 6,
        out_specs=(any_space,) * 7,
        scratch_shapes=[pltpu.VMEM(a.shape, a.dtype) for a in (sums, x, h, dg, du, gr)]
        + [pltpu.VMEM((6, 256, width), f32), DMA((4 * width // 256,)), DMA((5, 2)), DMA((6,))],
        name="finish",
        compiler_params=pltpu.CompilerParams(vmem_limit_bytes=60 << 20),
    )(sums, x, h, dg, du, gr)


def upright(line):
    n = line.shape[1]
    square = lax.broadcasted_iota(jnp.int32, (n, n), 0) == lax.broadcasted_iota(jnp.int32, (n, n), 1)
    return jnp.sum(jnp.where(square, jnp.broadcast_to(line, (n, n)), 0.0), axis=1, keepdims=True)


def flat_line(column):
    n = column.shape[0]
    square = lax.broadcasted_iota(jnp.int32, (n, n), 0) == lax.broadcasted_iota(jnp.int32, (n, n), 1)
    return jnp.sum(jnp.where(square, jnp.broadcast_to(column, (n, n)), 0.0), axis=0, keepdims=True)


def diagonals(values):
    n = values.shape[1]
    total = None
    for first in range(0, n, 8):
        wide = jnp.concatenate([values[first : first + 8, :], jnp.zeros((8, n), jnp.float32)], axis=1)
        wide = pltpu.roll(wide, n - first, 1)
        total = wide if total is None else total + wide
    row = lax.broadcasted_iota(jnp.int32, total.shape, 0)
    for bit in (1, 2, 4):
        total = jnp.where((row & bit) > 0, pltpu.roll(total, 2 * n - bit, 1), total)
    return jnp.sum(total, axis=0, keepdims=True)


def settle_kernel(
    sizes, rows_per, pieces,
    back_ref, info_ref, gate_ref, cot_ref, layer_in, residual, context, attn_in, query, key, value, probs,
    norm_attn, norm_moe, router_t, wq_hbm, wk_hbm, wv_hbm, wo_hbm,
    layer_out, grad_in, out_hbm, small_out,
    weights, sem_a, left_ref, right_ref, small_ref, lines, out, sem_out, buf_a, buf_b, acc, *boxes,
):
    bf, f32 = jnp.bfloat16, jnp.float32
    micro, cap, per_core = rows_per
    attn_w = []
    for i, src in ((3, wo_hbm), (0, wq_hbm), (1, wk_hbm), (2, wv_hbm)):
        attn_w.append(pltpu.make_async_copy(src, weights.at[i], sem_a.at[i]))
        attn_w[-1].start()
    me = Place(*sizes)
    c, mate = me.c, me.at(c=1 - me.c)
    n = me.nx
    seq = right_ref.shape[1]
    total_rows = width = out.shape[1]
    is0 = c == 0
    pair = jnp.where(is0, me.x, me.y)
    other = jnp.where(is0, me.y, me.x)
    lo, hi, nh = pair % 2, pair // 2, n // 2

    def along(pair_at, other_at, z=None):
        return me.at(x=jnp.where(is0, pair_at, other_at), y=jnp.where(is0, other_at, pair_at), z=z)

    flip_x, flip_y = me.x + 1 - 2 * (me.x % 2), me.y + 1 - 2 * (me.y % 2)
    dims = [
        (n, other, lambda q: along(pair, q)),
        (nh, hi, lambda q: along(q * 2 + lo, other)),
        (2, me.z % 2, lambda q: me.at(z=me.z // 2 * 2 + q)),
        (me.nz // 2, me.z // 2, lambda q: me.at(z=q * 2 + me.z % 2)),
    ]
    parts, gots = boxes[:4], boxes[4:8]
    half, small_half, small_got, fs, fr, os, ps, pr, gs, gr, ms, mr, cs, cr, ss, sr = boxes[8:]
    levels = [i for i, d in enumerate(dims) if d[0] > 1]
    x_peers = [me.at(x=(me.x + k) % n) for k in range(1, n)]
    y_peers = [me.at(y=(me.y + k) % n) for k in range(1, n)]
    z_peers = [me.at(z=(me.z + k) % me.nz) for k in range(1, me.nz)]
    greet(
        [mate, me.at(x=flip_x, c=1 - c), me.at(y=flip_y, c=1 - c)] + x_peers + y_peers + z_peers
    )

    def slot_a(slot):
        return buf_a.at[pl.ds(pl.multiple_of(slot * seq, seq), seq), :]

    def slot_b(slot):
        return buf_b.at[pl.ds(pl.multiple_of(slot * seq, seq), seq), :]

    left_ref[0] = attn_in[...]
    left_ref[1] = context[...]
    targets = [
        (mate, 1 - c, other % 2, c),
        (me.at(x=flip_x, c=0), 0, flip_x % 2, 2 + c),
        (me.at(y=flip_y, c=1), 1, flip_y % 2, 2 + c),
    ]
    factor = []
    for i, (device, role, parity, slot) in enumerate(targets):
        a = jnp.where(role == 0, 0, parity)
        factor.append(remote(left_ref.at[a], slot_a(slot), fs.at[i, 0], fr.at[slot, 0], device))
    own = [pltpu.make_async_copy(left_ref.at[jnp.where(is0, 0, lo)], slot_a(c), os.at[0])]
    own[0].start()

    size = 2 * per_core
    group = lax.broadcasted_iota(jnp.int32, (1, seq), 1) // (seq // micro)
    slot_ids = lax.broadcasted_iota(jnp.int32, (2 * me.n_expert * size, seq), 0)
    hots = []
    for k in range(2):
        route, slot = info_ref[k : k + 1, :], info_ref[2 + k : 3 + k, :]
        place = (route % 2) * (me.n_expert * size) + (route // 2) * size + c * per_core + group * cap + slot
        hots.append(jnp.where(slot_ids == jnp.where(slot >= 0, place, -1), 1.0, 0.0))
    low = [h.astype(bf) for h in hots] + [(hots[0] + hots[1]).astype(bf)]
    half_slots = me.n_expert * size

    def picked(hot, which):
        total = None
        for j in range(2):
            rows = back_ref[which, j].reshape(half_slots, width)
            term = dot_as(hot[j * half_slots : (j + 1) * half_slots, :], rows, TN)
            total = term if total is None else total + term
        return total

    cot = cot_ref[...].astype(f32)
    resid = residual[...]
    chosen = [picked(low[k], 0) for k in range(2)]
    gate = [upright(gate_ref[k : k + 1, :]) for k in range(2)]
    layer_out[...] = (resid + (gate[0] * chosen[0] + gate[1] * chosen[1])).astype(bf)
    grad_gate = [jnp.sum(cot * chosen[k], axis=-1, keepdims=True) for k in range(2)]
    mean_grad = gate[0] * grad_gate[0] + gate[1] * grad_gate[1]
    logit = [gate[k] * (grad_gate[k] - mean_grad) for k in range(2)]
    experts = router_t.shape[0]
    by_token, by_expert = None, None
    for k in range(2):
        route = info_ref[k : k + 1, :]
        line = jnp.where(
            lax.broadcasted_iota(jnp.int32, (experts, seq), 0) == route, flat_line(logit[k]), 0.0
        )
        by_expert = line if by_expert is None else by_expert + line
        route_up = upright(route.astype(f32)).astype(jnp.int32)
        line = jnp.where(
            lax.broadcasted_iota(jnp.int32, (seq, experts), 1) == route_up, logit[k], 0.0
        )
        by_token = line if by_token is None else by_token + line

    def exact(left, right):
        return lax.dot_general(
            left, right, (NN, ((), ())), preferred_element_type=f32, precision=highest
        )

    scale = row_scale(resid)
    normed = resid * scale
    small_ref[:experts] = exact(by_expert, normed * norm_moe[...])
    grad_moe = picked(low[2], 1) + exact(by_token, router_t[...])
    small_ref[experts:] = jnp.zeros((small_ref.shape[0] - experts, width), f32)
    small_ref[experts + 1 : experts + 2] = jnp.sum(grad_moe * normed, axis=0, keepdims=True)
    grad_n = grad_moe * norm_moe[...]
    grad_resid = cot + scale * (grad_n - normed * jnp.mean(grad_n * normed, axis=-1, keepdims=True))
    right_ref[3] = grad_resid.astype(bf)
    grad_in[...] = grad_resid
    attn_w[0].wait()
    grad_context = dot_as(right_ref[3], weights[3], NT).astype(bf)

    heads = probs.shape[0]
    pair_lanes = 2 * width // heads
    low_half = lax.broadcasted_iota(jnp.int32, (seq, pair_lanes), 1) < pair_lanes // 2
    for n2 in range(heads // 2):
        lanes = slice(n2 * pair_lanes, (n2 + 1) * pair_lanes)
        sums = [None, None, None]
        for h in range(2):
            mine = low_half if h == 0 else ~low_half
            head = 2 * n2 + h

            def only(value):
                return jnp.where(mine, value, jnp.zeros_like(value))

            prob = probs[head]
            grad_c = only(grad_context[:, lanes])
            grad_p = dot_as(grad_c, value[:, lanes], NT)
            grad_s = prob * (grad_p - jnp.sum(prob * grad_p, axis=-1, keepdims=True))
            lines[head : head + 1, :] = diagonals(grad_s)
            grad_s = grad_s.astype(bf)
            terms = (
                dot_as(grad_s, only(key[:, lanes]), NN),
                dot_as(grad_s, only(query[:, lanes]), TN),
                dot_as(prob.astype(bf), grad_c, TN),
            )
            sums = [t if s is None else s + t for s, t in zip(sums, terms)]
        for i in range(3):
            right_ref[i, :, lanes] = sums[i].astype(bf)
    for i, (device, role, parity, slot) in enumerate(targets):
        factor.append(
            remote(right_ref.at[role * 2 + parity], slot_b(slot), fs.at[i, 1], fr.at[slot, 1], device)
        )
    own.append(pltpu.make_async_copy(right_ref.at[c * 2 + lo], slot_b(c), os.at[1]))
    own[1].start()
    buckets = 32
    bucket = bucket_of(lax.broadcasted_iota(jnp.int32, (2 * seq, buckets), 0) - seq)
    hot = jnp.where(bucket == lax.broadcasted_iota(jnp.int32, (2 * seq, buckets), 1), 1.0, 0.0)
    small_ref[experts + 8 : experts + 8 + heads, :buckets] = exact(lines[...], hot)
    grad_attn = None
    for i in range(3):
        attn_w[1 + i].wait()
        term = dot_as(right_ref[i], weights[i], NT)
        grad_attn = term if grad_attn is None else grad_attn + term
    rows = layer_in[...].astype(f32)
    scale = row_scale(rows)
    normed = rows * scale
    small_ref[experts : experts + 1] = jnp.sum(grad_attn * normed, axis=0, keepdims=True)
    grad_n = grad_attn * norm_attn[...]
    grad_in[...] += scale * (grad_n - normed * jnp.mean(grad_n * normed, axis=-1, keepdims=True))

    rows_s = half.shape[0]
    small = [remote(small_ref.at[pl.ds((1 - c) * rows_s, rows_s)], half, ss.at[0], sr.at[0], mate)]
    small_dims = [
        (n, me.x, lambda q: me.at(x=q)),
        (n, me.y, lambda q: me.at(y=q)),
        (me.nz, me.z, lambda q: me.at(z=q)),
    ]
    small_wait = [small[0]]
    small_slot = [1]

    def small_step(step):
        for copy in small_wait:
            copy.wait_recv()
        small_wait.clear()
        if step == 0:
            total = small_ref[pl.ds(c * rows_s, rows_s)] + half[...]
        elif step <= 3:
            total = small_got[step - 1, 0]
            for k in range(1, small_dims[step - 1][0]):
                total = total + small_got[step - 1, k]
        if step < 3:
            count, index, peer = small_dims[step]
            small_half[step] = total
            small_got[step, index] = total
            for k in range(1, count):
                small_wait.append(
                    remote(
                        small_half.at[step], small_got.at[step, index], ss.at[small_slot[0]],
                        sr.at[small_slot[0]], peer((index + k) % count),
                    )
                )
                small_slot[0] += 1
        elif step == 3:
            small_out[pl.ds(c * rows_s, rows_s)] = total
            block = small_out.at[pl.ds(c * rows_s, rows_s)]
            small_wait.append(
                remote(block, block, ss.at[small_slot[0]], sr.at[small_slot[0]], mate)
            )
        small.extend(small_wait)

    for where in (1 - c, 2, 3):
        for i, (src, dst) in enumerate(((left_ref, slot_a(where)), (right_ref, slot_b(where)))):
            pltpu.make_async_remote_copy(
                src_ref=src.at[0], dst_ref=dst, send_sem=fs.at[0, i], recv_sem=fr.at[where, i],
                device_id=mate, device_id_type=MESH,
            ).wait_recv()
    for copy in own:
        copy.wait()

    rows_k = total_rows // pieces
    matrix = c * 2 + lo
    pending, written = {}, []

    def multiply(k):
        acc[k] = lax.dot_general(
            buf_a[:, k * rows_k : (k + 1) * rows_k], buf_b[...], (TN, ((), ())),
            preferred_element_type=jnp.float32,
        )
        push(k, 0, rows_k)

    def push(k, at, rows):
        level = levels[at]
        count, index, peer = dims[level]
        size = rows // count
        copies = []
        for s in range(1, count):
            to = (index + s) % count
            parts[level][k, s - 1] = acc[k, pl.ds(pl.multiple_of(to * size, 16), size), :].astype(jnp.bfloat16)
            copies.append(
                remote(
                    parts[level].at[k, s - 1], gots[level].at[k, s - 1],
                    ps.at[level, k, s - 1], pr.at[level, k, s - 1], peer(to),
                )
            )
        pending["push", at, k] = copies

    def rows_at(at):
        rows = rows_k
        for i in range(at):
            rows //= dims[levels[i]][0]
        return rows

    def add(k, at):
        level = levels[at]
        count, index, _ = dims[level]
        size = rows_at(at) // count
        for copy in pending["push", at, k]:
            copy.wait_recv()
        total = acc[k, pl.ds(pl.multiple_of(index * size, 16), size), :]
        for s in range(1, count):
            total = total + gots[level][k, s - 1].astype(jnp.float32)
        if at + 1 < len(levels):
            acc[k, :size, :] = total
            push(k, at + 1, size)
        else:
            out[matrix, pl.ds(offset(k, at), size), :] = total.astype(jnp.bfloat16)
            share(k, at)

    def offset(k, at):
        start, rows = k * rows_k, rows_k
        for i in range(at + 1):
            count, index, _ = dims[levels[i]]
            rows //= count
            start = start + index * rows
        return pl.multiple_of(start, 16)

    def share(k, at):
        level = levels[at]
        count, index, peer = dims[level]
        size = rows_at(at) // count
        block = out.at[matrix, pl.ds(offset(k, at), size), :]
        pending["share", at, k] = [
            remote(block, block, gs.at[level, k, s - 1], gr.at[level, k, s - 1], peer((index + s) % count))
            for s in range(1, count)
        ]

    def shared(k, at):
        for copy in pending["share", at, k]:
            copy.wait_recv()
        if at:
            share(k, at - 1)
        else:
            block = out.at[matrix, pl.ds(k * rows_k, rows_k), :]
            pending["mate", k] = remote(
                block, block, ms.at[k], mr.at[k], along(pair + 1 - 2 * lo, other)
            )

    def across(k):
        pending["mate", k].wait_recv()
        block = out.at[pl.ds(2 * c, 2), pl.ds(k * rows_k, rows_k), :]
        pending["core", k] = remote(block, block, cs.at[k], cr.at[k], mate)
        write(k, c)

    def write(k, core):
        part = pl.ds(2 * core, 2), pl.ds(k * rows_k, rows_k), slice(None)
        written.append(pltpu.make_async_copy(out.at[part], out_hbm.at[part], sem_out.at[core, k]))
        written[-1].start()

    def close(k):
        pending["core", k].wait_recv()
        write(k, 1 - c)

    steps = [multiply]
    steps += [functools.partial(add, at=i) for i in range(len(levels))]
    steps += [functools.partial(shared, at=i) for i in reversed(range(len(levels)))]
    events = sorted((0 if p == 0 else p + k, p, k) for p in range(len(steps)) for k in range(pieces))
    before = 0
    for t, p, k in events:
        if before < t <= 5:
            small_step(t - 1)
        before = t
        steps[p](k)
    for k in range(pieces):
        across(k)
    for k in range(pieces):
        close(k)
    for copy in factor + small:
        copy.wait_send()
    for copies in pending.values():
        for copy in copies if isinstance(copies, list) else [copies]:
            copy.wait_send()
    for copy in written:
        copy.wait()


def settle(sizes, micro, cap, arrays, norms, router_t, attn_w):
    n_expert, n_dp = sizes
    nz = math.gcd(n_expert, 4)
    n = n_expert // nz
    nh = n // 2
    assert n == n_dp // 2
    seq, width = arrays[4].shape
    heads = arrays[11].shape[0]
    splits = [n, nh, 2, nz // 2]
    pieces = max(1, min(8, width // (16 * math.prod(splits))))
    rows_k = width // pieces
    bf, f32 = jnp.bfloat16, jnp.float32
    small_rows = router_t.shape[0] + 8 + heads
    small_rows += -small_rows % 16
    rows_s = small_rows // 2
    sizes_at = [rows_k // math.prod(splits[: i + 1]) for i in range(4)]
    counts = [max(q - 1, 1) for q in splits]
    most = max(counts)
    boxes = [
        pltpu.VMEM((pieces, q, s if k > 1 else 16, width), bf) for q, s, k in zip(counts, sizes_at, splits)
    ]
    smalls = 2 * n + nz
    any_space = pl.BlockSpec(memory_space=pl.ANY)
    return pl.pallas_call(
        functools.partial(settle_kernel, sizes, (micro, cap, micro * cap), pieces),
        out_shape=(
            jax.ShapeDtypeStruct((seq, width), bf),
            jax.ShapeDtypeStruct((seq, width), f32),
            jax.ShapeDtypeStruct((4, width, width), bf),
            jax.ShapeDtypeStruct((small_rows, width), f32),
        ),
        in_specs=[VMEM] * 15 + [any_space] * 4,
        out_specs=(VMEM, VMEM, any_space, VMEM),
        scratch_shapes=[
            pltpu.VMEM((4, width, width), bf),
            DMA((4,)),
            pltpu.VMEM((2, seq, width), bf),
            pltpu.VMEM((4, seq, width), bf),
            pltpu.VMEM((small_rows, width), f32),
            pltpu.VMEM((heads, 2 * seq), f32),
            pltpu.VMEM((4, width, width), bf),
            DMA((2, pieces)),
            pltpu.VMEM((4 * seq, width), bf),
            pltpu.VMEM((4 * seq, width), bf),
            pltpu.VMEM((pieces, rows_k, width), f32),
            *boxes,
            *boxes,
            pltpu.VMEM((rows_s, width), f32),
            pltpu.VMEM((3, rows_s, width), f32),
            pltpu.VMEM((3, max(n, nz), rows_s, width), f32),
            DMA((3, 2)),
            DMA((4, 2)),
            DMA((2,)),
            DMA((4, pieces, most)),
            DMA((4, pieces, most)),
            DMA((4, pieces, most)),
            DMA((4, pieces, most)),
            DMA((pieces,)),
            DMA((pieces,)),
            DMA((pieces,)),
            DMA((pieces,)),
            DMA((smalls,)),
            DMA((smalls,)),
        ],
        name="settle",
        compiler_params=pltpu.CompilerParams(
            collective_id=3, has_side_effects=True, vmem_limit_bytes=58 << 20
        ),
    )(*arrays, *norms, router_t, *attn_w)


def rms_scale(values):
    return lax.rsqrt(jnp.mean(values * values, axis=-1, keepdims=True) + epsilon)


def bucket_hot(seq_len, buckets):
    position = jnp.arange(seq_len, dtype=jnp.int32)
    bucket_ids = jnp.arange(buckets, dtype=jnp.int32)
    bucketed = bucket_of(position[None, :] - position[:, None])
    return (bucketed[None, :, :] == bucket_ids[:, None, None]).astype(jnp.float32)


def dot32(pattern, left, right):
    return jnp.einsum(pattern, left, right, preferred_element_type=jnp.float32)


def shards(
    layer_in, routes, queue_slots, norm_attn, w_query, w_key, w_value, w_out, rel_table,
    norm_moe, router, w_gate, w_up, w_down, cotangent,
):
    bf, f32 = jnp.bfloat16, jnp.float32
    seq_len, width = layer_in.shape
    buckets, heads = rel_table.shape
    expert_count = router.shape[1]
    sizes = (lax.axis_size("expert"), lax.axis_size("dp"))
    n_expert, n_dp = sizes
    assert w_gate.shape[0] == 2 and expert_count == 2 * n_expert
    group_len = seq_len // MICRO
    capacity = (5 * group_len + 2 * expert_count - 1) // (2 * expert_count)
    split_heads = (seq_len, heads, width // heads)
    info = jnp.concatenate([routes.T, queue_slots.T, jnp.zeros((4, seq_len), jnp.int32)])
    expert_w = [jnp.swapaxes(w_gate, 1, 2), jnp.swapaxes(w_up, 1, 2), w_down]
    slots = n_dp // 2 * n_expert * 2 * MICRO * capacity
    fused = 2 * slots * width * 20 + 6 * w_gate.size < 52 << 20
    if fused:
        (
            back, rows_in, hidden, gate_grad, up_grad, grad_rows,
            query, key, value, probs, context, residual, attn_in, gates,
        ) = layer(
            sizes, MICRO, capacity, layer_in, (norm_attn[None], norm_moe[None]), rel_table.T, router.T,
            info, cotangent, (w_query, w_key, w_value, w_out), expert_w,
        )
    else:
        layer_rows = layer_in.astype(f32)
        attn_in = (layer_rows * rms_scale(layer_rows) * norm_attn).astype(bf)
        query = dot32("sd,de->se", attn_in, w_query).astype(bf)
        key = dot32("sd,de->se", attn_in, w_key).astype(bf)
        value = dot32("sd,de->se", attn_in, w_value).astype(bf)
        one_hot = bucket_hot(seq_len, buckets)
        bias = jnp.einsum("bij,bh->hij", one_hot, rel_table, precision=highest)
        scores = dot32("ihd,jhd->hij", query.reshape(split_heads), key.reshape(split_heads)) + bias
        exponent = jnp.exp(scores - jnp.max(scores, axis=-1, keepdims=True))
        probs = exponent / jnp.sum(exponent, axis=-1, keepdims=True)
        context = dot32("hij,jhd->ihd", probs.astype(bf), value.reshape(split_heads))
        context = context.astype(bf).reshape(seq_len, width)
        residual = layer_rows + dot32("se,ed->sd", context, w_out)
        moe_in = residual * rms_scale(residual) * norm_moe
        expert_ids = jnp.arange(expert_count, dtype=jnp.int32)
        first_hot = (routes[:, 0:1] == expert_ids).astype(f32)
        second_hot = (routes[:, 1:2] == expert_ids).astype(f32)
        gate_prob = jax.nn.softmax(jnp.dot(moe_in, router, precision=highest), axis=-1)
        prob_first, prob_second = jnp.sum(gate_prob * first_hot, axis=-1), jnp.sum(gate_prob * second_hot, axis=-1)
        gates = jnp.stack([prob_first, prob_second]) / (prob_first + prob_second)
        gates = jnp.pad(gates, ((0, 6), (0, 0)))
        rows_in, weight_in, grad_in = spread(
            sizes, MICRO, capacity, info, moe_in.astype(bf), cotangent, gates
        )
        blocks = rows_in.shape[:-1] + (-1,)
        rows_in, grad_in = [a.reshape(2, -1, width) for a in (rows_in, grad_in)]
        slot_weight = weight_in[:, :, 0, : 2 * MICRO * capacity].reshape(2, -1, 1)
        grad_rows = (slot_weight * grad_in.astype(f32)).astype(bf)
        gate_pre = dot32("jrd,jdf->jrf", rows_in, w_gate)
        up_pre = dot32("jrd,jdf->jrf", rows_in, w_up)
        hidden, active, lean = gated_terms(gate_pre, up_pre)
        hidden = hidden.astype(bf)
        partial_out = dot32("jrf,jfd->jrd", hidden, w_down).astype(bf)
        hidden_grad = dot32("jrd,jfd->jrf", grad_rows, w_down)
        gate_grad, up_grad = (hidden_grad * lean).astype(bf), (hidden_grad * active).astype(bf)
        rows_grad = dot32("jrf,jdf->jrd", gate_grad, w_gate) + dot32("jrf,jdf->jrd", up_grad, w_up)
        back = gather_back(sizes, partial_out.reshape(blocks), rows_grad.astype(bf).reshape(blocks))
    layer_out, grad_input, sums, small = settle(
        sizes, MICRO, capacity,
        (back, info, gates, cotangent, layer_in, residual, context, attn_in, query, key, value, probs),
        (norm_attn[None], norm_moe[None]), router.T, (w_query, w_key, w_value, w_out),
    )
    rows_in, hidden, gate_grad, up_grad, grad_rows = [
        a.reshape(2, -1, a.shape[-1]) for a in (rows_in, hidden, gate_grad, up_grad, grad_rows)
    ]
    *matrices, grad_w_gate, grad_w_up, grad_w_down = finish(
        sums, rows_in, hidden, gate_grad, up_grad, grad_rows
    )
    return (
        layer_out, grad_input, small[expert_count], *matrices,
        small[expert_count + 8 : expert_count + 8 + heads, :buckets].T,
        small[expert_count + 1], small[:expert_count].T,
        jnp.swapaxes(grad_w_gate, 1, 2), jnp.swapaxes(grad_w_up, 1, 2), grad_w_down,
    )


def solution(mesh):
    in_specs = (
        P(("expert", "dp"), None),
        P(("expert", "dp"), None),
        P(("expert", "dp"), None),
        P(),
        P(),
        P(),
        P(),
        P(),
        P(),
        P(),
        P(),
        P("expert", None, "dp"),
        P("expert", None, "dp"),
        P("expert", "dp", None),
        P(("expert", "dp"), None),
    )
    out_specs = (
        P(("expert", "dp"), None),
        P(("expert", "dp"), None),
        P(),
        P(),
        P(),
        P(),
        P(),
        P(),
        P(),
        P(),
        P("expert", None, "dp"),
        P("expert", None, "dp"),
        P("expert", "dp", None),
    )
    return jax.shard_map(shards, mesh=mesh, in_specs=in_specs, out_specs=out_specs, check_vma=False)
```

```python
import functools
import math

import jax
import jax.numpy as jnp
from jax import lax
from jax.experimental import pallas as pl
from jax.experimental.pallas import tpu as pltpu
from jax.sharding import PartitionSpec as P

MICRO = 4

epsilon = 1e-06
bucket_edges = (12, 16, 23, 32, 46, 64, 91)
highest = lax.Precision.HIGHEST

MESH = pl.DeviceIdType.MESH
VMEM = pl.BlockSpec(memory_space=pltpu.VMEM)
DMA = pltpu.SemaphoreType.DMA


class Place:
    def __init__(self, n_expert, n_dp):
        self.n_expert, self.n_dp = n_expert, n_dp
        self.nz = math.gcd(n_expert, 4)
        self.nx = n_expert // self.nz
        self.ny = n_dp // 2
        self.e = lax.axis_index("expert")
        self.d = lax.axis_index("dp")
        self.z, self.x = self.e // self.nx, self.e % self.nx
        self.y, self.c = self.d // 2, self.d % 2

    def seat(self, e):
        return e % self.nx * self.nz + e // self.nx

    def off(self, section, k, sign):
        x = (self.x + sign * section + self.nx) % self.nx
        z = (self.z + sign * k + self.nz) % self.nz
        return z * self.nx + x

    def start(self, section, sign):
        return (self.x + sign * section + self.nx) % self.nx * self.nz

    def at(self, z=None, x=None, y=None, c=None, e=None):
        z = self.z if z is None else z
        x = self.x if x is None else x
        y = self.y if y is None else y
        c = self.c if c is None else c
        e = z * self.nx + x if e is None else e
        return (e, y * 2 + c)


def remote(src, dst, send, recv, device):
    copy = pltpu.make_async_remote_copy(
        src_ref=src, dst_ref=dst, send_sem=send, recv_sem=recv, device_id=device, device_id_type=MESH
    )
    copy.start()
    return copy


def greet(devices):
    barrier = pltpu.get_barrier_semaphore()
    for device in devices:
        pl.semaphore_signal(barrier, inc=1, device_id=device, device_id_type=MESH)
    pl.semaphore_wait(barrier, len(devices))


def column_peers(me):
    out = [me.at(c=1 - me.c)]
    out += [me.at(y=(me.y + k) % me.ny) for k in range(1, me.ny)]
    out += [me.at(e=(me.e + k) % me.n_expert) for k in range(1, me.n_expert)]
    return out


class Spread:
    def __init__(self, me, rows, recv, sems):
        self.me, self.rows, self.recv = me, rows, recv
        self.se, self.re, self.sy, self.ry, self.sc, self.rc = sems
        self.came, self.along, self.crossed = {}, {}, {}

    def send(self):
        me = self.me
        here = me.y * me.n_expert + me.seat(me.e)
        for section in range(me.nx):
            for k in range(me.nz):
                to = me.off(section, k, 1)
                if section + k:
                    n = section * me.nz + k
                    self.came[section, k] = remote(
                        self.rows.at[me.seat(to)], self.recv.at[me.c, here],
                        self.se.at[n], self.re.at[n], me.at(e=to),
                    )
                else:
                    self.recv[me.c, here] = self.rows[me.seat(to)]

    def pass_on(self, section):
        me = self.me
        for k in range(me.nz):
            if section + k:
                self.came[section, k].wait_recv()
            n = section * me.nz + k
            block = self.recv.at[me.c, me.y * me.n_expert + me.seat(me.off(section, k, -1))]
            for s in range(1, me.ny):
                self.along[s, section, k] = remote(
                    block, block, self.sy.at[s - 1, n], self.ry.at[s - 1, n], me.at(y=(me.y + s) % me.ny)
                )

    def pass_column(self):
        me = self.me
        for copy in self.came.values():
            copy.wait_recv()
        block = self.recv.at[me.c, pl.ds(me.y * me.n_expert, me.n_expert)]
        for s in range(1, me.ny):
            self.along[s, -1, 0] = remote(
                block, block, self.sy.at[s - 1, 0], self.ry.at[s - 1, 0], me.at(y=(me.y + s) % me.ny)
            )

    def cross(self, s, section=-1):
        me = self.me
        if s:
            for key, copy in self.along.items():
                if key[:2] == (s, section):
                    copy.wait_recv()
        at = (me.y - s + me.ny) % me.ny * me.n_expert
        if section < 0:
            block = self.recv.at[me.c, pl.ds(at, me.n_expert)]
        else:
            block = self.recv.at[me.c, pl.ds(at + me.start(section, -1), me.nz)]
        n = max(section, 0)
        self.crossed[s, section] = remote(
            block, block, self.sc.at[s, n], self.rc.at[s, n], me.at(c=1 - me.c)
        )

    def arrive(self):
        for copy in self.crossed.values():
            copy.wait_recv()

    def close(self):
        for copies in (self.came, self.along, self.crossed):
            for copy in copies.values():
                copy.wait_send()


def spread_sems(sizes):
    n_expert, ny = sizes[0], sizes[1] // 2
    most, nx = max(ny - 1, 1), n_expert // math.gcd(n_expert, 4)
    return [
        DMA((3, n_expert)), DMA((3, n_expert)), DMA((3, most, n_expert)), DMA((3, most, n_expert)),
        DMA((3, ny, nx)), DMA((3, ny, nx)),
    ]


class Rows:
    def __init__(self, me, rows_per, info_all, gates, tok, send, recv):
        self.me, self.rows_per, self.info_all, self.gates, self.tok = me, rows_per, info_all, gates, tok
        self.send, self.recv, self.copies = send, recv, {}
        self.seq = tok.shape[2]

    def share(self, i, ref):
        block = ref.at[self.me.c]
        mate = self.me.at(c=1 - self.me.c)
        self.copies[i] = remote(block, block, self.send.at[i], self.recv.at[i], mate)

    def hots(self):
        me, seq = self.me, self.seq
        micro, cap, per_core = self.rows_per
        self.copies["info"].wait_recv()
        row_ids = lax.broadcasted_iota(jnp.int32, (me.n_expert * 2 * per_core, seq), 0)
        group = lax.broadcasted_iota(jnp.int32, (1, seq), 1) // (seq // micro)
        self.each = []
        for cc in range(2):
            for k in range(2):
                route = self.info_all[cc, k : k + 1, :]
                slot = self.info_all[cc, 2 + k : 3 + k, :]
                target = me.seat(route // 2) * (2 * per_core) + cc * per_core + group * cap + slot
                target = jnp.where((slot >= 0) & (route % 2 == me.c), target, -1)
                self.each.append(jnp.where(row_ids == target, 1.0, 0.0))
        self.both = [(self.each[2 * cc] + self.each[2 * cc + 1]).astype(jnp.bfloat16) for cc in range(2)]

    def gather(self, i):
        self.copies[i].wait_recv()
        total = None
        for cc in range(2):
            term = jnp.dot(self.both[cc], self.tok[i, cc], preferred_element_type=jnp.float32)
            total = term if total is None else total + term
        return total.astype(jnp.bfloat16).reshape(self.me.n_expert, 2 * self.rows_per[2], -1)

    def weights(self):
        self.copies["gates"].wait_recv()
        size = 2 * self.rows_per[2]
        column = None
        for n, hot in enumerate(self.each):
            term = jnp.sum(hot * self.gates[n // 2, n % 2 : n % 2 + 1, :], axis=1, keepdims=True)
            column = term if column is None else column + term
        lane = lax.broadcasted_iota(jnp.int32, (size, 128), 1)
        row = lax.broadcasted_iota(jnp.int32, (size, 128), 0)
        tiles = []
        for e in range(self.me.n_expert):
            block = jnp.where(lane == row, column[e * size : (e + 1) * size, :], 0.0)
            tiles.append(jnp.broadcast_to(jnp.sum(block, axis=0, keepdims=True), (8, 128)))
        return tiles

    def close(self):
        for copy in self.copies.values():
            copy.wait_send()


NAMED = ("info", "gates", 0, 1)


class Named:
    def __init__(self, sems):
        self.at = {name: sems.at[i] for i, name in enumerate(NAMED)}


def rows_scratch(sizes, per_core, seq, width):
    mine = (sizes[0], 2 * per_core, width)
    bf = jnp.bfloat16
    return [
        pltpu.VMEM((2, 8, seq), jnp.int32),
        pltpu.VMEM((2, 8, seq), jnp.float32),
        pltpu.VMEM((2, 2, seq, width), bf),
        DMA((4,)),
        DMA((4,)),
        pltpu.VMEM(mine, bf),
        pltpu.VMEM((sizes[0], 8, 128), jnp.float32),
        pltpu.VMEM(mine, bf),
    ]


def rows_of(me, rows_per, scratch):
    info_all, gates, tok, send, recv = scratch[:5]
    return Rows(me, rows_per, info_all, gates, tok, Named(send), Named(recv))


def spread_kernel(sizes, rows_per, info_ref, moe_ref, cot_ref, w_ref, x_out, w_out, g_out, *scratch):
    me = Place(*sizes)
    c = me.c
    greet(column_peers(me))
    scratch, sems = scratch[:8], scratch[8:]
    rows = rows_of(me, rows_per, scratch)
    info_all, gates, tok = scratch[:3]
    info_all[c] = info_ref[...]
    rows.share("info", info_all)
    gates[c] = w_ref[...]
    rows.share("gates", gates)
    for i, ref in enumerate((moe_ref, cot_ref)):
        tok[i, c] = ref[...]
        rows.share(i, tok.at[i])
    rows.hots()
    buf_x, buf_w, buf_g = scratch[5:]
    out_x, out_w, out_g = [
        Spread(me, buf, recv, [s.at[i] for s in sems])
        for i, (buf, recv) in enumerate(((buf_x, x_out), (buf_w, w_out), (buf_g, g_out)))
    ]
    for i, payload in enumerate((out_x, out_g)):
        payload.rows[...] = rows.gather(i)
        payload.send()
    for e, tile in enumerate(rows.weights()):
        buf_w[e] = tile
    out_w.send()
    for payload in (out_x, out_g):
        for section in range(me.nx):
            payload.pass_on(section)
            payload.cross(0, section)
    out_w.pass_column()
    out_w.cross(0)
    for s in range(1, me.ny):
        for payload in (out_x, out_g):
            for section in range(me.nx):
                payload.cross(s, section)
        out_w.cross(s)
    for payload in (out_x, out_g, out_w):
        payload.arrive()
        payload.close()
    rows.close()


def spread(sizes, micro, cap, info, moe, cot, weights):
    n_expert, ny, per_core = sizes[0], sizes[1] // 2, micro * cap
    seq, width = cot.shape
    block = (2, ny * n_expert, 2 * per_core)
    bf = jnp.bfloat16
    return pl.pallas_call(
        functools.partial(spread_kernel, sizes, (micro, cap, per_core)),
        out_shape=(
            jax.ShapeDtypeStruct(block + (width,), bf),
            jax.ShapeDtypeStruct(block[:2] + (8, 128), jnp.float32),
            jax.ShapeDtypeStruct(block + (width,), bf),
        ),
        in_specs=[VMEM] * 4,
        out_specs=(VMEM,) * 3,
        scratch_shapes=rows_scratch(sizes, per_core, seq, width) + spread_sems(sizes),
        name="spread",
        compiler_params=pltpu.CompilerParams(
            collective_id=1, has_side_effects=True, vmem_limit_bytes=48 << 20
        ),
    )(info, moe, cot, weights)


class Back:
    def __init__(self, me, away, own, q_out, r1, stage, r2, final, sems):
        self.me, self.away, self.own = me, away, own
        self.q_out, self.r1, self.stage, self.r2, self.final = q_out, r1, stage, r2, final
        self.sems = sems
        self.ys = [(me.y + k) % me.ny for k in range(me.ny)]
        self.order = list(range(1, me.nz)) + [0]
        self.first, self.second, self.third, self.fourth = {}, {}, {}, {}

    def to_mate(self, i, k, section):
        me = self.me
        some = pl.ds(self.ys[k] * me.n_expert + me.start(section, 1), me.nz)
        self.first[i, k, section] = remote(
            self.away(i).at[some], self.r1.at[i, some],
            self.sems[0].at[i, k, section], self.sems[1].at[i, k, section], me.at(c=1 - me.c),
        )

    def partial(self, i, y, seat):
        block = y * self.me.n_expert + seat
        return self.own(i, block) + self.r1[i, block].astype(jnp.float32)

    def along_y(self, i, section):
        me = self.me
        for k in range(1, me.ny):
            self.first[i, k, section].wait_recv()
            for j in self.order:
                seat = me.seat(me.off(section, j, 1))
                n = section * me.nz + j
                self.stage[i, k - 1, seat] = self.partial(i, self.ys[k], seat).astype(jnp.bfloat16)
                self.second[i, k, n] = remote(
                    self.stage.at[i, k - 1, seat], self.r2.at[i, k - 1, seat],
                    self.sems[2].at[i, k - 1, n], self.sems[3].at[i, k - 1, n], me.at(y=self.ys[k]),
                )

    def finish(self, i, section):
        me = self.me
        self.first[i, 0, section].wait_recv()
        for j in self.order:
            to = me.off(section, j, 1)
            seat = me.seat(to)
            n = section * me.nz + j
            total = self.partial(i, me.y, seat)
            for k in range(1, me.ny):
                self.second[i, k, n].wait_recv()
                total = total + self.r2[i, k - 1, seat].astype(jnp.float32)
            if n:
                self.final[i, seat] = total.astype(jnp.bfloat16)
                self.third[i, n] = remote(
                    self.final.at[i, seat], self.q_out.at[i, me.c, me.e],
                    self.sems[4].at[i, n], self.sems[5].at[i, n], me.at(e=to),
                )
            else:
                self.q_out[i, me.c, me.e] = total.astype(jnp.bfloat16)

    def across(self, i):
        for key, copy in self.third.items():
            if key[0] == i:
                copy.wait_recv()
        block = self.q_out.at[i, self.me.c]
        s, r = self.sems[6].at[i], self.sems[7].at[i]
        self.fourth[i] = remote(block, block, s, r, self.me.at(c=1 - self.me.c))

    def close(self):
        for copy in self.fourth.values():
            copy.wait()
        for copies in (self.first, self.second, self.third):
            for copy in copies.values():
                copy.wait_send()


def back_scratch(sizes, size, width):
    n_expert, ny = sizes[0], sizes[1] // 2
    most, nx = max(ny - 1, 1), n_expert // math.gcd(n_expert, 4)
    bf = jnp.bfloat16
    return [
        pltpu.VMEM((2, ny * n_expert, size, width), bf),
        pltpu.VMEM((2, most, n_expert, size, width), bf),
        pltpu.VMEM((2, most, n_expert, size, width), bf),
        pltpu.VMEM((2, n_expert, size, width), bf),
        DMA((2, ny, nx)),
        DMA((2, ny, nx)),
        DMA((2, most, n_expert)),
        DMA((2, most, n_expert)),
        DMA((2, n_expert)),
        DMA((2, n_expert)),
        DMA((2,)),
        DMA((2,)),
    ]


def gather_back_kernel(sizes, p0_ref, p1_ref, q_out, *scratch):
    me = Place(*sizes)
    greet(column_peers(me))
    p_refs = (p0_ref, p1_ref)
    back = Back(
        me, lambda i: p_refs[i].at[1 - me.c],
        lambda i, block: p_refs[i][me.c, block].astype(jnp.float32), q_out, *scratch[:4], scratch[4:],
    )
    for i in range(2):
        for section in range(me.nx):
            for k in reversed(range(me.ny)):
                back.to_mate(i, k, section)
    for i in range(2):
        for section in range(me.nx):
            back.along_y(i, section)
    for i in range(2):
        for section in range(me.nx):
            back.finish(i, section)
        back.across(i)
    back.close()


def gather_back(sizes, first, second):
    n_expert = sizes[0]
    _, _, size, width = first.shape
    return pl.pallas_call(
        functools.partial(gather_back_kernel, sizes),
        out_shape=jax.ShapeDtypeStruct((2, 2, n_expert, size, width), jnp.bfloat16),
        in_specs=[VMEM] * 2,
        out_specs=VMEM,
        scratch_shapes=back_scratch(sizes, size, width),
        name="gather_back",
        compiler_params=pltpu.CompilerParams(
            collective_id=2, has_side_effects=True, vmem_limit_bytes=48 << 20
        ),
    )(first, second)


def gated_terms(gate_pre, up_pre):
    root = math.sqrt(2.0 / math.pi)
    square = gate_pre * gate_pre
    bend = jnp.tanh(root * (gate_pre + 0.044715 * square * gate_pre))
    half = 0.5 * (1.0 + bend)
    active = gate_pre * half
    slope = half + 0.5 * gate_pre * (1.0 - bend * bend) * root * (1.0 + 3 * 0.044715 * square)
    return active * up_pre, active, up_pre * slope


def bucket_of(relative):
    distance = jnp.abs(relative)
    far_bucket = jnp.full_like(distance, 8)
    for threshold in bucket_edges:
        far_bucket = far_bucket + (distance >= threshold).astype(jnp.int32)
    return jnp.where(distance < 8, distance, far_bucket) + 16 * (relative > 0).astype(jnp.int32)


def row_scale(values):
    return lax.rsqrt(jnp.mean(values * values, axis=-1, keepdims=True) + epsilon)


def dot_as(left, right, contract):
    return lax.dot_general(left, right, (contract, ((), ())), preferred_element_type=jnp.float32)


NN, NT, TN = ((1,), (0,)), ((1,), (1,)), ((0,), (0,))


def layer_kernel(
    sizes, rows_per, layer_in, norm_attn, norm_moe, table_t, router_t, info_ref, cot_ref,
    wq_hbm, wk_hbm, wv_hbm, wo_hbm, wg_hbm, wu_hbm, wd_hbm,
    q_out, x_hbm, hid_hbm, dg_hbm, du_hbm, gr_hbm, query, key, value, probs, context, residual, attn_in, gate_out,
    x_ref, hid, dg_all, du_all, gr_all, g_ref, w_ref, weights, act, slope, away, own, sem_a, sem_w, sem_e, *scratch,
):
    me = Place(*sizes)
    c = me.c
    seq, width = layer_in.shape
    heads, buckets = table_t.shape
    units = wg_hbm.shape[1]
    bf, f32 = jnp.bfloat16, jnp.float32

    attn_w = []
    for i, src in enumerate((wq_hbm, wk_hbm, wv_hbm, wo_hbm)):
        dst = weights.at[pl.ds(i * width, width)]
        attn_w.append(pltpu.make_async_copy(src, dst, sem_a.at[i]))
        attn_w[-1].start()
    greet(column_peers(me))
    rows_in = rows_of(me, rows_per, scratch[:8])
    info_all, gates, tok = scratch[:3]
    buf_x, buf_w, buf_g = scratch[5:8]
    out_x, out_w, out_g = [
        Spread(me, buf, recv, [s.at[i] for s in scratch[8:14]])
        for i, (buf, recv) in enumerate(((buf_x, x_ref), (buf_w, w_ref), (buf_g, g_ref)))
    ]
    scratch = scratch[14:]
    column = me.n_expert
    info_all[c] = info_ref[...]
    rows_in.share("info", info_all)
    tok[1, c] = cot_ref[...]
    rows_in.share(1, tok.at[1])
    rows = layer_in[...].astype(f32)
    attn_in[...] = (rows * row_scale(rows) * norm_attn[...]).astype(bf)
    rows_in.hots()
    buf_g[...] = rows_in.gather(1)
    out_g.send()
    for i, ref in enumerate((query, key, value)):
        attn_w[i].wait()
        ref[...] = dot_as(attn_in[...], weights[i * width : (i + 1) * width, :], NN).astype(bf)
    relative = lax.broadcasted_iota(jnp.int32, (heads, 2 * seq), 1) - seq
    bucket = bucket_of(relative)
    bias_of = jnp.zeros((heads, 2 * seq), f32)
    for n in range(buckets):
        bias_of = jnp.where(bucket == n, table_t[:, n : n + 1], bias_of)
    pair = 2 * width // heads
    low_half = lax.broadcasted_iota(jnp.int32, (seq, pair), 1) < pair // 2
    for n in range(heads // 2):
        lanes = slice(n * pair, (n + 1) * pair)
        k2, v2 = key[:, lanes], value[:, lanes]
        total = None
        for h in range(2):
            mine = low_half if h == 0 else ~low_half
            head = 2 * n + h
            line = jnp.broadcast_to(bias_of[head : head + 1, :], (seq, 2 * seq))
            bias = pltpu.roll(line, seq, 1, stride=1, stride_axis=0)[:, :seq]
            scores = dot_as(query[:, lanes], jnp.where(mine, k2, jnp.zeros_like(k2)), NT) + bias
            exponent = jnp.exp(scores - jnp.max(scores, axis=-1, keepdims=True))
            prob = exponent / jnp.sum(exponent, axis=-1, keepdims=True)
            probs[head] = prob
            term = dot_as(prob.astype(bf), jnp.where(mine, v2, jnp.zeros_like(v2)), NN)
            total = term if total is None else total + term
        context[:, lanes] = total.astype(bf)
        if n == heads // 2 - 3:
            out_g.pass_on(0)
    attn_w[3].wait()
    resid = rows + dot_as(context[...], weights[3 * width : 4 * width, :], NN)
    residual[...] = resid
    fetch = {}
    for n, j in enumerate((c, 1 - c)):
        for i, src in enumerate((wg_hbm, wu_hbm, wd_hbm)):
            dst = weights.at[pl.ds(pl.multiple_of((2 * i + j) * units, 16), units)]
            fetch[n, i] = pltpu.make_async_copy(src.at[j], dst, sem_w.at[n, i])
            fetch[n, i].start()
    moe_in = resid * row_scale(resid) * norm_moe[...]
    tok[0, c] = moe_in.astype(bf)
    rows_in.share(0, tok.at[0])
    logits = lax.dot_general(
        router_t[...], moe_in, (NT, ((), ())), preferred_element_type=f32, precision=highest
    )
    logits = jnp.exp(logits - jnp.max(logits, axis=0, keepdims=True))
    gate_prob = logits / jnp.sum(logits, axis=0, keepdims=True)
    expert_ids = lax.broadcasted_iota(jnp.int32, gate_prob.shape, 0)
    picked = [
        jnp.sum(jnp.where(info_ref[k : k + 1, :] == expert_ids, gate_prob, 0.0), axis=0, keepdims=True)
        for k in range(2)
    ]
    both = picked[0] + picked[1]
    for k in range(2):
        gates[c, k : k + 1, :] = picked[k] / both
    gates[c, 2:, :] = jnp.zeros((6, seq), f32)
    gate_out[...] = gates[c]
    rows_in.share("gates", gates)
    buf_x[...] = rows_in.gather(0)
    out_x.send()
    for section in range(1, me.nx):
        out_g.pass_on(section)
    for e, tile in enumerate(rows_in.weights()):
        buf_w[e] = tile
    out_w.send()
    out_g.cross(0, 0)
    for section in range(1, me.nx):
        out_g.cross(0, section)

    size = x_ref.shape[2]
    step = me.nz
    chunk = step * size
    back = Back(
        me, lambda i: away.at[i],
        lambda i, block: own[i, pl.ds(pl.multiple_of(block * size, 8), size), :],
        q_out, *scratch[:4], scratch[4:],
    )

    def emit(i, src, dst):
        copy = pltpu.make_async_copy(src, dst, sem_e.at[i])
        copy.start()
        return copy

    def part(i, j):
        return weights[pl.ds(pl.multiple_of((2 * i + j) * units, 16), units), :]

    def flat(value):
        return value.reshape(chunk, value.shape[-1])

    def blocks(value):
        return value.reshape(step, size, value.shape[-1])

    def store(i, first, some, rows, value):
        if first:
            away[i, some] = blocks(value.astype(bf))
        else:
            own[i, rows, :] = value

    def part_of(k, section):
        at = back.ys[k] * column + me.start(section, 1)
        return pl.ds(at, step), pl.ds(pl.multiple_of(at * size, 16), chunk)

    def forward(first, k, section):
        j = 1 - c if first else c
        some, rows = part_of(k, section)
        x = flat(x_ref[j, some])
        gate_pre = dot_as(x, part(0, j), NT)
        up_pre = dot_as(x, part(1, j), NT)
        hidden, active, lean = gated_terms(gate_pre, up_pre)
        act[j, rows, :] = active
        slope[j, rows, :] = lean
        hidden = hidden.astype(bf)
        hid[j, some] = blocks(hidden)
        store(0, first, some, rows, dot_as(hidden, part(2, j), NN))
        if first:
            back.to_mate(0, k, section)

    lane = lax.broadcasted_iota(jnp.int32, (size, 128), 1)
    row = lax.broadcasted_iota(jnp.int32, (size, 128), 0)

    def backward(first, k, section):
        j = 1 - c if first else c
        some, rows = part_of(k, section)
        tiles = w_ref[j, some]
        grad = []
        for n in range(step):
            line = jnp.broadcast_to(tiles[n, 0:1, :], (size, 128))
            weight = jnp.sum(jnp.where(lane == row, line, 0.0), axis=1, keepdims=True)
            grad.append(weight * g_ref[j, some.start + n].astype(f32))
        grad = jnp.concatenate(grad, axis=0).astype(bf)
        gr_all[j, some] = blocks(grad)
        grad_hidden = dot_as(grad, part(2, j), NT)
        dg = (grad_hidden * slope[j, rows, :]).astype(bf)
        du = (grad_hidden * act[j, rows, :]).astype(bf)
        dg_all[j, some] = blocks(dg)
        du_all[j, some] = blocks(du)
        store(1, first, some, rows, dot_as(dg, part(0, j), NN) + dot_as(du, part(1, j), NN))
        if first:
            back.to_mate(1, k, section)

    ahead = [(me.nx - section) % me.nx for section in range(me.nx)]
    away_ks = range(1, me.ny)
    for section in range(me.nx):
        out_x.pass_on(section)
        out_x.cross(0, section)
        if section == 0:
            for s in away_ks:
                for other in range(me.nx):
                    out_g.cross(s, other)
            for i in range(3):
                fetch[0, i].wait()
            forward(False, 0, 0)
            for i in range(3):
                fetch[1, i].wait()
            out_x.crossed[0, 0].wait_recv()
            forward(True, 0, 0)
    for section in range(me.nx):
        to = ahead[section]
        if section:
            forward(False, 0, to)
            out_x.crossed[0, section].wait_recv()
            forward(True, 0, to)
        for s in away_ks:
            out_x.cross(s, section)
        if section == 0:
            out_w.pass_column()
            out_w.cross(0)
        for s in away_ks:
            out_x.crossed[s, section].wait_recv()
            forward(True, me.ny - s, to)
        for k in away_ks:
            forward(False, k, to)
        back.along_y(0, to)
    for s in away_ks:
        out_w.cross(s)
    copies = [emit(0, x_ref, x_hbm), emit(1, hid, hid_hbm)]
    out_g.arrive()
    out_w.arrive()
    for n, to in enumerate(ahead):
        for k in away_ks:
            backward(True, k, to)
        for k in away_ks:
            backward(False, k, to)
        back.along_y(1, to)
        if n < me.nx - 1:
            back.finish(0, to)
    backward(True, 0, ahead[0])
    back.finish(0, ahead[-1])
    backward(False, 0, ahead[0])
    back.finish(1, ahead[0])
    back.across(0)
    for to in ahead[1:]:
        backward(True, 0, to)
        backward(False, 0, to)
    copies += [emit(2, dg_all, dg_hbm), emit(3, du_all, du_hbm), emit(4, gr_all, gr_hbm)]
    for to in ahead[1:]:
        back.finish(1, to)
    back.across(1)
    back.close()
    for copy in copies:
        copy.wait()
    for payload in (out_x, out_w, out_g):
        payload.close()
    rows_in.close()


def layer(sizes, micro, cap, layer_in, norms, table_t, router_t, info, cot, attn_w, expert_w):
    n_expert, ny, per_core = sizes[0], sizes[1] // 2, micro * cap
    seq, width = cot.shape
    units = expert_w[0].shape[1]
    heads = table_t.shape[0]
    count, size = ny * n_expert, 2 * per_core
    bf, f32 = jnp.bfloat16, jnp.float32
    any_space = pl.BlockSpec(memory_space=pl.ANY)
    inner = jax.ShapeDtypeStruct((2, count, size, units), bf)
    outer = jax.ShapeDtypeStruct((2, count, size, width), bf)
    low, full = jax.ShapeDtypeStruct((seq, width), bf), jax.ShapeDtypeStruct((seq, width), f32)
    return pl.pallas_call(
        functools.partial(layer_kernel, sizes, (micro, cap, per_core)),
        out_shape=(
            jax.ShapeDtypeStruct((2, 2, n_expert, size, width), bf), outer, inner, inner, inner, outer,
            low, low, low, jax.ShapeDtypeStruct((heads, seq, seq), f32), low, full, low,
            jax.ShapeDtypeStruct((8, seq), f32),
        ),
        in_specs=[VMEM] * 7 + [any_space] * 7,
        out_specs=(VMEM,) + (any_space,) * 5 + (VMEM,) * 8,
        scratch_shapes=[
            pltpu.VMEM(outer.shape, bf),
            pltpu.VMEM(inner.shape, bf),
            pltpu.VMEM(inner.shape, bf),
            pltpu.VMEM(inner.shape, bf),
            pltpu.VMEM(outer.shape, bf),
            pltpu.VMEM((2, count, size, width), bf),
            pltpu.VMEM((2, count, 8, 128), f32),
            pltpu.VMEM((max(4 * width, 6 * units), width), bf),
            pltpu.VMEM((2, count * size, units), f32),
            pltpu.VMEM((2, count * size, units), f32),
            pltpu.VMEM((2, count, size, width), bf),
            pltpu.VMEM((2, count * size, width), f32),
            DMA((4,)),
            DMA((2, 3)),
            DMA((5,)),
        ]
        + rows_scratch(sizes, per_core, seq, width)
        + spread_sems(sizes)
        + back_scratch(sizes, size, width),
        name="layer",
        compiler_params=pltpu.CompilerParams(
            collective_id=4, has_side_effects=True, vmem_limit_bytes=60 << 20
        ),
    )(layer_in, *norms, table_t, router_t, info, cot, *attn_w, *expert_w)


def finish_kernel(small, sums_hbm, lo_hbm, gi_hbm, x_hbm, h_hbm, dg_hbm, du_hbm, gr_hbm, *refs):
    outs, (router_out, attn_out, moe_out, table_out, lo_out, gi_out) = refs[:7], refs[7:13]
    lo, gi, sums, x, h, dg, du, gr, stage, sem_sum, sem_in, sem_out, sem_pass = refs[13:]
    slots, rows = stage.shape[:2]
    width = sums.shape[1]
    units = h.shape[2]
    loads = {}

    def load(key, src, dst, sem):
        loads[key] = pltpu.make_async_copy(src, dst, sem)
        loads[key].start()

    def load_sums(keys):
        for n in keys:
            part = n * rows // width, pl.ds(n * rows % width, rows)
            load(("sums", n), sums_hbm.at[part], sums.at[part], sem_sum.at[n])

    casts = range(4 * width // rows)
    load_sums(casts[:4])
    for i, (key, src, dst) in enumerate(
        (("dg", dg_hbm, dg), ("x", x_hbm, x), ("du", du_hbm, du), ("h", h_hbm, h), ("gr", gr_hbm, gr))
    ):
        for j in range(2):
            load((key, j), src.at[j], dst.at[j], sem_in.at[i, j])
    load_sums(casts[4:])
    load("lo", lo_hbm, lo, sem_pass.at[0])
    load("gi", gi_hbm, gi, sem_pass.at[1])
    experts = router_out.shape[0]
    router_out[...] = small[:experts]
    attn_out[...] = small[experts : experts + 1]
    moe_out[...] = small[experts + 1 : experts + 2]
    table_out[...] = small[experts + 8 : experts + 8 + table_out.shape[0], : table_out.shape[1]]

    def need(key):
        if key in loads:
            loads.pop(key).wait()

    jobs = []
    products = [
        (left, right, out, j, f)
        for left, right, out in ((("dg", dg), ("x", x), 4), (("du", du), ("x", x), 5), (("h", h), ("gr", gr), 6))
        for j in range(2)
        for f in range(0, units, rows)
    ]
    casts = list(casts)
    while casts or products:
        if casts:
            jobs.append(casts.pop(0))
        if products and (len(jobs) > 3 or not casts):
            jobs.append(products.pop(0))
    need("lo")
    need("gi")
    passed = [
        pltpu.make_async_copy(src, dst, sem_pass.at[i]) for i, (src, dst) in enumerate(((lo, lo_out), (gi, gi_out)))
    ]
    for copy in passed:
        copy.start()
    flying = [None] * slots
    for n, job in enumerate(jobs):
        slot = n % slots
        if flying[slot] is not None:
            flying[slot].wait()
        if isinstance(job, int):
            need(("sums", job))
            m, r = job * rows // width, job * rows % width
            stage[slot] = sums[m, r : r + rows, :].astype(jnp.float32)
            src, dst = stage.at[slot], outs[m].at[pl.ds(r, rows)]
        else:
            (left_key, left), (right_key, right), out, j, f = job
            need((left_key, j))
            need((right_key, j))
            size = min(rows, units - f)
            stage[slot, :size] = lax.dot_general(
                left[j, :, f : f + size], right[j], (((0,), (0,)), ((), ())),
                preferred_element_type=jnp.float32,
            )
            src, dst = stage.at[slot, pl.ds(0, size)], outs[out].at[j, pl.ds(f, size)]
        flying[slot] = pltpu.make_async_copy(src, dst, sem_out.at[slot])
        flying[slot].start()
    for copy in flying + passed:
        if copy is not None:
            copy.wait()


def finish(sums, small, low, full, x, h, dg, du, gr, experts, table):
    f32 = jnp.float32
    width = sums.shape[1]
    units = h.shape[2]
    any_space = pl.BlockSpec(memory_space=pl.ANY)
    return pl.pallas_call(
        finish_kernel,
        out_shape=(jax.ShapeDtypeStruct((width, width), f32),) * 4
        + (jax.ShapeDtypeStruct((2, units, width), f32),) * 3
        + tuple(jax.ShapeDtypeStruct(a, f32) for a in ((experts, width), (1, width), (1, width), table))
        + (jax.ShapeDtypeStruct(low.shape, low.dtype), jax.ShapeDtypeStruct(full.shape, f32)),
        in_specs=[VMEM] + [any_space] * 8,
        out_specs=(any_space,) * 7 + (VMEM,) * 4 + (any_space,) * 2,
        scratch_shapes=[pltpu.VMEM(a.shape, a.dtype) for a in (low, full, sums, x, h, dg, du, gr)]
        + [pltpu.VMEM((6, 256, width), f32), DMA((4 * width // 256,)), DMA((5, 2)), DMA((6,)), DMA((2,))],
        name="finish",
        compiler_params=pltpu.CompilerParams(vmem_limit_bytes=60 << 20),
    )(small, sums, low, full, x, h, dg, du, gr)


def upright(line):
    n = line.shape[1]
    square = lax.broadcasted_iota(jnp.int32, (n, n), 0) == lax.broadcasted_iota(jnp.int32, (n, n), 1)
    return jnp.sum(jnp.where(square, jnp.broadcast_to(line, (n, n)), 0.0), axis=1, keepdims=True)


def flat_line(column):
    n = column.shape[0]
    square = lax.broadcasted_iota(jnp.int32, (n, n), 0) == lax.broadcasted_iota(jnp.int32, (n, n), 1)
    return jnp.sum(jnp.where(square, jnp.broadcast_to(column, (n, n)), 0.0), axis=0, keepdims=True)


def diagonals(values):
    n = values.shape[1]
    total = None
    for first in range(0, n, 8):
        wide = jnp.concatenate([values[first : first + 8, :], jnp.zeros((8, n), jnp.float32)], axis=1)
        wide = pltpu.roll(wide, n - first, 1)
        total = wide if total is None else total + wide
    row = lax.broadcasted_iota(jnp.int32, total.shape, 0)
    for bit in (1, 2, 4):
        total = jnp.where((row & bit) > 0, pltpu.roll(total, 2 * n - bit, 1), total)
    return jnp.sum(total, axis=0, keepdims=True)


def settle_kernel(
    sizes, rows_per, pieces,
    back_ref, info_ref, gate_ref, cot_ref, layer_in, residual, context, attn_in, query, key, value, probs,
    norm_attn, norm_moe, router_t, wq_hbm, wk_hbm, wv_hbm, wo_hbm,
    layer_out, grad_in, out_hbm, small_out,
    weights, sem_a, left_ref, right_ref, small_ref, lines, out, sem_out, buf_a, buf_b, acc, *boxes,
):
    bf, f32 = jnp.bfloat16, jnp.float32
    micro, cap, per_core = rows_per
    attn_w = []
    for i, src in ((3, wo_hbm), (0, wq_hbm), (1, wk_hbm), (2, wv_hbm)):
        attn_w.append(pltpu.make_async_copy(src, weights.at[i], sem_a.at[i]))
        attn_w[-1].start()
    me = Place(*sizes)
    c, mate = me.c, me.at(c=1 - me.c)
    n = me.nx
    seq = right_ref.shape[1]
    total_rows = width = out.shape[1]
    is0 = c == 0
    pair = jnp.where(is0, me.x, me.y)
    other = jnp.where(is0, me.y, me.x)
    lo, hi, nh = pair % 2, pair // 2, n // 2

    def along(pair_at, other_at, z=None):
        return me.at(x=jnp.where(is0, pair_at, other_at), y=jnp.where(is0, other_at, pair_at), z=z)

    flip_x, flip_y = me.x + 1 - 2 * (me.x % 2), me.y + 1 - 2 * (me.y % 2)
    dims = [
        (n, other, lambda q: along(pair, q)),
        (nh, hi, lambda q: along(q * 2 + lo, other)),
        (2, me.z % 2, lambda q: me.at(z=me.z // 2 * 2 + q)),
        (me.nz // 2, me.z // 2, lambda q: me.at(z=q * 2 + me.z % 2)),
    ]
    parts, gots = boxes[:4], boxes[4:8]
    half, small_half, small_got, fs, fr, os, ps, pr, gs, gr, ms, mr, cs, cr, ss, sr = boxes[8:]
    levels = [i for i, d in enumerate(dims) if d[0] > 1]
    x_peers = [me.at(x=(me.x + k) % n) for k in range(1, n)]
    y_peers = [me.at(y=(me.y + k) % n) for k in range(1, n)]
    z_peers = [me.at(z=(me.z + k) % me.nz) for k in range(1, me.nz)]
    greet(
        [mate, me.at(x=flip_x, c=1 - c), me.at(y=flip_y, c=1 - c)] + x_peers + y_peers + z_peers
    )

    def slot_a(slot):
        return buf_a.at[pl.ds(pl.multiple_of(slot * seq, seq), seq), :]

    def slot_b(slot):
        return buf_b.at[pl.ds(pl.multiple_of(slot * seq, seq), seq), :]

    left_ref[0] = attn_in[...]
    left_ref[1] = context[...]
    targets = [
        (mate, 1 - c, other % 2, c),
        (me.at(x=flip_x, c=0), 0, flip_x % 2, 2 + c),
        (me.at(y=flip_y, c=1), 1, flip_y % 2, 2 + c),
    ]
    factor = []
    for i, (device, role, parity, slot) in enumerate(targets):
        a = jnp.where(role == 0, 0, parity)
        factor.append(remote(left_ref.at[a], slot_a(slot), fs.at[i, 0], fr.at[slot, 0], device))
    own = [pltpu.make_async_copy(left_ref.at[jnp.where(is0, 0, lo)], slot_a(c), os.at[0])]
    own[0].start()

    size = 2 * per_core
    group = lax.broadcasted_iota(jnp.int32, (1, seq), 1) // (seq // micro)
    slot_ids = lax.broadcasted_iota(jnp.int32, (2 * me.n_expert * size, seq), 0)
    hots = []
    for k in range(2):
        route, slot = info_ref[k : k + 1, :], info_ref[2 + k : 3 + k, :]
        place = (route % 2) * (me.n_expert * size) + (route // 2) * size + c * per_core + group * cap + slot
        hots.append(jnp.where(slot_ids == jnp.where(slot >= 0, place, -1), 1.0, 0.0))
    low = [h.astype(bf) for h in hots] + [(hots[0] + hots[1]).astype(bf)]
    half_slots = me.n_expert * size

    def picked(hot, which):
        total = None
        for j in range(2):
            rows = back_ref[which, j].reshape(half_slots, width)
            term = dot_as(hot[j * half_slots : (j + 1) * half_slots, :], rows, TN)
            total = term if total is None else total + term
        return total

    cot = cot_ref[...].astype(f32)
    resid = residual[...]
    chosen = [picked(low[k], 0) for k in range(2)]
    gate = [upright(gate_ref[k : k + 1, :]) for k in range(2)]
    layer_out[...] = (resid + (gate[0] * chosen[0] + gate[1] * chosen[1])).astype(bf)
    grad_gate = [jnp.sum(cot * chosen[k], axis=-1, keepdims=True) for k in range(2)]
    mean_grad = gate[0] * grad_gate[0] + gate[1] * grad_gate[1]
    logit = [gate[k] * (grad_gate[k] - mean_grad) for k in range(2)]
    experts = router_t.shape[0]
    by_token, by_expert = None, None
    for k in range(2):
        route = info_ref[k : k + 1, :]
        line = jnp.where(
            lax.broadcasted_iota(jnp.int32, (experts, seq), 0) == route, flat_line(logit[k]), 0.0
        )
        by_expert = line if by_expert is None else by_expert + line
        route_up = upright(route.astype(f32)).astype(jnp.int32)
        line = jnp.where(
            lax.broadcasted_iota(jnp.int32, (seq, experts), 1) == route_up, logit[k], 0.0
        )
        by_token = line if by_token is None else by_token + line

    def exact(left, right):
        return lax.dot_general(
            left, right, (NN, ((), ())), preferred_element_type=f32, precision=highest
        )

    scale = row_scale(resid)
    normed = resid * scale
    small_ref[:experts] = exact(by_expert, normed * norm_moe[...])
    grad_moe = picked(low[2], 1) + exact(by_token, router_t[...])
    small_ref[experts:] = jnp.zeros((small_ref.shape[0] - experts, width), f32)
    small_ref[experts + 1 : experts + 2] = jnp.sum(grad_moe * normed, axis=0, keepdims=True)
    grad_n = grad_moe * norm_moe[...]
    grad_resid = cot + scale * (grad_n - normed * jnp.mean(grad_n * normed, axis=-1, keepdims=True))
    right_ref[3] = grad_resid.astype(bf)
    grad_in[...] = grad_resid
    attn_w[0].wait()
    grad_context = dot_as(right_ref[3], weights[3], NT).astype(bf)

    heads = probs.shape[0]
    pair_lanes = 2 * width // heads
    low_half = lax.broadcasted_iota(jnp.int32, (seq, pair_lanes), 1) < pair_lanes // 2
    for n2 in range(heads // 2):
        lanes = slice(n2 * pair_lanes, (n2 + 1) * pair_lanes)
        sums = [None, None, None]
        for h in range(2):
            mine = low_half if h == 0 else ~low_half
            head = 2 * n2 + h

            def only(value):
                return jnp.where(mine, value, jnp.zeros_like(value))

            prob = probs[head]
            grad_c = only(grad_context[:, lanes])
            grad_p = dot_as(grad_c, value[:, lanes], NT)
            grad_s = prob * (grad_p - jnp.sum(prob * grad_p, axis=-1, keepdims=True))
            lines[head : head + 1, :] = diagonals(grad_s)
            grad_s = grad_s.astype(bf)
            terms = (
                dot_as(grad_s, only(key[:, lanes]), NN),
                dot_as(grad_s, only(query[:, lanes]), TN),
                dot_as(prob.astype(bf), grad_c, TN),
            )
            sums = [t if s is None else s + t for s, t in zip(sums, terms)]
        for i in range(3):
            right_ref[i, :, lanes] = sums[i].astype(bf)
    for i, (device, role, parity, slot) in enumerate(targets):
        factor.append(
            remote(right_ref.at[role * 2 + parity], slot_b(slot), fs.at[i, 1], fr.at[slot, 1], device)
        )
    own.append(pltpu.make_async_copy(right_ref.at[c * 2 + lo], slot_b(c), os.at[1]))
    own[1].start()
    buckets = 32
    bucket = bucket_of(lax.broadcasted_iota(jnp.int32, (2 * seq, buckets), 0) - seq)
    hot = jnp.where(bucket == lax.broadcasted_iota(jnp.int32, (2 * seq, buckets), 1), 1.0, 0.0)
    small_ref[experts + 8 : experts + 8 + heads, :buckets] = exact(lines[...], hot)
    grad_attn = None
    for i in range(3):
        attn_w[1 + i].wait()
        term = dot_as(right_ref[i], weights[i], NT)
        grad_attn = term if grad_attn is None else grad_attn + term
    rows = layer_in[...].astype(f32)
    scale = row_scale(rows)
    normed = rows * scale
    small_ref[experts : experts + 1] = jnp.sum(grad_attn * normed, axis=0, keepdims=True)
    grad_n = grad_attn * norm_attn[...]
    grad_in[...] += scale * (grad_n - normed * jnp.mean(grad_n * normed, axis=-1, keepdims=True))

    rows_s = half.shape[0]
    small = [remote(small_ref.at[pl.ds((1 - c) * rows_s, rows_s)], half, ss.at[0], sr.at[0], mate)]
    small_dims = [
        (n, me.x, lambda q: me.at(x=q)),
        (n, me.y, lambda q: me.at(y=q)),
        (me.nz, me.z, lambda q: me.at(z=q)),
    ]
    small_wait = [small[0]]
    small_slot = [1]

    def small_step(step):
        for copy in small_wait:
            copy.wait_recv()
        small_wait.clear()
        if step == 0:
            total = small_ref[pl.ds(c * rows_s, rows_s)] + half[...]
        elif step <= 3:
            total = small_got[step - 1, 0]
            for k in range(1, small_dims[step - 1][0]):
                total = total + small_got[step - 1, k]
        if step < 3:
            count, index, peer = small_dims[step]
            small_half[step] = total
            small_got[step, index] = total
            for k in range(1, count):
                small_wait.append(
                    remote(
                        small_half.at[step], small_got.at[step, index], ss.at[small_slot[0]],
                        sr.at[small_slot[0]], peer((index + k) % count),
                    )
                )
                small_slot[0] += 1
        elif step == 3:
            small_out[pl.ds(c * rows_s, rows_s)] = total
            block = small_out.at[pl.ds(c * rows_s, rows_s)]
            small_wait.append(
                remote(block, block, ss.at[small_slot[0]], sr.at[small_slot[0]], mate)
            )
        small.extend(small_wait)

    for where in (1 - c, 2, 3):
        for i, (src, dst) in enumerate(((left_ref, slot_a(where)), (right_ref, slot_b(where)))):
            pltpu.make_async_remote_copy(
                src_ref=src.at[0], dst_ref=dst, send_sem=fs.at[0, i], recv_sem=fr.at[where, i],
                device_id=mate, device_id_type=MESH,
            ).wait_recv()
    for copy in own:
        copy.wait()

    rows_k = total_rows // pieces
    matrix = c * 2 + lo
    pending, written = {}, []

    def multiply(k):
        acc[k] = lax.dot_general(
            buf_a[:, k * rows_k : (k + 1) * rows_k], buf_b[...], (TN, ((), ())),
            preferred_element_type=jnp.float32,
        )
        push(k, 0, rows_k)

    def push(k, at, rows):
        level = levels[at]
        count, index, peer = dims[level]
        size = rows // count
        copies = []
        for s in range(1, count):
            to = (index + s) % count
            parts[level][k, s - 1] = acc[k, pl.ds(pl.multiple_of(to * size, 16), size), :].astype(jnp.bfloat16)
            copies.append(
                remote(
                    parts[level].at[k, s - 1], gots[level].at[k, s - 1],
                    ps.at[level, k, s - 1], pr.at[level, k, s - 1], peer(to),
                )
            )
        pending["push", at, k] = copies

    def rows_at(at):
        rows = rows_k
        for i in range(at):
            rows //= dims[levels[i]][0]
        return rows

    def add(k, at):
        level = levels[at]
        count, index, _ = dims[level]
        size = rows_at(at) // count
        for copy in pending["push", at, k]:
            copy.wait_recv()
        total = acc[k, pl.ds(pl.multiple_of(index * size, 16), size), :]
        for s in range(1, count):
            total = total + gots[level][k, s - 1].astype(jnp.float32)
        if at + 1 < len(levels):
            acc[k, :size, :] = total
            push(k, at + 1, size)
        else:
            out[matrix, pl.ds(offset(k, at), size), :] = total.astype(jnp.bfloat16)
            share(k, at)

    def offset(k, at):
        start, rows = k * rows_k, rows_k
        for i in range(at + 1):
            count, index, _ = dims[levels[i]]
            rows //= count
            start = start + index * rows
        return pl.multiple_of(start, 16)

    def share(k, at):
        level = levels[at]
        count, index, peer = dims[level]
        size = rows_at(at) // count
        block = out.at[matrix, pl.ds(offset(k, at), size), :]
        pending["share", at, k] = [
            remote(block, block, gs.at[level, k, s - 1], gr.at[level, k, s - 1], peer((index + s) % count))
            for s in range(1, count)
        ]

    def shared(k, at):
        for copy in pending["share", at, k]:
            copy.wait_recv()
        if at:
            share(k, at - 1)
        else:
            block = out.at[matrix, pl.ds(k * rows_k, rows_k), :]
            pending["mate", k] = remote(
                block, block, ms.at[k], mr.at[k], along(pair + 1 - 2 * lo, other)
            )

    def across(k):
        pending["mate", k].wait_recv()
        block = out.at[pl.ds(2 * c, 2), pl.ds(k * rows_k, rows_k), :]
        pending["core", k] = remote(block, block, cs.at[k], cr.at[k], mate)
        write(k, c)

    def write(k, core):
        part = pl.ds(2 * core, 2), pl.ds(k * rows_k, rows_k), slice(None)
        written.append(pltpu.make_async_copy(out.at[part], out_hbm.at[part], sem_out.at[core, k]))
        written[-1].start()

    def close(k):
        pending["core", k].wait_recv()
        write(k, 1 - c)

    steps = [multiply]
    steps += [functools.partial(add, at=i) for i in range(len(levels))]
    steps += [functools.partial(shared, at=i) for i in reversed(range(len(levels)))]
    events = sorted((0 if p == 0 else p + k, p, k) for p in range(len(steps)) for k in range(pieces))
    before = 0
    for t, p, k in events:
        if before < t <= 5:
            small_step(t - 1)
        before = t
        steps[p](k)
    for k in range(pieces):
        across(k)
    for k in range(pieces):
        close(k)
    for copy in factor + small:
        copy.wait_send()
    for copies in pending.values():
        for copy in copies if isinstance(copies, list) else [copies]:
            copy.wait_send()
    for copy in written:
        copy.wait()


def settle(sizes, micro, cap, arrays, norms, router_t, attn_w):
    n_expert, n_dp = sizes
    nz = math.gcd(n_expert, 4)
    n = n_expert // nz
    nh = n // 2
    assert n == n_dp // 2
    seq, width = arrays[4].shape
    heads = arrays[11].shape[0]
    splits = [n, nh, 2, nz // 2]
    pieces = max(1, min(8, width // (16 * math.prod(splits))))
    rows_k = width // pieces
    bf, f32 = jnp.bfloat16, jnp.float32
    small_rows = router_t.shape[0] + 8 + heads
    small_rows += -small_rows % 16
    rows_s = small_rows // 2
    sizes_at = [rows_k // math.prod(splits[: i + 1]) for i in range(4)]
    counts = [max(q - 1, 1) for q in splits]
    most = max(counts)
    boxes = [
        pltpu.VMEM((pieces, q, s if k > 1 else 16, width), bf) for q, s, k in zip(counts, sizes_at, splits)
    ]
    smalls = 2 * n + nz
    any_space = pl.BlockSpec(memory_space=pl.ANY)
    return pl.pallas_call(
        functools.partial(settle_kernel, sizes, (micro, cap, micro * cap), pieces),
        out_shape=(
            jax.ShapeDtypeStruct((seq, width), bf),
            jax.ShapeDtypeStruct((seq, width), f32),
            jax.ShapeDtypeStruct((4, width, width), bf),
            jax.ShapeDtypeStruct((small_rows, width), f32),
        ),
        in_specs=[VMEM] * 15 + [any_space] * 4,
        out_specs=(VMEM, VMEM, any_space, VMEM),
        scratch_shapes=[
            pltpu.VMEM((4, width, width), bf),
            DMA((4,)),
            pltpu.VMEM((2, seq, width), bf),
            pltpu.VMEM((4, seq, width), bf),
            pltpu.VMEM((small_rows, width), f32),
            pltpu.VMEM((heads, 2 * seq), f32),
            pltpu.VMEM((4, width, width), bf),
            DMA((2, pieces)),
            pltpu.VMEM((4 * seq, width), bf),
            pltpu.VMEM((4 * seq, width), bf),
            pltpu.VMEM((pieces, rows_k, width), f32),
            *boxes,
            *boxes,
            pltpu.VMEM((rows_s, width), f32),
            pltpu.VMEM((3, rows_s, width), f32),
            pltpu.VMEM((3, max(n, nz), rows_s, width), f32),
            DMA((3, 2)),
            DMA((4, 2)),
            DMA((2,)),
            DMA((4, pieces, most)),
            DMA((4, pieces, most)),
            DMA((4, pieces, most)),
            DMA((4, pieces, most)),
            DMA((pieces,)),
            DMA((pieces,)),
            DMA((pieces,)),
            DMA((pieces,)),
            DMA((smalls,)),
            DMA((smalls,)),
        ],
        name="settle",
        compiler_params=pltpu.CompilerParams(
            collective_id=3, has_side_effects=True, vmem_limit_bytes=58 << 20
        ),
    )(*arrays, *norms, router_t, *attn_w)


def rms_scale(values):
    return lax.rsqrt(jnp.mean(values * values, axis=-1, keepdims=True) + epsilon)


def bucket_hot(seq_len, buckets):
    position = jnp.arange(seq_len, dtype=jnp.int32)
    bucket_ids = jnp.arange(buckets, dtype=jnp.int32)
    bucketed = bucket_of(position[None, :] - position[:, None])
    return (bucketed[None, :, :] == bucket_ids[:, None, None]).astype(jnp.float32)


def dot32(pattern, left, right):
    return jnp.einsum(pattern, left, right, preferred_element_type=jnp.float32)


def shards(
    layer_in, routes, queue_slots, norm_attn, w_query, w_key, w_value, w_out, rel_table,
    norm_moe, router, w_gate, w_up, w_down, cotangent,
):
    bf, f32 = jnp.bfloat16, jnp.float32
    seq_len, width = layer_in.shape
    buckets, heads = rel_table.shape
    expert_count = router.shape[1]
    sizes = (lax.axis_size("expert"), lax.axis_size("dp"))
    n_expert, n_dp = sizes
    assert w_gate.shape[0] == 2 and expert_count == 2 * n_expert
    group_len = seq_len // MICRO
    capacity = (5 * group_len + 2 * expert_count - 1) // (2 * expert_count)
    split_heads = (seq_len, heads, width // heads)
    info = jnp.concatenate([routes.T, queue_slots.T, jnp.zeros((4, seq_len), jnp.int32)])
    expert_w = [jnp.swapaxes(w_gate, 1, 2), jnp.swapaxes(w_up, 1, 2), w_down]
    slots = n_dp // 2 * n_expert * 2 * MICRO * capacity
    fused = 2 * slots * width * 20 + 6 * w_gate.size < 52 << 20
    if fused:
        (
            back, rows_in, hidden, gate_grad, up_grad, grad_rows,
            query, key, value, probs, context, residual, attn_in, gates,
        ) = layer(
            sizes, MICRO, capacity, layer_in, (norm_attn[None], norm_moe[None]), rel_table.T, router.T,
            info, cotangent, (w_query, w_key, w_value, w_out), expert_w,
        )
    else:
        layer_rows = layer_in.astype(f32)
        attn_in = (layer_rows * rms_scale(layer_rows) * norm_attn).astype(bf)
        query = dot32("sd,de->se", attn_in, w_query).astype(bf)
        key = dot32("sd,de->se", attn_in, w_key).astype(bf)
        value = dot32("sd,de->se", attn_in, w_value).astype(bf)
        one_hot = bucket_hot(seq_len, buckets)
        bias = jnp.einsum("bij,bh->hij", one_hot, rel_table, precision=highest)
        scores = dot32("ihd,jhd->hij", query.reshape(split_heads), key.reshape(split_heads)) + bias
        exponent = jnp.exp(scores - jnp.max(scores, axis=-1, keepdims=True))
        probs = exponent / jnp.sum(exponent, axis=-1, keepdims=True)
        context = dot32("hij,jhd->ihd", probs.astype(bf), value.reshape(split_heads))
        context = context.astype(bf).reshape(seq_len, width)
        residual = layer_rows + dot32("se,ed->sd", context, w_out)
        moe_in = residual * rms_scale(residual) * norm_moe
        expert_ids = jnp.arange(expert_count, dtype=jnp.int32)
        first_hot = (routes[:, 0:1] == expert_ids).astype(f32)
        second_hot = (routes[:, 1:2] == expert_ids).astype(f32)
        gate_prob = jax.nn.softmax(jnp.dot(moe_in, router, precision=highest), axis=-1)
        prob_first, prob_second = jnp.sum(gate_prob * first_hot, axis=-1), jnp.sum(gate_prob * second_hot, axis=-1)
        gates = jnp.stack([prob_first, prob_second]) / (prob_first + prob_second)
        gates = jnp.pad(gates, ((0, 6), (0, 0)))
        rows_in, weight_in, grad_in = spread(
            sizes, MICRO, capacity, info, moe_in.astype(bf), cotangent, gates
        )
        blocks = rows_in.shape[:-1] + (-1,)
        rows_in, grad_in = [a.reshape(2, -1, width) for a in (rows_in, grad_in)]
        slot_weight = weight_in[:, :, 0, : 2 * MICRO * capacity].reshape(2, -1, 1)
        grad_rows = (slot_weight * grad_in.astype(f32)).astype(bf)
        gate_pre = dot32("jrd,jdf->jrf", rows_in, w_gate)
        up_pre = dot32("jrd,jdf->jrf", rows_in, w_up)
        hidden, active, lean = gated_terms(gate_pre, up_pre)
        hidden = hidden.astype(bf)
        partial_out = dot32("jrf,jfd->jrd", hidden, w_down).astype(bf)
        hidden_grad = dot32("jrd,jfd->jrf", grad_rows, w_down)
        gate_grad, up_grad = (hidden_grad * lean).astype(bf), (hidden_grad * active).astype(bf)
        rows_grad = dot32("jrf,jdf->jrd", gate_grad, w_gate) + dot32("jrf,jdf->jrd", up_grad, w_up)
        back = gather_back(sizes, partial_out.reshape(blocks), rows_grad.astype(bf).reshape(blocks))
    layer_out, grad_input, sums, small = settle(
        sizes, MICRO, capacity,
        (back, info, gates, cotangent, layer_in, residual, context, attn_in, query, key, value, probs),
        (norm_attn[None], norm_moe[None]), router.T, (w_query, w_key, w_value, w_out),
    )
    rows_in, hidden, gate_grad, up_grad, grad_rows = [
        a.reshape(2, -1, a.shape[-1]) for a in (rows_in, hidden, gate_grad, up_grad, grad_rows)
    ]
    (
        *matrices, grad_w_gate, grad_w_up, grad_w_down,
        grad_router, grad_norm_attn, grad_norm_moe, grad_table, layer_out, grad_input,
    ) = finish(
        sums, small, layer_out, grad_input, rows_in, hidden, gate_grad, up_grad, grad_rows,
        expert_count, (heads, buckets),
    )
    return (
        layer_out, grad_input, grad_norm_attn.reshape(width), *matrices, grad_table.T,
        grad_norm_moe.reshape(width), grad_router.T,
        jnp.swapaxes(grad_w_gate, 1, 2), jnp.swapaxes(grad_w_up, 1, 2), grad_w_down,
    )


def solution(mesh):
    in_specs = (
        P(("expert", "dp"), None),
        P(("expert", "dp"), None),
        P(("expert", "dp"), None),
        P(),
        P(),
        P(),
        P(),
        P(),
        P(),
        P(),
        P(),
        P("expert", None, "dp"),
        P("expert", None, "dp"),
        P("expert", "dp", None),
        P(("expert", "dp"), None),
    )
    out_specs = (
        P(("expert", "dp"), None),
        P(("expert", "dp"), None),
        P(),
        P(),
        P(),
        P(),
        P(),
        P(),
        P(),
        P(),
        P("expert", None, "dp"),
        P("expert", None, "dp"),
        P("expert", "dp", None),
    )
    return jax.shard_map(shards, mesh=mesh, in_specs=in_specs, out_specs=out_specs, check_vma=False)
```

```python
import functools
import math

import jax
import jax.numpy as jnp
from jax import lax
from jax.experimental import pallas as pl
from jax.experimental.pallas import tpu as pltpu
from jax.sharding import PartitionSpec as P

MICRO = 4

epsilon = 1e-06
bucket_edges = (12, 16, 23, 32, 46, 64, 91)
highest = lax.Precision.HIGHEST

MESH = pl.DeviceIdType.MESH
VMEM = pl.BlockSpec(memory_space=pltpu.VMEM)
DMA = pltpu.SemaphoreType.DMA


class Place:
    def __init__(self, n_expert, n_dp):
        self.n_expert, self.n_dp = n_expert, n_dp
        self.nz = math.gcd(n_expert, 4)
        self.nx = n_expert // self.nz
        self.ny = n_dp // 2
        self.e = lax.axis_index("expert")
        self.d = lax.axis_index("dp")
        self.z, self.x = self.e // self.nx, self.e % self.nx
        self.y, self.c = self.d // 2, self.d % 2

    def at(self, z=None, x=None, y=None, c=None, e=None):
        z = self.z if z is None else z
        x = self.x if x is None else x
        y = self.y if y is None else y
        c = self.c if c is None else c
        e = z * self.nx + x if e is None else e
        return (e, y * 2 + c)


def remote(src, dst, send, recv, device):
    copy = pltpu.make_async_remote_copy(
        src_ref=src, dst_ref=dst, send_sem=send, recv_sem=recv, device_id=device, device_id_type=MESH
    )
    copy.start()
    return copy


def greet(devices):
    barrier = pltpu.get_barrier_semaphore()
    for device in devices:
        pl.semaphore_signal(barrier, inc=1, device_id=device, device_id_type=MESH)
    pl.semaphore_wait(barrier, len(devices))


def column_peers(me):
    out = [me.at(c=1 - me.c)]
    out += [me.at(y=(me.y + k) % me.ny) for k in range(1, me.ny)]
    out += [me.at(e=(me.e + k) % me.n_expert) for k in range(1, me.n_expert)]
    return out


class Spread:
    def __init__(self, me, rows, recv, sems):
        self.me, self.rows, self.recv = me, rows, recv
        self.se, self.re, self.sy, self.ry, self.sc, self.rc = sems
        self.came, self.along, self.crossed = {}, {}, {}

    def send(self):
        me = self.me
        for k in range(1, me.n_expert):
            to = (me.e + k) % me.n_expert
            self.came[k] = remote(
                self.rows.at[to], self.recv.at[me.c, me.y * me.n_expert + me.e],
                self.se.at[k], self.re.at[k], me.at(e=to),
            )
        self.recv[me.c, me.y * me.n_expert + me.e] = self.rows[me.e]

    def pass_on(self, blocks):
        me = self.me
        for k in blocks:
            if k:
                self.came[k].wait_recv()
            src = (me.e - k + me.n_expert) % me.n_expert
            block = self.recv.at[me.c, me.y * me.n_expert + src]
            for s in range(1, me.ny):
                self.along[s, k] = remote(
                    block, block, self.sy.at[s - 1, k], self.ry.at[s - 1, k], me.at(y=(me.y + s) % me.ny)
                )

    def pass_column(self):
        me = self.me
        for k in range(1, me.n_expert):
            self.came[k].wait_recv()
        block = self.recv.at[me.c, pl.ds(me.y * me.n_expert, me.n_expert)]
        for s in range(1, me.ny):
            self.along[s, 0] = remote(
                block, block, self.sy.at[s - 1, 0], self.ry.at[s - 1, 0], me.at(y=(me.y + s) % me.ny)
            )

    def cross(self, s):
        me = self.me
        if s:
            for key, copy in self.along.items():
                if key[0] == s:
                    copy.wait_recv()
        block = self.recv.at[me.c, pl.ds((me.y - s + me.ny) % me.ny * me.n_expert, me.n_expert)]
        self.crossed[s] = remote(block, block, self.sc.at[s], self.rc.at[s], me.at(c=1 - me.c))

    def arrive(self):
        for copy in self.crossed.values():
            copy.wait_recv()

    def close(self):
        for copies in (self.came, self.along, self.crossed):
            for copy in copies.values():
                copy.wait_send()


def spread_sems(sizes):
    n_expert, ny = sizes[0], sizes[1] // 2
    most = max(ny - 1, 1)
    return [
        DMA((3, n_expert)), DMA((3, n_expert)), DMA((3, most, n_expert)), DMA((3, most, n_expert)),
        DMA((3, ny)), DMA((3, ny)),
    ]


class Rows:
    def __init__(self, me, rows_per, info_all, gates, tok, send, recv):
        self.me, self.rows_per, self.info_all, self.gates, self.tok = me, rows_per, info_all, gates, tok
        self.send, self.recv, self.copies = send, recv, {}
        self.seq = tok.shape[2]

    def share(self, i, ref):
        block = ref.at[self.me.c]
        mate = self.me.at(c=1 - self.me.c)
        self.copies[i] = remote(block, block, self.send.at[i], self.recv.at[i], mate)

    def hots(self):
        me, seq = self.me, self.seq
        micro, cap, per_core = self.rows_per
        self.copies["info"].wait_recv()
        row_ids = lax.broadcasted_iota(jnp.int32, (me.n_expert * 2 * per_core, seq), 0)
        group = lax.broadcasted_iota(jnp.int32, (1, seq), 1) // (seq // micro)
        self.each = []
        for cc in range(2):
            for k in range(2):
                route = self.info_all[cc, k : k + 1, :]
                slot = self.info_all[cc, 2 + k : 3 + k, :]
                target = (route // 2) * (2 * per_core) + cc * per_core + group * cap + slot
                target = jnp.where((slot >= 0) & (route % 2 == me.c), target, -1)
                self.each.append(jnp.where(row_ids == target, 1.0, 0.0))
        self.both = [(self.each[2 * cc] + self.each[2 * cc + 1]).astype(jnp.bfloat16) for cc in range(2)]

    def gather(self, i):
        self.copies[i].wait_recv()
        total = None
        for cc in range(2):
            term = jnp.dot(self.both[cc], self.tok[i, cc], preferred_element_type=jnp.float32)
            total = term if total is None else total + term
        return total.astype(jnp.bfloat16).reshape(self.me.n_expert, 2 * self.rows_per[2], -1)

    def weights(self):
        self.copies["gates"].wait_recv()
        size = 2 * self.rows_per[2]
        column = None
        for n, hot in enumerate(self.each):
            term = jnp.sum(hot * self.gates[n // 2, n % 2 : n % 2 + 1, :], axis=1, keepdims=True)
            column = term if column is None else column + term
        lane = lax.broadcasted_iota(jnp.int32, (size, 128), 1)
        row = lax.broadcasted_iota(jnp.int32, (size, 128), 0)
        tiles = []
        for e in range(self.me.n_expert):
            block = jnp.where(lane == row, column[e * size : (e + 1) * size, :], 0.0)
            tiles.append(jnp.broadcast_to(jnp.sum(block, axis=0, keepdims=True), (8, 128)))
        return tiles

    def close(self):
        for copy in self.copies.values():
            copy.wait_send()


NAMED = ("info", "gates", 0, 1)


class Named:
    def __init__(self, sems):
        self.at = {name: sems.at[i] for i, name in enumerate(NAMED)}


def rows_scratch(sizes, per_core, seq, width):
    mine = (sizes[0], 2 * per_core, width)
    bf = jnp.bfloat16
    return [
        pltpu.VMEM((2, 8, seq), jnp.int32),
        pltpu.VMEM((2, 8, seq), jnp.float32),
        pltpu.VMEM((2, 2, seq, width), bf),
        DMA((4,)),
        DMA((4,)),
        pltpu.VMEM(mine, bf),
        pltpu.VMEM((sizes[0], 8, 128), jnp.float32),
        pltpu.VMEM(mine, bf),
    ]


def rows_of(me, rows_per, scratch):
    info_all, gates, tok, send, recv = scratch[:5]
    return Rows(me, rows_per, info_all, gates, tok, Named(send), Named(recv))


def spread_kernel(sizes, rows_per, info_ref, moe_ref, cot_ref, w_ref, x_out, w_out, g_out, *scratch):
    me = Place(*sizes)
    c = me.c
    greet(column_peers(me))
    scratch, sems = scratch[:8], scratch[8:]
    rows = rows_of(me, rows_per, scratch)
    info_all, gates, tok = scratch[:3]
    info_all[c] = info_ref[...]
    rows.share("info", info_all)
    gates[c] = w_ref[...]
    rows.share("gates", gates)
    for i, ref in enumerate((moe_ref, cot_ref)):
        tok[i, c] = ref[...]
        rows.share(i, tok.at[i])
    rows.hots()
    buf_x, buf_w, buf_g = scratch[5:]
    out_x, out_w, out_g = [
        Spread(me, buf, recv, [s.at[i] for s in sems])
        for i, (buf, recv) in enumerate(((buf_x, x_out), (buf_w, w_out), (buf_g, g_out)))
    ]
    for i, payload in enumerate((out_x, out_g)):
        payload.rows[...] = rows.gather(i)
        payload.send()
    for e, tile in enumerate(rows.weights()):
        buf_w[e] = tile
    out_w.send()
    for payload in (out_x, out_g):
        payload.pass_on(range(me.n_expert))
        payload.cross(0)
    out_w.pass_column()
    out_w.cross(0)
    for payload in (out_x, out_g, out_w):
        for s in range(1, me.ny):
            payload.cross(s)
    for payload in (out_x, out_g, out_w):
        payload.arrive()
        payload.close()
    rows.close()


def spread(sizes, micro, cap, info, moe, cot, weights):
    n_expert, ny, per_core = sizes[0], sizes[1] // 2, micro * cap
    seq, width = cot.shape
    block = (2, ny * n_expert, 2 * per_core)
    bf = jnp.bfloat16
    return pl.pallas_call(
        functools.partial(spread_kernel, sizes, (micro, cap, per_core)),
        out_shape=(
            jax.ShapeDtypeStruct(block + (width,), bf),
            jax.ShapeDtypeStruct(block[:2] + (8, 128), jnp.float32),
            jax.ShapeDtypeStruct(block + (width,), bf),
        ),
        in_specs=[VMEM] * 4,
        out_specs=(VMEM,) * 3,
        scratch_shapes=rows_scratch(sizes, per_core, seq, width) + spread_sems(sizes),
        name="spread",
        compiler_params=pltpu.CompilerParams(
            collective_id=1, has_side_effects=True, vmem_limit_bytes=48 << 20
        ),
    )(info, moe, cot, weights)


class Back:
    def __init__(self, me, away, own, q_out, r1, stage, r2, final, sems):
        self.me, self.away, self.own = me, away, own
        self.q_out, self.r1, self.stage, self.r2, self.final = q_out, r1, stage, r2, final
        self.sems = sems
        self.ys = [(me.y + k) % me.ny for k in range(me.ny)]
        self.order = list(range(1, me.n_expert)) + [0]
        self.first, self.second, self.third, self.fourth = {}, {}, {}, {}
        self.arrived = set()

    def to_mate(self, i, k):
        me = self.me
        column = pl.ds(self.ys[k] * me.n_expert, me.n_expert)
        self.first[i, k] = remote(
            self.away(i).at[column], self.r1.at[i, column], self.sems[0].at[i, k], self.sems[1].at[i, k],
            me.at(c=1 - me.c),
        )

    def partial(self, i, y, e):
        block = y * self.me.n_expert + e
        return self.own(i, block) + self.r1[i, block].astype(jnp.float32)

    def along_y(self, i):
        me = self.me
        for k in range(1, me.ny):
            self.first[i, k].wait_recv()
            for j in self.order:
                e = (me.e + j) % me.n_expert
                self.stage[i, k - 1, e] = self.partial(i, self.ys[k], e).astype(jnp.bfloat16)
                self.second[i, k, j] = remote(
                    self.stage.at[i, k - 1, e], self.r2.at[i, k - 1, e],
                    self.sems[2].at[i, k - 1, j], self.sems[3].at[i, k - 1, j], me.at(y=self.ys[k]),
                )

    def finish(self, i, order):
        me = self.me
        if (i, 0) not in self.arrived:
            self.arrived.add((i, 0))
            self.first[i, 0].wait_recv()
        for j in order:
            e = (me.e + j) % me.n_expert
            total = self.partial(i, me.y, e)
            for k in range(1, me.ny):
                self.second[i, k, j].wait_recv()
                total = total + self.r2[i, k - 1, e].astype(jnp.float32)
            if j:
                self.final[i, e] = total.astype(jnp.bfloat16)
                self.third[i, j] = remote(
                    self.final.at[i, e], self.q_out.at[i, me.c, me.e],
                    self.sems[4].at[i, j], self.sems[5].at[i, j], me.at(e=e),
                )
            else:
                self.q_out[i, me.c, me.e] = total.astype(jnp.bfloat16)

    def across(self, i):
        for j in self.order[:-1]:
            self.third[i, j].wait_recv()
        block = self.q_out.at[i, self.me.c]
        s, r = self.sems[6].at[i], self.sems[7].at[i]
        self.fourth[i] = remote(block, block, s, r, self.me.at(c=1 - self.me.c))

    def close(self):
        for copy in self.fourth.values():
            copy.wait()
        for copies in (self.first, self.second, self.third):
            for copy in copies.values():
                copy.wait_send()


def back_scratch(sizes, size, width):
    n_expert, ny = sizes[0], sizes[1] // 2
    most = max(ny - 1, 1)
    bf = jnp.bfloat16
    return [
        pltpu.VMEM((2, ny * n_expert, size, width), bf),
        pltpu.VMEM((2, most, n_expert, size, width), bf),
        pltpu.VMEM((2, most, n_expert, size, width), bf),
        pltpu.VMEM((2, n_expert, size, width), bf),
        DMA((2, ny)),
        DMA((2, ny)),
        DMA((2, most, n_expert)),
        DMA((2, most, n_expert)),
        DMA((2, n_expert)),
        DMA((2, n_expert)),
        DMA((2,)),
        DMA((2,)),
    ]


def gather_back_kernel(sizes, p0_ref, p1_ref, q_out, *scratch):
    me = Place(*sizes)
    greet(column_peers(me))
    p_refs = (p0_ref, p1_ref)
    back = Back(
        me, lambda i: p_refs[i].at[1 - me.c],
        lambda i, block: p_refs[i][me.c, block].astype(jnp.float32), q_out, *scratch[:4], scratch[4:],
    )
    for i in range(2):
        for k in reversed(range(me.ny)):
            back.to_mate(i, k)
    for i in range(2):
        back.along_y(i)
    for i in range(2):
        back.finish(i, back.order)
        back.across(i)
    back.close()


def gather_back(sizes, first, second):
    n_expert = sizes[0]
    _, _, size, width = first.shape
    return pl.pallas_call(
        functools.partial(gather_back_kernel, sizes),
        out_shape=jax.ShapeDtypeStruct((2, 2, n_expert, size, width), jnp.bfloat16),
        in_specs=[VMEM] * 2,
        out_specs=VMEM,
        scratch_shapes=back_scratch(sizes, size, width),
        name="gather_back",
        compiler_params=pltpu.CompilerParams(
            collective_id=2, has_side_effects=True, vmem_limit_bytes=48 << 20
        ),
    )(first, second)


def gated_terms(gate_pre, up_pre):
    root = math.sqrt(2.0 / math.pi)
    square = gate_pre * gate_pre
    bend = jnp.tanh(root * (gate_pre + 0.044715 * square * gate_pre))
    half = 0.5 * (1.0 + bend)
    active = gate_pre * half
    slope = half + 0.5 * gate_pre * (1.0 - bend * bend) * root * (1.0 + 3 * 0.044715 * square)
    return active * up_pre, active, up_pre * slope


def bucket_of(relative):
    distance = jnp.abs(relative)
    far_bucket = jnp.full_like(distance, 8)
    for threshold in bucket_edges:
        far_bucket = far_bucket + (distance >= threshold).astype(jnp.int32)
    return jnp.where(distance < 8, distance, far_bucket) + 16 * (relative > 0).astype(jnp.int32)


def row_scale(values):
    return lax.rsqrt(jnp.mean(values * values, axis=-1, keepdims=True) + epsilon)


def dot_as(left, right, contract):
    return lax.dot_general(left, right, (contract, ((), ())), preferred_element_type=jnp.float32)


NN, NT, TN = ((1,), (0,)), ((1,), (1,)), ((0,), (0,))


def layer_kernel(
    sizes, rows_per, layer_in, norm_attn, norm_moe, table_t, router_t, route_ref, slot_ref, cot_ref,
    wq_hbm, wk_hbm, wv_hbm, wo_hbm, wg_hbm, wu_hbm, wd_hbm,
    q_out, x_hbm, hid_hbm, dg_hbm, du_hbm, gr_hbm, query, key, value, probs, context, residual, attn_in, gate_out,
    x_ref, hid_out, dg_out, du_out, gr_out, g_ref, w_ref, weights, act, slope, away, own,
    sem_a, sem_w, sem_e, *scratch,
):
    me = Place(*sizes)
    c = me.c
    seq, width = layer_in.shape
    heads, buckets = table_t.shape
    units = wg_hbm.shape[1]
    bf, f32 = jnp.bfloat16, jnp.float32

    attn_w = []
    for i, src in enumerate((wq_hbm, wk_hbm, wv_hbm, wo_hbm)):
        dst = weights.at[pl.ds(i * width, width)]
        attn_w.append(pltpu.make_async_copy(src, dst, sem_a.at[i]))
        attn_w[-1].start()
    greet(column_peers(me))
    rows_in = rows_of(me, rows_per, scratch[:8])
    info_all, gates, tok = scratch[:3]
    buf_x, buf_w, buf_g = scratch[5:8]
    out_x, out_w, out_g = [
        Spread(me, buf, recv, [s.at[i] for s in scratch[8:14]])
        for i, (buf, recv) in enumerate(((buf_x, x_ref), (buf_w, w_ref), (buf_g, g_ref)))
    ]
    scratch = scratch[14:]
    column = me.n_expert
    quarter = [range(i * column // 4, (i + 1) * column // 4) for i in range(4)]
    info_all[c, 0:2, :] = route_ref[...]
    info_all[c, 2:4, :] = slot_ref[...]
    info_all[c, 4:, :] = jnp.zeros((4, seq), jnp.int32)
    rows_in.share("info", info_all)
    tok[1, c] = cot_ref[...]
    rows_in.share(1, tok.at[1])
    rows = layer_in[...].astype(f32)
    attn_in[...] = (rows * row_scale(rows) * norm_attn[...]).astype(bf)
    rows_in.hots()
    buf_g[...] = rows_in.gather(1)
    out_g.send()
    for i, ref in enumerate((query, key, value)):
        attn_w[i].wait()
        ref[...] = dot_as(attn_in[...], weights[i * width : (i + 1) * width, :], NN).astype(bf)
    relative = lax.broadcasted_iota(jnp.int32, (heads, 2 * seq), 1) - seq
    bucket = bucket_of(relative)
    bias_of = jnp.zeros((heads, 2 * seq), f32)
    for n in range(buckets):
        bias_of = jnp.where(bucket == n, table_t[:, n : n + 1], bias_of)
    pair = 2 * width // heads
    low_half = lax.broadcasted_iota(jnp.int32, (seq, pair), 1) < pair // 2
    for n in range(heads // 2):
        lanes = slice(n * pair, (n + 1) * pair)
        k2, v2 = key[:, lanes], value[:, lanes]
        total = None
        for h in range(2):
            mine = low_half if h == 0 else ~low_half
            head = 2 * n + h
            line = jnp.broadcast_to(bias_of[head : head + 1, :], (seq, 2 * seq))
            bias = pltpu.roll(line, seq, 1, stride=1, stride_axis=0)[:, :seq]
            scores = dot_as(query[:, lanes], jnp.where(mine, k2, jnp.zeros_like(k2)), NT) + bias
            exponent = jnp.exp(scores - jnp.max(scores, axis=-1, keepdims=True))
            prob = exponent / jnp.sum(exponent, axis=-1, keepdims=True)
            probs[head] = prob
            term = dot_as(prob.astype(bf), jnp.where(mine, v2, jnp.zeros_like(v2)), NN)
            total = term if total is None else total + term
        context[:, lanes] = total.astype(bf)
        if n % 4 == 3:
            out_g.pass_on(quarter[n // 4])
    attn_w[3].wait()
    resid = rows + dot_as(context[...], weights[3 * width : 4 * width, :], NN)
    residual[...] = resid
    fetch = {}
    for n, j in enumerate((c, 1 - c)):
        for i, src in enumerate((wg_hbm, wu_hbm, wd_hbm)):
            dst = weights.at[pl.ds(pl.multiple_of((2 * i + j) * units, 16), units)]
            fetch[n, i] = pltpu.make_async_copy(src.at[j], dst, sem_w.at[n, i])
            fetch[n, i].start()
    moe_in = resid * row_scale(resid) * norm_moe[...]
    tok[0, c] = moe_in.astype(bf)
    rows_in.share(0, tok.at[0])
    logits = lax.dot_general(
        router_t[...], moe_in, (NT, ((), ())), preferred_element_type=f32, precision=highest
    )
    logits = jnp.exp(logits - jnp.max(logits, axis=0, keepdims=True))
    gate_prob = logits / jnp.sum(logits, axis=0, keepdims=True)
    expert_ids = lax.broadcasted_iota(jnp.int32, gate_prob.shape, 0)
    picked = [
        jnp.sum(jnp.where(route_ref[k : k + 1, :] == expert_ids, gate_prob, 0.0), axis=0, keepdims=True)
        for k in range(2)
    ]
    both = picked[0] + picked[1]
    for k in range(2):
        gates[c, k : k + 1, :] = picked[k] / both
    gates[c, 2:, :] = jnp.zeros((6, seq), f32)
    gate_out[...] = gates[c]
    rows_in.share("gates", gates)
    buf_x[...] = rows_in.gather(0)
    out_x.send()
    out_g.pass_on(quarter[2])
    for e, tile in enumerate(rows_in.weights()):
        buf_w[e] = tile
    out_w.send()
    out_g.pass_on(quarter[3])
    out_g.cross(0)

    size = x_ref.shape[2]
    step = math.gcd(column, 4)
    chunk = step * size
    back = Back(
        me, lambda i: away.at[i],
        lambda i, block: own[i, pl.ds(pl.multiple_of(block * size, 8), size), :],
        q_out, *scratch[:4], scratch[4:],
    )

    def emit(i, src, dst):
        copy = pltpu.make_async_copy(src, dst, sem_e.at[i])
        copy.start()
        return copy

    def part(i, j):
        return weights[pl.ds(pl.multiple_of((2 * i + j) * units, 16), units), :]

    def flat(value):
        return value.reshape(chunk, value.shape[-1])

    def blocks(value):
        return value.reshape(step, size, value.shape[-1])

    def store(i, first, some, rows, value):
        if first:
            away[i, some] = blocks(value.astype(bf))
        else:
            own[i, rows, :] = value

    def each(start, count, body):
        @pl.loop(0, count // step)
        def _(n):
            at = start + n * step
            body(pl.ds(at, step), pl.ds(pl.multiple_of(at * size, 8), chunk))

    def forward(first, j, start, count):
        def body(some, rows):
            x = flat(x_ref[j, some])
            gate_pre = dot_as(x, part(0, j), NT)
            up_pre = dot_as(x, part(1, j), NT)
            hidden, active, lean = gated_terms(gate_pre, up_pre)
            act[j, rows, :] = active
            slope[j, rows, :] = lean
            hidden = hidden.astype(bf)
            hid_out[j, some] = blocks(hidden)
            store(0, first, some, rows, dot_as(hidden, part(2, j), NN))

        each(start, count, body)

    lane = lax.broadcasted_iota(jnp.int32, (size, 128), 1)
    row = lax.broadcasted_iota(jnp.int32, (size, 128), 0)

    def backward(first, j, start, count):
        def body(some, rows):
            tiles = w_ref[j, some]
            grad = []
            for n in range(step):
                line = jnp.broadcast_to(tiles[n, 0:1, :], (size, 128))
                weight = jnp.sum(jnp.where(lane == row, line, 0.0), axis=1, keepdims=True)
                grad.append(weight * g_ref[j, some.start + n].astype(f32))
            grad = jnp.concatenate(grad, axis=0).astype(bf)
            gr_out[j, some] = blocks(grad)
            grad_hidden = dot_as(grad, part(2, j), NT)
            dg = (grad_hidden * slope[j, rows, :]).astype(bf)
            du = (grad_hidden * act[j, rows, :]).astype(bf)
            dg_out[j, some] = blocks(dg)
            du_out[j, some] = blocks(du)
            store(1, first, some, rows, dot_as(dg, part(0, j), NN) + dot_as(du, part(1, j), NN))

        each(start, count, body)

    here = me.y * column
    away_ys = [back.ys[k] * column for k in range(1, me.ny)]
    shares = [back.order[i * column // 4 : (i + 1) * column // 4] for i in range(4)]
    out_x.pass_on(range(column))
    out_x.cross(0)
    for s in range(1, me.ny):
        out_g.cross(s)
    for i in range(3):
        fetch[0, i].wait()
    forward(False, c, here, column)
    for i in range(3):
        fetch[1, i].wait()
    out_x.crossed[0].wait_recv()
    forward(True, 1 - c, here, column)
    back.to_mate(0, 0)
    out_w.pass_column()
    out_w.cross(0)
    for s in range(1, me.ny):
        out_x.cross(s)
    for k in range(1, me.ny):
        out_x.crossed[k].wait_recv()
        forward(True, 1 - c, away_ys[k - 1], column)
        back.to_mate(0, k)
    for s in range(1, me.ny):
        out_w.cross(s)
    for k in range(1, me.ny):
        forward(False, c, away_ys[k - 1], column)
    back.along_y(0)
    out_g.arrive()
    out_w.arrive()
    for k in range(1, me.ny):
        backward(True, 1 - c, away_ys[k - 1], column)
        back.to_mate(1, k)
    back.finish(0, shares[0])
    for k in range(1, me.ny):
        backward(False, c, away_ys[k - 1], column)
    back.along_y(1)
    back.finish(0, shares[1])
    backward(True, 1 - c, here, column)
    back.to_mate(1, 0)
    back.finish(0, shares[2])
    backward(False, c, here, column)
    saved = ((x_ref, x_hbm), (hid_out, hid_hbm), (dg_out, dg_hbm), (du_out, du_hbm), (gr_out, gr_hbm))
    copies = [emit(i, src, dst) for i, (src, dst) in enumerate(saved)]
    back.finish(0, shares[3])
    back.across(0)
    back.finish(1, back.order)
    back.across(1)
    back.close()
    for copy in copies:
        copy.wait()
    for payload in (out_x, out_w, out_g):
        payload.close()
    rows_in.close()


def layer(sizes, micro, cap, layer_in, norms, table_t, router_t, places, cot, attn_w, expert_w):
    n_expert, ny, per_core = sizes[0], sizes[1] // 2, micro * cap
    seq, width = cot.shape
    units = expert_w[0].shape[1]
    heads = table_t.shape[0]
    count, size = ny * n_expert, 2 * per_core
    bf, f32 = jnp.bfloat16, jnp.float32
    any_space = pl.BlockSpec(memory_space=pl.ANY)
    inner = jax.ShapeDtypeStruct((2, count, size, units), bf)
    outer = jax.ShapeDtypeStruct((2, count, size, width), bf)
    low, full = jax.ShapeDtypeStruct((seq, width), bf), jax.ShapeDtypeStruct((seq, width), f32)
    return pl.pallas_call(
        functools.partial(layer_kernel, sizes, (micro, cap, per_core)),
        out_shape=(
            jax.ShapeDtypeStruct((2, 2, n_expert, size, width), bf), outer, inner, inner, inner, outer,
            low, low, low, jax.ShapeDtypeStruct((heads, seq, seq), f32), low, full, low,
            jax.ShapeDtypeStruct((8, seq), f32),
        ),
        in_specs=[VMEM] * 8 + [any_space] * 7,
        out_specs=(VMEM,) + (any_space,) * 5 + (VMEM,) * 8,
        scratch_shapes=[
            pltpu.VMEM(outer.shape, bf),
            pltpu.VMEM(inner.shape, bf),
            pltpu.VMEM(inner.shape, bf),
            pltpu.VMEM(inner.shape, bf),
            pltpu.VMEM(outer.shape, bf),
            pltpu.VMEM((2, count, size, width), bf),
            pltpu.VMEM((2, count, 8, 128), f32),
            pltpu.VMEM((max(4 * width, 6 * units), width), bf),
            pltpu.VMEM((2, count * size, units), f32),
            pltpu.VMEM((2, count * size, units), f32),
            pltpu.VMEM((2, count, size, width), bf),
            pltpu.VMEM((2, count * size, width), f32),
            DMA((4,)),
            DMA((2, 3)),
            DMA((5,)),
        ]
        + rows_scratch(sizes, per_core, seq, width)
        + spread_sems(sizes)
        + back_scratch(sizes, size, width),
        name="layer",
        compiler_params=pltpu.CompilerParams(
            collective_id=4, has_side_effects=True, vmem_limit_bytes=60 << 20
        ),
    )(layer_in, *norms, table_t, router_t, *places, cot, *attn_w, *expert_w)


def finish_kernel(small, sums_hbm, x_hbm, h_hbm, dg_hbm, du_hbm, gr_hbm, *refs):
    outs, (router_out, attn_out, moe_out, table_out) = refs[:7], refs[7:11]
    sums, x, h, dg, du, gr, stage, sem_sum, sem_in, sem_out = refs[11:]
    slots, rows = stage.shape[:2]
    width = sums.shape[1]
    units = h.shape[2]
    loads = {}

    def load(key, src, dst, sem):
        loads[key] = pltpu.make_async_copy(src, dst, sem)
        loads[key].start()

    def load_sums(keys):
        for n in keys:
            part = n * rows // width, pl.ds(n * rows % width, rows)
            load(("sums", n), sums_hbm.at[part], sums.at[part], sem_sum.at[n])

    casts = range(4 * width // rows)
    load_sums(casts[:4])
    for i, (key, src, dst) in enumerate(
        (("dg", dg_hbm, dg), ("x", x_hbm, x), ("du", du_hbm, du), ("h", h_hbm, h), ("gr", gr_hbm, gr))
    ):
        for j in range(2):
            load((key, j), src.at[j], dst.at[j], sem_in.at[i, j])
    load_sums(casts[4:])
    experts = router_out.shape[0]
    router_out[...] = small[:experts]
    attn_out[...] = small[experts : experts + 1]
    moe_out[...] = small[experts + 1 : experts + 2]
    table_out[...] = small[experts + 8 : experts + 8 + table_out.shape[0], : table_out.shape[1]]

    def need(key):
        if key in loads:
            loads.pop(key).wait()

    jobs = []
    products = [
        (left, right, out, j, f)
        for left, right, out in ((("dg", dg), ("x", x), 4), (("du", du), ("x", x), 5), (("h", h), ("gr", gr), 6))
        for j in range(2)
        for f in range(0, units, rows)
    ]
    casts = list(casts)
    while casts or products:
        if casts:
            jobs.append(casts.pop(0))
        if products and (len(jobs) > 3 or not casts):
            jobs.append(products.pop(0))
    flying = [None] * slots
    for n, job in enumerate(jobs):
        slot = n % slots
        if flying[slot] is not None:
            flying[slot].wait()
        if isinstance(job, int):
            need(("sums", job))
            m, r = job * rows // width, job * rows % width
            stage[slot] = sums[m, r : r + rows, :].astype(jnp.float32)
            src, dst = stage.at[slot], outs[m].at[pl.ds(r, rows)]
        else:
            (left_key, left), (right_key, right), out, j, f = job
            need((left_key, j))
            need((right_key, j))
            size = min(rows, units - f)
            stage[slot, :size] = lax.dot_general(
                left[j, :, f : f + size], right[j], (((0,), (0,)), ((), ())),
                preferred_element_type=jnp.float32,
            )
            src, dst = stage.at[slot, pl.ds(0, size)], outs[out].at[j, pl.ds(f, size)]
        flying[slot] = pltpu.make_async_copy(src, dst, sem_out.at[slot])
        flying[slot].start()
    for copy in flying:
        if copy is not None:
            copy.wait()


def finish(sums, small, x, h, dg, du, gr, experts, table):
    f32 = jnp.float32
    width = sums.shape[1]
    units = h.shape[2]
    any_space = pl.BlockSpec(memory_space=pl.ANY)
    return pl.pallas_call(
        finish_kernel,
        out_shape=(jax.ShapeDtypeStruct((width, width), f32),) * 4
        + (jax.ShapeDtypeStruct((2, units, width), f32),) * 3
        + tuple(jax.ShapeDtypeStruct(a, f32) for a in ((experts, width), (1, width), (1, width), table)),
        in_specs=[VMEM] + [any_space] * 6,
        out_specs=(any_space,) * 7 + (VMEM,) * 4,
        scratch_shapes=[pltpu.VMEM(a.shape, a.dtype) for a in (sums, x, h, dg, du, gr)]
        + [pltpu.VMEM((6, 256, width), f32), DMA((4 * width // 256,)), DMA((5, 2)), DMA((6,))],
        name="finish",
        compiler_params=pltpu.CompilerParams(vmem_limit_bytes=60 << 20),
    )(small, sums, x, h, dg, du, gr)


def upright(line):
    n = line.shape[1]
    square = lax.broadcasted_iota(jnp.int32, (n, n), 0) == lax.broadcasted_iota(jnp.int32, (n, n), 1)
    return jnp.sum(jnp.where(square, jnp.broadcast_to(line, (n, n)), 0.0), axis=1, keepdims=True)


def flat_line(column):
    n = column.shape[0]
    square = lax.broadcasted_iota(jnp.int32, (n, n), 0) == lax.broadcasted_iota(jnp.int32, (n, n), 1)
    return jnp.sum(jnp.where(square, jnp.broadcast_to(column, (n, n)), 0.0), axis=0, keepdims=True)


def diagonals(values):
    n = values.shape[1]
    total = None
    for first in range(0, n, 8):
        wide = jnp.concatenate([values[first : first + 8, :], jnp.zeros((8, n), jnp.float32)], axis=1)
        wide = pltpu.roll(wide, n - first, 1)
        total = wide if total is None else total + wide
    row = lax.broadcasted_iota(jnp.int32, total.shape, 0)
    for bit in (1, 2, 4):
        total = jnp.where((row & bit) > 0, pltpu.roll(total, 2 * n - bit, 1), total)
    return jnp.sum(total, axis=0, keepdims=True)


def settle_kernel(
    sizes, rows_per, pieces,
    back_ref, route_ref, slot_ref, gate_ref, cot_ref, layer_in, residual, context, attn_in, query, key, value, probs,
    norm_attn, norm_moe, router_t, wq_hbm, wk_hbm, wv_hbm, wo_hbm,
    layer_out, grad_in, out_hbm, small_out,
    weights, sem_a, left_ref, right_ref, small_ref, lines, out, sem_out, buf_a, buf_b, acc, *boxes,
):
    bf, f32 = jnp.bfloat16, jnp.float32
    micro, cap, per_core = rows_per
    attn_w = []
    for i, src in ((3, wo_hbm), (0, wq_hbm), (1, wk_hbm), (2, wv_hbm)):
        attn_w.append(pltpu.make_async_copy(src, weights.at[i], sem_a.at[i]))
        attn_w[-1].start()
    me = Place(*sizes)
    c, mate = me.c, me.at(c=1 - me.c)
    n = me.nx
    seq = right_ref.shape[1]
    total_rows = width = out.shape[1]
    is0 = c == 0
    pair = jnp.where(is0, me.x, me.y)
    other = jnp.where(is0, me.y, me.x)
    lo, hi, nh = pair % 2, pair // 2, n // 2

    def along(pair_at, other_at, z=None):
        return me.at(x=jnp.where(is0, pair_at, other_at), y=jnp.where(is0, other_at, pair_at), z=z)

    flip_x, flip_y = me.x + 1 - 2 * (me.x % 2), me.y + 1 - 2 * (me.y % 2)
    dims = [
        (n, other, lambda q: along(pair, q)),
        (nh, hi, lambda q: along(q * 2 + lo, other)),
        (2, me.z % 2, lambda q: me.at(z=me.z // 2 * 2 + q)),
        (me.nz // 2, me.z // 2, lambda q: me.at(z=q * 2 + me.z % 2)),
    ]
    parts, gots = boxes[:4], boxes[4:8]
    half, small_half, small_got, fs, fr, os, ps, pr, gs, gr, ms, mr, cs, cr, ss, sr = boxes[8:]
    levels = [i for i, d in enumerate(dims) if d[0] > 1]
    x_peers = [me.at(x=(me.x + k) % n) for k in range(1, n)]
    y_peers = [me.at(y=(me.y + k) % n) for k in range(1, n)]
    z_peers = [me.at(z=(me.z + k) % me.nz) for k in range(1, me.nz)]
    greet(
        [mate, me.at(x=flip_x, c=1 - c), me.at(y=flip_y, c=1 - c)] + x_peers + y_peers + z_peers
    )

    def slot_a(slot):
        return buf_a.at[pl.ds(pl.multiple_of(slot * seq, seq), seq), :]

    def slot_b(slot):
        return buf_b.at[pl.ds(pl.multiple_of(slot * seq, seq), seq), :]

    left_ref[0] = attn_in[...]
    left_ref[1] = context[...]
    targets = [
        (mate, 1 - c, other % 2, c),
        (me.at(x=flip_x, c=0), 0, flip_x % 2, 2 + c),
        (me.at(y=flip_y, c=1), 1, flip_y % 2, 2 + c),
    ]
    factor = []
    for i, (device, role, parity, slot) in enumerate(targets):
        a = jnp.where(role == 0, 0, parity)
        factor.append(remote(left_ref.at[a], slot_a(slot), fs.at[i, 0], fr.at[slot, 0], device))
    own = [pltpu.make_async_copy(left_ref.at[jnp.where(is0, 0, lo)], slot_a(c), os.at[0])]
    own[0].start()

    size = 2 * per_core
    group = lax.broadcasted_iota(jnp.int32, (1, seq), 1) // (seq // micro)
    slot_ids = lax.broadcasted_iota(jnp.int32, (2 * me.n_expert * size, seq), 0)
    hots = []
    for k in range(2):
        route, slot = route_ref[k : k + 1, :], slot_ref[k : k + 1, :]
        place = (route % 2) * (me.n_expert * size) + (route // 2) * size + c * per_core + group * cap + slot
        hots.append(jnp.where(slot_ids == jnp.where(slot >= 0, place, -1), 1.0, 0.0))
    low = [h.astype(bf) for h in hots] + [(hots[0] + hots[1]).astype(bf)]
    half_slots = me.n_expert * size

    def picked(hot, which):
        total = None
        for j in range(2):
            rows = back_ref[which, j].reshape(half_slots, width)
            term = dot_as(hot[j * half_slots : (j + 1) * half_slots, :], rows, TN)
            total = term if total is None else total + term
        return total

    cot = cot_ref[...].astype(f32)
    resid = residual[...]
    chosen = [picked(low[k], 0) for k in range(2)]
    gate = [upright(gate_ref[k : k + 1, :]) for k in range(2)]
    layer_out[...] = (resid + (gate[0] * chosen[0] + gate[1] * chosen[1])).astype(bf)
    grad_gate = [jnp.sum(cot * chosen[k], axis=-1, keepdims=True) for k in range(2)]
    mean_grad = gate[0] * grad_gate[0] + gate[1] * grad_gate[1]
    logit = [gate[k] * (grad_gate[k] - mean_grad) for k in range(2)]
    experts = router_t.shape[0]
    by_token, by_expert = None, None
    for k in range(2):
        route = route_ref[k : k + 1, :]
        line = jnp.where(
            lax.broadcasted_iota(jnp.int32, (experts, seq), 0) == route, flat_line(logit[k]), 0.0
        )
        by_expert = line if by_expert is None else by_expert + line
        route_up = upright(route.astype(f32)).astype(jnp.int32)
        line = jnp.where(
            lax.broadcasted_iota(jnp.int32, (seq, experts), 1) == route_up, logit[k], 0.0
        )
        by_token = line if by_token is None else by_token + line

    def exact(left, right):
        return lax.dot_general(
            left, right, (NN, ((), ())), preferred_element_type=f32, precision=highest
        )

    scale = row_scale(resid)
    normed = resid * scale
    small_ref[:experts] = exact(by_expert, normed * norm_moe[...])
    grad_moe = picked(low[2], 1) + exact(by_token, router_t[...])
    small_ref[experts:] = jnp.zeros((small_ref.shape[0] - experts, width), f32)
    small_ref[experts + 1 : experts + 2] = jnp.sum(grad_moe * normed, axis=0, keepdims=True)
    grad_n = grad_moe * norm_moe[...]
    grad_resid = cot + scale * (grad_n - normed * jnp.mean(grad_n * normed, axis=-1, keepdims=True))
    right_ref[3] = grad_resid.astype(bf)
    grad_in[...] = grad_resid
    attn_w[0].wait()
    grad_context = dot_as(right_ref[3], weights[3], NT).astype(bf)

    heads = probs.shape[0]
    pair_lanes = 2 * width // heads
    low_half = lax.broadcasted_iota(jnp.int32, (seq, pair_lanes), 1) < pair_lanes // 2
    for n2 in range(heads // 2):
        lanes = slice(n2 * pair_lanes, (n2 + 1) * pair_lanes)
        sums = [None, None, None]
        for h in range(2):
            mine = low_half if h == 0 else ~low_half
            head = 2 * n2 + h

            def only(value):
                return jnp.where(mine, value, jnp.zeros_like(value))

            prob = probs[head]
            grad_c = only(grad_context[:, lanes])
            grad_p = dot_as(grad_c, value[:, lanes], NT)
            grad_s = prob * (grad_p - jnp.sum(prob * grad_p, axis=-1, keepdims=True))
            lines[head : head + 1, :] = diagonals(grad_s)
            grad_s = grad_s.astype(bf)
            terms = (
                dot_as(grad_s, only(key[:, lanes]), NN),
                dot_as(grad_s, only(query[:, lanes]), TN),
                dot_as(prob.astype(bf), grad_c, TN),
            )
            sums = [t if s is None else s + t for s, t in zip(sums, terms)]
        for i in range(3):
            right_ref[i, :, lanes] = sums[i].astype(bf)
    for i, (device, role, parity, slot) in enumerate(targets):
        factor.append(
            remote(right_ref.at[role * 2 + parity], slot_b(slot), fs.at[i, 1], fr.at[slot, 1], device)
        )
    own.append(pltpu.make_async_copy(right_ref.at[c * 2 + lo], slot_b(c), os.at[1]))
    own[1].start()
    buckets = 32
    bucket = bucket_of(lax.broadcasted_iota(jnp.int32, (2 * seq, buckets), 0) - seq)
    hot = jnp.where(bucket == lax.broadcasted_iota(jnp.int32, (2 * seq, buckets), 1), 1.0, 0.0)
    small_ref[experts + 8 : experts + 8 + heads, :buckets] = exact(lines[...], hot)
    grad_attn = None
    for i in range(3):
        attn_w[1 + i].wait()
        term = dot_as(right_ref[i], weights[i], NT)
        grad_attn = term if grad_attn is None else grad_attn + term
    rows = layer_in[...].astype(f32)
    scale = row_scale(rows)
    normed = rows * scale
    small_ref[experts : experts + 1] = jnp.sum(grad_attn * normed, axis=0, keepdims=True)
    grad_n = grad_attn * norm_attn[...]
    grad_in[...] += scale * (grad_n - normed * jnp.mean(grad_n * normed, axis=-1, keepdims=True))

    rows_s = half.shape[0]
    small = [remote(small_ref.at[pl.ds((1 - c) * rows_s, rows_s)], half, ss.at[0], sr.at[0], mate)]
    small_dims = [
        (n, me.x, lambda q: me.at(x=q)),
        (n, me.y, lambda q: me.at(y=q)),
        (me.nz, me.z, lambda q: me.at(z=q)),
    ]
    small_wait = [small[0]]
    small_slot = [1]

    def small_step(step):
        for copy in small_wait:
            copy.wait_recv()
        small_wait.clear()
        if step == 0:
            total = small_ref[pl.ds(c * rows_s, rows_s)] + half[...]
        elif step <= 3:
            total = small_got[step - 1, 0]
            for k in range(1, small_dims[step - 1][0]):
                total = total + small_got[step - 1, k]
        if step < 3:
            count, index, peer = small_dims[step]
            small_half[step] = total
            small_got[step, index] = total
            for k in range(1, count):
                small_wait.append(
                    remote(
                        small_half.at[step], small_got.at[step, index], ss.at[small_slot[0]],
                        sr.at[small_slot[0]], peer((index + k) % count),
                    )
                )
                small_slot[0] += 1
        elif step == 3:
            small_out[pl.ds(c * rows_s, rows_s)] = total
            block = small_out.at[pl.ds(c * rows_s, rows_s)]
            small_wait.append(
                remote(block, block, ss.at[small_slot[0]], sr.at[small_slot[0]], mate)
            )
        small.extend(small_wait)

    for where in (1 - c, 2, 3):
        for i, (src, dst) in enumerate(((left_ref, slot_a(where)), (right_ref, slot_b(where)))):
            pltpu.make_async_remote_copy(
                src_ref=src.at[0], dst_ref=dst, send_sem=fs.at[0, i], recv_sem=fr.at[where, i],
                device_id=mate, device_id_type=MESH,
            ).wait_recv()
    for copy in own:
        copy.wait()

    rows_k = total_rows // pieces
    matrix = c * 2 + lo
    pending, written = {}, []

    def multiply(k):
        acc[k] = lax.dot_general(
            buf_a[:, k * rows_k : (k + 1) * rows_k], buf_b[...], (TN, ((), ())),
            preferred_element_type=jnp.float32,
        )
        push(k, 0, rows_k)

    def push(k, at, rows):
        level = levels[at]
        count, index, peer = dims[level]
        size = rows // count
        copies = []
        for s in range(1, count):
            to = (index + s) % count
            parts[level][k, s - 1] = acc[k, pl.ds(pl.multiple_of(to * size, 16), size), :].astype(jnp.bfloat16)
            copies.append(
                remote(
                    parts[level].at[k, s - 1], gots[level].at[k, s - 1],
                    ps.at[level, k, s - 1], pr.at[level, k, s - 1], peer(to),
                )
            )
        pending["push", at, k] = copies

    def rows_at(at):
        rows = rows_k
        for i in range(at):
            rows //= dims[levels[i]][0]
        return rows

    def add(k, at):
        level = levels[at]
        count, index, _ = dims[level]
        size = rows_at(at) // count
        for copy in pending["push", at, k]:
            copy.wait_recv()
        total = acc[k, pl.ds(pl.multiple_of(index * size, 16), size), :]
        for s in range(1, count):
            total = total + gots[level][k, s - 1].astype(jnp.float32)
        if at + 1 < len(levels):
            acc[k, :size, :] = total
            push(k, at + 1, size)
        else:
            out[matrix, pl.ds(offset(k, at), size), :] = total.astype(jnp.bfloat16)
            share(k, at)

    def offset(k, at):
        start, rows = k * rows_k, rows_k
        for i in range(at + 1):
            count, index, _ = dims[levels[i]]
            rows //= count
            start = start + index * rows
        return pl.multiple_of(start, 16)

    def share(k, at):
        level = levels[at]
        count, index, peer = dims[level]
        size = rows_at(at) // count
        block = out.at[matrix, pl.ds(offset(k, at), size), :]
        pending["share", at, k] = [
            remote(block, block, gs.at[level, k, s - 1], gr.at[level, k, s - 1], peer((index + s) % count))
            for s in range(1, count)
        ]

    def shared(k, at):
        for copy in pending["share", at, k]:
            copy.wait_recv()
        if at:
            share(k, at - 1)
        else:
            block = out.at[matrix, pl.ds(k * rows_k, rows_k), :]
            pending["mate", k] = remote(
                block, block, ms.at[k], mr.at[k], along(pair + 1 - 2 * lo, other)
            )

    def across(k):
        pending["mate", k].wait_recv()
        block = out.at[pl.ds(2 * c, 2), pl.ds(k * rows_k, rows_k), :]
        pending["core", k] = remote(block, block, cs.at[k], cr.at[k], mate)
        write(k, c)

    def write(k, core):
        part = pl.ds(2 * core, 2), pl.ds(k * rows_k, rows_k), slice(None)
        written.append(pltpu.make_async_copy(out.at[part], out_hbm.at[part], sem_out.at[core, k]))
        written[-1].start()

    def close(k):
        pending["core", k].wait_recv()
        write(k, 1 - c)

    steps = [multiply]
    steps += [functools.partial(add, at=i) for i in range(len(levels))]
    steps += [functools.partial(shared, at=i) for i in reversed(range(len(levels)))]
    events = sorted((0 if p == 0 else p + k, p, k) for p in range(len(steps)) for k in range(pieces))
    before = 0
    for t, p, k in events:
        if before < t <= 5:
            small_step(t - 1)
        before = t
        steps[p](k)
    for k in range(pieces):
        across(k)
    for k in range(pieces):
        close(k)
    for copy in factor + small:
        copy.wait_send()
    for copies in pending.values():
        for copy in copies if isinstance(copies, list) else [copies]:
            copy.wait_send()
    for copy in written:
        copy.wait()


def settle(sizes, micro, cap, arrays, norms, router_t, attn_w):
    n_expert, n_dp = sizes
    nz = math.gcd(n_expert, 4)
    n = n_expert // nz
    nh = n // 2
    assert n == n_dp // 2
    seq, width = arrays[5].shape
    heads = arrays[12].shape[0]
    splits = [n, nh, 2, nz // 2]
    pieces = max(1, min(8, width // (16 * math.prod(splits))))
    rows_k = width // pieces
    bf, f32 = jnp.bfloat16, jnp.float32
    small_rows = router_t.shape[0] + 8 + heads
    small_rows += -small_rows % 16
    rows_s = small_rows // 2
    sizes_at = [rows_k // math.prod(splits[: i + 1]) for i in range(4)]
    counts = [max(q - 1, 1) for q in splits]
    most = max(counts)
    boxes = [
        pltpu.VMEM((pieces, q, s if k > 1 else 16, width), bf) for q, s, k in zip(counts, sizes_at, splits)
    ]
    smalls = 2 * n + nz
    any_space = pl.BlockSpec(memory_space=pl.ANY)
    return pl.pallas_call(
        functools.partial(settle_kernel, sizes, (micro, cap, micro * cap), pieces),
        out_shape=(
            jax.ShapeDtypeStruct((seq, width), bf),
            jax.ShapeDtypeStruct((seq, width), f32),
            jax.ShapeDtypeStruct((4, width, width), bf),
            jax.ShapeDtypeStruct((small_rows, width), f32),
        ),
        in_specs=[VMEM] * 16 + [any_space] * 4,
        out_specs=(VMEM, VMEM, any_space, VMEM),
        scratch_shapes=[
            pltpu.VMEM((4, width, width), bf),
            DMA((4,)),
            pltpu.VMEM((2, seq, width), bf),
            pltpu.VMEM((4, seq, width), bf),
            pltpu.VMEM((small_rows, width), f32),
            pltpu.VMEM((heads, 2 * seq), f32),
            pltpu.VMEM((4, width, width), bf),
            DMA((2, pieces)),
            pltpu.VMEM((4 * seq, width), bf),
            pltpu.VMEM((4 * seq, width), bf),
            pltpu.VMEM((pieces, rows_k, width), f32),
            *boxes,
            *boxes,
            pltpu.VMEM((rows_s, width), f32),
            pltpu.VMEM((3, rows_s, width), f32),
            pltpu.VMEM((3, max(n, nz), rows_s, width), f32),
            DMA((3, 2)),
            DMA((4, 2)),
            DMA((2,)),
            DMA((4, pieces, most)),
            DMA((4, pieces, most)),
            DMA((4, pieces, most)),
            DMA((4, pieces, most)),
            DMA((pieces,)),
            DMA((pieces,)),
            DMA((pieces,)),
            DMA((pieces,)),
            DMA((smalls,)),
            DMA((smalls,)),
        ],
        name="settle",
        compiler_params=pltpu.CompilerParams(
            collective_id=3, has_side_effects=True, vmem_limit_bytes=58 << 20
        ),
    )(*arrays, *norms, router_t, *attn_w)


def rms_scale(values):
    return lax.rsqrt(jnp.mean(values * values, axis=-1, keepdims=True) + epsilon)


def bucket_hot(seq_len, buckets):
    position = jnp.arange(seq_len, dtype=jnp.int32)
    bucket_ids = jnp.arange(buckets, dtype=jnp.int32)
    bucketed = bucket_of(position[None, :] - position[:, None])
    return (bucketed[None, :, :] == bucket_ids[:, None, None]).astype(jnp.float32)


def dot32(pattern, left, right):
    return jnp.einsum(pattern, left, right, preferred_element_type=jnp.float32)


def shards(
    layer_in, routes, queue_slots, norm_attn, w_query, w_key, w_value, w_out, rel_table,
    norm_moe, router, w_gate, w_up, w_down, cotangent,
):
    bf, f32 = jnp.bfloat16, jnp.float32
    seq_len, width = layer_in.shape
    buckets, heads = rel_table.shape
    expert_count = router.shape[1]
    sizes = (lax.axis_size("expert"), lax.axis_size("dp"))
    n_expert, n_dp = sizes
    assert w_gate.shape[0] == 2 and expert_count == 2 * n_expert
    group_len = seq_len // MICRO
    capacity = (5 * group_len + 2 * expert_count - 1) // (2 * expert_count)
    split_heads = (seq_len, heads, width // heads)
    places = (routes.T, queue_slots.T)
    expert_w = [jnp.swapaxes(w_gate, 1, 2), jnp.swapaxes(w_up, 1, 2), w_down]
    slots = n_dp // 2 * n_expert * 2 * MICRO * capacity
    fused = 2 * slots * width * 20 + 6 * w_gate.size < 52 << 20
    if fused:
        (
            back, rows_in, hidden, gate_grad, up_grad, grad_rows,
            query, key, value, probs, context, residual, attn_in, gates,
        ) = layer(
            sizes, MICRO, capacity, layer_in, (norm_attn[None], norm_moe[None]), rel_table.T, router.T,
            places, cotangent, (w_query, w_key, w_value, w_out), expert_w,
        )
    else:
        layer_rows = layer_in.astype(f32)
        attn_in = (layer_rows * rms_scale(layer_rows) * norm_attn).astype(bf)
        query = dot32("sd,de->se", attn_in, w_query).astype(bf)
        key = dot32("sd,de->se", attn_in, w_key).astype(bf)
        value = dot32("sd,de->se", attn_in, w_value).astype(bf)
        one_hot = bucket_hot(seq_len, buckets)
        bias = jnp.einsum("bij,bh->hij", one_hot, rel_table, precision=highest)
        scores = dot32("ihd,jhd->hij", query.reshape(split_heads), key.reshape(split_heads)) + bias
        exponent = jnp.exp(scores - jnp.max(scores, axis=-1, keepdims=True))
        probs = exponent / jnp.sum(exponent, axis=-1, keepdims=True)
        context = dot32("hij,jhd->ihd", probs.astype(bf), value.reshape(split_heads))
        context = context.astype(bf).reshape(seq_len, width)
        residual = layer_rows + dot32("se,ed->sd", context, w_out)
        moe_in = residual * rms_scale(residual) * norm_moe
        expert_ids = jnp.arange(expert_count, dtype=jnp.int32)
        first_hot = (routes[:, 0:1] == expert_ids).astype(f32)
        second_hot = (routes[:, 1:2] == expert_ids).astype(f32)
        gate_prob = jax.nn.softmax(jnp.dot(moe_in, router, precision=highest), axis=-1)
        prob_first, prob_second = jnp.sum(gate_prob * first_hot, axis=-1), jnp.sum(gate_prob * second_hot, axis=-1)
        gates = jnp.stack([prob_first, prob_second]) / (prob_first + prob_second)
        gates = jnp.pad(gates, ((0, 6), (0, 0)))
        info = jnp.concatenate([*places, jnp.zeros((4, seq_len), jnp.int32)])
        rows_in, weight_in, grad_in = spread(
            sizes, MICRO, capacity, info, moe_in.astype(bf), cotangent, gates
        )
        blocks = rows_in.shape[:-1] + (-1,)
        rows_in, grad_in = [a.reshape(2, -1, width) for a in (rows_in, grad_in)]
        slot_weight = weight_in[:, :, 0, : 2 * MICRO * capacity].reshape(2, -1, 1)
        grad_rows = (slot_weight * grad_in.astype(f32)).astype(bf)
        gate_pre = dot32("jrd,jdf->jrf", rows_in, w_gate)
        up_pre = dot32("jrd,jdf->jrf", rows_in, w_up)
        hidden, active, lean = gated_terms(gate_pre, up_pre)
        hidden = hidden.astype(bf)
        partial_out = dot32("jrf,jfd->jrd", hidden, w_down).astype(bf)
        hidden_grad = dot32("jrd,jfd->jrf", grad_rows, w_down)
        gate_grad, up_grad = (hidden_grad * lean).astype(bf), (hidden_grad * active).astype(bf)
        rows_grad = dot32("jrf,jdf->jrd", gate_grad, w_gate) + dot32("jrf,jdf->jrd", up_grad, w_up)
        back = gather_back(sizes, partial_out.reshape(blocks), rows_grad.astype(bf).reshape(blocks))
    layer_out, grad_input, sums, small = settle(
        sizes, MICRO, capacity,
        (back, *places, gates, cotangent, layer_in, residual, context, attn_in, query, key, value, probs),
        (norm_attn[None], norm_moe[None]), router.T, (w_query, w_key, w_value, w_out),
    )
    rows_in, hidden, gate_grad, up_grad, grad_rows = [
        a.reshape(2, -1, a.shape[-1]) for a in (rows_in, hidden, gate_grad, up_grad, grad_rows)
    ]
    (
        *matrices, grad_w_gate, grad_w_up, grad_w_down,
        grad_router, grad_norm_attn, grad_norm_moe, grad_table,
    ) = finish(
        sums, small, rows_in, hidden, gate_grad, up_grad, grad_rows, expert_count, (heads, buckets)
    )
    return (
        layer_out, grad_input, grad_norm_attn.reshape(width), *matrices, grad_table.T,
        grad_norm_moe.reshape(width), grad_router.T,
        jnp.swapaxes(grad_w_gate, 1, 2), jnp.swapaxes(grad_w_up, 1, 2), grad_w_down,
    )


def solution(mesh):
    in_specs = (
        P(("expert", "dp"), None),
        P(("expert", "dp"), None),
        P(("expert", "dp"), None),
        P(),
        P(),
        P(),
        P(),
        P(),
        P(),
        P(),
        P(),
        P("expert", None, "dp"),
        P("expert", None, "dp"),
        P("expert", "dp", None),
        P(("expert", "dp"), None),
    )
    out_specs = (
        P(("expert", "dp"), None),
        P(("expert", "dp"), None),
        P(),
        P(),
        P(),
        P(),
        P(),
        P(),
        P(),
        P(),
        P("expert", None, "dp"),
        P("expert", None, "dp"),
        P("expert", "dp", None),
    )
    return jax.shard_map(shards, mesh=mesh, in_specs=in_specs, out_specs=out_specs, check_vma=False)
```

```python
import functools
import math

import jax
import jax.numpy as jnp
from jax import lax
from jax.experimental import pallas as pl
from jax.experimental.pallas import tpu as pltpu
from jax.sharding import PartitionSpec as P

MICRO = 4

epsilon = 1e-06
bucket_edges = (12, 16, 23, 32, 46, 64, 91)
highest = lax.Precision.HIGHEST

MESH = pl.DeviceIdType.MESH
VMEM = pl.BlockSpec(memory_space=pltpu.VMEM)
DMA = pltpu.SemaphoreType.DMA


class Place:
    def __init__(self, n_expert, n_dp):
        self.n_expert, self.n_dp = n_expert, n_dp
        self.nz = math.gcd(n_expert, 4)
        self.nx = n_expert // self.nz
        self.ny = n_dp // 2
        self.e = lax.axis_index("expert")
        self.d = lax.axis_index("dp")
        self.z, self.x = self.e // self.nx, self.e % self.nx
        self.y, self.c = self.d // 2, self.d % 2

    def at(self, z=None, x=None, y=None, c=None, e=None):
        z = self.z if z is None else z
        x = self.x if x is None else x
        y = self.y if y is None else y
        c = self.c if c is None else c
        e = z * self.nx + x if e is None else e
        return (e, y * 2 + c)


def remote(src, dst, send, recv, device):
    copy = pltpu.make_async_remote_copy(
        src_ref=src, dst_ref=dst, send_sem=send, recv_sem=recv, device_id=device, device_id_type=MESH
    )
    copy.start()
    return copy


def greet(devices):
    barrier = pltpu.get_barrier_semaphore()
    for device in devices:
        pl.semaphore_signal(barrier, inc=1, device_id=device, device_id_type=MESH)
    pl.semaphore_wait(barrier, len(devices))


def column_peers(me):
    out = [me.at(c=1 - me.c)]
    out += [me.at(y=(me.y + k) % me.ny) for k in range(1, me.ny)]
    out += [me.at(e=(me.e + k) % me.n_expert) for k in range(1, me.n_expert)]
    return out


class Spread:
    def __init__(self, me, rows, recv, sems):
        self.me, self.rows, self.recv = me, rows, recv
        self.se, self.re, self.sy, self.ry, self.sc, self.rc = sems
        self.came, self.along, self.crossed = {}, {}, {}

    def send(self):
        me = self.me
        for k in range(1, me.n_expert):
            to = (me.e + k) % me.n_expert
            self.came[k] = remote(
                self.rows.at[to], self.recv.at[me.c, me.y * me.n_expert + me.e],
                self.se.at[k], self.re.at[k], me.at(e=to),
            )
        self.recv[me.c, me.y * me.n_expert + me.e] = self.rows[me.e]

    def pass_on(self, blocks):
        me = self.me
        for k in blocks:
            if k:
                self.came[k].wait_recv()
            src = (me.e - k + me.n_expert) % me.n_expert
            block = self.recv.at[me.c, me.y * me.n_expert + src]
            for s in range(1, me.ny):
                self.along[s, k] = remote(
                    block, block, self.sy.at[s - 1, k], self.ry.at[s - 1, k], me.at(y=(me.y + s) % me.ny)
                )

    def pass_column(self):
        me = self.me
        for k in range(1, me.n_expert):
            self.came[k].wait_recv()
        block = self.recv.at[me.c, pl.ds(me.y * me.n_expert, me.n_expert)]
        for s in range(1, me.ny):
            self.along[s, 0] = remote(
                block, block, self.sy.at[s - 1, 0], self.ry.at[s - 1, 0], me.at(y=(me.y + s) % me.ny)
            )

    def cross(self, s):
        me = self.me
        if s:
            for key, copy in self.along.items():
                if key[0] == s:
                    copy.wait_recv()
        block = self.recv.at[me.c, pl.ds((me.y - s + me.ny) % me.ny * me.n_expert, me.n_expert)]
        self.crossed[s] = remote(block, block, self.sc.at[s], self.rc.at[s], me.at(c=1 - me.c))

    def arrive(self):
        for copy in self.crossed.values():
            copy.wait_recv()

    def close(self):
        for copies in (self.came, self.along, self.crossed):
            for copy in copies.values():
                copy.wait_send()


def spread_sems(sizes):
    n_expert, ny = sizes[0], sizes[1] // 2
    most = max(ny - 1, 1)
    return [
        DMA((3, n_expert)), DMA((3, n_expert)), DMA((3, most, n_expert)), DMA((3, most, n_expert)),
        DMA((3, ny)), DMA((3, ny)),
    ]


class Rows:
    def __init__(self, me, rows_per, info_all, gates, tok, send, recv):
        self.me, self.rows_per, self.info_all, self.gates, self.tok = me, rows_per, info_all, gates, tok
        self.send, self.recv, self.copies = send, recv, {}
        self.seq = tok.shape[2]

    def share(self, i, ref):
        block = ref.at[self.me.c]
        mate = self.me.at(c=1 - self.me.c)
        self.copies[i] = remote(block, block, self.send.at[i], self.recv.at[i], mate)

    def hots(self):
        me, seq = self.me, self.seq
        micro, cap, per_core = self.rows_per
        self.copies["info"].wait_recv()
        row_ids = lax.broadcasted_iota(jnp.int32, (me.n_expert * 2 * per_core, seq), 0)
        group = lax.broadcasted_iota(jnp.int32, (1, seq), 1) // (seq // micro)
        self.each = []
        for cc in range(2):
            for k in range(2):
                route = self.info_all[cc, k : k + 1, :]
                slot = self.info_all[cc, 2 + k : 3 + k, :]
                target = (route // 2) * (2 * per_core) + cc * per_core + group * cap + slot
                target = jnp.where((slot >= 0) & (route % 2 == me.c), target, -1)
                self.each.append(jnp.where(row_ids == target, 1.0, 0.0))
        self.both = [(self.each[2 * cc] + self.each[2 * cc + 1]).astype(jnp.bfloat16) for cc in range(2)]

    def gather(self, i):
        self.copies[i].wait_recv()
        total = None
        for cc in range(2):
            term = jnp.dot(self.both[cc], self.tok[i, cc], preferred_element_type=jnp.float32)
            total = term if total is None else total + term
        return total.astype(jnp.bfloat16).reshape(self.me.n_expert, 2 * self.rows_per[2], -1)

    def weights(self):
        self.copies["gates"].wait_recv()
        size = 2 * self.rows_per[2]
        column = None
        for n, hot in enumerate(self.each):
            term = jnp.sum(hot * self.gates[n // 2, n % 2 : n % 2 + 1, :], axis=1, keepdims=True)
            column = term if column is None else column + term
        lane = lax.broadcasted_iota(jnp.int32, (size, 128), 1)
        row = lax.broadcasted_iota(jnp.int32, (size, 128), 0)
        tiles = []
        for e in range(self.me.n_expert):
            block = jnp.where(lane == row, column[e * size : (e + 1) * size, :], 0.0)
            tiles.append(jnp.broadcast_to(jnp.sum(block, axis=0, keepdims=True), (8, 128)))
        return tiles

    def close(self):
        for copy in self.copies.values():
            copy.wait_send()


NAMED = ("info", "gates", 0, 1)


class Named:
    def __init__(self, sems):
        self.at = {name: sems.at[i] for i, name in enumerate(NAMED)}


def rows_scratch(sizes, per_core, seq, width):
    mine = (sizes[0], 2 * per_core, width)
    bf = jnp.bfloat16
    return [
        pltpu.VMEM((2, 8, seq), jnp.int32),
        pltpu.VMEM((2, 8, seq), jnp.float32),
        pltpu.VMEM((2, 2, seq, width), bf),
        DMA((4,)),
        DMA((4,)),
        pltpu.VMEM(mine, bf),
        pltpu.VMEM((sizes[0], 8, 128), jnp.float32),
        pltpu.VMEM(mine, bf),
    ]


def rows_of(me, rows_per, scratch):
    info_all, gates, tok, send, recv = scratch[:5]
    return Rows(me, rows_per, info_all, gates, tok, Named(send), Named(recv))


def spread_kernel(sizes, rows_per, info_ref, moe_ref, cot_ref, w_ref, x_out, w_out, g_out, *scratch):
    me = Place(*sizes)
    c = me.c
    greet(column_peers(me))
    scratch, sems = scratch[:8], scratch[8:]
    rows = rows_of(me, rows_per, scratch)
    info_all, gates, tok = scratch[:3]
    info_all[c] = info_ref[...]
    rows.share("info", info_all)
    gates[c] = w_ref[...]
    rows.share("gates", gates)
    for i, ref in enumerate((moe_ref, cot_ref)):
        tok[i, c] = ref[...]
        rows.share(i, tok.at[i])
    rows.hots()
    buf_x, buf_w, buf_g = scratch[5:]
    out_x, out_w, out_g = [
        Spread(me, buf, recv, [s.at[i] for s in sems])
        for i, (buf, recv) in enumerate(((buf_x, x_out), (buf_w, w_out), (buf_g, g_out)))
    ]
    for i, payload in enumerate((out_x, out_g)):
        payload.rows[...] = rows.gather(i)
        payload.send()
    for e, tile in enumerate(rows.weights()):
        buf_w[e] = tile
    out_w.send()
    for payload in (out_x, out_g):
        payload.pass_on(range(me.n_expert))
        payload.cross(0)
    out_w.pass_column()
    out_w.cross(0)
    for payload in (out_x, out_g, out_w):
        for s in range(1, me.ny):
            payload.cross(s)
    for payload in (out_x, out_g, out_w):
        payload.arrive()
        payload.close()
    rows.close()


def spread(sizes, micro, cap, info, moe, cot, weights):
    n_expert, ny, per_core = sizes[0], sizes[1] // 2, micro * cap
    seq, width = cot.shape
    block = (2, ny * n_expert, 2 * per_core)
    bf = jnp.bfloat16
    return pl.pallas_call(
        functools.partial(spread_kernel, sizes, (micro, cap, per_core)),
        out_shape=(
            jax.ShapeDtypeStruct(block + (width,), bf),
            jax.ShapeDtypeStruct(block[:2] + (8, 128), jnp.float32),
            jax.ShapeDtypeStruct(block + (width,), bf),
        ),
        in_specs=[VMEM] * 4,
        out_specs=(VMEM,) * 3,
        scratch_shapes=rows_scratch(sizes, per_core, seq, width) + spread_sems(sizes),
        name="spread",
        compiler_params=pltpu.CompilerParams(
            collective_id=1, has_side_effects=True, vmem_limit_bytes=48 << 20
        ),
    )(info, moe, cot, weights)


class Back:
    def __init__(self, me, away, own, q_out, r1, stage, r2, final, sems):
        self.me, self.away, self.own = me, away, own
        self.q_out, self.r1, self.stage, self.r2, self.final = q_out, r1, stage, r2, final
        self.sems = sems
        self.ys = [(me.y + k) % me.ny for k in range(me.ny)]
        self.order = list(range(1, me.n_expert)) + [0]
        self.first, self.second, self.third, self.fourth = {}, {}, {}, {}
        self.arrived = set()

    def to_mate(self, i, k):
        me = self.me
        column = pl.ds(self.ys[k] * me.n_expert, me.n_expert)
        self.first[i, k] = remote(
            self.away(i).at[column], self.r1.at[i, column], self.sems[0].at[i, k], self.sems[1].at[i, k],
            me.at(c=1 - me.c),
        )

    def partial(self, i, y, e):
        block = y * self.me.n_expert + e
        return self.own(i, block) + self.r1[i, block].astype(jnp.float32)

    def along_y(self, i):
        me = self.me
        for k in range(1, me.ny):
            self.first[i, k].wait_recv()
            for j in self.order:
                e = (me.e + j) % me.n_expert
                self.stage[i, k - 1, e] = self.partial(i, self.ys[k], e).astype(jnp.bfloat16)
                self.second[i, k, j] = remote(
                    self.stage.at[i, k - 1, e], self.r2.at[i, k - 1, e],
                    self.sems[2].at[i, k - 1, j], self.sems[3].at[i, k - 1, j], me.at(y=self.ys[k]),
                )

    def finish(self, i, order):
        me = self.me
        if (i, 0) not in self.arrived:
            self.arrived.add((i, 0))
            self.first[i, 0].wait_recv()
        for j in order:
            e = (me.e + j) % me.n_expert
            total = self.partial(i, me.y, e)
            for k in range(1, me.ny):
                self.second[i, k, j].wait_recv()
                total = total + self.r2[i, k - 1, e].astype(jnp.float32)
            if j:
                self.final[i, e] = total.astype(jnp.bfloat16)
                self.third[i, j] = remote(
                    self.final.at[i, e], self.q_out.at[i, me.c, me.e],
                    self.sems[4].at[i, j], self.sems[5].at[i, j], me.at(e=e),
                )
            else:
                self.q_out[i, me.c, me.e] = total.astype(jnp.bfloat16)

    def across(self, i):
        for j in self.order[:-1]:
            self.third[i, j].wait_recv()
        block = self.q_out.at[i, self.me.c]
        s, r = self.sems[6].at[i], self.sems[7].at[i]
        self.fourth[i] = remote(block, block, s, r, self.me.at(c=1 - self.me.c))

    def close(self):
        for copy in self.fourth.values():
            copy.wait()
        for copies in (self.first, self.second, self.third):
            for copy in copies.values():
                copy.wait_send()


def back_scratch(sizes, size, width):
    n_expert, ny = sizes[0], sizes[1] // 2
    most = max(ny - 1, 1)
    bf = jnp.bfloat16
    return [
        pltpu.VMEM((2, ny * n_expert, size, width), bf),
        pltpu.VMEM((2, most, n_expert, size, width), bf),
        pltpu.VMEM((2, most, n_expert, size, width), bf),
        pltpu.VMEM((2, n_expert, size, width), bf),
        DMA((2, ny)),
        DMA((2, ny)),
        DMA((2, most, n_expert)),
        DMA((2, most, n_expert)),
        DMA((2, n_expert)),
        DMA((2, n_expert)),
        DMA((2,)),
        DMA((2,)),
    ]


def gather_back_kernel(sizes, p0_ref, p1_ref, q_out, *scratch):
    me = Place(*sizes)
    greet(column_peers(me))
    p_refs = (p0_ref, p1_ref)
    back = Back(
        me, lambda i: p_refs[i].at[1 - me.c],
        lambda i, block: p_refs[i][me.c, block].astype(jnp.float32), q_out, *scratch[:4], scratch[4:],
    )
    for i in range(2):
        for k in reversed(range(me.ny)):
            back.to_mate(i, k)
    for i in range(2):
        back.along_y(i)
    for i in range(2):
        back.finish(i, back.order)
        back.across(i)
    back.close()


def gather_back(sizes, first, second):
    n_expert = sizes[0]
    _, _, size, width = first.shape
    return pl.pallas_call(
        functools.partial(gather_back_kernel, sizes),
        out_shape=jax.ShapeDtypeStruct((2, 2, n_expert, size, width), jnp.bfloat16),
        in_specs=[VMEM] * 2,
        out_specs=VMEM,
        scratch_shapes=back_scratch(sizes, size, width),
        name="gather_back",
        compiler_params=pltpu.CompilerParams(
            collective_id=2, has_side_effects=True, vmem_limit_bytes=48 << 20
        ),
    )(first, second)


def gated_terms(gate_pre, up_pre):
    root = math.sqrt(2.0 / math.pi)
    square = gate_pre * gate_pre
    bend = jnp.tanh(root * (gate_pre + 0.044715 * square * gate_pre))
    half = 0.5 * (1.0 + bend)
    active = gate_pre * half
    slope = half + 0.5 * gate_pre * (1.0 - bend * bend) * root * (1.0 + 3 * 0.044715 * square)
    return active * up_pre, active, up_pre * slope


def bucket_of(relative):
    distance = jnp.abs(relative)
    far_bucket = jnp.full_like(distance, 8)
    for threshold in bucket_edges:
        far_bucket = far_bucket + (distance >= threshold).astype(jnp.int32)
    return jnp.where(distance < 8, distance, far_bucket) + 16 * (relative > 0).astype(jnp.int32)


def row_scale(values):
    return lax.rsqrt(jnp.mean(values * values, axis=-1, keepdims=True) + epsilon)


def dot_as(left, right, contract):
    return lax.dot_general(left, right, (contract, ((), ())), preferred_element_type=jnp.float32)


NN, NT, TN = ((1,), (0,)), ((1,), (1,)), ((0,), (0,))


def layer_kernel(
    sizes, rows_per, layer_in, norm_attn, norm_moe, table_t, router_t, route_ref, slot_ref, cot_ref,
    wq_hbm, wk_hbm, wv_hbm, wo_hbm, wg_hbm, wu_hbm, wd_hbm,
    q_out, x_hbm, hid_hbm, dg_hbm, du_hbm, gr_hbm, *attn_hbm_and_scratch,
):
    attn_hbm, (gate_out, *scratch) = attn_hbm_and_scratch[:7], attn_hbm_and_scratch[7:]
    query, key, value, probs, context, residual, attn_in = scratch[:7]
    x_ref, hid_out, dg_out, du_out, gr_out, g_ref, w_ref, weights, act, slope, away, own = scratch[7:19]
    sem_a, sem_w, sem_e, *scratch = scratch[19:]
    me = Place(*sizes)
    c = me.c
    seq, width = layer_in.shape
    heads, buckets = table_t.shape
    units = wg_hbm.shape[1]
    bf, f32 = jnp.bfloat16, jnp.float32

    def emit(i, src, dst):
        copy = pltpu.make_async_copy(src, dst, sem_e.at[i])
        copy.start()
        return copy

    attn_w = []
    for i, src in enumerate((wq_hbm, wk_hbm, wv_hbm, wo_hbm)):
        dst = weights.at[pl.ds(i * width, width)]
        attn_w.append(pltpu.make_async_copy(src, dst, sem_a.at[i]))
        attn_w[-1].start()
    greet(column_peers(me))
    rows_in = rows_of(me, rows_per, scratch[:8])
    info_all, gates, tok = scratch[:3]
    buf_x, buf_w, buf_g = scratch[5:8]
    out_x, out_w, out_g = [
        Spread(me, buf, recv, [s.at[i] for s in scratch[8:14]])
        for i, (buf, recv) in enumerate(((buf_x, x_ref), (buf_w, w_ref), (buf_g, g_ref)))
    ]
    scratch = scratch[14:]
    column = me.n_expert
    quarter = [range(i * column // 4, (i + 1) * column // 4) for i in range(4)]
    info_all[c, 0:2, :] = route_ref[...]
    info_all[c, 2:4, :] = slot_ref[...]
    info_all[c, 4:, :] = jnp.zeros((4, seq), jnp.int32)
    rows_in.share("info", info_all)
    tok[1, c] = cot_ref[...]
    rows_in.share(1, tok.at[1])
    rows = layer_in[...].astype(f32)
    attn_in[...] = (rows * row_scale(rows) * norm_attn[...]).astype(bf)
    rows_in.hots()
    buf_g[...] = rows_in.gather(1)
    out_g.send()
    for i, ref in enumerate((query, key, value)):
        attn_w[i].wait()
        ref[...] = dot_as(attn_in[...], weights[i * width : (i + 1) * width, :], NN).astype(bf)
    relative = lax.broadcasted_iota(jnp.int32, (heads, 2 * seq), 1) - seq
    bucket = bucket_of(relative)
    bias_of = jnp.zeros((heads, 2 * seq), f32)
    for n in range(buckets):
        bias_of = jnp.where(bucket == n, table_t[:, n : n + 1], bias_of)
    pair = 2 * width // heads
    low_half = lax.broadcasted_iota(jnp.int32, (seq, pair), 1) < pair // 2
    for n in range(heads // 2):
        lanes = slice(n * pair, (n + 1) * pair)
        k2, v2 = key[:, lanes], value[:, lanes]
        total = None
        for h in range(2):
            mine = low_half if h == 0 else ~low_half
            head = 2 * n + h
            line = jnp.broadcast_to(bias_of[head : head + 1, :], (seq, 2 * seq))
            bias = pltpu.roll(line, seq, 1, stride=1, stride_axis=0)[:, :seq]
            scores = dot_as(query[:, lanes], jnp.where(mine, k2, jnp.zeros_like(k2)), NT) + bias
            exponent = jnp.exp(scores - jnp.max(scores, axis=-1, keepdims=True))
            prob = exponent / jnp.sum(exponent, axis=-1, keepdims=True)
            probs[head] = prob
            term = dot_as(prob.astype(bf), jnp.where(mine, v2, jnp.zeros_like(v2)), NN)
            total = term if total is None else total + term
        context[:, lanes] = total.astype(bf)
        if n % 4 == 3:
            out_g.pass_on(quarter[n // 4])
    attn_w[3].wait()
    resid = rows + dot_as(context[...], weights[3 * width : 4 * width, :], NN)
    residual[...] = resid
    fetch = {}
    attn_saved = (query, key, value, probs, context, residual, attn_in)
    for n, j in enumerate((c, 1 - c)):
        for i, src in enumerate((wg_hbm, wu_hbm, wd_hbm)):
            dst = weights.at[pl.ds(pl.multiple_of((2 * i + j) * units, 16), units)]
            fetch[n, i] = pltpu.make_async_copy(src.at[j], dst, sem_w.at[n, i])
            fetch[n, i].start()
    moe_in = resid * row_scale(resid) * norm_moe[...]
    tok[0, c] = moe_in.astype(bf)
    rows_in.share(0, tok.at[0])
    logits = lax.dot_general(
        router_t[...], moe_in, (NT, ((), ())), preferred_element_type=f32, precision=highest
    )
    logits = jnp.exp(logits - jnp.max(logits, axis=0, keepdims=True))
    gate_prob = logits / jnp.sum(logits, axis=0, keepdims=True)
    expert_ids = lax.broadcasted_iota(jnp.int32, gate_prob.shape, 0)
    picked = [
        jnp.sum(jnp.where(route_ref[k : k + 1, :] == expert_ids, gate_prob, 0.0), axis=0, keepdims=True)
        for k in range(2)
    ]
    both = picked[0] + picked[1]
    for k in range(2):
        gates[c, k : k + 1, :] = picked[k] / both
    gates[c, 2:, :] = jnp.zeros((6, seq), f32)
    gate_out[...] = gates[c]
    rows_in.share("gates", gates)
    buf_x[...] = rows_in.gather(0)
    out_x.send()
    copies = [emit(5 + i, src, dst) for i, (src, dst) in enumerate(zip(attn_saved, attn_hbm))]
    out_g.pass_on(quarter[2])
    for e, tile in enumerate(rows_in.weights()):
        buf_w[e] = tile
    out_w.send()
    out_g.pass_on(quarter[3])
    out_g.cross(0)

    size = x_ref.shape[2]
    step = math.gcd(column, 8)
    chunk = step * size
    back = Back(
        me, lambda i: away.at[i],
        lambda i, block: own[i, pl.ds(pl.multiple_of(block * size, 8), size), :],
        q_out, *scratch[:4], scratch[4:],
    )

    def part(i, j):
        return weights[pl.ds(pl.multiple_of((2 * i + j) * units, 16), units), :]

    def flat(value):
        return value.reshape(chunk, value.shape[-1])

    def blocks(value):
        return value.reshape(step, size, value.shape[-1])

    def store(i, first, some, rows, value):
        if first:
            away[i, some] = blocks(value.astype(bf))
        else:
            own[i, rows, :] = value

    def each(start, count, body):
        @pl.loop(0, count // step)
        def _(n):
            at = start + n * step
            body(pl.ds(at, step), pl.ds(pl.multiple_of(at * size, 8), chunk))

    def forward(first, j, start, count):
        def body(some, rows):
            x = flat(x_ref[j, some])
            gate_pre = dot_as(x, part(0, j), NT)
            up_pre = dot_as(x, part(1, j), NT)
            hidden, active, lean = gated_terms(gate_pre, up_pre)
            act[j, rows, :] = active
            slope[j, rows, :] = lean
            hidden = hidden.astype(bf)
            hid_out[j, some] = blocks(hidden)
            store(0, first, some, rows, dot_as(hidden, part(2, j), NN))

        each(start, count, body)

    lane = lax.broadcasted_iota(jnp.int32, (size, 128), 1)
    row = lax.broadcasted_iota(jnp.int32, (size, 128), 0)

    def backward(first, j, start, count):
        def body(some, rows):
            tiles = w_ref[j, some]
            grad = []
            for n in range(step):
                line = jnp.broadcast_to(tiles[n, 0:1, :], (size, 128))
                weight = jnp.sum(jnp.where(lane == row, line, 0.0), axis=1, keepdims=True)
                grad.append(weight * g_ref[j, some.start + n].astype(f32))
            grad = jnp.concatenate(grad, axis=0).astype(bf)
            gr_out[j, some] = blocks(grad)
            grad_hidden = dot_as(grad, part(2, j), NT)
            dg = (grad_hidden * slope[j, rows, :]).astype(bf)
            du = (grad_hidden * act[j, rows, :]).astype(bf)
            dg_out[j, some] = blocks(dg)
            du_out[j, some] = blocks(du)
            store(1, first, some, rows, dot_as(dg, part(0, j), NN) + dot_as(du, part(1, j), NN))

        each(start, count, body)

    here = me.y * column
    away_ys = [back.ys[k] * column for k in range(1, me.ny)]
    shares = [back.order[i * column // 4 : (i + 1) * column // 4] for i in range(4)]
    out_x.pass_on(range(column))
    out_x.cross(0)
    for s in range(1, me.ny):
        out_g.cross(s)
    for i in range(3):
        fetch[0, i].wait()
    forward(False, c, here, column)
    for i in range(3):
        fetch[1, i].wait()
    out_x.crossed[0].wait_recv()
    forward(True, 1 - c, here, column)
    back.to_mate(0, 0)
    out_w.pass_column()
    out_w.cross(0)
    for s in range(1, me.ny):
        out_x.cross(s)
    for k in range(1, me.ny):
        out_x.crossed[k].wait_recv()
        forward(True, 1 - c, away_ys[k - 1], column)
        back.to_mate(0, k)
    for s in range(1, me.ny):
        out_w.cross(s)
    for k in range(1, me.ny):
        forward(False, c, away_ys[k - 1], column)
    back.along_y(0)
    out_g.arrive()
    out_w.arrive()
    for k in range(1, me.ny):
        backward(True, 1 - c, away_ys[k - 1], column)
        back.to_mate(1, k)
    back.finish(0, shares[0])
    for k in range(1, me.ny):
        backward(False, c, away_ys[k - 1], column)
    back.along_y(1)
    back.finish(0, shares[1])
    backward(True, 1 - c, here, column)
    back.to_mate(1, 0)
    back.finish(0, shares[2])
    backward(False, c, here, column)
    saved = ((x_ref, x_hbm), (hid_out, hid_hbm), (dg_out, dg_hbm), (du_out, du_hbm), (gr_out, gr_hbm))
    copies += [emit(i, src, dst) for i, (src, dst) in enumerate(saved)]
    back.finish(0, shares[3])
    back.across(0)
    back.finish(1, back.order)
    back.across(1)
    back.close()
    for copy in copies:
        copy.wait()
    for payload in (out_x, out_w, out_g):
        payload.close()
    rows_in.close()


def layer(sizes, micro, cap, layer_in, norms, table_t, router_t, places, cot, attn_w, expert_w):
    n_expert, ny, per_core = sizes[0], sizes[1] // 2, micro * cap
    seq, width = cot.shape
    units = expert_w[0].shape[1]
    heads = table_t.shape[0]
    count, size = ny * n_expert, 2 * per_core
    bf, f32 = jnp.bfloat16, jnp.float32
    any_space = pl.BlockSpec(memory_space=pl.ANY)
    inner = jax.ShapeDtypeStruct((2, count, size, units), bf)
    outer = jax.ShapeDtypeStruct((2, count, size, width), bf)
    low, full = jax.ShapeDtypeStruct((seq, width), bf), jax.ShapeDtypeStruct((seq, width), f32)
    return pl.pallas_call(
        functools.partial(layer_kernel, sizes, (micro, cap, per_core)),
        out_shape=(
            jax.ShapeDtypeStruct((2, 2, n_expert, size, width), bf), outer, inner, inner, inner, outer,
            low, low, low, jax.ShapeDtypeStruct((heads, seq, seq), f32), low, full, low,
            jax.ShapeDtypeStruct((8, seq), f32),
        ),
        in_specs=[VMEM] * 8 + [any_space] * 7,
        out_specs=(VMEM,) + (any_space,) * 12 + (VMEM,),
        scratch_shapes=[
            pltpu.VMEM((seq, width), bf),
            pltpu.VMEM((seq, width), bf),
            pltpu.VMEM((seq, width), bf),
            pltpu.VMEM((heads, seq, seq), f32),
            pltpu.VMEM((seq, width), bf),
            pltpu.VMEM((seq, width), f32),
            pltpu.VMEM((seq, width), bf),
            pltpu.VMEM(outer.shape, bf),
            pltpu.VMEM(inner.shape, bf),
            pltpu.VMEM(inner.shape, bf),
            pltpu.VMEM(inner.shape, bf),
            pltpu.VMEM(outer.shape, bf),
            pltpu.VMEM((2, count, size, width), bf),
            pltpu.VMEM((2, count, 8, 128), f32),
            pltpu.VMEM((max(4 * width, 6 * units), width), bf),
            pltpu.VMEM((2, count * size, units), f32),
            pltpu.VMEM((2, count * size, units), f32),
            pltpu.VMEM((2, count, size, width), bf),
            pltpu.VMEM((2, count * size, width), f32),
            DMA((4,)),
            DMA((2, 3)),
            DMA((12,)),
        ]
        + rows_scratch(sizes, per_core, seq, width)
        + spread_sems(sizes)
        + back_scratch(sizes, size, width),
        name="layer",
        compiler_params=pltpu.CompilerParams(
            collective_id=4, has_side_effects=True, vmem_limit_bytes=60 << 20
        ),
    )(layer_in, *norms, table_t, router_t, *places, cot, *attn_w, *expert_w)


def finish_kernel(small, sums_hbm, x_hbm, h_hbm, dg_hbm, du_hbm, gr_hbm, *refs):
    outs, (router_out, attn_out, moe_out, table_out) = refs[:7], refs[7:11]
    sums, x, h, dg, du, gr, stage, wide, sem_sum, sem_in, sem_out, sem_wide = refs[11:]
    rows = stage.shape[1]
    width = sums.shape[1]
    units = h.shape[2]
    loads = {}

    def load(key, src, dst, sem):
        loads[key] = pltpu.make_async_copy(src, dst, sem)
        loads[key].start()

    def load_sums(keys):
        for n in keys:
            part = n * rows // width, pl.ds(n * rows % width, rows)
            load(("sums", n), sums_hbm.at[part], sums.at[part], sem_sum.at[n])

    casts = range(4 * width // rows)
    load_sums(casts[:4])
    for i, (key, src, dst) in enumerate(
        (("dg", dg_hbm, dg), ("x", x_hbm, x), ("du", du_hbm, du), ("h", h_hbm, h), ("gr", gr_hbm, gr))
    ):
        for j in range(2):
            load((key, j), src.at[j], dst.at[j], sem_in.at[i, j])
    load_sums(casts[4:])
    experts = router_out.shape[0]
    router_out[...] = small[:experts]
    attn_out[...] = small[experts : experts + 1]
    moe_out[...] = small[experts + 1 : experts + 2]
    table_out[...] = small[experts + 8 : experts + 8 + table_out.shape[0], : table_out.shape[1]]

    def need(key):
        if key in loads:
            loads.pop(key).wait()

    jobs = []
    products = [
        (left, right, out, j)
        for left, right, out in ((("dg", dg), ("x", x), 4), (("du", du), ("x", x), 5), (("h", h), ("gr", gr), 6))
        for j in range(2)
    ]
    casts = list(casts)
    every = max(1, len(casts) // len(products))
    while casts or products:
        jobs += casts[:every]
        casts = casts[every:]
        jobs += products[:1]
        products = products[1:]
    flying = {}
    counts = [0, 0]
    for job in jobs:
        product = not isinstance(job, int)
        box, sem = (wide, sem_wide) if product else (stage, sem_out)
        slot = counts[product] % box.shape[0]
        counts[product] += 1
        if (product, slot) in flying:
            flying[product, slot].wait()
        if product:
            (left_key, left), (right_key, right), out, j = job
            need((left_key, j))
            need((right_key, j))
            box[slot] = dot_as(left[j], right[j], TN)
            dst = outs[out].at[j]
        else:
            need(("sums", job))
            m, r = job * rows // width, job * rows % width
            box[slot] = sums[m, r : r + rows, :].astype(jnp.float32)
            dst = outs[m].at[pl.ds(r, rows)]
        flying[product, slot] = pltpu.make_async_copy(box.at[slot], dst, sem.at[slot])
        flying[product, slot].start()
    for copy in flying.values():
        copy.wait()


def finish(sums, small, x, h, dg, du, gr, experts, table):
    f32 = jnp.float32
    width = sums.shape[1]
    units = h.shape[2]
    any_space = pl.BlockSpec(memory_space=pl.ANY)
    return pl.pallas_call(
        finish_kernel,
        out_shape=(jax.ShapeDtypeStruct((width, width), f32),) * 4
        + (jax.ShapeDtypeStruct((2, units, width), f32),) * 3
        + tuple(jax.ShapeDtypeStruct(a, f32) for a in ((experts, width), (1, width), (1, width), table)),
        in_specs=[VMEM] + [any_space] * 6,
        out_specs=(any_space,) * 7 + (VMEM,) * 4,
        scratch_shapes=[pltpu.VMEM(a.shape, a.dtype) for a in (sums, x, h, dg, du, gr)]
        + [pltpu.VMEM((4, 256, width), f32), pltpu.VMEM((2, units, width), f32)]
        + [DMA((4 * width // 256,)), DMA((5, 2)), DMA((4,)), DMA((2,))],
        name="finish",
        compiler_params=pltpu.CompilerParams(vmem_limit_bytes=60 << 20),
    )(small, sums, x, h, dg, du, gr)


def upright(line):
    n = line.shape[1]
    square = lax.broadcasted_iota(jnp.int32, (n, n), 0) == lax.broadcasted_iota(jnp.int32, (n, n), 1)
    return jnp.sum(jnp.where(square, jnp.broadcast_to(line, (n, n)), 0.0), axis=1, keepdims=True)


def flat_line(column):
    n = column.shape[0]
    square = lax.broadcasted_iota(jnp.int32, (n, n), 0) == lax.broadcasted_iota(jnp.int32, (n, n), 1)
    return jnp.sum(jnp.where(square, jnp.broadcast_to(column, (n, n)), 0.0), axis=0, keepdims=True)


def diagonals(values):
    n = values.shape[1]
    total = None
    for first in range(0, n, 8):
        wide = jnp.concatenate([values[first : first + 8, :], jnp.zeros((8, n), jnp.float32)], axis=1)
        wide = pltpu.roll(wide, n - first, 1)
        total = wide if total is None else total + wide
    row = lax.broadcasted_iota(jnp.int32, total.shape, 0)
    for bit in (1, 2, 4):
        total = jnp.where((row & bit) > 0, pltpu.roll(total, 2 * n - bit, 1), total)
    return jnp.sum(total, axis=0, keepdims=True)


def settle_kernel(
    sizes, rows_per, pieces,
    back_hbm, route_ref, slot_ref, gate_ref, *inputs_hbm_and_rest,
):
    inputs_hbm, rest = inputs_hbm_and_rest[:9], inputs_hbm_and_rest[9:]
    settle_body(sizes, rows_per, pieces, (back_hbm, *inputs_hbm), route_ref, slot_ref, gate_ref, *rest)


def settle_body(
    sizes, rows_per, pieces, inputs_hbm, route_ref, slot_ref, gate_ref, norm_attn, norm_moe, router_t, wq_hbm, wk_hbm, wv_hbm, wo_hbm,
    layer_out, grad_in, out_hbm, small_out,
    back_ref, cot_ref, layer_in, residual, context, attn_in, query, key, value, probs, sem_l,
    weights, sem_a, left_ref, right_ref, small_ref, lines, out, sem_out, buf_a, buf_b, acc, *boxes,
):
    bf, f32 = jnp.bfloat16, jnp.float32
    micro, cap, per_core = rows_per
    inputs = (back_ref, cot_ref, layer_in, residual, context, attn_in, query, key, value, probs)
    loads = {}
    for i in (5, 4, 0, 1, 3, 8, 9, 6, 7, 2):
        loads[i] = pltpu.make_async_copy(inputs_hbm[i], inputs[i], sem_l.at[i])
        loads[i].start()

    def need(*which):
        for i in which:
            loads[i].wait()

    attn_w = []
    for i, src in ((3, wo_hbm), (0, wq_hbm), (1, wk_hbm), (2, wv_hbm)):
        attn_w.append(pltpu.make_async_copy(src, weights.at[i], sem_a.at[i]))
        attn_w[-1].start()
    me = Place(*sizes)
    c, mate = me.c, me.at(c=1 - me.c)
    n = me.nx
    seq = right_ref.shape[1]
    total_rows = width = out.shape[1]
    is0 = c == 0
    pair = jnp.where(is0, me.x, me.y)
    other = jnp.where(is0, me.y, me.x)
    lo, hi, nh = pair % 2, pair // 2, n // 2

    def along(pair_at, other_at, z=None):
        return me.at(x=jnp.where(is0, pair_at, other_at), y=jnp.where(is0, other_at, pair_at), z=z)

    flip_x, flip_y = me.x + 1 - 2 * (me.x % 2), me.y + 1 - 2 * (me.y % 2)
    dims = [
        (n, other, lambda q: along(pair, q)),
        (nh, hi, lambda q: along(q * 2 + lo, other)),
        (2, me.z % 2, lambda q: me.at(z=me.z // 2 * 2 + q)),
        (me.nz // 2, me.z // 2, lambda q: me.at(z=q * 2 + me.z % 2)),
    ]
    parts, gots = boxes[:4], boxes[4:8]
    half, small_half, small_got, fs, fr, os, ps, pr, gs, gr, ms, mr, cs, cr, ss, sr = boxes[8:]
    levels = [i for i, d in enumerate(dims) if d[0] > 1]
    x_peers = [me.at(x=(me.x + k) % n) for k in range(1, n)]
    y_peers = [me.at(y=(me.y + k) % n) for k in range(1, n)]
    z_peers = [me.at(z=(me.z + k) % me.nz) for k in range(1, me.nz)]
    greet(
        [mate, me.at(x=flip_x, c=1 - c), me.at(y=flip_y, c=1 - c)] + x_peers + y_peers + z_peers
    )

    def slot_a(slot):
        return buf_a.at[pl.ds(pl.multiple_of(slot * seq, seq), seq), :]

    def slot_b(slot):
        return buf_b.at[pl.ds(pl.multiple_of(slot * seq, seq), seq), :]

    need(5, 4)
    left_ref[0] = attn_in[...]
    left_ref[1] = context[...]
    targets = [
        (mate, 1 - c, other % 2, c),
        (me.at(x=flip_x, c=0), 0, flip_x % 2, 2 + c),
        (me.at(y=flip_y, c=1), 1, flip_y % 2, 2 + c),
    ]
    factor = []
    for i, (device, role, parity, slot) in enumerate(targets):
        a = jnp.where(role == 0, 0, parity)
        factor.append(remote(left_ref.at[a], slot_a(slot), fs.at[i, 0], fr.at[slot, 0], device))
    own = [pltpu.make_async_copy(left_ref.at[jnp.where(is0, 0, lo)], slot_a(c), os.at[0])]
    own[0].start()

    size = 2 * per_core
    group = lax.broadcasted_iota(jnp.int32, (1, seq), 1) // (seq // micro)
    slot_ids = lax.broadcasted_iota(jnp.int32, (2 * me.n_expert * size, seq), 0)
    hots = []
    for k in range(2):
        route, slot = route_ref[k : k + 1, :], slot_ref[k : k + 1, :]
        place = (route % 2) * (me.n_expert * size) + (route // 2) * size + c * per_core + group * cap + slot
        hots.append(jnp.where(slot_ids == jnp.where(slot >= 0, place, -1), 1.0, 0.0))
    low = [h.astype(bf) for h in hots] + [(hots[0] + hots[1]).astype(bf)]
    half_slots = me.n_expert * size

    def picked(hot, which):
        total = None
        for j in range(2):
            rows = back_ref[which, j].reshape(half_slots, width)
            term = dot_as(hot[j * half_slots : (j + 1) * half_slots, :], rows, TN)
            total = term if total is None else total + term
        return total

    need(0, 1, 3)
    cot = cot_ref[...].astype(f32)
    resid = residual[...]
    chosen = [picked(low[k], 0) for k in range(2)]
    gate = [upright(gate_ref[k : k + 1, :]) for k in range(2)]
    layer_out[...] = (resid + (gate[0] * chosen[0] + gate[1] * chosen[1])).astype(bf)
    grad_gate = [jnp.sum(cot * chosen[k], axis=-1, keepdims=True) for k in range(2)]
    mean_grad = gate[0] * grad_gate[0] + gate[1] * grad_gate[1]
    logit = [gate[k] * (grad_gate[k] - mean_grad) for k in range(2)]
    experts = router_t.shape[0]
    by_token, by_expert = None, None
    for k in range(2):
        route = route_ref[k : k + 1, :]
        line = jnp.where(
            lax.broadcasted_iota(jnp.int32, (experts, seq), 0) == route, flat_line(logit[k]), 0.0
        )
        by_expert = line if by_expert is None else by_expert + line
        route_up = upright(route.astype(f32)).astype(jnp.int32)
        line = jnp.where(
            lax.broadcasted_iota(jnp.int32, (seq, experts), 1) == route_up, logit[k], 0.0
        )
        by_token = line if by_token is None else by_token + line

    def exact(left, right):
        return lax.dot_general(
            left, right, (NN, ((), ())), preferred_element_type=f32, precision=highest
        )

    scale = row_scale(resid)
    normed = resid * scale
    small_ref[:experts] = exact(by_expert, normed * norm_moe[...])
    grad_moe = picked(low[2], 1) + exact(by_token, router_t[...])
    small_ref[experts:] = jnp.zeros((small_ref.shape[0] - experts, width), f32)
    small_ref[experts + 1 : experts + 2] = jnp.sum(grad_moe * normed, axis=0, keepdims=True)
    grad_n = grad_moe * norm_moe[...]
    grad_resid = cot + scale * (grad_n - normed * jnp.mean(grad_n * normed, axis=-1, keepdims=True))
    right_ref[3] = grad_resid.astype(bf)
    grad_in[...] = grad_resid
    attn_w[0].wait()
    grad_context = dot_as(right_ref[3], weights[3], NT).astype(bf)

    need(8, 9, 6, 7, 2)
    heads = probs.shape[0]
    pair_lanes = 2 * width // heads
    low_half = lax.broadcasted_iota(jnp.int32, (seq, pair_lanes), 1) < pair_lanes // 2
    for n2 in range(heads // 2):
        lanes = slice(n2 * pair_lanes, (n2 + 1) * pair_lanes)
        sums = [None, None, None]
        for h in range(2):
            mine = low_half if h == 0 else ~low_half
            head = 2 * n2 + h

            def only(value):
                return jnp.where(mine, value, jnp.zeros_like(value))

            prob = probs[head]
            grad_c = only(grad_context[:, lanes])
            grad_p = dot_as(grad_c, value[:, lanes], NT)
            grad_s = prob * (grad_p - jnp.sum(prob * grad_p, axis=-1, keepdims=True))
            lines[head : head + 1, :] = diagonals(grad_s)
            grad_s = grad_s.astype(bf)
            terms = (
                dot_as(grad_s, only(key[:, lanes]), NN),
                dot_as(grad_s, only(query[:, lanes]), TN),
                dot_as(prob.astype(bf), grad_c, TN),
            )
            sums = [t if s is None else s + t for s, t in zip(sums, terms)]
        for i in range(3):
            right_ref[i, :, lanes] = sums[i].astype(bf)
    for i, (device, role, parity, slot) in enumerate(targets):
        factor.append(
            remote(right_ref.at[role * 2 + parity], slot_b(slot), fs.at[i, 1], fr.at[slot, 1], device)
        )
    own.append(pltpu.make_async_copy(right_ref.at[c * 2 + lo], slot_b(c), os.at[1]))
    own[1].start()
    buckets = 32
    bucket = bucket_of(lax.broadcasted_iota(jnp.int32, (2 * seq, buckets), 0) - seq)
    hot = jnp.where(bucket == lax.broadcasted_iota(jnp.int32, (2 * seq, buckets), 1), 1.0, 0.0)
    small_ref[experts + 8 : experts + 8 + heads, :buckets] = exact(lines[...], hot)
    grad_attn = None
    for i in range(3):
        attn_w[1 + i].wait()
        term = dot_as(right_ref[i], weights[i], NT)
        grad_attn = term if grad_attn is None else grad_attn + term
    rows = layer_in[...].astype(f32)
    scale = row_scale(rows)
    normed = rows * scale
    small_ref[experts : experts + 1] = jnp.sum(grad_attn * normed, axis=0, keepdims=True)
    grad_n = grad_attn * norm_attn[...]
    grad_in[...] += scale * (grad_n - normed * jnp.mean(grad_n * normed, axis=-1, keepdims=True))

    rows_s = half.shape[0]
    small = [remote(small_ref.at[pl.ds((1 - c) * rows_s, rows_s)], half, ss.at[0], sr.at[0], mate)]
    small_dims = [
        (n, me.x, lambda q: me.at(x=q)),
        (n, me.y, lambda q: me.at(y=q)),
        (me.nz, me.z, lambda q: me.at(z=q)),
    ]
    small_wait = [small[0]]
    small_slot = [1]

    def small_step(step):
        for copy in small_wait:
            copy.wait_recv()
        small_wait.clear()
        if step == 0:
            total = small_ref[pl.ds(c * rows_s, rows_s)] + half[...]
        elif step <= 3:
            total = small_got[step - 1, 0]
            for k in range(1, small_dims[step - 1][0]):
                total = total + small_got[step - 1, k]
        if step < 3:
            count, index, peer = small_dims[step]
            small_half[step] = total
            small_got[step, index] = total
            for k in range(1, count):
                small_wait.append(
                    remote(
                        small_half.at[step], small_got.at[step, index], ss.at[small_slot[0]],
                        sr.at[small_slot[0]], peer((index + k) % count),
                    )
                )
                small_slot[0] += 1
        elif step == 3:
            small_out[pl.ds(c * rows_s, rows_s)] = total
            block = small_out.at[pl.ds(c * rows_s, rows_s)]
            small_wait.append(
                remote(block, block, ss.at[small_slot[0]], sr.at[small_slot[0]], mate)
            )
        small.extend(small_wait)

    for where in (1 - c, 2, 3):
        for i, (src, dst) in enumerate(((left_ref, slot_a(where)), (right_ref, slot_b(where)))):
            pltpu.make_async_remote_copy(
                src_ref=src.at[0], dst_ref=dst, send_sem=fs.at[0, i], recv_sem=fr.at[where, i],
                device_id=mate, device_id_type=MESH,
            ).wait_recv()
    for copy in own:
        copy.wait()

    rows_k = total_rows // pieces
    matrix = c * 2 + lo
    pending, written = {}, []

    def multiply(k):
        acc[k] = lax.dot_general(
            buf_a[:, k * rows_k : (k + 1) * rows_k], buf_b[...], (TN, ((), ())),
            preferred_element_type=jnp.float32,
        )
        push(k, 0, rows_k)

    def push(k, at, rows):
        level = levels[at]
        count, index, peer = dims[level]
        size = rows // count
        copies = []
        for s in range(1, count):
            to = (index + s) % count
            parts[level][k, s - 1] = acc[k, pl.ds(pl.multiple_of(to * size, 16), size), :].astype(jnp.bfloat16)
            copies.append(
                remote(
                    parts[level].at[k, s - 1], gots[level].at[k, s - 1],
                    ps.at[level, k, s - 1], pr.at[level, k, s - 1], peer(to),
                )
            )
        pending["push", at, k] = copies

    def rows_at(at):
        rows = rows_k
        for i in range(at):
            rows //= dims[levels[i]][0]
        return rows

    def add(k, at):
        level = levels[at]
        count, index, _ = dims[level]
        size = rows_at(at) // count
        for copy in pending["push", at, k]:
            copy.wait_recv()
        total = acc[k, pl.ds(pl.multiple_of(index * size, 16), size), :]
        for s in range(1, count):
            total = total + gots[level][k, s - 1].astype(jnp.float32)
        if at + 1 < len(levels):
            acc[k, :size, :] = total
            push(k, at + 1, size)
        else:
            out[matrix, pl.ds(offset(k, at), size), :] = total.astype(jnp.bfloat16)
            share(k, at)

    def offset(k, at):
        start, rows = k * rows_k, rows_k
        for i in range(at + 1):
            count, index, _ = dims[levels[i]]
            rows //= count
            start = start + index * rows
        return pl.multiple_of(start, 16)

    def share(k, at):
        level = levels[at]
        count, index, peer = dims[level]
        size = rows_at(at) // count
        block = out.at[matrix, pl.ds(offset(k, at), size), :]
        pending["share", at, k] = [
            remote(block, block, gs.at[level, k, s - 1], gr.at[level, k, s - 1], peer((index + s) % count))
            for s in range(1, count)
        ]

    def shared(k, at):
        for copy in pending["share", at, k]:
            copy.wait_recv()
        if at:
            share(k, at - 1)
        else:
            block = out.at[matrix, pl.ds(k * rows_k, rows_k), :]
            pending["mate", k] = remote(
                block, block, ms.at[k], mr.at[k], along(pair + 1 - 2 * lo, other)
            )

    def across(k):
        pending["mate", k].wait_recv()
        block = out.at[pl.ds(2 * c, 2), pl.ds(k * rows_k, rows_k), :]
        pending["core", k] = remote(block, block, cs.at[k], cr.at[k], mate)
        write(k, c)

    def write(k, core):
        part = pl.ds(2 * core, 2), pl.ds(k * rows_k, rows_k), slice(None)
        written.append(pltpu.make_async_copy(out.at[part], out_hbm.at[part], sem_out.at[core, k]))
        written[-1].start()

    def close(k):
        pending["core", k].wait_recv()
        write(k, 1 - c)

    steps = [multiply]
    steps += [functools.partial(add, at=i) for i in range(len(levels))]
    steps += [functools.partial(shared, at=i) for i in reversed(range(len(levels)))]
    events = sorted((0 if p == 0 else p + k, p, k) for p in range(len(steps)) for k in range(pieces))
    before = 0
    for t, p, k in events:
        if before < t <= 5:
            small_step(t - 1)
        before = t
        steps[p](k)
    for k in range(pieces):
        across(k)
    for k in range(pieces):
        close(k)
    for copy in factor + small:
        copy.wait_send()
    for copies in pending.values():
        for copy in copies if isinstance(copies, list) else [copies]:
            copy.wait_send()
    for copy in written:
        copy.wait()


def settle(sizes, micro, cap, arrays, norms, router_t, attn_w):
    n_expert, n_dp = sizes
    nz = math.gcd(n_expert, 4)
    n = n_expert // nz
    nh = n // 2
    assert n == n_dp // 2
    seq, width = arrays[5].shape
    heads = arrays[12].shape[0]
    splits = [n, nh, 2, nz // 2]
    pieces = max(1, min(8, width // (16 * math.prod(splits))))
    rows_k = width // pieces
    bf, f32 = jnp.bfloat16, jnp.float32
    small_rows = router_t.shape[0] + 8 + heads
    small_rows += -small_rows % 16
    rows_s = small_rows // 2
    sizes_at = [rows_k // math.prod(splits[: i + 1]) for i in range(4)]
    counts = [max(q - 1, 1) for q in splits]
    most = max(counts)
    boxes = [
        pltpu.VMEM((pieces, q, s if k > 1 else 16, width), bf) for q, s, k in zip(counts, sizes_at, splits)
    ]
    smalls = 2 * n + nz
    any_space = pl.BlockSpec(memory_space=pl.ANY)
    return pl.pallas_call(
        functools.partial(settle_kernel, sizes, (micro, cap, micro * cap), pieces),
        out_shape=(
            jax.ShapeDtypeStruct((seq, width), bf),
            jax.ShapeDtypeStruct((seq, width), f32),
            jax.ShapeDtypeStruct((4, width, width), bf),
            jax.ShapeDtypeStruct((small_rows, width), f32),
        ),
        in_specs=[any_space] + [VMEM] * 3 + [any_space] * 9 + [VMEM] * 3 + [any_space] * 4,
        out_specs=(VMEM, VMEM, any_space, VMEM),
        scratch_shapes=[pltpu.VMEM(a.shape, a.dtype) for a in (arrays[0], *arrays[4:])]
        + [
            DMA((10,)),
            pltpu.VMEM((4, width, width), bf),
            DMA((4,)),
            pltpu.VMEM((2, seq, width), bf),
            pltpu.VMEM((4, seq, width), bf),
            pltpu.VMEM((small_rows, width), f32),
            pltpu.VMEM((heads, 2 * seq), f32),
            pltpu.VMEM((4, width, width), bf),
            DMA((2, pieces)),
            pltpu.VMEM((4 * seq, width), bf),
            pltpu.VMEM((4 * seq, width), bf),
            pltpu.VMEM((pieces, rows_k, width), f32),
            *boxes,
            *boxes,
            pltpu.VMEM((rows_s, width), f32),
            pltpu.VMEM((3, rows_s, width), f32),
            pltpu.VMEM((3, max(n, nz), rows_s, width), f32),
            DMA((3, 2)),
            DMA((4, 2)),
            DMA((2,)),
            DMA((4, pieces, most)),
            DMA((4, pieces, most)),
            DMA((4, pieces, most)),
            DMA((4, pieces, most)),
            DMA((pieces,)),
            DMA((pieces,)),
            DMA((pieces,)),
            DMA((pieces,)),
            DMA((smalls,)),
            DMA((smalls,)),
        ],
        name="settle",
        compiler_params=pltpu.CompilerParams(
            collective_id=3, has_side_effects=True, vmem_limit_bytes=58 << 20
        ),
    )(*arrays, *norms, router_t, *attn_w)


def rms_scale(values):
    return lax.rsqrt(jnp.mean(values * values, axis=-1, keepdims=True) + epsilon)


def bucket_hot(seq_len, buckets):
    position = jnp.arange(seq_len, dtype=jnp.int32)
    bucket_ids = jnp.arange(buckets, dtype=jnp.int32)
    bucketed = bucket_of(position[None, :] - position[:, None])
    return (bucketed[None, :, :] == bucket_ids[:, None, None]).astype(jnp.float32)


def dot32(pattern, left, right):
    return jnp.einsum(pattern, left, right, preferred_element_type=jnp.float32)


def shards(
    layer_in, routes, queue_slots, norm_attn, w_query, w_key, w_value, w_out, rel_table,
    norm_moe, router, w_gate, w_up, w_down, cotangent,
):
    bf, f32 = jnp.bfloat16, jnp.float32
    seq_len, width = layer_in.shape
    buckets, heads = rel_table.shape
    expert_count = router.shape[1]
    sizes = (lax.axis_size("expert"), lax.axis_size("dp"))
    n_expert, n_dp = sizes
    assert w_gate.shape[0] == 2 and expert_count == 2 * n_expert
    group_len = seq_len // MICRO
    capacity = (5 * group_len + 2 * expert_count - 1) // (2 * expert_count)
    split_heads = (seq_len, heads, width // heads)
    places = (routes.T, queue_slots.T)
    expert_w = [jnp.swapaxes(w_gate, 1, 2), jnp.swapaxes(w_up, 1, 2), w_down]
    slots = n_dp // 2 * n_expert * 2 * MICRO * capacity
    fused = 2 * slots * width * 20 + 6 * w_gate.size < 52 << 20
    if fused:
        (
            back, rows_in, hidden, gate_grad, up_grad, grad_rows,
            query, key, value, probs, context, residual, attn_in, gates,
        ) = layer(
            sizes, MICRO, capacity, layer_in, (norm_attn[None], norm_moe[None]), rel_table.T, router.T,
            places, cotangent, (w_query, w_key, w_value, w_out), expert_w,
        )
    else:
        layer_rows = layer_in.astype(f32)
        attn_in = (layer_rows * rms_scale(layer_rows) * norm_attn).astype(bf)
        query = dot32("sd,de->se", attn_in, w_query).astype(bf)
        key = dot32("sd,de->se", attn_in, w_key).astype(bf)
        value = dot32("sd,de->se", attn_in, w_value).astype(bf)
        one_hot = bucket_hot(seq_len, buckets)
        bias = jnp.einsum("bij,bh->hij", one_hot, rel_table, precision=highest)
        scores = dot32("ihd,jhd->hij", query.reshape(split_heads), key.reshape(split_heads)) + bias
        exponent = jnp.exp(scores - jnp.max(scores, axis=-1, keepdims=True))
        probs = exponent / jnp.sum(exponent, axis=-1, keepdims=True)
        context = dot32("hij,jhd->ihd", probs.astype(bf), value.reshape(split_heads))
        context = context.astype(bf).reshape(seq_len, width)
        residual = layer_rows + dot32("se,ed->sd", context, w_out)
        moe_in = residual * rms_scale(residual) * norm_moe
        expert_ids = jnp.arange(expert_count, dtype=jnp.int32)
        first_hot = (routes[:, 0:1] == expert_ids).astype(f32)
        second_hot = (routes[:, 1:2] == expert_ids).astype(f32)
        gate_prob = jax.nn.softmax(jnp.dot(moe_in, router, precision=highest), axis=-1)
        prob_first, prob_second = jnp.sum(gate_prob * first_hot, axis=-1), jnp.sum(gate_prob * second_hot, axis=-1)
        gates = jnp.stack([prob_first, prob_second]) / (prob_first + prob_second)
        gates = jnp.pad(gates, ((0, 6), (0, 0)))
        info = jnp.concatenate([*places, jnp.zeros((4, seq_len), jnp.int32)])
        rows_in, weight_in, grad_in = spread(
            sizes, MICRO, capacity, info, moe_in.astype(bf), cotangent, gates
        )
        blocks = rows_in.shape[:-1] + (-1,)
        rows_in, grad_in = [a.reshape(2, -1, width) for a in (rows_in, grad_in)]
        slot_weight = weight_in[:, :, 0, : 2 * MICRO * capacity].reshape(2, -1, 1)
        grad_rows = (slot_weight * grad_in.astype(f32)).astype(bf)
        gate_pre = dot32("jrd,jdf->jrf", rows_in, w_gate)
        up_pre = dot32("jrd,jdf->jrf", rows_in, w_up)
        hidden, active, lean = gated_terms(gate_pre, up_pre)
        hidden = hidden.astype(bf)
        partial_out = dot32("jrf,jfd->jrd", hidden, w_down).astype(bf)
        hidden_grad = dot32("jrd,jfd->jrf", grad_rows, w_down)
        gate_grad, up_grad = (hidden_grad * lean).astype(bf), (hidden_grad * active).astype(bf)
        rows_grad = dot32("jrf,jdf->jrd", gate_grad, w_gate) + dot32("jrf,jdf->jrd", up_grad, w_up)
        back = gather_back(sizes, partial_out.reshape(blocks), rows_grad.astype(bf).reshape(blocks))
    layer_out, grad_input, sums, small = settle(
        sizes, MICRO, capacity,
        (back, *places, gates, cotangent, layer_in, residual, context, attn_in, query, key, value, probs),
        (norm_attn[None], norm_moe[None]), router.T, (w_query, w_key, w_value, w_out),
    )
    rows_in, hidden, gate_grad, up_grad, grad_rows = [
        a.reshape(2, -1, a.shape[-1]) for a in (rows_in, hidden, gate_grad, up_grad, grad_rows)
    ]
    (
        *matrices, grad_w_gate, grad_w_up, grad_w_down,
        grad_router, grad_norm_attn, grad_norm_moe, grad_table,
    ) = finish(
        sums, small, rows_in, hidden, gate_grad, up_grad, grad_rows, expert_count, (heads, buckets)
    )
    return (
        layer_out, grad_input, grad_norm_attn.reshape(width), *matrices, grad_table.T,
        grad_norm_moe.reshape(width), grad_router.T,
        jnp.swapaxes(grad_w_gate, 1, 2), jnp.swapaxes(grad_w_up, 1, 2), grad_w_down,
    )


def solution(mesh):
    in_specs = (
        P(("expert", "dp"), None),
        P(("expert", "dp"), None),
        P(("expert", "dp"), None),
        P(),
        P(),
        P(),
        P(),
        P(),
        P(),
        P(),
        P(),
        P("expert", None, "dp"),
        P("expert", None, "dp"),
        P("expert", "dp", None),
        P(("expert", "dp"), None),
    )
    out_specs = (
        P(("expert", "dp"), None),
        P(("expert", "dp"), None),
        P(),
        P(),
        P(),
        P(),
        P(),
        P(),
        P(),
        P(),
        P("expert", None, "dp"),
        P("expert", None, "dp"),
        P("expert", "dp", None),
    )
    return jax.shard_map(shards, mesh=mesh, in_specs=in_specs, out_specs=out_specs, check_vma=False)
```

```python
import functools
import math

import jax
import jax.numpy as jnp
from jax import lax
from jax.experimental import pallas as pl
from jax.experimental.pallas import tpu as pltpu
from jax.sharding import PartitionSpec as P

MICRO = 4

epsilon = 1e-06
bucket_edges = (12, 16, 23, 32, 46, 64, 91)
highest = lax.Precision.HIGHEST

MESH = pl.DeviceIdType.MESH
VMEM = pl.BlockSpec(memory_space=pltpu.VMEM)
DMA = pltpu.SemaphoreType.DMA


class Place:
    def __init__(self, n_expert, n_dp):
        self.n_expert, self.n_dp = n_expert, n_dp
        self.nz = math.gcd(n_expert, 4)
        self.nx = n_expert // self.nz
        self.ny = n_dp // 2
        self.e = lax.axis_index("expert")
        self.d = lax.axis_index("dp")
        self.z, self.x = self.e // self.nx, self.e % self.nx
        self.y, self.c = self.d // 2, self.d % 2

    def at(self, z=None, x=None, y=None, c=None, e=None):
        z = self.z if z is None else z
        x = self.x if x is None else x
        y = self.y if y is None else y
        c = self.c if c is None else c
        e = z * self.nx + x if e is None else e
        return (e, y * 2 + c)


def remote(src, dst, send, recv, device):
    copy = pltpu.make_async_remote_copy(
        src_ref=src, dst_ref=dst, send_sem=send, recv_sem=recv, device_id=device, device_id_type=MESH
    )
    copy.start()
    return copy


def greet(devices):
    barrier = pltpu.get_barrier_semaphore()
    for device in devices:
        pl.semaphore_signal(barrier, inc=1, device_id=device, device_id_type=MESH)
    pl.semaphore_wait(barrier, len(devices))


def column_peers(me):
    out = [me.at(c=1 - me.c)]
    out += [me.at(y=(me.y + k) % me.ny) for k in range(1, me.ny)]
    out += [me.at(e=(me.e + k) % me.n_expert) for k in range(1, me.n_expert)]
    return out


class Spread:
    def __init__(self, me, rows, recv, sems):
        self.me, self.rows, self.recv = me, rows, recv
        self.se, self.re, self.sy, self.ry, self.sc, self.rc = sems
        self.came, self.along, self.crossed = {}, {}, {}

    def send(self):
        me = self.me
        for k in range(1, me.n_expert):
            to = (me.e + k) % me.n_expert
            self.came[k] = remote(
                self.rows.at[to], self.recv.at[me.c, me.y * me.n_expert + me.e],
                self.se.at[k], self.re.at[k], me.at(e=to),
            )
        self.recv[me.c, me.y * me.n_expert + me.e] = self.rows[me.e]

    def pass_on(self, blocks):
        me = self.me
        for k in blocks:
            if k:
                self.came[k].wait_recv()
            src = (me.e - k + me.n_expert) % me.n_expert
            block = self.recv.at[me.c, me.y * me.n_expert + src]
            for s in range(1, me.ny):
                self.along[s, k] = remote(
                    block, block, self.sy.at[s - 1, k], self.ry.at[s - 1, k], me.at(y=(me.y + s) % me.ny)
                )

    def pass_column(self):
        me = self.me
        for k in range(1, me.n_expert):
            self.came[k].wait_recv()
        block = self.recv.at[me.c, pl.ds(me.y * me.n_expert, me.n_expert)]
        for s in range(1, me.ny):
            self.along[s, 0] = remote(
                block, block, self.sy.at[s - 1, 0], self.ry.at[s - 1, 0], me.at(y=(me.y + s) % me.ny)
            )

    def cross(self, s):
        me = self.me
        if s:
            for key, copy in self.along.items():
                if key[0] == s:
                    copy.wait_recv()
        block = self.recv.at[me.c, pl.ds((me.y - s + me.ny) % me.ny * me.n_expert, me.n_expert)]
        self.crossed[s] = remote(block, block, self.sc.at[s], self.rc.at[s], me.at(c=1 - me.c))

    def arrive(self):
        for copy in self.crossed.values():
            copy.wait_recv()

    def close(self):
        for copies in (self.came, self.along, self.crossed):
            for copy in copies.values():
                copy.wait_send()


def spread_sems(sizes):
    n_expert, ny = sizes[0], sizes[1] // 2
    most = max(ny - 1, 1)
    return [
        DMA((3, n_expert)), DMA((3, n_expert)), DMA((3, most, n_expert)), DMA((3, most, n_expert)),
        DMA((3, ny)), DMA((3, ny)),
    ]


class Rows:
    def __init__(self, me, rows_per, info_all, gates, tok, send, recv):
        self.me, self.rows_per, self.info_all, self.gates, self.tok = me, rows_per, info_all, gates, tok
        self.send, self.recv, self.copies = send, recv, {}
        self.seq = tok.shape[2]

    def share(self, i, ref):
        block = ref.at[self.me.c]
        mate = self.me.at(c=1 - self.me.c)
        self.copies[i] = remote(block, block, self.send.at[i], self.recv.at[i], mate)

    def hots(self):
        me, seq = self.me, self.seq
        micro, cap, per_core = self.rows_per
        self.copies["info"].wait_recv()
        row_ids = lax.broadcasted_iota(jnp.int32, (me.n_expert * 2 * per_core, seq), 0)
        group = lax.broadcasted_iota(jnp.int32, (1, seq), 1) // (seq // micro)
        self.each = []
        for cc in range(2):
            for k in range(2):
                route = self.info_all[cc, k : k + 1, :]
                slot = self.info_all[cc, 2 + k : 3 + k, :]
                target = (route // 2) * (2 * per_core) + cc * per_core + group * cap + slot
                target = jnp.where((slot >= 0) & (route % 2 == me.c), target, -1)
                self.each.append(jnp.where(row_ids == target, 1.0, 0.0))
        self.both = [(self.each[2 * cc] + self.each[2 * cc + 1]).astype(jnp.bfloat16) for cc in range(2)]

    def gather(self, i):
        self.copies[i].wait_recv()
        total = None
        for cc in range(2):
            term = jnp.dot(self.both[cc], self.tok[i, cc], preferred_element_type=jnp.float32)
            total = term if total is None else total + term
        return total.astype(jnp.bfloat16).reshape(self.me.n_expert, 2 * self.rows_per[2], -1)

    def weights(self):
        self.copies["gates"].wait_recv()
        size = 2 * self.rows_per[2]
        column = None
        for n, hot in enumerate(self.each):
            term = jnp.sum(hot * self.gates[n // 2, n % 2 : n % 2 + 1, :], axis=1, keepdims=True)
            column = term if column is None else column + term
        lane = lax.broadcasted_iota(jnp.int32, (size, 128), 1)
        row = lax.broadcasted_iota(jnp.int32, (size, 128), 0)
        tiles = []
        for e in range(self.me.n_expert):
            block = jnp.where(lane == row, column[e * size : (e + 1) * size, :], 0.0)
            tiles.append(jnp.broadcast_to(jnp.sum(block, axis=0, keepdims=True), (8, 128)))
        return tiles

    def close(self):
        for copy in self.copies.values():
            copy.wait_send()


NAMED = ("info", "gates", 0, 1)


class Named:
    def __init__(self, sems):
        self.at = {name: sems.at[i] for i, name in enumerate(NAMED)}


def rows_scratch(sizes, per_core, seq, width):
    mine = (sizes[0], 2 * per_core, width)
    bf = jnp.bfloat16
    return [
        pltpu.VMEM((2, 8, seq), jnp.int32),
        pltpu.VMEM((2, 8, seq), jnp.float32),
        pltpu.VMEM((2, 2, seq, width), bf),
        DMA((4,)),
        DMA((4,)),
        pltpu.VMEM(mine, bf),
        pltpu.VMEM((sizes[0], 8, 128), jnp.float32),
        pltpu.VMEM(mine, bf),
    ]


def rows_of(me, rows_per, scratch):
    info_all, gates, tok, send, recv = scratch[:5]
    return Rows(me, rows_per, info_all, gates, tok, Named(send), Named(recv))


def spread_kernel(sizes, rows_per, info_ref, moe_ref, cot_ref, w_ref, x_out, w_out, g_out, *scratch):
    me = Place(*sizes)
    c = me.c
    greet(column_peers(me))
    scratch, sems = scratch[:8], scratch[8:]
    rows = rows_of(me, rows_per, scratch)
    info_all, gates, tok = scratch[:3]
    info_all[c] = info_ref[...]
    rows.share("info", info_all)
    gates[c] = w_ref[...]
    rows.share("gates", gates)
    for i, ref in enumerate((moe_ref, cot_ref)):
        tok[i, c] = ref[...]
        rows.share(i, tok.at[i])
    rows.hots()
    buf_x, buf_w, buf_g = scratch[5:]
    out_x, out_w, out_g = [
        Spread(me, buf, recv, [s.at[i] for s in sems])
        for i, (buf, recv) in enumerate(((buf_x, x_out), (buf_w, w_out), (buf_g, g_out)))
    ]
    for i, payload in enumerate((out_x, out_g)):
        payload.rows[...] = rows.gather(i)
        payload.send()
    for e, tile in enumerate(rows.weights()):
        buf_w[e] = tile
    out_w.send()
    for payload in (out_x, out_g):
        payload.pass_on(range(me.n_expert))
        payload.cross(0)
    out_w.pass_column()
    out_w.cross(0)
    for payload in (out_x, out_g, out_w):
        for s in range(1, me.ny):
            payload.cross(s)
    for payload in (out_x, out_g, out_w):
        payload.arrive()
        payload.close()
    rows.close()


def spread(sizes, micro, cap, info, moe, cot, weights):
    n_expert, ny, per_core = sizes[0], sizes[1] // 2, micro * cap
    seq, width = cot.shape
    block = (2, ny * n_expert, 2 * per_core)
    bf = jnp.bfloat16
    return pl.pallas_call(
        functools.partial(spread_kernel, sizes, (micro, cap, per_core)),
        out_shape=(
            jax.ShapeDtypeStruct(block + (width,), bf),
            jax.ShapeDtypeStruct(block[:2] + (8, 128), jnp.float32),
            jax.ShapeDtypeStruct(block + (width,), bf),
        ),
        in_specs=[VMEM] * 4,
        out_specs=(VMEM,) * 3,
        scratch_shapes=rows_scratch(sizes, per_core, seq, width) + spread_sems(sizes),
        name="spread",
        compiler_params=pltpu.CompilerParams(
            collective_id=1, has_side_effects=True, vmem_limit_bytes=48 << 20
        ),
    )(info, moe, cot, weights)


class Back:
    def __init__(self, me, away, own, q_out, r1, stage, r2, final, sems):
        self.me, self.away, self.own = me, away, own
        self.q_out, self.r1, self.stage, self.r2, self.final = q_out, r1, stage, r2, final
        self.sems = sems
        self.ys = [(me.y + k) % me.ny for k in range(me.ny)]
        self.order = list(range(1, me.n_expert)) + [0]
        self.first, self.second, self.third, self.fourth = {}, {}, {}, {}
        self.arrived = set()

    def to_mate(self, i, k):
        me = self.me
        column = pl.ds(self.ys[k] * me.n_expert, me.n_expert)
        self.first[i, k] = remote(
            self.away(i).at[column], self.r1.at[i, column], self.sems[0].at[i, k], self.sems[1].at[i, k],
            me.at(c=1 - me.c),
        )

    def partial(self, i, y, e):
        block = y * self.me.n_expert + e
        return self.own(i, block) + self.r1[i, block].astype(jnp.float32)

    def along_y(self, i):
        me = self.me
        for k in range(1, me.ny):
            self.first[i, k].wait_recv()
            for j in self.order:
                e = (me.e + j) % me.n_expert
                self.stage[i, k - 1, e] = self.partial(i, self.ys[k], e).astype(jnp.bfloat16)
                self.second[i, k, j] = remote(
                    self.stage.at[i, k - 1, e], self.r2.at[i, k - 1, e],
                    self.sems[2].at[i, k - 1, j], self.sems[3].at[i, k - 1, j], me.at(y=self.ys[k]),
                )

    def finish(self, i, order):
        me = self.me
        if (i, 0) not in self.arrived:
            self.arrived.add((i, 0))
            self.first[i, 0].wait_recv()
        for j in order:
            e = (me.e + j) % me.n_expert
            total = self.partial(i, me.y, e)
            for k in range(1, me.ny):
                self.second[i, k, j].wait_recv()
                total = total + self.r2[i, k - 1, e].astype(jnp.float32)
            if j:
                self.final[i, e] = total.astype(jnp.bfloat16)
                self.third[i, j] = remote(
                    self.final.at[i, e], self.q_out.at[i, me.c, me.e],
                    self.sems[4].at[i, j], self.sems[5].at[i, j], me.at(e=e),
                )
            else:
                self.q_out[i, me.c, me.e] = total.astype(jnp.bfloat16)

    def across(self, i):
        for j in self.order[:-1]:
            self.third[i, j].wait_recv()
        block = self.q_out.at[i, self.me.c]
        s, r = self.sems[6].at[i], self.sems[7].at[i]
        self.fourth[i] = remote(block, block, s, r, self.me.at(c=1 - self.me.c))

    def close(self):
        for copy in self.fourth.values():
            copy.wait()
        for copies in (self.first, self.second, self.third):
            for copy in copies.values():
                copy.wait_send()


def back_scratch(sizes, size, width):
    n_expert, ny = sizes[0], sizes[1] // 2
    most = max(ny - 1, 1)
    bf = jnp.bfloat16
    return [
        pltpu.VMEM((2, ny * n_expert, size, width), bf),
        pltpu.VMEM((2, most, n_expert, size, width), bf),
        pltpu.VMEM((2, most, n_expert, size, width), bf),
        pltpu.VMEM((2, n_expert, size, width), bf),
        DMA((2, ny)),
        DMA((2, ny)),
        DMA((2, most, n_expert)),
        DMA((2, most, n_expert)),
        DMA((2, n_expert)),
        DMA((2, n_expert)),
        DMA((2,)),
        DMA((2,)),
    ]


def gather_back_kernel(sizes, p0_ref, p1_ref, q_out, *scratch):
    me = Place(*sizes)
    greet(column_peers(me))
    p_refs = (p0_ref, p1_ref)
    back = Back(
        me, lambda i: p_refs[i].at[1 - me.c],
        lambda i, block: p_refs[i][me.c, block].astype(jnp.float32), q_out, *scratch[:4], scratch[4:],
    )
    for i in range(2):
        for k in reversed(range(me.ny)):
            back.to_mate(i, k)
    for i in range(2):
        back.along_y(i)
    for i in range(2):
        back.finish(i, back.order)
        back.across(i)
    back.close()


def gather_back(sizes, first, second):
    n_expert = sizes[0]
    _, _, size, width = first.shape
    return pl.pallas_call(
        functools.partial(gather_back_kernel, sizes),
        out_shape=jax.ShapeDtypeStruct((2, 2, n_expert, size, width), jnp.bfloat16),
        in_specs=[VMEM] * 2,
        out_specs=VMEM,
        scratch_shapes=back_scratch(sizes, size, width),
        name="gather_back",
        compiler_params=pltpu.CompilerParams(
            collective_id=2, has_side_effects=True, vmem_limit_bytes=48 << 20
        ),
    )(first, second)


def gated_terms(gate_pre, up_pre):
    root = math.sqrt(2.0 / math.pi)
    square = gate_pre * gate_pre
    bend = jnp.tanh(root * (gate_pre + 0.044715 * square * gate_pre))
    half = 0.5 * (1.0 + bend)
    active = gate_pre * half
    slope = half + 0.5 * gate_pre * (1.0 - bend * bend) * root * (1.0 + 3 * 0.044715 * square)
    return active * up_pre, active, up_pre * slope


def bucket_of(relative):
    distance = jnp.abs(relative)
    far_bucket = jnp.full_like(distance, 8)
    for threshold in bucket_edges:
        far_bucket = far_bucket + (distance >= threshold).astype(jnp.int32)
    return jnp.where(distance < 8, distance, far_bucket) + 16 * (relative > 0).astype(jnp.int32)


def row_scale(values):
    return lax.rsqrt(jnp.mean(values * values, axis=-1, keepdims=True) + epsilon)


def dot_as(left, right, contract):
    return lax.dot_general(left, right, (contract, ((), ())), preferred_element_type=jnp.float32)


NN, NT, TN = ((1,), (0,)), ((1,), (1,)), ((0,), (0,))


def layer_kernel(
    sizes, rows_per, layer_in, norm_attn, norm_moe, table_t, router_t, route_ref, slot_ref, cot_ref,
    wq_hbm, wk_hbm, wv_hbm, wo_hbm, wg_hbm, wu_hbm, wd_hbm,
    q_out, x_hbm, hid_hbm, dg_hbm, du_hbm, gr_hbm, *attn_hbm_and_scratch,
):
    attn_hbm, (gate_out, *scratch) = attn_hbm_and_scratch[:7], attn_hbm_and_scratch[7:]
    query, key, value, probs, context, residual, attn_in = scratch[:7]
    x_ref, hid_out, dg_out, du_out, gr_out, g_ref, w_ref, weights, act, slope, away, own = scratch[7:19]
    sem_a, sem_w, sem_e, *scratch = scratch[19:]
    me = Place(*sizes)
    c = me.c
    seq, width = layer_in.shape
    heads, buckets = table_t.shape
    units = wg_hbm.shape[1]
    bf, f32 = jnp.bfloat16, jnp.float32

    def emit(i, src, dst):
        copy = pltpu.make_async_copy(src, dst, sem_e.at[i])
        copy.start()
        return copy

    attn_w = []
    for i, src in enumerate((wq_hbm, wk_hbm, wv_hbm, wo_hbm)):
        dst = weights.at[pl.ds(i * width, width)]
        attn_w.append(pltpu.make_async_copy(src, dst, sem_a.at[i]))
        attn_w[-1].start()
    greet(column_peers(me))
    rows_in = rows_of(me, rows_per, scratch[:8])
    info_all, gates, tok = scratch[:3]
    buf_x, buf_w, buf_g = scratch[5:8]
    out_x, out_w, out_g = [
        Spread(me, buf, recv, [s.at[i] for s in scratch[8:14]])
        for i, (buf, recv) in enumerate(((buf_x, x_ref), (buf_w, w_ref), (buf_g, g_ref)))
    ]
    scratch = scratch[14:]
    column = me.n_expert
    quarter = [range(i * column // 4, (i + 1) * column // 4) for i in range(4)]
    info_all[c, 0:2, :] = route_ref[...]
    info_all[c, 2:4, :] = slot_ref[...]
    info_all[c, 4:, :] = jnp.zeros((4, seq), jnp.int32)
    rows_in.share("info", info_all)
    tok[1, c] = cot_ref[...]
    rows_in.share(1, tok.at[1])
    rows = layer_in[...].astype(f32)
    attn_in[...] = (rows * row_scale(rows) * norm_attn[...]).astype(bf)
    rows_in.hots()
    buf_g[...] = rows_in.gather(1)
    out_g.send()
    for i, ref in enumerate((query, key, value)):
        attn_w[i].wait()
        ref[...] = dot_as(attn_in[...], weights[i * width : (i + 1) * width, :], NN).astype(bf)
    relative = lax.broadcasted_iota(jnp.int32, (heads, 2 * seq), 1) - seq
    bucket = bucket_of(relative)
    bias_of = jnp.zeros((heads, 2 * seq), f32)
    for n in range(buckets):
        bias_of = jnp.where(bucket == n, table_t[:, n : n + 1], bias_of)
    pair = 2 * width // heads
    low_half = lax.broadcasted_iota(jnp.int32, (seq, pair), 1) < pair // 2
    for n in range(heads // 2):
        lanes = slice(n * pair, (n + 1) * pair)
        k2, v2 = key[:, lanes], value[:, lanes]
        total = None
        for h in range(2):
            mine = low_half if h == 0 else ~low_half
            head = 2 * n + h
            line = jnp.broadcast_to(bias_of[head : head + 1, :], (seq, 2 * seq))
            bias = pltpu.roll(line, seq, 1, stride=1, stride_axis=0)[:, :seq]
            scores = dot_as(query[:, lanes], jnp.where(mine, k2, jnp.zeros_like(k2)), NT) + bias
            exponent = jnp.exp(scores - jnp.max(scores, axis=-1, keepdims=True))
            prob = exponent / jnp.sum(exponent, axis=-1, keepdims=True)
            probs[head] = prob
            term = dot_as(prob.astype(bf), jnp.where(mine, v2, jnp.zeros_like(v2)), NN)
            total = term if total is None else total + term
        context[:, lanes] = total.astype(bf)
        if n % 4 == 3:
            out_g.pass_on(quarter[n // 4])
    attn_w[3].wait()
    resid = rows + dot_as(context[...], weights[3 * width : 4 * width, :], NN)
    residual[...] = resid
    fetch = {}
    attn_saved = (query, key, value, probs, context, residual, attn_in)
    for n, j in enumerate((c, 1 - c)):
        for i, src in enumerate((wg_hbm, wu_hbm, wd_hbm)):
            dst = weights.at[pl.ds(pl.multiple_of((2 * i + j) * units, 16), units)]
            fetch[n, i] = pltpu.make_async_copy(src.at[j], dst, sem_w.at[n, i])
            fetch[n, i].start()
    moe_in = resid * row_scale(resid) * norm_moe[...]
    tok[0, c] = moe_in.astype(bf)
    rows_in.share(0, tok.at[0])
    logits = lax.dot_general(
        router_t[...], moe_in, (NT, ((), ())), preferred_element_type=f32, precision=highest
    )
    logits = jnp.exp(logits - jnp.max(logits, axis=0, keepdims=True))
    gate_prob = logits / jnp.sum(logits, axis=0, keepdims=True)
    expert_ids = lax.broadcasted_iota(jnp.int32, gate_prob.shape, 0)
    picked = [
        jnp.sum(jnp.where(route_ref[k : k + 1, :] == expert_ids, gate_prob, 0.0), axis=0, keepdims=True)
        for k in range(2)
    ]
    both = picked[0] + picked[1]
    for k in range(2):
        gates[c, k : k + 1, :] = picked[k] / both
    gates[c, 2:, :] = jnp.zeros((6, seq), f32)
    gate_out[...] = gates[c]
    rows_in.share("gates", gates)
    buf_x[...] = rows_in.gather(0)
    out_x.send()
    copies = [emit(5 + i, src, dst) for i, (src, dst) in enumerate(zip(attn_saved, attn_hbm))]
    out_g.pass_on(quarter[2])
    for e, tile in enumerate(rows_in.weights()):
        buf_w[e] = tile
    out_w.send()
    out_g.pass_on(quarter[3])
    out_g.cross(0)

    size = x_ref.shape[2]
    step = math.gcd(column, 8)
    chunk = step * size
    back = Back(
        me, lambda i: away.at[i],
        lambda i, block: own[i, pl.ds(pl.multiple_of(block * size, 8), size), :],
        q_out, *scratch[:4], scratch[4:],
    )

    def part(i, j):
        return weights[pl.ds(pl.multiple_of((2 * i + j) * units, 16), units), :]

    def flat(value):
        return value.reshape(chunk, value.shape[-1])

    def blocks(value):
        return value.reshape(step, size, value.shape[-1])

    def store(i, first, some, rows, value):
        if first:
            away[i, some] = blocks(value.astype(bf))
        else:
            own[i, rows, :] = value

    def each(start, count, body):
        @pl.loop(0, count // step)
        def _(n):
            at = start + n * step
            body(pl.ds(at, step), pl.ds(pl.multiple_of(at * size, 8), chunk))

    def forward(first, j, start, count):
        def body(some, rows):
            x = flat(x_ref[j, some])
            gate_pre = dot_as(x, part(0, j), NT)
            up_pre = dot_as(x, part(1, j), NT)
            hidden, active, lean = gated_terms(gate_pre, up_pre)
            act[j, rows, :] = active
            slope[j, rows, :] = lean
            hidden = hidden.astype(bf)
            hid_out[j, some] = blocks(hidden)
            store(0, first, some, rows, dot_as(hidden, part(2, j), NN))

        each(start, count, body)

    lane = lax.broadcasted_iota(jnp.int32, (size, 128), 1)
    row = lax.broadcasted_iota(jnp.int32, (size, 128), 0)

    def backward(first, j, start, count):
        def body(some, rows):
            tiles = w_ref[j, some]
            grad = []
            for n in range(step):
                line = jnp.broadcast_to(tiles[n, 0:1, :], (size, 128))
                weight = jnp.sum(jnp.where(lane == row, line, 0.0), axis=1, keepdims=True)
                grad.append(weight * g_ref[j, some.start + n].astype(f32))
            grad = jnp.concatenate(grad, axis=0).astype(bf)
            gr_out[j, some] = blocks(grad)
            grad_hidden = dot_as(grad, part(2, j), NT)
            dg = (grad_hidden * slope[j, rows, :]).astype(bf)
            du = (grad_hidden * act[j, rows, :]).astype(bf)
            dg_out[j, some] = blocks(dg)
            du_out[j, some] = blocks(du)
            store(1, first, some, rows, dot_as(dg, part(0, j), NN) + dot_as(du, part(1, j), NN))

        each(start, count, body)

    here = me.y * column
    away_ys = [back.ys[k] * column for k in range(1, me.ny)]
    shares = [back.order[i * column // 4 : (i + 1) * column // 4] for i in range(4)]
    out_x.pass_on(range(column))
    out_x.cross(0)
    for s in range(1, me.ny):
        out_g.cross(s)
    for i in range(3):
        fetch[0, i].wait()
    forward(False, c, here, column)
    for i in range(3):
        fetch[1, i].wait()
    out_w.pass_column()
    out_w.cross(0)
    for s in range(1, me.ny):
        out_x.cross(s)
    out_x.crossed[0].wait_recv()
    forward(True, 1 - c, here, column)
    back.to_mate(0, 0)
    for k in range(1, me.ny):
        out_x.crossed[k].wait_recv()
        forward(True, 1 - c, away_ys[k - 1], column)
        back.to_mate(0, k)
    for s in range(1, me.ny):
        out_w.cross(s)
    for k in range(1, me.ny):
        forward(False, c, away_ys[k - 1], column)
    back.along_y(0)
    out_g.arrive()
    out_w.arrive()
    for k in range(1, me.ny):
        backward(True, 1 - c, away_ys[k - 1], column)
        back.to_mate(1, k)
    back.finish(0, shares[0])
    for k in range(1, me.ny):
        backward(False, c, away_ys[k - 1], column)
    back.along_y(1)
    back.finish(0, shares[1])
    backward(True, 1 - c, here, column)
    back.to_mate(1, 0)
    back.finish(0, shares[2])
    backward(False, c, here, column)
    saved = ((x_ref, x_hbm), (hid_out, hid_hbm), (dg_out, dg_hbm), (du_out, du_hbm), (gr_out, gr_hbm))
    copies += [emit(i, src, dst) for i, (src, dst) in enumerate(saved)]
    back.finish(0, shares[3])
    back.across(0)
    back.finish(1, back.order)
    back.across(1)
    back.close()
    for copy in copies:
        copy.wait()
    for payload in (out_x, out_w, out_g):
        payload.close()
    rows_in.close()


def layer(sizes, micro, cap, layer_in, norms, table_t, router_t, places, cot, attn_w, expert_w):
    n_expert, ny, per_core = sizes[0], sizes[1] // 2, micro * cap
    seq, width = cot.shape
    units = expert_w[0].shape[1]
    heads = table_t.shape[0]
    count, size = ny * n_expert, 2 * per_core
    bf, f32 = jnp.bfloat16, jnp.float32
    any_space = pl.BlockSpec(memory_space=pl.ANY)
    inner = jax.ShapeDtypeStruct((2, count, size, units), bf)
    outer = jax.ShapeDtypeStruct((2, count, size, width), bf)
    low, full = jax.ShapeDtypeStruct((seq, width), bf), jax.ShapeDtypeStruct((seq, width), f32)
    return pl.pallas_call(
        functools.partial(layer_kernel, sizes, (micro, cap, per_core)),
        out_shape=(
            jax.ShapeDtypeStruct((2, 2, n_expert, size, width), bf), outer, inner, inner, inner, outer,
            low, low, low, jax.ShapeDtypeStruct((heads, seq, seq), f32), low, full, low,
            jax.ShapeDtypeStruct((8, seq), f32),
        ),
        in_specs=[VMEM] * 8 + [any_space] * 7,
        out_specs=(VMEM,) + (any_space,) * 12 + (VMEM,),
        scratch_shapes=[
            pltpu.VMEM((seq, width), bf),
            pltpu.VMEM((seq, width), bf),
            pltpu.VMEM((seq, width), bf),
            pltpu.VMEM((heads, seq, seq), f32),
            pltpu.VMEM((seq, width), bf),
            pltpu.VMEM((seq, width), f32),
            pltpu.VMEM((seq, width), bf),
            pltpu.VMEM(outer.shape, bf),
            pltpu.VMEM(inner.shape, bf),
            pltpu.VMEM(inner.shape, bf),
            pltpu.VMEM(inner.shape, bf),
            pltpu.VMEM(outer.shape, bf),
            pltpu.VMEM((2, count, size, width), bf),
            pltpu.VMEM((2, count, 8, 128), f32),
            pltpu.VMEM((max(4 * width, 6 * units), width), bf),
            pltpu.VMEM((2, count * size, units), f32),
            pltpu.VMEM((2, count * size, units), f32),
            pltpu.VMEM((2, count, size, width), bf),
            pltpu.VMEM((2, count * size, width), f32),
            DMA((4,)),
            DMA((2, 3)),
            DMA((12,)),
        ]
        + rows_scratch(sizes, per_core, seq, width)
        + spread_sems(sizes)
        + back_scratch(sizes, size, width),
        name="layer",
        compiler_params=pltpu.CompilerParams(
            collective_id=4, has_side_effects=True, vmem_limit_bytes=60 << 20
        ),
    )(layer_in, *norms, table_t, router_t, *places, cot, *attn_w, *expert_w)


def finish_kernel(small, sums_hbm, x_hbm, h_hbm, dg_hbm, du_hbm, gr_hbm, *refs):
    outs, (router_out, attn_out, moe_out, table_out) = refs[:7], refs[7:11]
    sums, x, h, dg, du, gr, stage, wide, sem_sum, sem_in, sem_out, sem_wide = refs[11:]
    rows = stage.shape[1]
    width = sums.shape[1]
    units = h.shape[2]
    loads = {}

    def load(key, src, dst, sem):
        loads[key] = pltpu.make_async_copy(src, dst, sem)
        loads[key].start()

    def load_sums(keys):
        for n in keys:
            part = n * rows // width, pl.ds(n * rows % width, rows)
            load(("sums", n), sums_hbm.at[part], sums.at[part], sem_sum.at[n])

    casts = range(4 * width // rows)
    load_sums(casts[:4])
    for i, (key, src, dst) in enumerate(
        (("dg", dg_hbm, dg), ("x", x_hbm, x), ("du", du_hbm, du), ("h", h_hbm, h), ("gr", gr_hbm, gr))
    ):
        for j in range(2):
            load((key, j), src.at[j], dst.at[j], sem_in.at[i, j])
    load_sums(casts[4:])
    experts = router_out.shape[0]
    router_out[...] = small[:experts]
    attn_out[...] = small[experts : experts + 1]
    moe_out[...] = small[experts + 1 : experts + 2]
    table_out[...] = small[experts + 8 : experts + 8 + table_out.shape[0], : table_out.shape[1]]

    def need(key):
        if key in loads:
            loads.pop(key).wait()

    jobs = []
    products = [
        (left, right, out, j)
        for left, right, out in ((("dg", dg), ("x", x), 4), (("du", du), ("x", x), 5), (("h", h), ("gr", gr), 6))
        for j in range(2)
    ]
    casts = list(casts)
    every = max(1, len(casts) // len(products))
    while casts or products:
        jobs += casts[:every]
        casts = casts[every:]
        jobs += products[:1]
        products = products[1:]
    flying = {}
    counts = [0, 0]
    for job in jobs:
        product = not isinstance(job, int)
        box, sem = (wide, sem_wide) if product else (stage, sem_out)
        slot = counts[product] % box.shape[0]
        counts[product] += 1
        if (product, slot) in flying:
            flying[product, slot].wait()
        if product:
            (left_key, left), (right_key, right), out, j = job
            need((left_key, j))
            need((right_key, j))
            box[slot] = dot_as(left[j], right[j], TN)
            dst = outs[out].at[j]
        else:
            need(("sums", job))
            m, r = job * rows // width, job * rows % width
            box[slot] = sums[m, r : r + rows, :].astype(jnp.float32)
            dst = outs[m].at[pl.ds(r, rows)]
        flying[product, slot] = pltpu.make_async_copy(box.at[slot], dst, sem.at[slot])
        flying[product, slot].start()
    for copy in flying.values():
        copy.wait()


def finish(sums, small, x, h, dg, du, gr, experts, table):
    f32 = jnp.float32
    width = sums.shape[1]
    units = h.shape[2]
    any_space = pl.BlockSpec(memory_space=pl.ANY)
    return pl.pallas_call(
        finish_kernel,
        out_shape=(jax.ShapeDtypeStruct((width, width), f32),) * 4
        + (jax.ShapeDtypeStruct((2, units, width), f32),) * 3
        + tuple(jax.ShapeDtypeStruct(a, f32) for a in ((experts, width), (1, width), (1, width), table)),
        in_specs=[VMEM] + [any_space] * 6,
        out_specs=(any_space,) * 7 + (VMEM,) * 4,
        scratch_shapes=[pltpu.VMEM(a.shape, a.dtype) for a in (sums, x, h, dg, du, gr)]
        + [pltpu.VMEM((4, 256, width), f32), pltpu.VMEM((2, units, width), f32)]
        + [DMA((4 * width // 256,)), DMA((5, 2)), DMA((4,)), DMA((2,))],
        name="finish",
        compiler_params=pltpu.CompilerParams(vmem_limit_bytes=60 << 20),
    )(small, sums, x, h, dg, du, gr)


def upright(line):
    n = line.shape[1]
    square = lax.broadcasted_iota(jnp.int32, (n, n), 0) == lax.broadcasted_iota(jnp.int32, (n, n), 1)
    return jnp.sum(jnp.where(square, jnp.broadcast_to(line, (n, n)), 0.0), axis=1, keepdims=True)


def flat_line(column):
    n = column.shape[0]
    square = lax.broadcasted_iota(jnp.int32, (n, n), 0) == lax.broadcasted_iota(jnp.int32, (n, n), 1)
    return jnp.sum(jnp.where(square, jnp.broadcast_to(column, (n, n)), 0.0), axis=0, keepdims=True)


def diagonals(values):
    n = values.shape[1]
    total = None
    for first in range(0, n, 8):
        wide = jnp.concatenate([values[first : first + 8, :], jnp.zeros((8, n), jnp.float32)], axis=1)
        wide = pltpu.roll(wide, n - first, 1)
        total = wide if total is None else total + wide
    row = lax.broadcasted_iota(jnp.int32, total.shape, 0)
    for bit in (1, 2, 4):
        total = jnp.where((row & bit) > 0, pltpu.roll(total, 2 * n - bit, 1), total)
    return jnp.sum(total, axis=0, keepdims=True)


def settle_kernel(
    sizes, rows_per, pieces,
    back_hbm, route_ref, slot_ref, gate_ref, *inputs_hbm_and_rest,
):
    inputs_hbm, rest = inputs_hbm_and_rest[:9], inputs_hbm_and_rest[9:]
    settle_body(sizes, rows_per, pieces, (back_hbm, *inputs_hbm), route_ref, slot_ref, gate_ref, *rest)


def settle_body(
    sizes, rows_per, pieces, inputs_hbm, route_ref, slot_ref, gate_ref, norm_attn, norm_moe, router_t, wq_hbm, wk_hbm, wv_hbm, wo_hbm,
    layer_out, grad_in, out_hbm, small_out,
    back_ref, cot_ref, layer_in, residual, context, attn_in, query, key, value, probs, sem_l,
    weights, sem_a, left_ref, right_ref, small_ref, lines, out, sem_out, buf_a, buf_b, acc, *boxes,
):
    bf, f32 = jnp.bfloat16, jnp.float32
    micro, cap, per_core = rows_per
    inputs = (back_ref, cot_ref, layer_in, residual, context, attn_in, query, key, value, probs)
    loads = {}
    for i in (5, 4, 0, 1, 3, 8, 9, 6, 7, 2):
        loads[i] = pltpu.make_async_copy(inputs_hbm[i], inputs[i], sem_l.at[i])
        loads[i].start()

    def need(*which):
        for i in which:
            loads[i].wait()

    attn_w = []
    for i, src in ((3, wo_hbm), (0, wq_hbm), (1, wk_hbm), (2, wv_hbm)):
        attn_w.append(pltpu.make_async_copy(src, weights.at[i], sem_a.at[i]))
        attn_w[-1].start()
    me = Place(*sizes)
    c, mate = me.c, me.at(c=1 - me.c)
    n = me.nx
    seq = right_ref.shape[1]
    total_rows = width = out.shape[1]
    is0 = c == 0
    pair = jnp.where(is0, me.x, me.y)
    other = jnp.where(is0, me.y, me.x)
    lo, hi, nh = pair % 2, pair // 2, n // 2

    def along(pair_at, other_at, z=None):
        return me.at(x=jnp.where(is0, pair_at, other_at), y=jnp.where(is0, other_at, pair_at), z=z)

    flip_x, flip_y = me.x + 1 - 2 * (me.x % 2), me.y + 1 - 2 * (me.y % 2)
    dims = [
        (n, other, lambda q: along(pair, q)),
        (nh, hi, lambda q: along(q * 2 + lo, other)),
        (2, me.z % 2, lambda q: me.at(z=me.z // 2 * 2 + q)),
        (me.nz // 2, me.z // 2, lambda q: me.at(z=q * 2 + me.z % 2)),
    ]
    parts, gots = boxes[:4], boxes[4:8]
    half, small_half, small_got, fs, fr, os, ps, pr, gs, gr, ms, mr, cs, cr, ss, sr = boxes[8:]
    levels = [i for i, d in enumerate(dims) if d[0] > 1]
    x_peers = [me.at(x=(me.x + k) % n) for k in range(1, n)]
    y_peers = [me.at(y=(me.y + k) % n) for k in range(1, n)]
    z_peers = [me.at(z=(me.z + k) % me.nz) for k in range(1, me.nz)]
    greet(
        [mate, me.at(x=flip_x, c=1 - c), me.at(y=flip_y, c=1 - c)] + x_peers + y_peers + z_peers
    )

    def slot_a(slot):
        return buf_a.at[pl.ds(pl.multiple_of(slot * seq, seq), seq), :]

    def slot_b(slot):
        return buf_b.at[pl.ds(pl.multiple_of(slot * seq, seq), seq), :]

    need(5, 4)
    left_ref[0] = attn_in[...]
    left_ref[1] = context[...]
    targets = [
        (mate, 1 - c, other % 2, c),
        (me.at(x=flip_x, c=0), 0, flip_x % 2, 2 + c),
        (me.at(y=flip_y, c=1), 1, flip_y % 2, 2 + c),
    ]
    factor = []
    for i, (device, role, parity, slot) in enumerate(targets):
        a = jnp.where(role == 0, 0, parity)
        factor.append(remote(left_ref.at[a], slot_a(slot), fs.at[i, 0], fr.at[slot, 0], device))
    own = [pltpu.make_async_copy(left_ref.at[jnp.where(is0, 0, lo)], slot_a(c), os.at[0])]
    own[0].start()

    size = 2 * per_core
    group = lax.broadcasted_iota(jnp.int32, (1, seq), 1) // (seq // micro)
    slot_ids = lax.broadcasted_iota(jnp.int32, (2 * me.n_expert * size, seq), 0)
    hots = []
    for k in range(2):
        route, slot = route_ref[k : k + 1, :], slot_ref[k : k + 1, :]
        place = (route % 2) * (me.n_expert * size) + (route // 2) * size + c * per_core + group * cap + slot
        hots.append(jnp.where(slot_ids == jnp.where(slot >= 0, place, -1), 1.0, 0.0))
    low = [h.astype(bf) for h in hots] + [(hots[0] + hots[1]).astype(bf)]
    half_slots = me.n_expert * size

    def picked(hot, which):
        total = None
        for j in range(2):
            rows = back_ref[which, j].reshape(half_slots, width)
            term = dot_as(hot[j * half_slots : (j + 1) * half_slots, :], rows, TN)
            total = term if total is None else total + term
        return total

    need(0, 1, 3)
    cot = cot_ref[...].astype(f32)
    resid = residual[...]
    chosen = [picked(low[k], 0) for k in range(2)]
    gate = [upright(gate_ref[k : k + 1, :]) for k in range(2)]
    layer_out[...] = (resid + (gate[0] * chosen[0] + gate[1] * chosen[1])).astype(bf)
    grad_gate = [jnp.sum(cot * chosen[k], axis=-1, keepdims=True) for k in range(2)]
    mean_grad = gate[0] * grad_gate[0] + gate[1] * grad_gate[1]
    logit = [gate[k] * (grad_gate[k] - mean_grad) for k in range(2)]
    experts = router_t.shape[0]
    by_token, by_expert = None, None
    for k in range(2):
        route = route_ref[k : k + 1, :]
        line = jnp.where(
            lax.broadcasted_iota(jnp.int32, (experts, seq), 0) == route, flat_line(logit[k]), 0.0
        )
        by_expert = line if by_expert is None else by_expert + line
        route_up = upright(route.astype(f32)).astype(jnp.int32)
        line = jnp.where(
            lax.broadcasted_iota(jnp.int32, (seq, experts), 1) == route_up, logit[k], 0.0
        )
        by_token = line if by_token is None else by_token + line

    def exact(left, right):
        return lax.dot_general(
            left, right, (NN, ((), ())), preferred_element_type=f32, precision=highest
        )

    scale = row_scale(resid)
    normed = resid * scale
    small_ref[:experts] = exact(by_expert, normed * norm_moe[...])
    grad_moe = picked(low[2], 1) + exact(by_token, router_t[...])
    small_ref[experts:] = jnp.zeros((small_ref.shape[0] - experts, width), f32)
    small_ref[experts + 1 : experts + 2] = jnp.sum(grad_moe * normed, axis=0, keepdims=True)
    grad_n = grad_moe * norm_moe[...]
    grad_resid = cot + scale * (grad_n - normed * jnp.mean(grad_n * normed, axis=-1, keepdims=True))
    right_ref[3] = grad_resid.astype(bf)
    grad_in[...] = grad_resid
    attn_w[0].wait()
    grad_context = dot_as(right_ref[3], weights[3], NT).astype(bf)

    need(8, 9, 6, 7, 2)
    heads = probs.shape[0]
    pair_lanes = 2 * width // heads
    low_half = lax.broadcasted_iota(jnp.int32, (seq, pair_lanes), 1) < pair_lanes // 2
    for n2 in range(heads // 2):
        lanes = slice(n2 * pair_lanes, (n2 + 1) * pair_lanes)
        sums = [None, None, None]
        for h in range(2):
            mine = low_half if h == 0 else ~low_half
            head = 2 * n2 + h

            def only(value):
                return jnp.where(mine, value, jnp.zeros_like(value))

            prob = probs[head]
            grad_c = only(grad_context[:, lanes])
            grad_p = dot_as(grad_c, value[:, lanes], NT)
            grad_s = prob * (grad_p - jnp.sum(prob * grad_p, axis=-1, keepdims=True))
            lines[head : head + 1, :] = diagonals(grad_s)
            grad_s = grad_s.astype(bf)
            terms = (
                dot_as(grad_s, only(key[:, lanes]), NN),
                dot_as(grad_s, only(query[:, lanes]), TN),
                dot_as(prob.astype(bf), grad_c, TN),
            )
            sums = [t if s is None else s + t for s, t in zip(sums, terms)]
        for i in range(3):
            right_ref[i, :, lanes] = sums[i].astype(bf)
    for i, (device, role, parity, slot) in enumerate(targets):
        factor.append(
            remote(right_ref.at[role * 2 + parity], slot_b(slot), fs.at[i, 1], fr.at[slot, 1], device)
        )
    own.append(pltpu.make_async_copy(right_ref.at[c * 2 + lo], slot_b(c), os.at[1]))
    own[1].start()
    buckets = 32
    bucket = bucket_of(lax.broadcasted_iota(jnp.int32, (2 * seq, buckets), 0) - seq)
    hot = jnp.where(bucket == lax.broadcasted_iota(jnp.int32, (2 * seq, buckets), 1), 1.0, 0.0)
    small_ref[experts + 8 : experts + 8 + heads, :buckets] = exact(lines[...], hot)
    grad_attn = None
    for i in range(3):
        attn_w[1 + i].wait()
        term = dot_as(right_ref[i], weights[i], NT)
        grad_attn = term if grad_attn is None else grad_attn + term
    rows = layer_in[...].astype(f32)
    scale = row_scale(rows)
    normed = rows * scale
    small_ref[experts : experts + 1] = jnp.sum(grad_attn * normed, axis=0, keepdims=True)
    grad_n = grad_attn * norm_attn[...]
    grad_in[...] += scale * (grad_n - normed * jnp.mean(grad_n * normed, axis=-1, keepdims=True))

    rows_s = half.shape[0]
    small = [remote(small_ref.at[pl.ds((1 - c) * rows_s, rows_s)], half, ss.at[0], sr.at[0], mate)]
    small_dims = [
        (n, me.x, lambda q: me.at(x=q)),
        (n, me.y, lambda q: me.at(y=q)),
        (me.nz, me.z, lambda q: me.at(z=q)),
    ]
    small_wait = [small[0]]
    small_slot = [1]

    def small_step(step):
        for copy in small_wait:
            copy.wait_recv()
        small_wait.clear()
        if step == 0:
            total = small_ref[pl.ds(c * rows_s, rows_s)] + half[...]
        elif step <= 3:
            total = small_got[step - 1, 0]
            for k in range(1, small_dims[step - 1][0]):
                total = total + small_got[step - 1, k]
        if step < 3:
            count, index, peer = small_dims[step]
            small_half[step] = total
            small_got[step, index] = total
            for k in range(1, count):
                small_wait.append(
                    remote(
                        small_half.at[step], small_got.at[step, index], ss.at[small_slot[0]],
                        sr.at[small_slot[0]], peer((index + k) % count),
                    )
                )
                small_slot[0] += 1
        elif step == 3:
            small_out[pl.ds(c * rows_s, rows_s)] = total
            block = small_out.at[pl.ds(c * rows_s, rows_s)]
            small_wait.append(
                remote(block, block, ss.at[small_slot[0]], sr.at[small_slot[0]], mate)
            )
        small.extend(small_wait)

    for where in (1 - c, 2, 3):
        for i, (src, dst) in enumerate(((left_ref, slot_a(where)), (right_ref, slot_b(where)))):
            pltpu.make_async_remote_copy(
                src_ref=src.at[0], dst_ref=dst, send_sem=fs.at[0, i], recv_sem=fr.at[where, i],
                device_id=mate, device_id_type=MESH,
            ).wait_recv()
    for copy in own:
        copy.wait()

    rows_k = total_rows // pieces
    matrix = c * 2 + lo
    pending, written = {}, []

    def multiply(k):
        acc[k] = lax.dot_general(
            buf_a[:, k * rows_k : (k + 1) * rows_k], buf_b[...], (TN, ((), ())),
            preferred_element_type=jnp.float32,
        )
        push(k, 0, rows_k)

    def push(k, at, rows):
        level = levels[at]
        count, index, peer = dims[level]
        size = rows // count
        copies = []
        for s in range(1, count):
            to = (index + s) % count
            parts[level][k, s - 1] = acc[k, pl.ds(pl.multiple_of(to * size, 16), size), :].astype(jnp.bfloat16)
            copies.append(
                remote(
                    parts[level].at[k, s - 1], gots[level].at[k, s - 1],
                    ps.at[level, k, s - 1], pr.at[level, k, s - 1], peer(to),
                )
            )
        pending["push", at, k] = copies

    def rows_at(at):
        rows = rows_k
        for i in range(at):
            rows //= dims[levels[i]][0]
        return rows

    def add(k, at):
        level = levels[at]
        count, index, _ = dims[level]
        size = rows_at(at) // count
        for copy in pending["push", at, k]:
            copy.wait_recv()
        total = acc[k, pl.ds(pl.multiple_of(index * size, 16), size), :]
        for s in range(1, count):
            total = total + gots[level][k, s - 1].astype(jnp.float32)
        if at + 1 < len(levels):
            acc[k, :size, :] = total
            push(k, at + 1, size)
        else:
            out[matrix, pl.ds(offset(k, at), size), :] = total.astype(jnp.bfloat16)
            share(k, at)

    def offset(k, at):
        start, rows = k * rows_k, rows_k
        for i in range(at + 1):
            count, index, _ = dims[levels[i]]
            rows //= count
            start = start + index * rows
        return pl.multiple_of(start, 16)

    def share(k, at):
        level = levels[at]
        count, index, peer = dims[level]
        size = rows_at(at) // count
        block = out.at[matrix, pl.ds(offset(k, at), size), :]
        pending["share", at, k] = [
            remote(block, block, gs.at[level, k, s - 1], gr.at[level, k, s - 1], peer((index + s) % count))
            for s in range(1, count)
        ]

    def shared(k, at):
        for copy in pending["share", at, k]:
            copy.wait_recv()
        if at:
            share(k, at - 1)
        else:
            block = out.at[matrix, pl.ds(k * rows_k, rows_k), :]
            pending["mate", k] = remote(
                block, block, ms.at[k], mr.at[k], along(pair + 1 - 2 * lo, other)
            )

    def across(k):
        pending["mate", k].wait_recv()
        block = out.at[pl.ds(2 * c, 2), pl.ds(k * rows_k, rows_k), :]
        pending["core", k] = remote(block, block, cs.at[k], cr.at[k], mate)
        write(k, c)

    def write(k, core):
        part = pl.ds(2 * core, 2), pl.ds(k * rows_k, rows_k), slice(None)
        written.append(pltpu.make_async_copy(out.at[part], out_hbm.at[part], sem_out.at[core, k]))
        written[-1].start()

    def close(k):
        pending["core", k].wait_recv()
        write(k, 1 - c)

    steps = [multiply]
    steps += [functools.partial(add, at=i) for i in range(len(levels))]
    steps += [functools.partial(shared, at=i) for i in reversed(range(len(levels)))]
    events = sorted((0 if p == 0 else p + k, p, k) for p in range(len(steps)) for k in range(pieces))
    before = 0
    for t, p, k in events:
        if before < t <= 5:
            small_step(t - 1)
        before = t
        steps[p](k)
    for k in range(pieces):
        across(k)
    for k in range(pieces):
        close(k)
    for copy in factor + small:
        copy.wait_send()
    for copies in pending.values():
        for copy in copies if isinstance(copies, list) else [copies]:
            copy.wait_send()
    for copy in written:
        copy.wait()


def settle(sizes, micro, cap, arrays, norms, router_t, attn_w):
    n_expert, n_dp = sizes
    nz = math.gcd(n_expert, 4)
    n = n_expert // nz
    nh = n // 2
    assert n == n_dp // 2
    seq, width = arrays[5].shape
    heads = arrays[12].shape[0]
    splits = [n, nh, 2, nz // 2]
    pieces = max(1, min(8, width // (16 * math.prod(splits))))
    rows_k = width // pieces
    bf, f32 = jnp.bfloat16, jnp.float32
    small_rows = router_t.shape[0] + 8 + heads
    small_rows += -small_rows % 16
    rows_s = small_rows // 2
    sizes_at = [rows_k // math.prod(splits[: i + 1]) for i in range(4)]
    counts = [max(q - 1, 1) for q in splits]
    most = max(counts)
    boxes = [
        pltpu.VMEM((pieces, q, s if k > 1 else 16, width), bf) for q, s, k in zip(counts, sizes_at, splits)
    ]
    smalls = 2 * n + nz
    any_space = pl.BlockSpec(memory_space=pl.ANY)
    return pl.pallas_call(
        functools.partial(settle_kernel, sizes, (micro, cap, micro * cap), pieces),
        out_shape=(
            jax.ShapeDtypeStruct((seq, width), bf),
            jax.ShapeDtypeStruct((seq, width), f32),
            jax.ShapeDtypeStruct((4, width, width), bf),
            jax.ShapeDtypeStruct((small_rows, width), f32),
        ),
        in_specs=[any_space] + [VMEM] * 3 + [any_space] * 9 + [VMEM] * 3 + [any_space] * 4,
        out_specs=(VMEM, VMEM, any_space, VMEM),
        scratch_shapes=[pltpu.VMEM(a.shape, a.dtype) for a in (arrays[0], *arrays[4:])]
        + [
            DMA((10,)),
            pltpu.VMEM((4, width, width), bf),
            DMA((4,)),
            pltpu.VMEM((2, seq, width), bf),
            pltpu.VMEM((4, seq, width), bf),
            pltpu.VMEM((small_rows, width), f32),
            pltpu.VMEM((heads, 2 * seq), f32),
            pltpu.VMEM((4, width, width), bf),
            DMA((2, pieces)),
            pltpu.VMEM((4 * seq, width), bf),
            pltpu.VMEM((4 * seq, width), bf),
            pltpu.VMEM((pieces, rows_k, width), f32),
            *boxes,
            *boxes,
            pltpu.VMEM((rows_s, width), f32),
            pltpu.VMEM((3, rows_s, width), f32),
            pltpu.VMEM((3, max(n, nz), rows_s, width), f32),
            DMA((3, 2)),
            DMA((4, 2)),
            DMA((2,)),
            DMA((4, pieces, most)),
            DMA((4, pieces, most)),
            DMA((4, pieces, most)),
            DMA((4, pieces, most)),
            DMA((pieces,)),
            DMA((pieces,)),
            DMA((pieces,)),
            DMA((pieces,)),
            DMA((smalls,)),
            DMA((smalls,)),
        ],
        name="settle",
        compiler_params=pltpu.CompilerParams(
            collective_id=3, has_side_effects=True, vmem_limit_bytes=58 << 20
        ),
    )(*arrays, *norms, router_t, *attn_w)


def rms_scale(values):
    return lax.rsqrt(jnp.mean(values * values, axis=-1, keepdims=True) + epsilon)


def bucket_hot(seq_len, buckets):
    position = jnp.arange(seq_len, dtype=jnp.int32)
    bucket_ids = jnp.arange(buckets, dtype=jnp.int32)
    bucketed = bucket_of(position[None, :] - position[:, None])
    return (bucketed[None, :, :] == bucket_ids[:, None, None]).astype(jnp.float32)


def dot32(pattern, left, right):
    return jnp.einsum(pattern, left, right, preferred_element_type=jnp.float32)


def shards(
    layer_in, routes, queue_slots, norm_attn, w_query, w_key, w_value, w_out, rel_table,
    norm_moe, router, w_gate, w_up, w_down, cotangent,
):
    bf, f32 = jnp.bfloat16, jnp.float32
    seq_len, width = layer_in.shape
    buckets, heads = rel_table.shape
    expert_count = router.shape[1]
    sizes = (lax.axis_size("expert"), lax.axis_size("dp"))
    n_expert, n_dp = sizes
    assert w_gate.shape[0] == 2 and expert_count == 2 * n_expert
    group_len = seq_len // MICRO
    capacity = (5 * group_len + 2 * expert_count - 1) // (2 * expert_count)
    split_heads = (seq_len, heads, width // heads)
    places = (routes.T, queue_slots.T)
    expert_w = [jnp.swapaxes(w_gate, 1, 2), jnp.swapaxes(w_up, 1, 2), w_down]
    slots = n_dp // 2 * n_expert * 2 * MICRO * capacity
    fused = 2 * slots * width * 20 + 6 * w_gate.size < 52 << 20
    if fused:
        (
            back, rows_in, hidden, gate_grad, up_grad, grad_rows,
            query, key, value, probs, context, residual, attn_in, gates,
        ) = layer(
            sizes, MICRO, capacity, layer_in, (norm_attn[None], norm_moe[None]), rel_table.T, router.T,
            places, cotangent, (w_query, w_key, w_value, w_out), expert_w,
        )
    else:
        layer_rows = layer_in.astype(f32)
        attn_in = (layer_rows * rms_scale(layer_rows) * norm_attn).astype(bf)
        query = dot32("sd,de->se", attn_in, w_query).astype(bf)
        key = dot32("sd,de->se", attn_in, w_key).astype(bf)
        value = dot32("sd,de->se", attn_in, w_value).astype(bf)
        one_hot = bucket_hot(seq_len, buckets)
        bias = jnp.einsum("bij,bh->hij", one_hot, rel_table, precision=highest)
        scores = dot32("ihd,jhd->hij", query.reshape(split_heads), key.reshape(split_heads)) + bias
        exponent = jnp.exp(scores - jnp.max(scores, axis=-1, keepdims=True))
        probs = exponent / jnp.sum(exponent, axis=-1, keepdims=True)
        context = dot32("hij,jhd->ihd", probs.astype(bf), value.reshape(split_heads))
        context = context.astype(bf).reshape(seq_len, width)
        residual = layer_rows + dot32("se,ed->sd", context, w_out)
        moe_in = residual * rms_scale(residual) * norm_moe
        expert_ids = jnp.arange(expert_count, dtype=jnp.int32)
        first_hot = (routes[:, 0:1] == expert_ids).astype(f32)
        second_hot = (routes[:, 1:2] == expert_ids).astype(f32)
        gate_prob = jax.nn.softmax(jnp.dot(moe_in, router, precision=highest), axis=-1)
        prob_first, prob_second = jnp.sum(gate_prob * first_hot, axis=-1), jnp.sum(gate_prob * second_hot, axis=-1)
        gates = jnp.stack([prob_first, prob_second]) / (prob_first + prob_second)
        gates = jnp.pad(gates, ((0, 6), (0, 0)))
        info = jnp.concatenate([*places, jnp.zeros((4, seq_len), jnp.int32)])
        rows_in, weight_in, grad_in = spread(
            sizes, MICRO, capacity, info, moe_in.astype(bf), cotangent, gates
        )
        blocks = rows_in.shape[:-1] + (-1,)
        rows_in, grad_in = [a.reshape(2, -1, width) for a in (rows_in, grad_in)]
        slot_weight = weight_in[:, :, 0, : 2 * MICRO * capacity].reshape(2, -1, 1)
        grad_rows = (slot_weight * grad_in.astype(f32)).astype(bf)
        gate_pre = dot32("jrd,jdf->jrf", rows_in, w_gate)
        up_pre = dot32("jrd,jdf->jrf", rows_in, w_up)
        hidden, active, lean = gated_terms(gate_pre, up_pre)
        hidden = hidden.astype(bf)
        partial_out = dot32("jrf,jfd->jrd", hidden, w_down).astype(bf)
        hidden_grad = dot32("jrd,jfd->jrf", grad_rows, w_down)
        gate_grad, up_grad = (hidden_grad * lean).astype(bf), (hidden_grad * active).astype(bf)
        rows_grad = dot32("jrf,jdf->jrd", gate_grad, w_gate) + dot32("jrf,jdf->jrd", up_grad, w_up)
        back = gather_back(sizes, partial_out.reshape(blocks), rows_grad.astype(bf).reshape(blocks))
    layer_out, grad_input, sums, small = settle(
        sizes, MICRO, capacity,
        (back, *places, gates, cotangent, layer_in, residual, context, attn_in, query, key, value, probs),
        (norm_attn[None], norm_moe[None]), router.T, (w_query, w_key, w_value, w_out),
    )
    rows_in, hidden, gate_grad, up_grad, grad_rows = [
        a.reshape(2, -1, a.shape[-1]) for a in (rows_in, hidden, gate_grad, up_grad, grad_rows)
    ]
    (
        *matrices, grad_w_gate, grad_w_up, grad_w_down,
        grad_router, grad_norm_attn, grad_norm_moe, grad_table,
    ) = finish(
        sums, small, rows_in, hidden, gate_grad, up_grad, grad_rows, expert_count, (heads, buckets)
    )
    return (
        layer_out, grad_input, grad_norm_attn.reshape(width), *matrices, grad_table.T,
        grad_norm_moe.reshape(width), grad_router.T,
        jnp.swapaxes(grad_w_gate, 1, 2), jnp.swapaxes(grad_w_up, 1, 2), grad_w_down,
    )


def solution(mesh):
    in_specs = (
        P(("expert", "dp"), None),
        P(("expert", "dp"), None),
        P(("expert", "dp"), None),
        P(),
        P(),
        P(),
        P(),
        P(),
        P(),
        P(),
        P(),
        P("expert", None, "dp"),
        P("expert", None, "dp"),
        P("expert", "dp", None),
        P(("expert", "dp"), None),
    )
    out_specs = (
        P(("expert", "dp"), None),
        P(("expert", "dp"), None),
        P(),
        P(),
        P(),
        P(),
        P(),
        P(),
        P(),
        P(),
        P("expert", None, "dp"),
        P("expert", None, "dp"),
        P("expert", "dp", None),
    )
    return jax.shard_map(shards, mesh=mesh, in_specs=in_specs, out_specs=out_specs, check_vma=False)
```
